32 devices in a mesh: corr: 8 (over z, x), tm: 4 (over y, core).
Axes of the slice: x: 2, y: 2, z: 4, core: 2. Of those that a mesh axis runs over, the one named last changes fastest.
Arguments:
- flows: bfloat16 [2, 96, 8192], P(None, 'tm', 'corr'), may hold values from 0.049804688 to 2
- counts: float32 [2, 96, 8192], P(None, 'tm', 'corr'), may hold values from 0.5 to 4
- local_blocks: bfloat16 [512, 128, 128], P('corr'), may hold values from 0 to 0.00390625
- local_path: int32 [512], P('corr'), may hold values from 0 to 7
- local_link: int32 [512], P('corr'), may hold values from 0 to 7
- local_lag: int32 [512], P('corr'), may hold values from 0 to 15
- remote_blocks: bfloat16 [512, 128, 128], P('corr'), may hold values from 0 to 0.00390625
- remote_path: int32 [512], P('corr'), may hold values from 0 to 7
- remote_link: int32 [512], P('corr'), may hold values from 0 to 7
- remote_lag: int32 [512], P('corr'), may hold values from 0 to 15
- remote_slot: int32 [512], P('corr'), may hold values from 0 to 79, as said below
Outputs:
- link_residual: float32 [2, 96, 8192], P(None, 'tm', 'corr')
- gradient: float32 [2, 96, 8192], P(None, 'tm', 'corr')
- new_flows: float32 [2, 96, 8192], P(None, 'tm', 'corr')
The draws below stay inside these ranges and needn't reach their ends.
Inputs may be any that keep to these rules, and one draw needn't show every extreme that they name: remote_slot // 10 is the corridor that owns the block's links and never the block's own corridor; the slots of one corridor's remote blocks are distinct.
All inputs are finite; a program needn't handle non-finite values.
Results may differ from the reference program's by a relative error of at most 0.0003.
Values may be sent and summed in bfloat16 or wider, within the bound.
No kernel may reach another device: no remote copies, remote signals or barrier semaphores. Data moves between devices by JAX's collectives and lax.ppermute only.
A program may use at most 64 MiB of HBM per device.

```python
import math
import jax
import jax.numpy as jnp
from jax import lax

BLOCK = 128
PATH_BLOCKS = 8
LOCAL_BLOCKS = 64
REMOTE_BLOCKS = 64
SLOT_CAP = 10
DAYS = 2
MINUTES = 96
LAGS = 16
PATHS = 8192
LINKS = 8192
N_CORR = 8


def draw_remote_slot(key, part):

    def corridor_slots(corridor):
        order = jax.random.permutation(jax.random.fold_in(key, corridor), N_CORR - 1).astype(jnp.int32)
        index = jnp.arange(REMOTE_BLOCKS, dtype=jnp.int32)
        offset = jnp.take(order, index % (N_CORR - 1))
        owner = (corridor + 1 + offset) % N_CORR
        return owner * SLOT_CAP + index // (N_CORR - 1)
    slots = jax.vmap(corridor_slots)(jnp.arange(N_CORR, dtype=jnp.int32))
    return slots.reshape(-1).astype(jnp.int32)


def place_ends(drawn, key, smallest, high):
    shape = drawn.shape
    spot = [jax.random.randint(jax.random.fold_in(key, axis), (), 0, shape[axis]) for axis in range(len(shape))]
    drawn = drawn.at[tuple(spot)].set(smallest)
    longest = shape.index(max(shape))
    spot[longest] = (spot[longest] + 1) % shape[longest]
    return drawn.at[tuple(spot)].set(high)


def steps_of(key, dims, cuts, low, largest):
    def one(axis_at, parts):
        heights = jax.random.uniform(jax.random.fold_in(jax.random.fold_in(key, 6), axis_at), (parts,), jnp.float32, low / len(cuts), largest / len(cuts))
        return jnp.repeat(jnp.exp(heights), dims[axis_at] // parts).reshape((-1,) + (1,) * (len(dims) - axis_at - 1))

    level = one(*cuts[0])
    for cut in cuts[1:]:
        level = level * one(*cut)
    return level


def setup_inputs(seed: int = 0) -> dict:
    arg_keys = jax.random.split(jax.random.key(seed), 12)
    return {
        "flows": jnp.clip(jnp.exp(math.log(2.0) - 3.6927934 * jax.random.uniform(arg_keys[0], (DAYS, MINUTES, PATHS), jnp.float32) ** steps_of(arg_keys[0], (DAYS, MINUTES, PATHS), ((1, 4), (2, 8)), -0.2, 0.2)), 0.049804688, 2.0).astype(jnp.bfloat16),
        "counts": jnp.clip(jnp.exp(math.log(4.0) - 2.0794415 * jax.random.uniform(arg_keys[1], (DAYS, MINUTES, LINKS), jnp.float32) ** steps_of(arg_keys[1], (DAYS, MINUTES, LINKS), ((1, 4), (2, 8)), -0.2, 0.2)), 0.5, 4.0),
        "local_blocks": jnp.clip(0.00390625 * jax.random.uniform(arg_keys[2], (N_CORR * LOCAL_BLOCKS, BLOCK, BLOCK), jnp.float32) ** steps_of(arg_keys[2], (N_CORR * LOCAL_BLOCKS, BLOCK, BLOCK), ((0, 8),), -0.2, 0.2), 0.0, 0.00390625).astype(jnp.bfloat16),
        "local_path": place_ends(jax.random.randint(arg_keys[3], (N_CORR * LOCAL_BLOCKS,), 0, PATH_BLOCKS), jax.random.fold_in(arg_keys[3], 1), 0, PATH_BLOCKS - 1).astype(jnp.int32),
        "local_link": place_ends(jax.random.randint(arg_keys[4], (N_CORR * LOCAL_BLOCKS,), 0, PATH_BLOCKS), jax.random.fold_in(arg_keys[4], 1), 0, PATH_BLOCKS - 1).astype(jnp.int32),
        "local_lag": place_ends(jax.random.randint(arg_keys[5], (N_CORR * LOCAL_BLOCKS,), 0, LAGS), jax.random.fold_in(arg_keys[5], 1), 0, LAGS - 1).astype(jnp.int32),
        "remote_blocks": jnp.clip(0.00390625 * jax.random.uniform(arg_keys[6], (N_CORR * REMOTE_BLOCKS, BLOCK, BLOCK), jnp.float32) ** steps_of(arg_keys[6], (N_CORR * REMOTE_BLOCKS, BLOCK, BLOCK), ((0, 8),), -0.2, 0.2), 0.0, 0.00390625).astype(jnp.bfloat16),
        "remote_path": place_ends(jax.random.randint(arg_keys[7], (N_CORR * REMOTE_BLOCKS,), 0, PATH_BLOCKS), jax.random.fold_in(arg_keys[7], 1), 0, PATH_BLOCKS - 1).astype(jnp.int32),
        "remote_link": place_ends(jax.random.randint(arg_keys[8], (N_CORR * REMOTE_BLOCKS,), 0, PATH_BLOCKS), jax.random.fold_in(arg_keys[8], 1), 0, PATH_BLOCKS - 1).astype(jnp.int32),
        "remote_lag": place_ends(jax.random.randint(arg_keys[9], (N_CORR * REMOTE_BLOCKS,), 0, LAGS), jax.random.fold_in(arg_keys[9], 1), 0, LAGS - 1).astype(jnp.int32),
        "remote_slot": draw_remote_slot(jax.random.fold_in(arg_keys[11], 71), 0),
    }


HIGH = lax.Precision.HIGHEST
RATE = 0.5


def lag_windows(source, chosen_ids, firsts, length):
    chosen = jnp.take(source, chosen_ids, axis=2)

    def window(column, first):
        return lax.dynamic_slice_in_dim(column, first, length, 1)

    return jax.vmap(window, in_axes=(2, 0), out_axes=2)(chosen, firsts)


def corridor_slice(values, corridor, count):
    return lax.dynamic_slice_in_dim(values, corridor * count, count, 0)


def reference(flows, counts, local_blocks, local_path, local_link, local_lag, remote_blocks, remote_path, remote_link, remote_lag, remote_slot):
    lag_span = LAGS - 1
    all_blocks = N_CORR * PATH_BLOCKS
    flow_cube = flows.reshape(DAYS, MINUTES, all_blocks, BLOCK)
    flow_padded = jnp.pad(flow_cube, ((0, 0), (lag_span, 0), (0, 0), (0, 0)))

    def block_terms(mats, path_ids, lags):
        window_in = lag_windows(flow_padded, path_ids, lag_span - lags, MINUTES).astype(jnp.float32)
        return jnp.einsum('dtbp,blp->dtbl', window_in, mats.astype(jnp.float32), precision=HIGH)

    def forward_step(totals, corridor):
        path_offset = corridor * PATH_BLOCKS
        part_local = block_terms(corridor_slice(local_blocks, corridor, LOCAL_BLOCKS),
                                 corridor_slice(local_path, corridor, LOCAL_BLOCKS) + path_offset,
                                 corridor_slice(local_lag, corridor, LOCAL_BLOCKS))
        link_local = corridor_slice(local_link, corridor, LOCAL_BLOCKS) + path_offset
        totals = totals.at[:, :, link_local, :].add(part_local)
        part_remote = block_terms(corridor_slice(remote_blocks, corridor, REMOTE_BLOCKS),
                                  corridor_slice(remote_path, corridor, REMOTE_BLOCKS) + path_offset,
                                  corridor_slice(remote_lag, corridor, REMOTE_BLOCKS))
        owners = corridor_slice(remote_slot, corridor, REMOTE_BLOCKS) // SLOT_CAP
        link_remote = owners * PATH_BLOCKS + corridor_slice(remote_link, corridor, REMOTE_BLOCKS)
        totals = totals.at[:, :, link_remote, :].add(part_remote)
        return totals, None

    start_totals = jnp.zeros((DAYS, MINUTES, all_blocks, BLOCK), jnp.float32)
    totals, _ = lax.scan(forward_step, start_totals, jnp.arange(N_CORR, dtype=jnp.int32))
    link_flow = totals.reshape(DAYS, MINUTES, LINKS)
    link_residual = (link_flow - counts) / (counts + 1.0)
    signal = (link_residual / (counts + 1.0)).astype(jnp.bfloat16)
    signal_cube = signal.reshape(DAYS, MINUTES, all_blocks, BLOCK)
    signal_padded = jnp.pad(signal_cube, ((0, 0), (0, lag_span), (0, 0), (0, 0)))

    def back_terms(mats, link_ids, lags):
        window_in = lag_windows(signal_padded, link_ids, lags, MINUTES).astype(jnp.float32)
        return jnp.einsum('dtbl,blp->dtbp', window_in, mats.astype(jnp.float32), precision=HIGH)

    def backward_one(corridor):
        path_offset = corridor * PATH_BLOCKS
        result = jnp.zeros((DAYS, MINUTES, PATH_BLOCKS, BLOCK), jnp.float32)
        grad_local = back_terms(corridor_slice(local_blocks, corridor, LOCAL_BLOCKS),
                                corridor_slice(local_link, corridor, LOCAL_BLOCKS) + path_offset,
                                corridor_slice(local_lag, corridor, LOCAL_BLOCKS))
        result = result.at[:, :, corridor_slice(local_path, corridor, LOCAL_BLOCKS), :].add(grad_local)
        owners = corridor_slice(remote_slot, corridor, REMOTE_BLOCKS) // SLOT_CAP
        link_remote = owners * PATH_BLOCKS + corridor_slice(remote_link, corridor, REMOTE_BLOCKS)
        grad_remote = back_terms(corridor_slice(remote_blocks, corridor, REMOTE_BLOCKS), link_remote,
                                 corridor_slice(remote_lag, corridor, REMOTE_BLOCKS))
        result = result.at[:, :, corridor_slice(remote_path, corridor, REMOTE_BLOCKS), :].add(grad_remote)
        return result

    pieces = lax.map(backward_one, jnp.arange(N_CORR, dtype=jnp.int32))
    gradient = jnp.transpose(pieces, (1, 2, 0, 3, 4)).reshape(DAYS, MINUTES, PATHS)
    new_flows = jnp.maximum(flows.astype(jnp.float32) - RATE * gradient, 0.0)
    return (link_residual, gradient, new_flows)
```

```python
import functools
import jax
import jax.numpy as jnp
from jax import lax
from jax.experimental import pallas as pl
from jax.experimental.pallas import tpu as pltpu
from jax.sharding import PartitionSpec as P

LAGS = 16


HIGH = lax.Precision.HIGHEST
RATE = 0.5


def passed_along(block, axis, distance):
    devices = range(lax.axis_size(axis))
    route = [(i - distance, i) for i in devices if i - distance in devices]
    return lax.ppermute(block, axis, route)


def one_hot(labels, classes, dtype):
    return (labels[:, None] == jnp.arange(classes, dtype=jnp.int32)[None, :]).astype(dtype)


def shift_table(deltas, out_len, in_len, dtype):
    out_pos = jnp.arange(out_len, dtype=jnp.int32)[:, None]
    in_pos = jnp.arange(in_len, dtype=jnp.int32)[None, :]
    return ((in_pos - out_pos)[None, :, :] == deltas[:, None, None]).astype(dtype)


def pick_blocks(cube, hot):
    return jnp.einsum("dsqp,bq->dsbp", cube, hot, preferred_element_type=jnp.float32).astype(
        jnp.bfloat16
    )


def shift_narrow(picked, table):
    return jnp.einsum("dsbp,bts->dtbp", picked, table, preferred_element_type=jnp.float32).astype(
        jnp.bfloat16
    )


def route_partials(local_part, remote_part, local_route, remote_link, slot_hot, link_blocks):
    own = jnp.einsum("dtbl,bk->dtkl", local_part, local_route, precision=HIGH)
    outgoing = jnp.einsum("bdtl,bs->sdtl", remote_part, slot_hot, precision=HIGH)
    slot_int = slot_hot.astype(jnp.int32)
    labels = link_blocks + jnp.sum(slot_int * (remote_link[:, None] - link_blocks), axis=0)
    return (own, outgoing, labels)


def absorb(own, received, got_labels, link_blocks):
    landing = one_hot(got_labels, link_blocks, jnp.float32)
    return own + jnp.einsum("sdtl,sk->dtkl", received, landing, precision=HIGH)


def collect_paths(local_grad, remote_grad, local_paths, remote_paths):
    first_sum = jnp.einsum("dtbp,bq->dtqp", local_grad, local_paths, precision=HIGH)
    return first_sum + jnp.einsum("bdtp,bq->dtqp", remote_grad, remote_paths, precision=HIGH)


def per_device_slots(
    flows,
    counts,
    local_blocks,
    local_path,
    local_link,
    local_lag,
    remote_blocks,
    remote_path,
    remote_link,
    remote_lag,
    remote_slot,
):
    day_count, minutes, path_width = flows.shape
    block_width = local_blocks.shape[1]
    path_blocks = path_width // block_width
    link_blocks = counts.shape[2] // block_width
    lag_span = LAGS - 1
    corridors = lax.axis_size("corr")
    remote_count = remote_lag.shape[0]
    slot_count = corridors * ((remote_count + corridors - 2) // (corridors - 1))
    flow_cube = flows.reshape(day_count, minutes, path_blocks, block_width)
    local_route = one_hot(local_link, link_blocks, jnp.float32)
    slot_hot = one_hot(remote_slot, slot_count, jnp.float32)
    slot_pick = slot_hot.astype(jnp.bfloat16)
    local_path_hot = one_hot(local_path, path_blocks, jnp.bfloat16)
    remote_path_hot = one_hot(remote_path, path_blocks, jnp.bfloat16)
    local_link_hot = one_hot(local_link, link_blocks, jnp.bfloat16)
    local_in = pick_blocks(flow_cube, local_path_hot)
    remote_in = pick_blocks(flow_cube, remote_path_hot)
    local_plain = jnp.einsum(
        "dtbp,blp->dtbl", local_in, local_blocks, preferred_element_type=jnp.float32
    )
    remote_plain = jnp.einsum(
        "dtbp,blp->bdtl", remote_in, remote_blocks, preferred_element_type=jnp.float32
    )
    local_part = jnp.einsum(
        "dsbl,bts->dtbl",
        local_plain,
        shift_table(-local_lag, minutes + lag_span, minutes, jnp.float32),
        precision=HIGH,
    )
    remote_part = jnp.einsum(
        "bdsl,bts->bdtl",
        remote_plain,
        shift_table(-remote_lag, minutes + lag_span, minutes, jnp.float32),
        precision=HIGH,
    )
    own, outgoing, labels = route_partials(
        local_part, remote_part, local_route, remote_link, slot_hot, link_blocks
    )
    received, got_labels = (
        lax.all_to_all(outgoing, "corr", split_axis=0, concat_axis=0, tiled=True),
        lax.all_to_all(labels, "corr", split_axis=0, concat_axis=0, tiled=True),
    )
    extended = absorb(own, received, got_labels, link_blocks)
    spill = passed_along(extended[:, minutes:], "tm", 1)
    totals = extended[:, :minutes] + jnp.pad(
        spill, ((0, 0), (0, minutes - lag_span), (0, 0), (0, 0))
    )
    link_flow = totals.reshape(day_count, minutes, link_blocks * block_width)
    link_residual = (link_flow - counts) / (counts + 1.0)
    signal = (link_residual / (counts + 1.0)).astype(jnp.bfloat16)
    slot_route = one_hot(got_labels, link_blocks, jnp.bfloat16)
    local_paths = one_hot(local_path, path_blocks, jnp.float32)
    remote_paths = one_hot(remote_path, path_blocks, jnp.float32)
    ahead = passed_along(signal[:, :lag_span, :], "tm", -1)
    extended_signal = jnp.concatenate([signal, ahead], axis=1).reshape(
        day_count, minutes + lag_span, link_blocks, block_width
    )
    slot_signal = jnp.einsum(
        "dtkl,sk->sdtl", extended_signal, slot_route, preferred_element_type=jnp.float32
    ).astype(jnp.bfloat16)
    returned = lax.all_to_all(slot_signal, "corr", split_axis=0, concat_axis=0, tiled=True)
    remote_pick = jnp.einsum(
        "sdtl,bs->bdtl", returned, slot_pick, preferred_element_type=jnp.float32
    ).astype(jnp.bfloat16)
    remote_sig = jnp.einsum(
        "bdsl,bts->bdtl",
        remote_pick,
        shift_table(remote_lag, minutes, minutes + lag_span, jnp.bfloat16),
        preferred_element_type=jnp.float32,
    ).astype(jnp.bfloat16)
    local_sig = shift_narrow(
        pick_blocks(extended_signal, local_link_hot),
        shift_table(local_lag, minutes, minutes + lag_span, jnp.bfloat16),
    )
    local_grad = jnp.einsum(
        "dtbl,blp->dtbp", local_sig, local_blocks, preferred_element_type=jnp.float32
    )
    remote_grad = jnp.einsum(
        "bdtl,blp->bdtp", remote_sig, remote_blocks, preferred_element_type=jnp.float32
    )
    grad_cube = collect_paths(local_grad, remote_grad, local_paths, remote_paths)
    gradient = grad_cube.reshape(day_count, minutes, path_width)
    new_flows = jnp.maximum(flows.astype(jnp.float32) - RATE * gradient, 0.0)
    return (link_residual, gradient, new_flows)


HALO = 16
WIRE = jnp.float16


def window_rows(path, day, lag, days, span):
    return (path * days + day) * span + HALO - lag


def stage_flows(flows_ref, halo_ref, wide, days, minutes, width):
    span = HALO + minutes
    for p in range(flows_ref.shape[2] // width):
        cols = slice(p * width, (p + 1) * width)
        for d in range(days):
            row = (p * days + d) * span
            wide[row : row + HALO, :] = halo_ref[d, :, cols].astype(jnp.float32)
            wide[row + HALO : row + span, :] = flows_ref[d, :, cols].astype(jnp.float32)


def forward_blocks(count, unroll, mats, path, lag, target, wide, acc, days, minutes):
    span = HALO + minutes

    def group(g, carry):
        parts = []
        for u in range(unroll):
            j = g * unroll + u
            rows = [
                wide[pl.ds(window_rows(path[j], d, lag[j], days, span), minutes), :]
                for d in range(days)
            ]
            taken = jnp.concatenate(rows, axis=0).astype(jnp.bfloat16)
            parts.append(
                lax.dot_general(
                    taken,
                    mats[j],
                    (((1,), (1,)), ((), ())),
                    preferred_element_type=jnp.float32,
                )
            )
        for u in range(unroll):
            t = target(g * unroll + u)
            acc[t] += parts[u]
        return carry

    lax.fori_loop(0, count // unroll, group, 0)


def backward_blocks(count, unroll, mats, path, lag, source, signals, acc, days, minutes):
    span = HALO + minutes

    def group(g, carry):
        parts = []
        for u in range(unroll):
            j = g * unroll + u
            parts.append(
                jnp.dot(signals(j), mats[j], preferred_element_type=jnp.float32)
            )
        for u in range(unroll):
            j = g * unroll + u
            for d in range(days):
                rows = pl.ds(window_rows(path[j], d, lag[j], days, span), minutes)
                acc[rows, :] += parts[u][d * minutes : (d + 1) * minutes]
        return carry

    lax.fori_loop(0, count // unroll, group, 0)


def forward_remote_kernel(days, cap, blocks, me, path, link, lag, slot, flows, halo, mats, *rest):
    outs, (wide, acc) = rest[:-2], rest[-2:]
    minutes = flows.shape[1]
    stage_flows(flows, halo, wide, days, minutes, mats.shape[2])
    acc[...] = jnp.zeros_like(acc)

    def target(j):
        return (lax.div(slot[j], cap) ^ me[0]) * blocks + link[j]

    forward_blocks(mats.shape[0], 8, mats, path, lag, target, wide, acc, days, minutes)
    for s, out in enumerate(outs):
        out[...] = acc[(s + 1) * blocks : (s + 2) * blocks].astype(out.dtype)


def forward_local_kernel(days, path, link, lag, flows, halo, mats, out, wide):
    minutes = flows.shape[1]
    stage_flows(flows, halo, wide, days, minutes, mats.shape[2])
    out[...] = jnp.zeros_like(out)
    forward_blocks(
        mats.shape[0], 8, mats, path, lag, lambda j: link[j], wide, out, days, minutes
    )


def signal_kernel(days, totals, counts, residual, signal):
    blocks, _, width = totals.shape
    minutes = counts.shape[1]
    for b in range(blocks):
        cols = slice(b * width, (b + 1) * width)
        total = totals[b]
        for d in range(days):
            rows = slice(d * minutes, (d + 1) * minutes)
            seen = counts[d, :, cols]
            weight = seen + 1.0
            res = (total[rows] - seen) / weight
            residual[d, :, cols] = res
            signal[b, rows, :] = (res / weight).astype(signal.dtype)


def backward_local_kernel(days, path, link, lag, signal, mats, out):
    minutes = signal.shape[1] // days
    out[...] = jnp.zeros_like(out)
    backward_blocks(
        mats.shape[0],
        8,
        mats,
        path,
        lag,
        None,
        lambda j: signal[link[j]],
        out,
        days,
        minutes,
    )


def backward_remote_kernel(days, cap, blocks, me, path, link, lag, slot, mats, start, *rest):
    signals, (out, everyone) = rest[:-2], rest[-2:]
    minutes = signals[0].shape[1] // days
    for s, part in enumerate(signals):
        everyone[(s + 1) * blocks : (s + 2) * blocks] = part[...]
    out[...] = start[...]

    def chosen(j):
        return everyone[(lax.div(slot[j], cap) ^ me[0]) * blocks + link[j]]

    backward_blocks(mats.shape[0], 8, mats, path, lag, None, chosen, out, days, minutes)


def finish_kernel(days, total, spill, flows, gradient, new_flows):
    minutes = flows.shape[1]
    width = total.shape[1]
    span = HALO + minutes
    for p in range(flows.shape[2] // width):
        cols = slice(p * width, (p + 1) * width)
        for d in range(days):
            row = (p * days + d) * span + HALO
            own = total[row : row + minutes, :]
            keep = minutes - HALO
            late = own[keep:] + spill[p * days + d]
            for rows, grad in ((slice(0, keep), own[:keep]), (slice(keep, minutes), late)):
                gradient[d, rows, cols] = grad
                new_flows[d, rows, cols] = jnp.maximum(
                    flows[d, rows, cols].astype(jnp.float32) - RATE * grad, 0.0
                )


def kernel_call(body, scalars, arrays, out_shape, scratch=()):
    smem = pl.BlockSpec(memory_space=pltpu.SMEM)
    vmem = pl.BlockSpec(memory_space=pltpu.VMEM)
    single = isinstance(out_shape, jax.ShapeDtypeStruct)
    return pl.pallas_call(
        body,
        out_shape=out_shape,
        in_specs=[smem] * len(scalars) + [vmem] * len(arrays),
        out_specs=vmem if single else [vmem] * len(out_shape),
        scratch_shapes=list(scratch),
        compiler_params=pltpu.CompilerParams(vmem_limit_bytes=48 * 1024 * 1024),
    )(*scalars, *arrays)


def per_device_dense(
    flows,
    counts,
    local_blocks,
    local_path,
    local_link,
    local_lag,
    remote_blocks,
    remote_path,
    remote_link,
    remote_lag,
    remote_slot,
):
    days, minutes, path_width = flows.shape
    width = local_blocks.shape[1]
    paths = path_width // width
    links = counts.shape[2] // width
    corridors = lax.axis_size("corr")
    cap = (remote_lag.shape[0] + corridors - 2) // (corridors - 1)
    span = HALO + minutes
    others = range(1, corridors)
    me = lax.axis_index("corr").astype(jnp.int32).reshape(1)
    shape = jax.ShapeDtypeStruct
    piece = (links, days * minutes, width)
    wide = pltpu.VMEM((paths * days * span, width), jnp.float32)

    halo = passed_along(flows[:, minutes - HALO :], "tm", 1)
    outgoing = kernel_call(
        functools.partial(forward_remote_kernel, days, cap, links),
        (me, remote_path, remote_link, remote_lag, remote_slot),
        (flows, halo, remote_blocks),
        [shape(piece, jnp.float32) for _ in others],
        [wide, pltpu.VMEM((corridors * links, days * minutes, width), jnp.float32)],
    )

    def exchanged(part, s):
        return lax.ppermute(part, "corr", [(i, i ^ s) for i in range(corridors)])

    received = [exchanged(outgoing[s - 1].astype(WIRE), s) for s in others]
    own = kernel_call(
        functools.partial(forward_local_kernel, days),
        (local_path, local_link, local_lag),
        (flows, halo, local_blocks),
        shape(piece, jnp.float32),
        [wide],
    )
    link_residual, signal = kernel_call(
        functools.partial(signal_kernel, days),
        (),
        (functools.reduce(jnp.add, [p.astype(jnp.float32) for p in received], own), counts),
        [shape(counts.shape, jnp.float32), shape(piece, jnp.bfloat16)],
    )
    signals = [exchanged(signal, s) for s in others]
    rows = shape((paths * days * span, width), jnp.float32)
    local_total = kernel_call(
        functools.partial(backward_local_kernel, days),
        (local_path, local_link, local_lag),
        (signal, local_blocks),
        rows,
    )
    total = kernel_call(
        functools.partial(backward_remote_kernel, days, cap, links),
        (me, remote_path, remote_link, remote_lag, remote_slot),
        (remote_blocks, local_total, *signals),
        rows,
        [pltpu.VMEM((corridors * links, days * minutes, width), jnp.bfloat16)],
    )
    early = total.reshape(paths * days, span, width)[:, :HALO]
    spill = passed_along(early, "tm", -1)
    gradient, new_flows = kernel_call(
        functools.partial(finish_kernel, days),
        (),
        (total, spill, flows),
        [shape(flows.shape, jnp.float32)] * 2,
    )
    return (link_residual, gradient, new_flows)


def per_device(*args):
    counts, blocks, lags = args[1], args[2], args[9]
    corridors = lax.axis_size("corr")
    links = counts.shape[2] // blocks.shape[1]
    cap = (lags.shape[0] + corridors - 2) // (corridors - 1)
    if cap >= links:
        return per_device_dense(*args)
    return per_device_slots(*args)


def solution(mesh):
    placed = (
        P(None, "tm", "corr"),
        P(None, "tm", "corr"),
        P("corr", None, None),
        P("corr"),
        P("corr"),
        P("corr"),
        P("corr", None, None),
        P("corr"),
        P("corr"),
        P("corr"),
        P("corr"),
    )
    return jax.shard_map(
        per_device,
        mesh=mesh,
        in_specs=placed,
        out_specs=(P(None, "tm", "corr"), P(None, "tm", "corr"), P(None, "tm", "corr")),
        check_vma=False,
    )
```

```python
import functools
import jax
import jax.numpy as jnp
from jax import lax
from jax.experimental import pallas as pl
from jax.experimental.pallas import tpu as pltpu
from jax.sharding import PartitionSpec as P

LAGS = 16


HIGH = lax.Precision.HIGHEST
RATE = 0.5


def passed_along(block, axis, distance):
    devices = range(lax.axis_size(axis))
    route = [(i - distance, i) for i in devices if i - distance in devices]
    return lax.ppermute(block, axis, route)


def one_hot(labels, classes, dtype):
    return (labels[:, None] == jnp.arange(classes, dtype=jnp.int32)[None, :]).astype(dtype)


def shift_table(deltas, out_len, in_len, dtype):
    out_pos = jnp.arange(out_len, dtype=jnp.int32)[:, None]
    in_pos = jnp.arange(in_len, dtype=jnp.int32)[None, :]
    return ((in_pos - out_pos)[None, :, :] == deltas[:, None, None]).astype(dtype)


def pick_blocks(cube, hot):
    return jnp.einsum("dsqp,bq->dsbp", cube, hot, preferred_element_type=jnp.float32).astype(
        jnp.bfloat16
    )


def shift_narrow(picked, table):
    return jnp.einsum("dsbp,bts->dtbp", picked, table, preferred_element_type=jnp.float32).astype(
        jnp.bfloat16
    )


def route_partials(local_part, remote_part, local_route, remote_link, slot_hot, link_blocks):
    own = jnp.einsum("dtbl,bk->dtkl", local_part, local_route, precision=HIGH)
    outgoing = jnp.einsum("bdtl,bs->sdtl", remote_part, slot_hot, precision=HIGH)
    slot_int = slot_hot.astype(jnp.int32)
    labels = link_blocks + jnp.sum(slot_int * (remote_link[:, None] - link_blocks), axis=0)
    return (own, outgoing, labels)


def absorb(own, received, got_labels, link_blocks):
    landing = one_hot(got_labels, link_blocks, jnp.float32)
    return own + jnp.einsum("sdtl,sk->dtkl", received, landing, precision=HIGH)


def collect_paths(local_grad, remote_grad, local_paths, remote_paths):
    first_sum = jnp.einsum("dtbp,bq->dtqp", local_grad, local_paths, precision=HIGH)
    return first_sum + jnp.einsum("bdtp,bq->dtqp", remote_grad, remote_paths, precision=HIGH)


def per_device_slots(
    flows,
    counts,
    local_blocks,
    local_path,
    local_link,
    local_lag,
    remote_blocks,
    remote_path,
    remote_link,
    remote_lag,
    remote_slot,
):
    day_count, minutes, path_width = flows.shape
    block_width = local_blocks.shape[1]
    path_blocks = path_width // block_width
    link_blocks = counts.shape[2] // block_width
    lag_span = LAGS - 1
    corridors = lax.axis_size("corr")
    remote_count = remote_lag.shape[0]
    slot_count = corridors * ((remote_count + corridors - 2) // (corridors - 1))
    flow_cube = flows.reshape(day_count, minutes, path_blocks, block_width)
    local_route = one_hot(local_link, link_blocks, jnp.float32)
    slot_hot = one_hot(remote_slot, slot_count, jnp.float32)
    slot_pick = slot_hot.astype(jnp.bfloat16)
    local_path_hot = one_hot(local_path, path_blocks, jnp.bfloat16)
    remote_path_hot = one_hot(remote_path, path_blocks, jnp.bfloat16)
    local_link_hot = one_hot(local_link, link_blocks, jnp.bfloat16)
    local_in = pick_blocks(flow_cube, local_path_hot)
    remote_in = pick_blocks(flow_cube, remote_path_hot)
    local_plain = jnp.einsum(
        "dtbp,blp->dtbl", local_in, local_blocks, preferred_element_type=jnp.float32
    )
    remote_plain = jnp.einsum(
        "dtbp,blp->bdtl", remote_in, remote_blocks, preferred_element_type=jnp.float32
    )
    local_part = jnp.einsum(
        "dsbl,bts->dtbl",
        local_plain,
        shift_table(-local_lag, minutes + lag_span, minutes, jnp.float32),
        precision=HIGH,
    )
    remote_part = jnp.einsum(
        "bdsl,bts->bdtl",
        remote_plain,
        shift_table(-remote_lag, minutes + lag_span, minutes, jnp.float32),
        precision=HIGH,
    )
    own, outgoing, labels = route_partials(
        local_part, remote_part, local_route, remote_link, slot_hot, link_blocks
    )
    received, got_labels = (
        lax.all_to_all(outgoing, "corr", split_axis=0, concat_axis=0, tiled=True),
        lax.all_to_all(labels, "corr", split_axis=0, concat_axis=0, tiled=True),
    )
    extended = absorb(own, received, got_labels, link_blocks)
    spill = passed_along(extended[:, minutes:], "tm", 1)
    totals = extended[:, :minutes] + jnp.pad(
        spill, ((0, 0), (0, minutes - lag_span), (0, 0), (0, 0))
    )
    link_flow = totals.reshape(day_count, minutes, link_blocks * block_width)
    link_residual = (link_flow - counts) / (counts + 1.0)
    signal = (link_residual / (counts + 1.0)).astype(jnp.bfloat16)
    slot_route = one_hot(got_labels, link_blocks, jnp.bfloat16)
    local_paths = one_hot(local_path, path_blocks, jnp.float32)
    remote_paths = one_hot(remote_path, path_blocks, jnp.float32)
    ahead = passed_along(signal[:, :lag_span, :], "tm", -1)
    extended_signal = jnp.concatenate([signal, ahead], axis=1).reshape(
        day_count, minutes + lag_span, link_blocks, block_width
    )
    slot_signal = jnp.einsum(
        "dtkl,sk->sdtl", extended_signal, slot_route, preferred_element_type=jnp.float32
    ).astype(jnp.bfloat16)
    returned = lax.all_to_all(slot_signal, "corr", split_axis=0, concat_axis=0, tiled=True)
    remote_pick = jnp.einsum(
        "sdtl,bs->bdtl", returned, slot_pick, preferred_element_type=jnp.float32
    ).astype(jnp.bfloat16)
    remote_sig = jnp.einsum(
        "bdsl,bts->bdtl",
        remote_pick,
        shift_table(remote_lag, minutes, minutes + lag_span, jnp.bfloat16),
        preferred_element_type=jnp.float32,
    ).astype(jnp.bfloat16)
    local_sig = shift_narrow(
        pick_blocks(extended_signal, local_link_hot),
        shift_table(local_lag, minutes, minutes + lag_span, jnp.bfloat16),
    )
    local_grad = jnp.einsum(
        "dtbl,blp->dtbp", local_sig, local_blocks, preferred_element_type=jnp.float32
    )
    remote_grad = jnp.einsum(
        "bdtl,blp->bdtp", remote_sig, remote_blocks, preferred_element_type=jnp.float32
    )
    grad_cube = collect_paths(local_grad, remote_grad, local_paths, remote_paths)
    gradient = grad_cube.reshape(day_count, minutes, path_width)
    new_flows = jnp.maximum(flows.astype(jnp.float32) - RATE * gradient, 0.0)
    return (link_residual, gradient, new_flows)


HALO = 16
WIRE = jnp.float16


def stage_flows(flows_ref, before_ref, wide, days, width):
    minutes = flows_ref.shape[1]
    span = HALO + minutes
    for p in range(flows_ref.shape[2] // width):
        cols = slice(p * width, (p + 1) * width)
        for d in range(days):
            row = (p * days + d) * span
            before = before_ref[d, :, cols].astype(jnp.float32)
            wide[row : row + HALO, :] = before[minutes - HALO :]
            wide[row + HALO : row + span, :] = flows_ref[d, :, cols].astype(jnp.float32)


def forward_blocks(start, count, unroll, mat, base, target, wide, acc, days, minutes):
    span = HALO + minutes

    def group(g, carry):
        parts = []
        for u in range(unroll):
            j = start + g * unroll + u
            rows = [
                wide[pl.ds(base(j) + d * span, minutes), :] for d in range(days)
            ]
            taken = jnp.concatenate(rows, axis=0).astype(jnp.bfloat16)
            parts.append(
                lax.dot_general(
                    taken,
                    mat(j),
                    (((1,), (1,)), ((), ())),
                    preferred_element_type=jnp.float32,
                )
            )
        for u in range(unroll):
            acc[target(start + g * unroll + u)] += parts[u]
        return carry

    lax.fori_loop(0, count // unroll, group, 0)


def backward_blocks(start, count, unroll, mat, base, signal, acc, days, minutes):
    span = HALO + minutes

    def group(g, carry):
        parts = []
        for u in range(unroll):
            j = start + g * unroll + u
            parts.append(jnp.dot(signal(j), mat(j), preferred_element_type=jnp.float32))
        for u in range(unroll):
            for d in range(days):
                rows = pl.ds(base(start + g * unroll + u) + d * span, minutes)
                acc[rows, :] += parts[u][d * minutes : (d + 1) * minutes]
        return carry

    lax.fori_loop(0, count // unroll, group, 0)


class Table:
    def __init__(self, slots, blocks):
        self.mat = 0
        self.base = slots
        self.block = 2 * slots
        self.local_base = 3 * slots
        self.local_block = 3 * slots + blocks
        self.size = 3 * slots + 2 * blocks


def prepare_kernel(
    days,
    span,
    cap,
    corridors,
    links,
    order,
    me,
    local_path,
    local_link,
    local_lag,
    remote_path,
    remote_link,
    remote_lag,
    remote_slot,
    local_mats,
    remote_mats,
    table,
    local_out,
    remote_out,
    lp,
    ll,
    lk,
    rp,
    rl,
    rk,
    rs,
    sems,
):
    slots = (corridors - 1) * cap
    locals_, remotes = lp.shape[0], rp.shape[0]
    t = Table(slots, locals_)
    pairs = (
        (local_path, lp),
        (local_link, ll),
        (local_lag, lk),
        (remote_path, rp),
        (remote_link, rl),
        (remote_lag, rk),
        (remote_slot, rs),
        (remote_mats, remote_out),
        (local_mats, local_out),
    )
    copies = [pltpu.make_async_copy(a, b, sems.at[i]) for i, (a, b) in enumerate(pairs)]
    for copy in copies:
        copy.start()

    def blank(i, carry):
        table[t.mat + i] = 0
        table[t.base + i] = HALO
        table[t.block + i] = (corridors - 1) * links
        return carry

    lax.fori_loop(0, slots, blank, 0, unroll=10 if slots % 10 == 0 else 1)
    for copy in copies[:7]:
        copy.wait()

    def remote(j, carry):
        owner = lax.div(rs[j], cap)
        rel = owner ^ me[0]
        place = jnp.int32(0)
        for p, s in enumerate(order):
            place = jnp.where(rel == s, p, place)
        i = place * cap + rs[j] - owner * cap
        table[t.mat + i] = j
        table[t.base + i] = rp[j] * (days * span) + HALO - rk[j]
        table[t.block + i] = place * links + rl[j]
        return carry

    def local(j, carry):
        table[t.local_base + j] = lp[j] * (days * span) + HALO - lk[j]
        table[t.local_block + j] = ll[j]
        return carry

    lax.fori_loop(0, remotes, remote, 0, unroll=8)
    lax.fori_loop(0, locals_, local, 0, unroll=8)
    for copy in copies[7:]:
        copy.wait()


def slot_views(table, t, mats):
    return (
        lambda i: mats[table[t.mat + i]],
        lambda i: table[t.base + i],
        lambda i: table[t.block + i],
    )


def local_views(table, t, mats):
    return (
        lambda j: mats[j],
        lambda j: table[t.local_base + j],
        lambda j: table[t.local_block + j],
    )


def forward_remote_kernel(days, cap, cuts, links, t, table, flows, before, mats, *rest):
    outs, (wide, acc) = rest[:-2], rest[-2:]
    minutes, width = flows.shape[1], mats.shape[2]
    stage_flows(flows, before, wide, days, width)
    acc[...] = jnp.zeros_like(acc)
    mat, base, block = slot_views(table, t, mats)
    forward_blocks(0, cuts[-1] * cap, cap, mat, base, block, wide, acc, days, minutes)
    for first, end, out in zip(cuts, cuts[1:], outs):
        out[...] = acc[first * links : end * links]


def forward_local_kernel(days, t, table, flows, before, mats, own, wide):
    minutes, width = flows.shape[1], mats.shape[2]
    stage_flows(flows, before, wide, days, width)
    own[...] = jnp.zeros_like(own)
    mat, base, block = local_views(table, t, mats)
    forward_blocks(0, mats.shape[0], 8, mat, base, block, wide, own, days, minutes)


def signal_kernel(days, totals, counts, residual, signal):
    blocks, _, width = totals.shape
    minutes = counts.shape[1]
    for b in range(blocks):
        cols = slice(b * width, (b + 1) * width)
        total = totals[b]
        for d in range(days):
            rows = slice(d * minutes, (d + 1) * minutes)
            seen = counts[d, :, cols]
            weight = seen + 1.0
            res = (total[rows] - seen) / weight
            residual[d, :, cols] = res
            signal[b, rows, :] = (res / weight).astype(signal.dtype)


def backward_local_kernel(days, t, table, signal, mats, out):
    minutes = signal.shape[1] // days
    out[...] = jnp.zeros_like(out)
    mat, base, block = local_views(table, t, mats)
    backward_blocks(
        0, mats.shape[0], 8, mat, base, lambda j: signal[block(j)], out, days, minutes
    )


def backward_remote_kernel(days, cap, first, end, links, t, table, mats, start, *rest):
    signals, (out, everyone) = rest[:-2], rest[-2:]
    minutes = signals[0].shape[1] // days
    place = first * links
    for part in signals:
        everyone[place : place + part.shape[0]] = part[...]
        place += part.shape[0]
    blank = everyone.shape[0] - 1
    everyone[blank] = jnp.zeros(everyone.shape[1:], everyone.dtype)
    out[...] = start[...]
    mat, base, block = slot_views(table, t, mats)
    backward_blocks(
        first * cap,
        (end - first) * cap,
        cap,
        mat,
        base,
        lambda i: everyone[block(i)],
        out,
        days,
        minutes,
    )


def finish_kernel(days, total, spill, flows, gradient, new_flows):
    minutes = flows.shape[1]
    width = total.shape[1]
    span = HALO + minutes
    for p in range(flows.shape[2] // width):
        cols = slice(p * width, (p + 1) * width)
        for d in range(days):
            row = (p * days + d) * span + HALO
            own = total[row : row + minutes, :]
            keep = minutes - HALO
            late = own[keep:] + spill[p * days + d]
            for rows, grad in ((slice(0, keep), own[:keep]), (slice(keep, minutes), late)):
                gradient[d, rows, cols] = grad
                new_flows[d, rows, cols] = jnp.maximum(
                    flows[d, rows, cols].astype(jnp.float32) - RATE * grad, 0.0
                )


SMEM = pl.BlockSpec(memory_space=pltpu.SMEM)
VMEM = pl.BlockSpec(memory_space=pltpu.VMEM)
HBM = pl.BlockSpec(memory_space=pltpu.HBM)


def kernel_call(body, scalars, arrays, out_shape, scratch=(), cost=None):
    return pl.pallas_call(
        body,
        out_shape=out_shape,
        in_specs=[SMEM] * len(scalars) + [VMEM] * len(arrays),
        out_specs=[VMEM] * len(out_shape),
        scratch_shapes=list(scratch),
        compiler_params=pltpu.CompilerParams(vmem_limit_bytes=40 * 1024 * 1024),
        cost_estimate=cost,
    )(*scalars, *arrays)


def per_device_dense(
    flows,
    counts,
    local_blocks,
    local_path,
    local_link,
    local_lag,
    remote_blocks,
    remote_path,
    remote_link,
    remote_lag,
    remote_slot,
):
    days, minutes, path_width = flows.shape
    width = local_blocks.shape[1]
    paths = path_width // width
    links = counts.shape[2] // width
    corridors = lax.axis_size("corr")
    locals_, remotes = local_lag.shape[0], remote_lag.shape[0]
    cap = (remotes + corridors - 2) // (corridors - 1)
    span = HALO + minutes
    through = sorted({2, corridors - 2}, reverse=True)
    crossing = [s ^ 1 for s in through]
    direct = [s for s in range(corridors - 1, 1, -1) if s not in through + crossing]
    order = crossing + [1] + direct + through
    many = len(through)
    cuts = [0, *range(many, len(order) - many + 1), len(order)]
    t = Table((corridors - 1) * cap, locals_)
    me = lax.axis_index("corr").astype(jnp.int32).reshape(1)
    shape = jax.ShapeDtypeStruct
    piece = (links, days * minutes, width)
    wide = pltpu.VMEM((paths * days * span, width), jnp.float32)
    slots_shape = (len(order) * links + 1, days * minutes, width)
    index = [local_path, local_link, local_lag, remote_path, remote_link, remote_lag, remote_slot]

    before = passed_along(flows, "tm", 1)
    table, local_mats, remote_mats = pl.pallas_call(
        functools.partial(prepare_kernel, days, span, cap, corridors, links, order),
        out_shape=[
            shape((t.size,), jnp.int32),
            shape(local_blocks.shape, local_blocks.dtype),
            shape(remote_blocks.shape, remote_blocks.dtype),
        ],
        in_specs=[SMEM] + [HBM] * (len(index) + 2),
        out_specs=[SMEM, VMEM, VMEM],
        scratch_shapes=[pltpu.SMEM(i.shape, jnp.int32) for i in index]
        + [pltpu.SemaphoreType.DMA((len(index) + 2,))],
        compiler_params=pltpu.CompilerParams(vmem_limit_bytes=40 * 1024 * 1024),
    )(
        me,
        *(
            pltpu.with_memory_space_constraint(i, pltpu.HBM)
            for i in (*index, local_blocks, remote_blocks)
        ),
    )

    def exchanged(part, s):
        return lax.ppermute(part, "corr", [(i, i ^ s) for i in range(corridors)])

    f32 = jnp.float32
    crossed, *parts, kept = kernel_call(
        functools.partial(forward_remote_kernel, days, cap, cuts, links, t),
        (table,),
        (flows, before, remote_mats),
        [shape(((end - first) * links, *piece[1:]), f32) for first, end in zip(cuts, cuts[1:])],
        [wide, pltpu.VMEM(slots_shape, f32)],
    )
    crossed = exchanged(crossed.astype(WIRE), 1)
    received = [exchanged(p.astype(WIRE), s) for p, s in zip(parts, (1, *direct))]
    (own,) = kernel_call(
        functools.partial(forward_local_kernel, days, t),
        (table,),
        (flows, before, local_mats),
        [shape(piece, f32)],
        [wide],
    )
    kept = (kept + crossed.astype(f32)).astype(WIRE).reshape(many, *piece)
    received += [exchanged(kept[i], s) for i, s in enumerate(through)]
    totals = functools.reduce(jnp.add, [p.astype(f32) for p in received], own)
    link_residual, signal = kernel_call(
        functools.partial(signal_kernel, days),
        (),
        (totals, counts),
        [shape(counts.shape, f32), shape(piece, jnp.bfloat16)],
    )
    arrived = [exchanged(signal, s) for s in (*through, 1, *direct)]
    both = jnp.concatenate(arrived[:many], axis=0)
    both, signal = lax.optimization_barrier((both, signal))
    rows = [shape((paths * days * span, width), f32)]
    (total,) = kernel_call(
        functools.partial(backward_local_kernel, days, t),
        (table,),
        (signal, local_mats),
        rows,
    )
    passed = exchanged(both, 1)
    late = many + 1

    def weigh(first):
        if first == 0:
            return None
        return pl.CostEstimate(
            flops=2_000_000_000, transcendentals=0, bytes_accessed=6_000_000
        )

    for first, end, signals in (
        (late, len(order), [*arrived[late:], *arrived[:many]]),
        (0, late, [passed, arrived[many]]),
    ):
        (total,) = kernel_call(
            functools.partial(backward_remote_kernel, days, cap, first, end, links, t),
            (table,),
            (remote_mats, total, *signals),
            rows,
            [pltpu.VMEM(slots_shape, jnp.bfloat16)],
            weigh(first),
        )
    early = total.reshape(paths * days, span, width)[:, :HALO]
    spill = passed_along(early, "tm", -1)
    gradient, new_flows = kernel_call(
        functools.partial(finish_kernel, days),
        (),
        (total, spill, flows),
        [shape(flows.shape, f32)] * 2,
    )
    return (link_residual, gradient, new_flows)


def per_device(*args):
    counts, blocks, lags = args[1], args[2], args[9]
    corridors = lax.axis_size("corr")
    links = counts.shape[2] // blocks.shape[1]
    cap = (lags.shape[0] + corridors - 2) // (corridors - 1)
    if cap >= links and corridors >= 4 and corridors & (corridors - 1) == 0:
        return per_device_dense(*args)
    return per_device_slots(*args)


def solution(mesh):
    placed = (
        P(None, "tm", "corr"),
        P(None, "tm", "corr"),
        P("corr", None, None),
        P("corr"),
        P("corr"),
        P("corr"),
        P("corr", None, None),
        P("corr"),
        P("corr"),
        P("corr"),
        P("corr"),
    )
    return jax.shard_map(
        per_device,
        mesh=mesh,
        in_specs=placed,
        out_specs=(P(None, "tm", "corr"), P(None, "tm", "corr"), P(None, "tm", "corr")),
        check_vma=False,
    )
```

```python
import functools
import jax
import jax.numpy as jnp
from jax import lax
from jax.experimental import pallas as pl
from jax.experimental.pallas import tpu as pltpu
from jax.sharding import PartitionSpec as P

LAGS = 16


HIGH = lax.Precision.HIGHEST
RATE = 0.5


def passed_along(block, axis, distance):
    devices = range(lax.axis_size(axis))
    route = [(i - distance, i) for i in devices if i - distance in devices]
    return lax.ppermute(block, axis, route)


def one_hot(labels, classes, dtype):
    return (labels[:, None] == jnp.arange(classes, dtype=jnp.int32)[None, :]).astype(dtype)


def shift_table(deltas, out_len, in_len, dtype):
    out_pos = jnp.arange(out_len, dtype=jnp.int32)[:, None]
    in_pos = jnp.arange(in_len, dtype=jnp.int32)[None, :]
    return ((in_pos - out_pos)[None, :, :] == deltas[:, None, None]).astype(dtype)


def pick_blocks(cube, hot):
    return jnp.einsum("dsqp,bq->dsbp", cube, hot, preferred_element_type=jnp.float32).astype(
        jnp.bfloat16
    )


def shift_narrow(picked, table):
    return jnp.einsum("dsbp,bts->dtbp", picked, table, preferred_element_type=jnp.float32).astype(
        jnp.bfloat16
    )


def route_partials(local_part, remote_part, local_route, remote_link, slot_hot, link_blocks):
    own = jnp.einsum("dtbl,bk->dtkl", local_part, local_route, precision=HIGH)
    outgoing = jnp.einsum("bdtl,bs->sdtl", remote_part, slot_hot, precision=HIGH)
    slot_int = slot_hot.astype(jnp.int32)
    labels = link_blocks + jnp.sum(slot_int * (remote_link[:, None] - link_blocks), axis=0)
    return (own, outgoing, labels)


def absorb(own, received, got_labels, link_blocks):
    landing = one_hot(got_labels, link_blocks, jnp.float32)
    return own + jnp.einsum("sdtl,sk->dtkl", received, landing, precision=HIGH)


def collect_paths(local_grad, remote_grad, local_paths, remote_paths):
    first_sum = jnp.einsum("dtbp,bq->dtqp", local_grad, local_paths, precision=HIGH)
    return first_sum + jnp.einsum("bdtp,bq->dtqp", remote_grad, remote_paths, precision=HIGH)


def per_device_slots(
    flows,
    counts,
    local_blocks,
    local_path,
    local_link,
    local_lag,
    remote_blocks,
    remote_path,
    remote_link,
    remote_lag,
    remote_slot,
):
    day_count, minutes, path_width = flows.shape
    block_width = local_blocks.shape[1]
    path_blocks = path_width // block_width
    link_blocks = counts.shape[2] // block_width
    lag_span = LAGS - 1
    corridors = lax.axis_size("corr")
    remote_count = remote_lag.shape[0]
    slot_count = corridors * ((remote_count + corridors - 2) // (corridors - 1))
    flow_cube = flows.reshape(day_count, minutes, path_blocks, block_width)
    local_route = one_hot(local_link, link_blocks, jnp.float32)
    slot_hot = one_hot(remote_slot, slot_count, jnp.float32)
    slot_pick = slot_hot.astype(jnp.bfloat16)
    local_path_hot = one_hot(local_path, path_blocks, jnp.bfloat16)
    remote_path_hot = one_hot(remote_path, path_blocks, jnp.bfloat16)
    local_link_hot = one_hot(local_link, link_blocks, jnp.bfloat16)
    local_in = pick_blocks(flow_cube, local_path_hot)
    remote_in = pick_blocks(flow_cube, remote_path_hot)
    local_plain = jnp.einsum(
        "dtbp,blp->dtbl", local_in, local_blocks, preferred_element_type=jnp.float32
    )
    remote_plain = jnp.einsum(
        "dtbp,blp->bdtl", remote_in, remote_blocks, preferred_element_type=jnp.float32
    )
    local_part = jnp.einsum(
        "dsbl,bts->dtbl",
        local_plain,
        shift_table(-local_lag, minutes + lag_span, minutes, jnp.float32),
        precision=HIGH,
    )
    remote_part = jnp.einsum(
        "bdsl,bts->bdtl",
        remote_plain,
        shift_table(-remote_lag, minutes + lag_span, minutes, jnp.float32),
        precision=HIGH,
    )
    own, outgoing, labels = route_partials(
        local_part, remote_part, local_route, remote_link, slot_hot, link_blocks
    )
    received, got_labels = (
        lax.all_to_all(outgoing, "corr", split_axis=0, concat_axis=0, tiled=True),
        lax.all_to_all(labels, "corr", split_axis=0, concat_axis=0, tiled=True),
    )
    extended = absorb(own, received, got_labels, link_blocks)
    spill = passed_along(extended[:, minutes:], "tm", 1)
    totals = extended[:, :minutes] + jnp.pad(
        spill, ((0, 0), (0, minutes - lag_span), (0, 0), (0, 0))
    )
    link_flow = totals.reshape(day_count, minutes, link_blocks * block_width)
    link_residual = (link_flow - counts) / (counts + 1.0)
    signal = (link_residual / (counts + 1.0)).astype(jnp.bfloat16)
    slot_route = one_hot(got_labels, link_blocks, jnp.bfloat16)
    local_paths = one_hot(local_path, path_blocks, jnp.float32)
    remote_paths = one_hot(remote_path, path_blocks, jnp.float32)
    ahead = passed_along(signal[:, :lag_span, :], "tm", -1)
    extended_signal = jnp.concatenate([signal, ahead], axis=1).reshape(
        day_count, minutes + lag_span, link_blocks, block_width
    )
    slot_signal = jnp.einsum(
        "dtkl,sk->sdtl", extended_signal, slot_route, preferred_element_type=jnp.float32
    ).astype(jnp.bfloat16)
    returned = lax.all_to_all(slot_signal, "corr", split_axis=0, concat_axis=0, tiled=True)
    remote_pick = jnp.einsum(
        "sdtl,bs->bdtl", returned, slot_pick, preferred_element_type=jnp.float32
    ).astype(jnp.bfloat16)
    remote_sig = jnp.einsum(
        "bdsl,bts->bdtl",
        remote_pick,
        shift_table(remote_lag, minutes, minutes + lag_span, jnp.bfloat16),
        preferred_element_type=jnp.float32,
    ).astype(jnp.bfloat16)
    local_sig = shift_narrow(
        pick_blocks(extended_signal, local_link_hot),
        shift_table(local_lag, minutes, minutes + lag_span, jnp.bfloat16),
    )
    local_grad = jnp.einsum(
        "dtbl,blp->dtbp", local_sig, local_blocks, preferred_element_type=jnp.float32
    )
    remote_grad = jnp.einsum(
        "bdtl,blp->bdtp", remote_sig, remote_blocks, preferred_element_type=jnp.float32
    )
    grad_cube = collect_paths(local_grad, remote_grad, local_paths, remote_paths)
    gradient = grad_cube.reshape(day_count, minutes, path_width)
    new_flows = jnp.maximum(flows.astype(jnp.float32) - RATE * gradient, 0.0)
    return (link_residual, gradient, new_flows)


HALO = 16
WIRE = jnp.float16


def stage_flows(flows_ref, before_ref, wide, days, width):
    minutes = flows_ref.shape[1]
    span = HALO + minutes
    for p in range(flows_ref.shape[2] // width):
        cols = slice(p * width, (p + 1) * width)
        for d in range(days):
            row = (p * days + d) * span
            before = before_ref[d, :, cols].astype(jnp.float32)
            wide[row : row + HALO, :] = before[minutes - HALO :]
            wide[row + HALO : row + span, :] = flows_ref[d, :, cols].astype(jnp.float32)


def forward_blocks(groups, unroll, mat, base, target, wide, acc, days, minutes):
    span = HALO + minutes

    def group(g, carry):
        parts = []
        for u in range(unroll):
            rows = [wide[pl.ds(base(g, u) + d * span, minutes), :] for d in range(days)]
            taken = jnp.concatenate(rows, axis=0).astype(jnp.bfloat16)
            parts.append(
                lax.dot_general(
                    taken,
                    mat(g, u),
                    (((1,), (1,)), ((), ())),
                    preferred_element_type=jnp.float32,
                )
            )
        for u in range(unroll):
            acc[target(g, u)] += parts[u]
        return carry

    lax.fori_loop(*groups, group, 0)


def backward_blocks(groups, unroll, mat, base, signal, acc, days, minutes):
    span = HALO + minutes

    def group(g, carry):
        parts = [
            jnp.dot(signal(g, u), mat(g, u), preferred_element_type=jnp.float32)
            for u in range(unroll)
        ]
        for u in range(unroll):
            for d in range(days):
                rows = pl.ds(base(g, u) + d * span, minutes)
                acc[rows, :] += parts[u][d * minutes : (d + 1) * minutes]
        return carry

    lax.fori_loop(*groups, group, 0)


class Table:
    def __init__(self, places, slots, blocks):
        self.start = 0
        self.block = self.start + places
        self.base = self.block + slots
        self.link = self.base + blocks
        self.size = self.link + blocks


def prepare_kernel(cap, order, t, row_step, me, *rest):
    sources, (table, mats_out, path, link, lag, slot, sems) = rest[:5], rest[5:]
    blocks = slot.shape[0]
    pairs = zip(sources, (path, link, lag, slot, mats_out))
    copies = [pltpu.make_async_copy(a, b, sems.at[i]) for i, (a, b) in enumerate(pairs)]
    for copy in copies:
        copy.start()
    for p, s in enumerate(order):
        table[t.start + p] = t.block + (me[0] ^ s) * cap
    for i in range((len(order) + 1) * cap):
        table[t.block + i] = -1
    for copy in copies[:4]:
        copy.wait()

    def place(j, carry):
        table[t.block + slot[j]] = j
        table[t.base + j] = path[j] * row_step + HALO - lag[j]
        table[t.link + j] = link[j]
        return carry

    lax.fori_loop(0, blocks, place, 0, unroll=8)
    copies[4].wait()


def slot_views(table, t, mats, links, blank):
    def index(place, rank):
        return table[table[t.start + place] + rank]

    def mat(place, rank):
        return mats[jnp.maximum(index(place, rank), 0)]

    def base(place, rank):
        return table[t.base + jnp.maximum(index(place, rank), 0)]

    def block(place, rank):
        j = index(place, rank)
        spot = place * links + table[t.link + jnp.maximum(j, 0)]
        return jnp.where(j < 0, blank, spot)

    return mat, base, block


def local_views(path, link, lag, mats, unroll, row_step):
    return (
        lambda g, u: mats[g * unroll + u],
        lambda g, u: path[g * unroll + u] * row_step + HALO - lag[g * unroll + u],
        lambda g, u: link[g * unroll + u],
    )


def forward_remote_kernel(days, cap, cuts, links, t, table, flows, before, mats, *rest):
    outs, (wide, acc) = rest[:-2], rest[-2:]
    minutes, width = flows.shape[1], mats.shape[2]
    stage_flows(flows, before, wide, days, width)
    acc[...] = jnp.zeros_like(acc)
    views = slot_views(table, t, mats, links, acc.shape[0] - 1)
    forward_blocks((cuts[0], cuts[-1]), cap, *views, wide, acc, days, minutes)
    for first, end, out in zip(cuts, cuts[1:], outs):
        out[...] = acc[first * links : end * links]


def forward_local_kernel(days, path, link, lag, flows, before, mats, own, wide):
    minutes, width = flows.shape[1], mats.shape[2]
    stage_flows(flows, before, wide, days, width)
    own[...] = jnp.zeros_like(own)
    views = local_views(path, link, lag, mats, 8, days * (HALO + minutes))
    forward_blocks((0, mats.shape[0] // 8), 8, *views, wide, own, days, minutes)


def signal_kernel(days, totals, counts, residual, signal):
    blocks, _, width = totals.shape
    minutes = counts.shape[1]
    for b in range(blocks):
        cols = slice(b * width, (b + 1) * width)
        total = totals[b]
        for d in range(days):
            rows = slice(d * minutes, (d + 1) * minutes)
            seen = counts[d, :, cols]
            weight = seen + 1.0
            res = (total[rows] - seen) / weight
            residual[d, :, cols] = res
            signal[b, rows, :] = (res / weight).astype(signal.dtype)


def backward_local_kernel(days, path, link, lag, signal, mats, out):
    minutes = signal.shape[1] // days
    out[...] = jnp.zeros_like(out)
    mat, base, block = local_views(path, link, lag, mats, 8, days * (HALO + minutes))
    backward_blocks(
        (0, mats.shape[0] // 8),
        8,
        mat,
        base,
        lambda g, u: signal[block(g, u)],
        out,
        days,
        minutes,
    )


def backward_remote_kernel(days, cap, first, end, links, t, table, mats, start, *rest):
    count = (end - first) * links
    signals, sources, rest = [], 0, list(rest)
    while sources < count:
        signals.append(rest.pop(0))
        sources += signals[-1].shape[0]
    out, early, everyone = rest[0], rest[1:-1], rest[-1]
    minutes = signals[0].shape[1] // days
    place = first * links
    for part in signals:
        everyone[place : place + part.shape[0]] = part[...]
        place += part.shape[0]
    blank = everyone.shape[0] - 1
    everyone[blank] = jnp.zeros(everyone.shape[1:], everyone.dtype)
    out[...] = start[...]
    span = HALO + minutes
    mat, base, block = slot_views(table, t, mats, links, blank)
    backward_blocks(
        (first, end), cap, mat, base, lambda g, u: everyone[block(g, u)], out, days, minutes
    )
    if early:
        for i in range(early[0].shape[0]):
            early[0][i] = out[i * span : i * span + HALO, :]


def finish_kernel(days, total, spill, flows, gradient, new_flows):
    minutes = flows.shape[1]
    width = total.shape[1]
    span = HALO + minutes
    for p in range(flows.shape[2] // width):
        cols = slice(p * width, (p + 1) * width)
        for d in range(days):
            row = (p * days + d) * span + HALO
            own = total[row : row + minutes, :]
            keep = minutes - HALO
            late = own[keep:] + spill[p * days + d]
            for rows, grad in ((slice(0, keep), own[:keep]), (slice(keep, minutes), late)):
                gradient[d, rows, cols] = grad
                new_flows[d, rows, cols] = jnp.maximum(
                    flows[d, rows, cols].astype(jnp.float32) - RATE * grad, 0.0
                )


SMEM = pl.BlockSpec(memory_space=pltpu.SMEM)
VMEM = pl.BlockSpec(memory_space=pltpu.VMEM)
HBM = pl.BlockSpec(memory_space=pltpu.HBM)


def kernel_call(body, scalars, arrays, out_shape, scratch=(), cost=None):
    return pl.pallas_call(
        body,
        out_shape=out_shape,
        in_specs=[SMEM] * len(scalars) + [VMEM] * len(arrays),
        out_specs=[VMEM] * len(out_shape),
        scratch_shapes=list(scratch),
        compiler_params=pltpu.CompilerParams(vmem_limit_bytes=40 * 1024 * 1024),
        cost_estimate=cost,
    )(*scalars, *arrays)


def per_device_dense(
    flows,
    counts,
    local_blocks,
    local_path,
    local_link,
    local_lag,
    remote_blocks,
    remote_path,
    remote_link,
    remote_lag,
    remote_slot,
):
    days, minutes, path_width = flows.shape
    width = local_blocks.shape[1]
    paths = path_width // width
    links = counts.shape[2] // width
    corridors = lax.axis_size("corr")
    remotes = remote_lag.shape[0]
    cap = (remotes + corridors - 2) // (corridors - 1)
    span = HALO + minutes
    through = sorted({2, corridors - 2})
    crossing = [s ^ 1 for s in through]
    direct = [s for s in range(corridors - 1, 1, -1) if s not in through + crossing]
    order = crossing + [1] + direct + through
    many = len(through)
    cuts = [0, *range(many, len(order) - many + 1), len(order)]
    t = Table(len(order), corridors * cap, remotes)
    me = lax.axis_index("corr").astype(jnp.int32).reshape(1)
    shape = jax.ShapeDtypeStruct
    piece = (links, days * minutes, width)
    wide = pltpu.VMEM((paths * days * span, width), jnp.float32)
    slots_shape = (len(order) * links + 1, days * minutes, width)
    local_index = (local_path, local_link, local_lag)

    before = passed_along(flows, "tm", 1)
    fixed = (remote_path, remote_link, remote_lag, remote_slot, remote_blocks)
    table, remote_mats = pl.pallas_call(
        functools.partial(prepare_kernel, cap, order, t, days * span),
        out_shape=[
            shape((t.size,), jnp.int32),
            shape(remote_blocks.shape, remote_blocks.dtype),
        ],
        in_specs=[SMEM] + [HBM] * len(fixed),
        out_specs=[SMEM, VMEM],
        scratch_shapes=[pltpu.SMEM(remote_slot.shape, jnp.int32) for _ in fixed[1:]]
        + [pltpu.SemaphoreType.DMA((len(fixed),))],
        compiler_params=pltpu.CompilerParams(vmem_limit_bytes=40 * 1024 * 1024),
    )(me, *(pltpu.with_memory_space_constraint(i, pltpu.HBM) for i in fixed))

    def exchanged(part, s):
        return lax.ppermute(part, "corr", [(i, i ^ s) for i in range(corridors)])

    f32 = jnp.float32
    crossed, *parts, kept = kernel_call(
        functools.partial(forward_remote_kernel, days, cap, cuts, links, t),
        (table,),
        (flows, before, remote_mats),
        [shape(((end - first) * links, *piece[1:]), f32) for first, end in zip(cuts, cuts[1:])],
        [wide, pltpu.VMEM(slots_shape, f32)],
    )
    crossed = exchanged(crossed.astype(WIRE), 1)
    received = [exchanged(p.astype(WIRE), s) for p, s in zip(parts, (1, *direct))]
    (own,) = kernel_call(
        functools.partial(forward_local_kernel, days),
        local_index,
        (flows, before, local_blocks),
        [shape(piece, f32)],
        [wide],
    )
    kept = (kept + crossed.astype(f32)).astype(WIRE).reshape(many, *piece)
    received += [exchanged(kept[i], through[i]) for i in reversed(range(many))]
    totals = functools.reduce(jnp.add, [p.astype(f32) for p in received], own)
    link_residual, signal = kernel_call(
        functools.partial(signal_kernel, days),
        (),
        (totals, counts),
        [shape(counts.shape, f32), shape(piece, jnp.bfloat16)],
    )
    arrived = [exchanged(signal, s) for s in (*through, 1, *direct)]
    both = jnp.concatenate(arrived[:many], axis=0)
    both, signal = lax.optimization_barrier((both, signal))
    rows = [shape((paths * days * span, width), f32)]
    (total,) = kernel_call(
        functools.partial(backward_local_kernel, days),
        local_index,
        (signal, local_blocks),
        rows,
    )
    passed = exchanged(both, 1)
    def weigh(first):
        if first == 0:
            return None
        return pl.CostEstimate(
            flops=2_000_000_000, transcendentals=0, bytes_accessed=6_000_000
        )

    edge = shape((paths * days, HALO, width), f32)
    for first, end, signals, made in (
        (many, len(order), [*arrived[many:], *arrived[:many]], rows),
        (0, many, [passed], [*rows, edge]),
    ):
        total, *early = kernel_call(
            functools.partial(backward_remote_kernel, days, cap, first, end, links, t),
            (table,),
            (remote_mats, total, *signals),
            made,
            [pltpu.VMEM(slots_shape, jnp.bfloat16)],
            weigh(first),
        )
    spill = passed_along(early[0], "tm", -1)
    gradient, new_flows = kernel_call(
        functools.partial(finish_kernel, days),
        (),
        (total, spill, flows),
        [shape(flows.shape, f32)] * 2,
    )
    return (link_residual, gradient, new_flows)


def per_device(*args):
    counts, blocks, lags = args[1], args[2], args[9]
    corridors = lax.axis_size("corr")
    links = counts.shape[2] // blocks.shape[1]
    cap = (lags.shape[0] + corridors - 2) // (corridors - 1)
    if cap >= links and corridors >= 4 and corridors & (corridors - 1) == 0:
        return per_device_dense(*args)
    return per_device_slots(*args)


def solution(mesh):
    placed = (
        P(None, "tm", "corr"),
        P(None, "tm", "corr"),
        P("corr", None, None),
        P("corr"),
        P("corr"),
        P("corr"),
        P("corr", None, None),
        P("corr"),
        P("corr"),
        P("corr"),
        P("corr"),
    )
    return jax.shard_map(
        per_device,
        mesh=mesh,
        in_specs=placed,
        out_specs=(P(None, "tm", "corr"), P(None, "tm", "corr"), P(None, "tm", "corr")),
        check_vma=False,
    )
```

```python
import functools
import jax
import jax.numpy as jnp
from jax import lax
from jax.experimental import pallas as pl
from jax.experimental.pallas import tpu as pltpu
from jax.sharding import PartitionSpec as P

LAGS = 16


HIGH = lax.Precision.HIGHEST
RATE = 0.5


def passed_along(block, axis, distance):
    devices = range(lax.axis_size(axis))
    route = [(i - distance, i) for i in devices if i - distance in devices]
    return lax.ppermute(block, axis, route)


def one_hot(labels, classes, dtype):
    return (labels[:, None] == jnp.arange(classes, dtype=jnp.int32)[None, :]).astype(dtype)


def shift_table(deltas, out_len, in_len, dtype):
    out_pos = jnp.arange(out_len, dtype=jnp.int32)[:, None]
    in_pos = jnp.arange(in_len, dtype=jnp.int32)[None, :]
    return ((in_pos - out_pos)[None, :, :] == deltas[:, None, None]).astype(dtype)


def pick_blocks(cube, hot):
    return jnp.einsum("dsqp,bq->dsbp", cube, hot, preferred_element_type=jnp.float32).astype(
        jnp.bfloat16
    )


def shift_narrow(picked, table):
    return jnp.einsum("dsbp,bts->dtbp", picked, table, preferred_element_type=jnp.float32).astype(
        jnp.bfloat16
    )


def route_partials(local_part, remote_part, local_route, remote_link, slot_hot, link_blocks):
    own = jnp.einsum("dtbl,bk->dtkl", local_part, local_route, precision=HIGH)
    outgoing = jnp.einsum("bdtl,bs->sdtl", remote_part, slot_hot, precision=HIGH)
    slot_int = slot_hot.astype(jnp.int32)
    labels = link_blocks + jnp.sum(slot_int * (remote_link[:, None] - link_blocks), axis=0)
    return (own, outgoing, labels)


def absorb(own, received, got_labels, link_blocks):
    landing = one_hot(got_labels, link_blocks, jnp.float32)
    return own + jnp.einsum("sdtl,sk->dtkl", received, landing, precision=HIGH)


def collect_paths(local_grad, remote_grad, local_paths, remote_paths):
    first_sum = jnp.einsum("dtbp,bq->dtqp", local_grad, local_paths, precision=HIGH)
    return first_sum + jnp.einsum("bdtp,bq->dtqp", remote_grad, remote_paths, precision=HIGH)


def per_device_slots(
    flows,
    counts,
    local_blocks,
    local_path,
    local_link,
    local_lag,
    remote_blocks,
    remote_path,
    remote_link,
    remote_lag,
    remote_slot,
):
    day_count, minutes, path_width = flows.shape
    block_width = local_blocks.shape[1]
    path_blocks = path_width // block_width
    link_blocks = counts.shape[2] // block_width
    lag_span = LAGS - 1
    corridors = lax.axis_size("corr")
    remote_count = remote_lag.shape[0]
    slot_count = corridors * ((remote_count + corridors - 2) // (corridors - 1))
    flow_cube = flows.reshape(day_count, minutes, path_blocks, block_width)
    local_route = one_hot(local_link, link_blocks, jnp.float32)
    slot_hot = one_hot(remote_slot, slot_count, jnp.float32)
    slot_pick = slot_hot.astype(jnp.bfloat16)
    local_path_hot = one_hot(local_path, path_blocks, jnp.bfloat16)
    remote_path_hot = one_hot(remote_path, path_blocks, jnp.bfloat16)
    local_link_hot = one_hot(local_link, link_blocks, jnp.bfloat16)
    local_in = pick_blocks(flow_cube, local_path_hot)
    remote_in = pick_blocks(flow_cube, remote_path_hot)
    local_plain = jnp.einsum(
        "dtbp,blp->dtbl", local_in, local_blocks, preferred_element_type=jnp.float32
    )
    remote_plain = jnp.einsum(
        "dtbp,blp->bdtl", remote_in, remote_blocks, preferred_element_type=jnp.float32
    )
    local_part = jnp.einsum(
        "dsbl,bts->dtbl",
        local_plain,
        shift_table(-local_lag, minutes + lag_span, minutes, jnp.float32),
        precision=HIGH,
    )
    remote_part = jnp.einsum(
        "bdsl,bts->bdtl",
        remote_plain,
        shift_table(-remote_lag, minutes + lag_span, minutes, jnp.float32),
        precision=HIGH,
    )
    own, outgoing, labels = route_partials(
        local_part, remote_part, local_route, remote_link, slot_hot, link_blocks
    )
    received, got_labels = (
        lax.all_to_all(outgoing, "corr", split_axis=0, concat_axis=0, tiled=True),
        lax.all_to_all(labels, "corr", split_axis=0, concat_axis=0, tiled=True),
    )
    extended = absorb(own, received, got_labels, link_blocks)
    spill = passed_along(extended[:, minutes:], "tm", 1)
    totals = extended[:, :minutes] + jnp.pad(
        spill, ((0, 0), (0, minutes - lag_span), (0, 0), (0, 0))
    )
    link_flow = totals.reshape(day_count, minutes, link_blocks * block_width)
    link_residual = (link_flow - counts) / (counts + 1.0)
    signal = (link_residual / (counts + 1.0)).astype(jnp.bfloat16)
    slot_route = one_hot(got_labels, link_blocks, jnp.bfloat16)
    local_paths = one_hot(local_path, path_blocks, jnp.float32)
    remote_paths = one_hot(remote_path, path_blocks, jnp.float32)
    ahead = passed_along(signal[:, :lag_span, :], "tm", -1)
    extended_signal = jnp.concatenate([signal, ahead], axis=1).reshape(
        day_count, minutes + lag_span, link_blocks, block_width
    )
    slot_signal = jnp.einsum(
        "dtkl,sk->sdtl", extended_signal, slot_route, preferred_element_type=jnp.float32
    ).astype(jnp.bfloat16)
    returned = lax.all_to_all(slot_signal, "corr", split_axis=0, concat_axis=0, tiled=True)
    remote_pick = jnp.einsum(
        "sdtl,bs->bdtl", returned, slot_pick, preferred_element_type=jnp.float32
    ).astype(jnp.bfloat16)
    remote_sig = jnp.einsum(
        "bdsl,bts->bdtl",
        remote_pick,
        shift_table(remote_lag, minutes, minutes + lag_span, jnp.bfloat16),
        preferred_element_type=jnp.float32,
    ).astype(jnp.bfloat16)
    local_sig = shift_narrow(
        pick_blocks(extended_signal, local_link_hot),
        shift_table(local_lag, minutes, minutes + lag_span, jnp.bfloat16),
    )
    local_grad = jnp.einsum(
        "dtbl,blp->dtbp", local_sig, local_blocks, preferred_element_type=jnp.float32
    )
    remote_grad = jnp.einsum(
        "bdtl,blp->bdtp", remote_sig, remote_blocks, preferred_element_type=jnp.float32
    )
    grad_cube = collect_paths(local_grad, remote_grad, local_paths, remote_paths)
    gradient = grad_cube.reshape(day_count, minutes, path_width)
    new_flows = jnp.maximum(flows.astype(jnp.float32) - RATE * gradient, 0.0)
    return (link_residual, gradient, new_flows)


HALO = 16
WIRE = jnp.float16


def stage_flows(flows_ref, before_ref, wide, days, width):
    minutes = flows_ref.shape[1]
    span = HALO + minutes
    for p in range(flows_ref.shape[2] // width):
        cols = slice(p * width, (p + 1) * width)
        for d in range(days):
            row = (p * days + d) * span
            before = before_ref[d, :, cols].astype(jnp.float32)
            wide[row : row + HALO, :] = before[minutes - HALO :]
            wide[row + HALO : row + span, :] = flows_ref[d, :, cols].astype(jnp.float32)


def forward_blocks(groups, unroll, mat, base, target, wide, acc, days, minutes):
    span = HALO + minutes

    def group(g, carry):
        parts = []
        for u in range(unroll):
            rows = [wide[pl.ds(base(g, u) + d * span, minutes), :] for d in range(days)]
            taken = jnp.concatenate(rows, axis=0).astype(jnp.bfloat16)
            parts.append(
                lax.dot_general(
                    taken,
                    mat(g, u),
                    (((1,), (1,)), ((), ())),
                    preferred_element_type=jnp.float32,
                )
            )
        for u in range(unroll):
            acc[target(g, u)] += parts[u]
        return carry

    lax.fori_loop(*groups, group, 0)


def backward_blocks(groups, unroll, mat, base, signal, acc, days, minutes):
    span = HALO + minutes

    def group(g, carry):
        parts = [
            jnp.dot(signal(g, u), mat(g, u), preferred_element_type=jnp.float32)
            for u in range(unroll)
        ]
        for u in range(unroll):
            for d in range(days):
                rows = pl.ds(base(g, u) + d * span, minutes)
                acc[rows, :] += parts[u][d * minutes : (d + 1) * minutes]
        return carry

    lax.fori_loop(*groups, group, 0)


class Table:
    def __init__(self, places, slots, blocks):
        self.start = 0
        self.block = self.start + places
        self.base = self.block + slots
        self.link = self.base + blocks
        self.size = self.link + blocks


def prepare_kernel(cap, order, t, row_step, me, *rest):
    sources, (table, mats_out, path, link, lag, slot, sems) = rest[:5], rest[5:]
    blocks = slot.shape[0]
    pairs = zip(sources, (path, link, lag, slot, mats_out))
    copies = [pltpu.make_async_copy(a, b, sems.at[i]) for i, (a, b) in enumerate(pairs)]
    for copy in copies:
        copy.start()
    for p, s in enumerate(order):
        table[t.start + p] = t.block + (me[0] ^ s) * cap
    for i in range((len(order) + 1) * cap):
        table[t.block + i] = -1
    for copy in copies[:4]:
        copy.wait()

    def place(j, carry):
        table[t.block + slot[j]] = j
        table[t.base + j] = path[j] * row_step + HALO - lag[j]
        table[t.link + j] = link[j]
        return carry

    lax.fori_loop(0, blocks, place, 0, unroll=8)
    copies[4].wait()


def slot_views(table, t, mats, links, blank):
    def index(place, rank):
        return table[table[t.start + place] + rank]

    def mat(place, rank):
        return mats[jnp.maximum(index(place, rank), 0)]

    def base(place, rank):
        return table[t.base + jnp.maximum(index(place, rank), 0)]

    def block(place, rank):
        j = index(place, rank)
        spot = place * links + table[t.link + jnp.maximum(j, 0)]
        return jnp.where(j < 0, blank, spot)

    return mat, base, block


def local_views(path, link, lag, mats, unroll, row_step):
    return (
        lambda g, u: mats[g * unroll + u],
        lambda g, u: path[g * unroll + u] * row_step + HALO - lag[g * unroll + u],
        lambda g, u: link[g * unroll + u],
    )


def forward_remote_kernel(days, cap, cuts, links, t, table, flows, before, mats, *rest):
    outs, (wide, acc) = rest[:-2], rest[-2:]
    minutes, width = flows.shape[1], mats.shape[2]
    stage_flows(flows, before, wide, days, width)
    acc[...] = jnp.zeros_like(acc)
    views = slot_views(table, t, mats, links, acc.shape[0] - 1)
    forward_blocks((cuts[0], cuts[-1]), cap, *views, wide, acc, days, minutes)
    for first, end, out in zip(cuts, cuts[1:], outs):
        out[...] = acc[first * links : end * links]


def forward_local_kernel(days, path, link, lag, flows, before, mats, own, wide):
    minutes, width = flows.shape[1], mats.shape[2]
    stage_flows(flows, before, wide, days, width)
    own[...] = jnp.zeros_like(own)
    views = local_views(path, link, lag, mats, 8, days * (HALO + minutes))
    forward_blocks((0, mats.shape[0] // 8), 8, *views, wide, own, days, minutes)


def signal_kernel(days, totals, counts, residual, signal):
    blocks, _, width = totals.shape
    minutes = counts.shape[1]
    for b in range(blocks):
        cols = slice(b * width, (b + 1) * width)
        total = totals[b]
        for d in range(days):
            rows = slice(d * minutes, (d + 1) * minutes)
            seen = counts[d, :, cols]
            weight = seen + 1.0
            res = (total[rows] - seen) / weight
            residual[d, :, cols] = res
            signal[b, rows, :] = (res / weight).astype(signal.dtype)


def backward_local_kernel(days, path, link, lag, signal, mats, out):
    minutes = signal.shape[1] // days
    out[...] = jnp.zeros_like(out)
    mat, base, block = local_views(path, link, lag, mats, 8, days * (HALO + minutes))
    backward_blocks(
        (0, mats.shape[0] // 8),
        8,
        mat,
        base,
        lambda g, u: signal[block(g, u)],
        out,
        days,
        minutes,
    )


def backward_remote_kernel(days, cap, first, end, links, t, table, mats, start, *rest):
    count = (end - first) * links
    signals, sources, rest = [], 0, list(rest)
    while sources < count:
        signals.append(rest.pop(0))
        sources += signals[-1].shape[0]
    out, early, everyone = rest[0], rest[1:-1], rest[-1]
    minutes = signals[0].shape[1] // days
    place = first * links
    for part in signals:
        everyone[place : place + part.shape[0]] = part[...]
        place += part.shape[0]
    blank = everyone.shape[0] - 1
    everyone[blank] = jnp.zeros(everyone.shape[1:], everyone.dtype)
    out[...] = start[...]
    span = HALO + minutes
    mat, base, block = slot_views(table, t, mats, links, blank)
    backward_blocks(
        (first, end), cap, mat, base, lambda g, u: everyone[block(g, u)], out, days, minutes
    )
    if early:
        for i in range(early[0].shape[0]):
            early[0][i] = out[i * span : i * span + HALO, :]


def finish_kernel(days, total, spill, flows, gradient, new_flows):
    minutes = flows.shape[1]
    width = total.shape[1]
    span = HALO + minutes
    for p in range(flows.shape[2] // width):
        cols = slice(p * width, (p + 1) * width)
        for d in range(days):
            row = (p * days + d) * span + HALO
            own = total[row : row + minutes, :]
            keep = minutes - HALO
            late = own[keep:] + spill[p * days + d]
            for rows, grad in ((slice(0, keep), own[:keep]), (slice(keep, minutes), late)):
                gradient[d, rows, cols] = grad
                new_flows[d, rows, cols] = jnp.maximum(
                    flows[d, rows, cols].astype(jnp.float32) - RATE * grad, 0.0
                )


SMEM = pl.BlockSpec(memory_space=pltpu.SMEM)
VMEM = pl.BlockSpec(memory_space=pltpu.VMEM)
HBM = pl.BlockSpec(memory_space=pltpu.HBM)


def kernel_call(body, scalars, arrays, out_shape, scratch=(), cost=None):
    return pl.pallas_call(
        body,
        out_shape=out_shape,
        in_specs=[SMEM] * len(scalars) + [VMEM] * len(arrays),
        out_specs=[VMEM] * len(out_shape),
        scratch_shapes=list(scratch),
        compiler_params=pltpu.CompilerParams(vmem_limit_bytes=40 * 1024 * 1024),
        cost_estimate=cost,
    )(*scalars, *arrays)


def per_device_dense(
    flows,
    counts,
    local_blocks,
    local_path,
    local_link,
    local_lag,
    remote_blocks,
    remote_path,
    remote_link,
    remote_lag,
    remote_slot,
):
    days, minutes, path_width = flows.shape
    width = local_blocks.shape[1]
    paths = path_width // width
    links = counts.shape[2] // width
    corridors = lax.axis_size("corr")
    remotes = remote_lag.shape[0]
    cap = (remotes + corridors - 2) // (corridors - 1)
    span = HALO + minutes
    through = sorted({2, corridors - 2})
    crossing = [s ^ 1 for s in through]
    direct = [s for s in range(corridors - 1, 1, -1) if s not in through + crossing]
    order = crossing + [1] + direct + through
    many = len(through)
    cuts = [0, *range(many, len(order) - many + 1), len(order)]
    t = Table(len(order), corridors * cap, remotes)
    me = lax.axis_index("corr").astype(jnp.int32).reshape(1)
    shape = jax.ShapeDtypeStruct
    piece = (links, days * minutes, width)
    wide = pltpu.VMEM((paths * days * span, width), jnp.float32)
    slots_shape = (len(order) * links + 1, days * minutes, width)
    local_index = (local_path, local_link, local_lag)

    before = passed_along(flows, "tm", 1)
    fixed = (remote_path, remote_link, remote_lag, remote_slot, remote_blocks)
    table, remote_mats = pl.pallas_call(
        functools.partial(prepare_kernel, cap, order, t, days * span),
        out_shape=[
            shape((t.size,), jnp.int32),
            shape(remote_blocks.shape, remote_blocks.dtype),
        ],
        in_specs=[SMEM] + [HBM] * len(fixed),
        out_specs=[SMEM, VMEM],
        scratch_shapes=[pltpu.SMEM(remote_slot.shape, jnp.int32) for _ in fixed[1:]]
        + [pltpu.SemaphoreType.DMA((len(fixed),))],
        compiler_params=pltpu.CompilerParams(vmem_limit_bytes=40 * 1024 * 1024),
    )(me, *(pltpu.with_memory_space_constraint(i, pltpu.HBM) for i in fixed))

    def exchanged(part, s):
        return lax.ppermute(part, "corr", [(i, i ^ s) for i in range(corridors)])

    f32 = jnp.float32
    crossed, *parts, kept = kernel_call(
        functools.partial(forward_remote_kernel, days, cap, cuts, links, t),
        (table,),
        (flows, before, remote_mats),
        [shape(((end - first) * links, *piece[1:]), f32) for first, end in zip(cuts, cuts[1:])],
        [wide, pltpu.VMEM(slots_shape, f32)],
    )
    crossed = exchanged(crossed.astype(WIRE), 1)
    received = [exchanged(p.astype(WIRE), s) for p, s in zip(parts, (1, *direct))]
    (own,) = kernel_call(
        functools.partial(forward_local_kernel, days),
        local_index,
        (flows, before, local_blocks),
        [shape(piece, f32)],
        [wide],
    )
    kept = (kept + crossed.astype(f32)).astype(WIRE).reshape(many, *piece)
    received += [exchanged(kept[i], s) for i, s in enumerate(through)]
    totals = functools.reduce(jnp.add, [p.astype(f32) for p in received], own)
    link_residual, signal = kernel_call(
        functools.partial(signal_kernel, days),
        (),
        (totals, counts),
        [shape(counts.shape, f32), shape(piece, jnp.bfloat16)],
    )
    arrived = [exchanged(signal, s) for s in (*through, 1, *direct)]
    both = jnp.concatenate(arrived[:many], axis=0)
    both, signal = lax.optimization_barrier((both, signal))
    rows = [shape((paths * days * span, width), f32)]
    (total,) = kernel_call(
        functools.partial(backward_local_kernel, days),
        local_index,
        (signal, local_blocks),
        rows,
    )
    passed = exchanged(both, 1)
    def weigh(first):
        if first == 0:
            return None
        return pl.CostEstimate(
            flops=2_000_000_000, transcendentals=0, bytes_accessed=6_000_000
        )

    edge = shape((paths * days, HALO, width), f32)
    for first, end, signals, made in (
        (many, len(order), [*arrived[many:], *arrived[:many]], rows),
        (0, many, [passed], [*rows, edge]),
    ):
        total, *early = kernel_call(
            functools.partial(backward_remote_kernel, days, cap, first, end, links, t),
            (table,),
            (remote_mats, total, *signals),
            made,
            [pltpu.VMEM(slots_shape, jnp.bfloat16)],
            weigh(first),
        )
    spill = passed_along(early[0], "tm", -1)
    gradient, new_flows = kernel_call(
        functools.partial(finish_kernel, days),
        (),
        (total, spill, flows),
        [shape(flows.shape, f32)] * 2,
    )
    return (link_residual, gradient, new_flows)


def per_device(*args):
    counts, blocks, lags = args[1], args[2], args[9]
    corridors = lax.axis_size("corr")
    links = counts.shape[2] // blocks.shape[1]
    cap = (lags.shape[0] + corridors - 2) // (corridors - 1)
    if cap >= links and corridors >= 4 and corridors & (corridors - 1) == 0:
        return per_device_dense(*args)
    return per_device_slots(*args)


def solution(mesh):
    placed = (
        P(None, "tm", "corr"),
        P(None, "tm", "corr"),
        P("corr", None, None),
        P("corr"),
        P("corr"),
        P("corr"),
        P("corr", None, None),
        P("corr"),
        P("corr"),
        P("corr"),
        P("corr"),
    )
    return jax.shard_map(
        per_device,
        mesh=mesh,
        in_specs=placed,
        out_specs=(P(None, "tm", "corr"), P(None, "tm", "corr"), P(None, "tm", "corr")),
        check_vma=False,
    )
```

```python
import functools
import jax
import jax.numpy as jnp
from jax import lax
from jax.experimental import pallas as pl
from jax.experimental.pallas import tpu as pltpu
from jax.sharding import PartitionSpec as P

LAGS = 16


HIGH = lax.Precision.HIGHEST
RATE = 0.5


def passed_along(block, axis, distance):
    devices = range(lax.axis_size(axis))
    route = [(i - distance, i) for i in devices if i - distance in devices]
    return lax.ppermute(block, axis, route)


def one_hot(labels, classes, dtype):
    return (labels[:, None] == jnp.arange(classes, dtype=jnp.int32)[None, :]).astype(dtype)


def shift_table(deltas, out_len, in_len, dtype):
    out_pos = jnp.arange(out_len, dtype=jnp.int32)[:, None]
    in_pos = jnp.arange(in_len, dtype=jnp.int32)[None, :]
    return ((in_pos - out_pos)[None, :, :] == deltas[:, None, None]).astype(dtype)


def pick_blocks(cube, hot):
    return jnp.einsum("dsqp,bq->dsbp", cube, hot, preferred_element_type=jnp.float32).astype(
        jnp.bfloat16
    )


def shift_narrow(picked, table):
    return jnp.einsum("dsbp,bts->dtbp", picked, table, preferred_element_type=jnp.float32).astype(
        jnp.bfloat16
    )


def route_partials(local_part, remote_part, local_route, remote_link, slot_hot, link_blocks):
    own = jnp.einsum("dtbl,bk->dtkl", local_part, local_route, precision=HIGH)
    outgoing = jnp.einsum("bdtl,bs->sdtl", remote_part, slot_hot, precision=HIGH)
    slot_int = slot_hot.astype(jnp.int32)
    labels = link_blocks + jnp.sum(slot_int * (remote_link[:, None] - link_blocks), axis=0)
    return (own, outgoing, labels)


def absorb(own, received, got_labels, link_blocks):
    landing = one_hot(got_labels, link_blocks, jnp.float32)
    return own + jnp.einsum("sdtl,sk->dtkl", received, landing, precision=HIGH)


def collect_paths(local_grad, remote_grad, local_paths, remote_paths):
    first_sum = jnp.einsum("dtbp,bq->dtqp", local_grad, local_paths, precision=HIGH)
    return first_sum + jnp.einsum("bdtp,bq->dtqp", remote_grad, remote_paths, precision=HIGH)


def per_device_slots(
    flows,
    counts,
    local_blocks,
    local_path,
    local_link,
    local_lag,
    remote_blocks,
    remote_path,
    remote_link,
    remote_lag,
    remote_slot,
):
    day_count, minutes, path_width = flows.shape
    block_width = local_blocks.shape[1]
    path_blocks = path_width // block_width
    link_blocks = counts.shape[2] // block_width
    lag_span = LAGS - 1
    corridors = lax.axis_size("corr")
    remote_count = remote_lag.shape[0]
    slot_count = corridors * ((remote_count + corridors - 2) // (corridors - 1))
    flow_cube = flows.reshape(day_count, minutes, path_blocks, block_width)
    local_route = one_hot(local_link, link_blocks, jnp.float32)
    slot_hot = one_hot(remote_slot, slot_count, jnp.float32)
    slot_pick = slot_hot.astype(jnp.bfloat16)
    local_path_hot = one_hot(local_path, path_blocks, jnp.bfloat16)
    remote_path_hot = one_hot(remote_path, path_blocks, jnp.bfloat16)
    local_link_hot = one_hot(local_link, link_blocks, jnp.bfloat16)
    local_in = pick_blocks(flow_cube, local_path_hot)
    remote_in = pick_blocks(flow_cube, remote_path_hot)
    local_plain = jnp.einsum(
        "dtbp,blp->dtbl", local_in, local_blocks, preferred_element_type=jnp.float32
    )
    remote_plain = jnp.einsum(
        "dtbp,blp->bdtl", remote_in, remote_blocks, preferred_element_type=jnp.float32
    )
    local_part = jnp.einsum(
        "dsbl,bts->dtbl",
        local_plain,
        shift_table(-local_lag, minutes + lag_span, minutes, jnp.float32),
        precision=HIGH,
    )
    remote_part = jnp.einsum(
        "bdsl,bts->bdtl",
        remote_plain,
        shift_table(-remote_lag, minutes + lag_span, minutes, jnp.float32),
        precision=HIGH,
    )
    own, outgoing, labels = route_partials(
        local_part, remote_part, local_route, remote_link, slot_hot, link_blocks
    )
    received, got_labels = (
        lax.all_to_all(outgoing, "corr", split_axis=0, concat_axis=0, tiled=True),
        lax.all_to_all(labels, "corr", split_axis=0, concat_axis=0, tiled=True),
    )
    extended = absorb(own, received, got_labels, link_blocks)
    spill = passed_along(extended[:, minutes:], "tm", 1)
    totals = extended[:, :minutes] + jnp.pad(
        spill, ((0, 0), (0, minutes - lag_span), (0, 0), (0, 0))
    )
    link_flow = totals.reshape(day_count, minutes, link_blocks * block_width)
    link_residual = (link_flow - counts) / (counts + 1.0)
    signal = (link_residual / (counts + 1.0)).astype(jnp.bfloat16)
    slot_route = one_hot(got_labels, link_blocks, jnp.bfloat16)
    local_paths = one_hot(local_path, path_blocks, jnp.float32)
    remote_paths = one_hot(remote_path, path_blocks, jnp.float32)
    ahead = passed_along(signal[:, :lag_span, :], "tm", -1)
    extended_signal = jnp.concatenate([signal, ahead], axis=1).reshape(
        day_count, minutes + lag_span, link_blocks, block_width
    )
    slot_signal = jnp.einsum(
        "dtkl,sk->sdtl", extended_signal, slot_route, preferred_element_type=jnp.float32
    ).astype(jnp.bfloat16)
    returned = lax.all_to_all(slot_signal, "corr", split_axis=0, concat_axis=0, tiled=True)
    remote_pick = jnp.einsum(
        "sdtl,bs->bdtl", returned, slot_pick, preferred_element_type=jnp.float32
    ).astype(jnp.bfloat16)
    remote_sig = jnp.einsum(
        "bdsl,bts->bdtl",
        remote_pick,
        shift_table(remote_lag, minutes, minutes + lag_span, jnp.bfloat16),
        preferred_element_type=jnp.float32,
    ).astype(jnp.bfloat16)
    local_sig = shift_narrow(
        pick_blocks(extended_signal, local_link_hot),
        shift_table(local_lag, minutes, minutes + lag_span, jnp.bfloat16),
    )
    local_grad = jnp.einsum(
        "dtbl,blp->dtbp", local_sig, local_blocks, preferred_element_type=jnp.float32
    )
    remote_grad = jnp.einsum(
        "bdtl,blp->bdtp", remote_sig, remote_blocks, preferred_element_type=jnp.float32
    )
    grad_cube = collect_paths(local_grad, remote_grad, local_paths, remote_paths)
    gradient = grad_cube.reshape(day_count, minutes, path_width)
    new_flows = jnp.maximum(flows.astype(jnp.float32) - RATE * gradient, 0.0)
    return (link_residual, gradient, new_flows)


HALO = 16
WIRE = jnp.float16
UNROLL = 32
CHUNKS = 8


def step_of(count):
    return next(u for u in range(min(count, UNROLL), 0, -1) if count % u == 0)


def stage_flows(flows_ref, before_ref, wide, days, width):
    minutes = flows_ref.shape[1]
    span = HALO + minutes
    for p in range(flows_ref.shape[2] // width):
        cols = slice(p * width, (p + 1) * width)
        for d in range(days):
            row = (p * days + d) * span
            before = before_ref[d, :, cols].astype(jnp.float32)
            wide[row : row + HALO, :] = before[minutes - HALO :]
            wide[row + HALO : row + span, :] = flows_ref[d, :, cols].astype(jnp.float32)


def forward_blocks(groups, unroll, mat, base, target, wide, acc, days, minutes):
    span = HALO + minutes

    def group(g, carry):
        parts = []
        for u in range(unroll):
            rows = [wide[pl.ds(base(g, u) + d * span, minutes), :] for d in range(days)]
            taken = jnp.concatenate(rows, axis=0).astype(jnp.bfloat16)
            parts.append(
                lax.dot_general(
                    taken,
                    mat(g, u),
                    (((1,), (1,)), ((), ())),
                    preferred_element_type=jnp.float32,
                )
            )
        for u in range(unroll):
            acc[target(g, u)] += parts[u]
        return carry

    lax.fori_loop(0, groups, group, 0)


def backward_blocks(groups, unroll, mat, base, signal, acc, days, minutes):
    span = HALO + minutes

    def group(g, carry):
        parts = [
            jnp.dot(signal(g, u), mat(g, u), preferred_element_type=jnp.float32)
            for u in range(unroll)
        ]
        for u in range(unroll):
            for d in range(days):
                rows = pl.ds(base(g, u) + d * span, minutes)
                acc[rows, :] += parts[u][d * minutes : (d + 1) * minutes]
        return carry

    lax.fori_loop(0, groups, group, 0)


class Table:
    def __init__(self, places, slots, blocks):
        self.start = 0
        self.block = self.start + places
        self.base = self.block + slots
        self.link = self.base + blocks
        self.size = self.link + blocks


def prepare_kernel(cap, order, links, chunks, row_step, me, *rest):
    sources, (ahead, mats_out, path, link, lag, slot, place, sems) = rest[:5], rest[5:]
    blocks = slot.shape[0]
    pairs = list(zip(sources[:4], (path, link, lag, slot)))
    step = blocks // chunks
    for c in range(chunks):
        rows = slice(c * step, blocks if c == chunks - 1 else (c + 1) * step)
        pairs.append((sources[4].at[rows], mats_out.at[rows]))
    copies = [pltpu.make_async_copy(a, b, sems.at[i]) for i, (a, b) in enumerate(pairs)]
    for copy in copies:
        copy.start()
    place[0] = 0
    for p, s in enumerate(order):
        place[s] = p * links
    for copy in copies[:4]:
        copy.wait()

    def entry(j, carry):
        ahead[j] = path[j] * row_step + HALO - lag[j]
        ahead[blocks + j] = place[lax.div(slot[j], cap) ^ me[0]] + link[j]
        return carry

    lax.fori_loop(0, blocks, entry, 0, unroll=16)
    for copy in copies[4:]:
        copy.wait()


def fill_table(cap, order, links, t, me, ahead, slot, table):
    blocks = slot.shape[0]
    for p, s in enumerate(order):
        table[t.start + p] = t.block + (me[0] ^ s) * cap
    for i in range((len(order) + 1) * cap):
        table[t.block + i] = -1

    def entry(j, carry):
        table[t.block + slot[j]] = j
        table[t.base + j] = ahead[j]
        table[t.link + j] = ahead[blocks + j]
        return carry

    lax.fori_loop(0, blocks, entry, 0, unroll=16)


def slot_views(table, t, mats, cap, first, unroll, blank):
    def index(g, u):
        at = first * cap + g * unroll + u
        place = lax.div(at, cap)
        return table[table[t.start + place] + at - place * cap]

    def mat(g, u):
        return mats[jnp.maximum(index(g, u), 0)]

    def base(g, u):
        return table[t.base + jnp.maximum(index(g, u), 0)]

    def block(g, u):
        j = index(g, u)
        return jnp.where(j < 0, blank, table[t.link + jnp.maximum(j, 0)])

    return mat, base, block


def forward_remote_kernel(days, cuts, links, ahead, flows, before, mats, *rest):
    outs, (wide, acc) = rest[:-2], rest[-2:]
    minutes, width = flows.shape[1], mats.shape[2]
    blocks = mats.shape[0]
    stage_flows(flows, before, wide, days, width)
    acc[...] = jnp.zeros_like(acc)
    unroll = step_of(blocks)
    forward_blocks(
        blocks // unroll,
        unroll,
        lambda g, u: mats[g * unroll + u],
        lambda g, u: ahead[g * unroll + u],
        lambda g, u: ahead[blocks + g * unroll + u],
        wide,
        acc,
        days,
        minutes,
    )
    for first, end, out in zip(cuts, cuts[1:], outs):
        out[...] = acc[first * links : end * links]


def local_views(path, link, lag, mats, unroll, row_step):
    return (
        lambda g, u: mats[g * unroll + u],
        lambda g, u: path[g * unroll + u] * row_step + HALO - lag[g * unroll + u],
        lambda g, u: link[g * unroll + u],
    )


def forward_local_kernel(
    days, cap, order, t, links, me, ahead, slot, path, link, lag, flows, before, mats, own, table, wide
):
    minutes, width = flows.shape[1], mats.shape[2]
    stage_flows(flows, before, wide, days, width)
    own[...] = jnp.zeros_like(own)
    unroll = step_of(mats.shape[0])
    views = local_views(path, link, lag, mats, unroll, days * (HALO + minutes))
    forward_blocks(mats.shape[0] // unroll, unroll, *views, wide, own, days, minutes)
    fill_table(cap, order, links, t, me, ahead, slot, table)


def signal_kernel(days, totals, counts, residual, signal):
    blocks, _, width = totals.shape
    minutes = counts.shape[1]
    for b in range(blocks):
        cols = slice(b * width, (b + 1) * width)
        total = totals[b]
        for d in range(days):
            rows = slice(d * minutes, (d + 1) * minutes)
            seen = counts[d, :, cols]
            weight = seen + 1.0
            res = (total[rows] - seen) / weight
            residual[d, :, cols] = res
            signal[b, rows, :] = (res / weight).astype(signal.dtype)


def backward_local_kernel(days, path, link, lag, signal, mats, out):
    minutes = signal.shape[1] // days
    out[...] = jnp.zeros_like(out)
    unroll = step_of(mats.shape[0])
    mat, base, block = local_views(path, link, lag, mats, unroll, days * (HALO + minutes))
    backward_blocks(
        mats.shape[0] // unroll,
        unroll,
        mat,
        base,
        lambda g, u: signal[block(g, u)],
        out,
        days,
        minutes,
    )


def backward_remote_kernel(days, cap, first, end, links, t, table, mats, start, *rest):
    count = (end - first) * links
    signals, sources, rest = [], 0, list(rest)
    while sources < count:
        signals.append(rest.pop(0))
        sources += signals[-1].shape[0]
    out, early, everyone = rest[0], rest[1:-1], rest[-1]
    minutes = signals[0].shape[1] // days
    place = first * links
    for part in signals:
        everyone[place : place + part.shape[0]] = part[...]
        place += part.shape[0]
    blank = everyone.shape[0] - 1
    everyone[blank] = jnp.zeros(everyone.shape[1:], everyone.dtype)
    out[...] = start[...]
    span = HALO + minutes
    slots = (end - first) * cap
    unroll = step_of(slots)
    mat, base, block = slot_views(table, t, mats, cap, first, unroll, blank)
    backward_blocks(
        slots // unroll,
        unroll,
        mat,
        base,
        lambda g, u: everyone[block(g, u)],
        out,
        days,
        minutes,
    )
    if early:
        for i in range(early[0].shape[0]):
            early[0][i] = out[i * span : i * span + HALO, :]


def finish_kernel(days, total, spill, flows, gradient, new_flows):
    minutes = flows.shape[1]
    width = total.shape[1]
    span = HALO + minutes
    for p in range(flows.shape[2] // width):
        cols = slice(p * width, (p + 1) * width)
        for d in range(days):
            row = (p * days + d) * span + HALO
            own = total[row : row + minutes, :]
            keep = minutes - HALO
            late = own[keep:] + spill[p * days + d]
            for rows, grad in ((slice(0, keep), own[:keep]), (slice(keep, minutes), late)):
                gradient[d, rows, cols] = grad
                new_flows[d, rows, cols] = jnp.maximum(
                    flows[d, rows, cols].astype(jnp.float32) - RATE * grad, 0.0
                )


SMEM = pl.BlockSpec(memory_space=pltpu.SMEM)
VMEM = pl.BlockSpec(memory_space=pltpu.VMEM)
HBM = pl.BlockSpec(memory_space=pltpu.HBM)


def kernel_call(body, scalars, arrays, out_shape, scratch=(), cost=None, outs=None):
    return pl.pallas_call(
        body,
        out_shape=out_shape,
        in_specs=[SMEM] * len(scalars) + [VMEM] * len(arrays),
        out_specs=outs or [VMEM] * len(out_shape),
        scratch_shapes=list(scratch),
        compiler_params=pltpu.CompilerParams(vmem_limit_bytes=40 * 1024 * 1024),
        cost_estimate=cost,
    )(*scalars, *arrays)


def per_device_dense(
    flows,
    counts,
    local_blocks,
    local_path,
    local_link,
    local_lag,
    remote_blocks,
    remote_path,
    remote_link,
    remote_lag,
    remote_slot,
):
    days, minutes, path_width = flows.shape
    width = local_blocks.shape[1]
    paths = path_width // width
    links = counts.shape[2] // width
    corridors = lax.axis_size("corr")
    remotes = remote_lag.shape[0]
    cap = (remotes + corridors - 2) // (corridors - 1)
    span = HALO + minutes
    through = sorted({2, corridors - 2})
    crossing = [s ^ 1 for s in through]
    direct = [s for s in range(corridors - 1, 1, -1) if s not in through + crossing]
    order = crossing + [1] + direct + through
    many = len(through)
    cuts = [0, *range(many, len(order) - many + 1), len(order)]
    t = Table(len(order), corridors * cap, remotes)
    me = lax.axis_index("corr").astype(jnp.int32).reshape(1)
    shape = jax.ShapeDtypeStruct
    piece = (links, days * minutes, width)
    wide = pltpu.VMEM((paths * days * span, width), jnp.float32)
    slots_shape = (len(order) * links + 1, days * minutes, width)
    local_index = (local_path, local_link, local_lag)

    before = passed_along(flows, "tm", 1)
    fixed = (remote_path, remote_link, remote_lag, remote_slot, remote_blocks)
    ahead, remote_mats = pl.pallas_call(
        functools.partial(prepare_kernel, cap, order, links, CHUNKS, days * span),
        out_shape=[
            shape((2 * remotes,), jnp.int32),
            shape(remote_blocks.shape, remote_blocks.dtype),
        ],
        in_specs=[SMEM] + [HBM] * len(fixed),
        out_specs=[SMEM, VMEM],
        scratch_shapes=[pltpu.SMEM(remote_slot.shape, jnp.int32) for _ in fixed[1:]]
        + [pltpu.SMEM((corridors,), jnp.int32), pltpu.SemaphoreType.DMA((len(fixed) - 1 + CHUNKS,))],
        compiler_params=pltpu.CompilerParams(vmem_limit_bytes=40 * 1024 * 1024),
    )(me, *(pltpu.with_memory_space_constraint(i, pltpu.HBM) for i in fixed))

    def exchanged(part, s):
        return lax.ppermute(part, "corr", [(i, i ^ s) for i in range(corridors)])

    f32 = jnp.float32
    crossed, *parts, kept = kernel_call(
        functools.partial(forward_remote_kernel, days, cuts, links),
        (ahead,),
        (flows, before, remote_mats),
        [shape(((end - first) * links, *piece[1:]), f32) for first, end in zip(cuts, cuts[1:])],
        [wide, pltpu.VMEM((len(order) * links, *piece[1:]), f32)],
    )
    crossed = exchanged(crossed.astype(WIRE), 1)
    near, crossed = lax.optimization_barrier((parts[0].astype(WIRE), crossed))
    received = [exchanged(p.astype(WIRE), s) for p, s in zip(parts[1:], direct)]
    received.append(exchanged(near, 1))
    own, table = kernel_call(
        functools.partial(forward_local_kernel, days, cap, order, t, links),
        (me, ahead, remote_slot, *local_index),
        (flows, before, local_blocks),
        [shape(piece, f32), shape((t.size,), jnp.int32)],
        [wide],
        outs=[VMEM, SMEM],
    )
    kept = (kept + crossed.astype(f32)).astype(WIRE).reshape(many, *piece)
    received += [exchanged(kept[i], s) for i, s in enumerate(through)]
    totals = functools.reduce(jnp.add, [p.astype(f32) for p in received], own)
    link_residual, signal = kernel_call(
        functools.partial(signal_kernel, days),
        (),
        (totals, counts),
        [shape(counts.shape, f32), shape(piece, jnp.bfloat16)],
    )
    arrived = [exchanged(signal, s) for s in (*through, *direct)]
    both = jnp.concatenate([*arrived[:many], signal], axis=0)
    both, signal = lax.optimization_barrier((both, signal))
    rows = [shape((paths * days * span, width), f32)]
    (total,) = kernel_call(
        functools.partial(backward_local_kernel, days),
        local_index,
        (signal, local_blocks),
        rows,
    )
    passed = exchanged(both, 1)
    def weigh(first):
        if first == 0:
            return None
        return pl.CostEstimate(
            flops=2_000_000_000, transcendentals=0, bytes_accessed=6_000_000
        )

    edge = shape((paths * days, HALO, width), f32)
    for first, end, signals, made in (
        (many + 1, len(order), [*arrived[many:], *arrived[:many]], rows),
        (0, many + 1, [passed], [*rows, edge]),
    ):
        total, *early = kernel_call(
            functools.partial(backward_remote_kernel, days, cap, first, end, links, t),
            (table,),
            (remote_mats, total, *signals),
            made,
            [pltpu.VMEM(slots_shape, jnp.bfloat16)],
            weigh(first),
        )
    spill = passed_along(early[0], "tm", -1)
    gradient, new_flows = kernel_call(
        functools.partial(finish_kernel, days),
        (),
        (total, spill, flows),
        [shape(flows.shape, f32)] * 2,
    )
    return (link_residual, gradient, new_flows)


def per_device(*args):
    counts, blocks, lags = args[1], args[2], args[9]
    corridors = lax.axis_size("corr")
    links = counts.shape[2] // blocks.shape[1]
    cap = (lags.shape[0] + corridors - 2) // (corridors - 1)
    if cap >= links and corridors >= 4 and corridors & (corridors - 1) == 0:
        return per_device_dense(*args)
    return per_device_slots(*args)


def solution(mesh):
    placed = (
        P(None, "tm", "corr"),
        P(None, "tm", "corr"),
        P("corr", None, None),
        P("corr"),
        P("corr"),
        P("corr"),
        P("corr", None, None),
        P("corr"),
        P("corr"),
        P("corr"),
        P("corr"),
    )
    return jax.shard_map(
        per_device,
        mesh=mesh,
        in_specs=placed,
        out_specs=(P(None, "tm", "corr"), P(None, "tm", "corr"), P(None, "tm", "corr")),
        check_vma=False,
    )
```

```python
import functools
import jax
import jax.numpy as jnp
from jax import lax
from jax.experimental import pallas as pl
from jax.experimental.pallas import tpu as pltpu
from jax.sharding import PartitionSpec as P

LAGS = 16


HIGH = lax.Precision.HIGHEST
RATE = 0.5


def passed_along(block, axis, distance):
    devices = range(lax.axis_size(axis))
    route = [(i - distance, i) for i in devices if i - distance in devices]
    return lax.ppermute(block, axis, route)


def one_hot(labels, classes, dtype):
    return (labels[:, None] == jnp.arange(classes, dtype=jnp.int32)[None, :]).astype(dtype)


def shift_table(deltas, out_len, in_len, dtype):
    out_pos = jnp.arange(out_len, dtype=jnp.int32)[:, None]
    in_pos = jnp.arange(in_len, dtype=jnp.int32)[None, :]
    return ((in_pos - out_pos)[None, :, :] == deltas[:, None, None]).astype(dtype)


def pick_blocks(cube, hot):
    return jnp.einsum("dsqp,bq->dsbp", cube, hot, preferred_element_type=jnp.float32).astype(
        jnp.bfloat16
    )


def shift_narrow(picked, table):
    return jnp.einsum("dsbp,bts->dtbp", picked, table, preferred_element_type=jnp.float32).astype(
        jnp.bfloat16
    )


def route_partials(local_part, remote_part, local_route, remote_link, slot_hot, link_blocks):
    own = jnp.einsum("dtbl,bk->dtkl", local_part, local_route, precision=HIGH)
    outgoing = jnp.einsum("bdtl,bs->sdtl", remote_part, slot_hot, precision=HIGH)
    slot_int = slot_hot.astype(jnp.int32)
    labels = link_blocks + jnp.sum(slot_int * (remote_link[:, None] - link_blocks), axis=0)
    return (own, outgoing, labels)


def absorb(own, received, got_labels, link_blocks):
    landing = one_hot(got_labels, link_blocks, jnp.float32)
    return own + jnp.einsum("sdtl,sk->dtkl", received, landing, precision=HIGH)


def collect_paths(local_grad, remote_grad, local_paths, remote_paths):
    first_sum = jnp.einsum("dtbp,bq->dtqp", local_grad, local_paths, precision=HIGH)
    return first_sum + jnp.einsum("bdtp,bq->dtqp", remote_grad, remote_paths, precision=HIGH)


def per_device_slots(
    flows,
    counts,
    local_blocks,
    local_path,
    local_link,
    local_lag,
    remote_blocks,
    remote_path,
    remote_link,
    remote_lag,
    remote_slot,
):
    day_count, minutes, path_width = flows.shape
    block_width = local_blocks.shape[1]
    path_blocks = path_width // block_width
    link_blocks = counts.shape[2] // block_width
    lag_span = LAGS - 1
    corridors = lax.axis_size("corr")
    remote_count = remote_lag.shape[0]
    slot_count = corridors * ((remote_count + corridors - 2) // (corridors - 1))
    flow_cube = flows.reshape(day_count, minutes, path_blocks, block_width)
    local_route = one_hot(local_link, link_blocks, jnp.float32)
    slot_hot = one_hot(remote_slot, slot_count, jnp.float32)
    slot_pick = slot_hot.astype(jnp.bfloat16)
    local_path_hot = one_hot(local_path, path_blocks, jnp.bfloat16)
    remote_path_hot = one_hot(remote_path, path_blocks, jnp.bfloat16)
    local_link_hot = one_hot(local_link, link_blocks, jnp.bfloat16)
    local_in = pick_blocks(flow_cube, local_path_hot)
    remote_in = pick_blocks(flow_cube, remote_path_hot)
    local_plain = jnp.einsum(
        "dtbp,blp->dtbl", local_in, local_blocks, preferred_element_type=jnp.float32
    )
    remote_plain = jnp.einsum(
        "dtbp,blp->bdtl", remote_in, remote_blocks, preferred_element_type=jnp.float32
    )
    local_part = jnp.einsum(
        "dsbl,bts->dtbl",
        local_plain,
        shift_table(-local_lag, minutes + lag_span, minutes, jnp.float32),
        precision=HIGH,
    )
    remote_part = jnp.einsum(
        "bdsl,bts->bdtl",
        remote_plain,
        shift_table(-remote_lag, minutes + lag_span, minutes, jnp.float32),
        precision=HIGH,
    )
    own, outgoing, labels = route_partials(
        local_part, remote_part, local_route, remote_link, slot_hot, link_blocks
    )
    received, got_labels = (
        lax.all_to_all(outgoing, "corr", split_axis=0, concat_axis=0, tiled=True),
        lax.all_to_all(labels, "corr", split_axis=0, concat_axis=0, tiled=True),
    )
    extended = absorb(own, received, got_labels, link_blocks)
    spill = passed_along(extended[:, minutes:], "tm", 1)
    totals = extended[:, :minutes] + jnp.pad(
        spill, ((0, 0), (0, minutes - lag_span), (0, 0), (0, 0))
    )
    link_flow = totals.reshape(day_count, minutes, link_blocks * block_width)
    link_residual = (link_flow - counts) / (counts + 1.0)
    signal = (link_residual / (counts + 1.0)).astype(jnp.bfloat16)
    slot_route = one_hot(got_labels, link_blocks, jnp.bfloat16)
    local_paths = one_hot(local_path, path_blocks, jnp.float32)
    remote_paths = one_hot(remote_path, path_blocks, jnp.float32)
    ahead = passed_along(signal[:, :lag_span, :], "tm", -1)
    extended_signal = jnp.concatenate([signal, ahead], axis=1).reshape(
        day_count, minutes + lag_span, link_blocks, block_width
    )
    slot_signal = jnp.einsum(
        "dtkl,sk->sdtl", extended_signal, slot_route, preferred_element_type=jnp.float32
    ).astype(jnp.bfloat16)
    returned = lax.all_to_all(slot_signal, "corr", split_axis=0, concat_axis=0, tiled=True)
    remote_pick = jnp.einsum(
        "sdtl,bs->bdtl", returned, slot_pick, preferred_element_type=jnp.float32
    ).astype(jnp.bfloat16)
    remote_sig = jnp.einsum(
        "bdsl,bts->bdtl",
        remote_pick,
        shift_table(remote_lag, minutes, minutes + lag_span, jnp.bfloat16),
        preferred_element_type=jnp.float32,
    ).astype(jnp.bfloat16)
    local_sig = shift_narrow(
        pick_blocks(extended_signal, local_link_hot),
        shift_table(local_lag, minutes, minutes + lag_span, jnp.bfloat16),
    )
    local_grad = jnp.einsum(
        "dtbl,blp->dtbp", local_sig, local_blocks, preferred_element_type=jnp.float32
    )
    remote_grad = jnp.einsum(
        "bdtl,blp->bdtp", remote_sig, remote_blocks, preferred_element_type=jnp.float32
    )
    grad_cube = collect_paths(local_grad, remote_grad, local_paths, remote_paths)
    gradient = grad_cube.reshape(day_count, minutes, path_width)
    new_flows = jnp.maximum(flows.astype(jnp.float32) - RATE * gradient, 0.0)
    return (link_residual, gradient, new_flows)


HALO = 16
WIRE = jnp.float16
UNROLL = 32
CHUNKS = 8


def step_of(count):
    return next(u for u in range(min(count, UNROLL), 0, -1) if count % u == 0)


def stage_flows(group, flows_ref, before_ref, wide, days, width):
    real = jnp.where(group[0] > 0, 1.0, 0.0)
    minutes = flows_ref.shape[1]
    span = HALO + minutes
    for p in range(flows_ref.shape[2] // width):
        cols = slice(p * width, (p + 1) * width)
        for d in range(days):
            row = (p * days + d) * span
            before = before_ref[d, :, cols].astype(jnp.float32)
            wide[row : row + HALO, :] = before[minutes - HALO :] * real
            wide[row + HALO : row + span, :] = flows_ref[d, :, cols].astype(jnp.float32)


def forward_blocks(groups, unroll, mat, base, target, wide, acc, days, minutes):
    span = HALO + minutes

    def group(g, carry):
        parts = []
        for u in range(unroll):
            rows = [wide[pl.ds(base(g, u) + d * span, minutes), :] for d in range(days)]
            taken = jnp.concatenate(rows, axis=0).astype(jnp.bfloat16)
            parts.append(
                lax.dot_general(
                    taken,
                    mat(g, u),
                    (((1,), (1,)), ((), ())),
                    preferred_element_type=jnp.float32,
                )
            )
        for u in range(unroll):
            acc[target(g, u)] += parts[u]
        return carry

    lax.fori_loop(0, groups, group, 0)


def backward_blocks(groups, unroll, mat, base, signal, acc, days, minutes):
    span = HALO + minutes

    def group(g, carry):
        parts = [
            jnp.dot(signal(g, u), mat(g, u), preferred_element_type=jnp.float32)
            for u in range(unroll)
        ]
        for u in range(unroll):
            for d in range(days):
                rows = pl.ds(base(g, u) + d * span, minutes)
                acc[rows, :] += parts[u][d * minutes : (d + 1) * minutes]
        return carry

    lax.fori_loop(0, groups, group, 0)


class Table:
    def __init__(self, places, slots, blocks):
        self.start = 0
        self.block = self.start + places
        self.base = self.block + slots
        self.link = self.base + blocks
        self.size = self.link + blocks


def prepare_kernel(cap, order, links, chunks, row_step, me, *rest):
    sources, (ahead, mats_out, path, link, lag, slot, place, sems) = rest[:5], rest[5:]
    blocks = slot.shape[0]
    pairs = list(zip(sources[:4], (path, link, lag, slot)))
    step = blocks // chunks
    for c in range(chunks):
        rows = slice(c * step, blocks if c == chunks - 1 else (c + 1) * step)
        pairs.append((sources[4].at[rows], mats_out.at[rows]))
    copies = [pltpu.make_async_copy(a, b, sems.at[i]) for i, (a, b) in enumerate(pairs)]
    for copy in copies:
        copy.start()
    place[0] = 0
    for p, s in enumerate(order):
        place[s] = p * links
    for copy in copies[:4]:
        copy.wait()

    def entry(j, carry):
        ahead[j] = path[j] * row_step + HALO - lag[j]
        ahead[blocks + j] = place[lax.div(slot[j], cap) ^ me[0]] + link[j]
        return carry

    lax.fori_loop(0, blocks, entry, 0, unroll=16)
    for copy in copies[4:]:
        copy.wait()


def fill_table(cap, order, links, t, me, ahead, slot, table):
    blocks = slot.shape[0]
    for p, s in enumerate(order):
        table[t.start + p] = t.block + (me[0] ^ s) * cap
    for i in range((len(order) + 1) * cap):
        table[t.block + i] = -1

    def entry(j, carry):
        table[t.block + slot[j]] = j
        table[t.base + j] = ahead[j]
        table[t.link + j] = ahead[blocks + j]
        return carry

    lax.fori_loop(0, blocks, entry, 0, unroll=16)


def slot_views(table, t, mats, cap, first, unroll, blank):
    def index(g, u):
        at = first * cap + g * unroll + u
        place = lax.div(at, cap)
        return table[table[t.start + place] + at - place * cap]

    def mat(g, u):
        return mats[jnp.maximum(index(g, u), 0)]

    def base(g, u):
        return table[t.base + jnp.maximum(index(g, u), 0)]

    def block(g, u):
        j = index(g, u)
        return jnp.where(j < 0, blank, table[t.link + jnp.maximum(j, 0)])

    return mat, base, block


def forward_remote_kernel(days, cuts, links, group, ahead, flows, before, mats, *rest):
    outs, (wide, acc) = rest[:-2], rest[-2:]
    minutes, width = flows.shape[1], mats.shape[2]
    blocks = mats.shape[0]
    stage_flows(group, flows, before, wide, days, width)
    acc[...] = jnp.zeros_like(acc)
    unroll = step_of(blocks)
    forward_blocks(
        blocks // unroll,
        unroll,
        lambda g, u: mats[g * unroll + u],
        lambda g, u: ahead[g * unroll + u],
        lambda g, u: ahead[blocks + g * unroll + u],
        wide,
        acc,
        days,
        minutes,
    )
    for first, end, out in zip(cuts, cuts[1:], outs):
        out[...] = acc[first * links : end * links]


def local_views(path, link, lag, mats, unroll, row_step):
    return (
        lambda g, u: mats[g * unroll + u],
        lambda g, u: path[g * unroll + u] * row_step + HALO - lag[g * unroll + u],
        lambda g, u: link[g * unroll + u],
    )


def forward_local_kernel(
    days, cap, order, t, links, group, me, ahead, slot, path, link, lag, flows, before, mats, own, table, wide
):
    minutes, width = flows.shape[1], mats.shape[2]
    stage_flows(group, flows, before, wide, days, width)
    own[...] = jnp.zeros_like(own)
    unroll = step_of(mats.shape[0])
    views = local_views(path, link, lag, mats, unroll, days * (HALO + minutes))
    forward_blocks(mats.shape[0] // unroll, unroll, *views, wide, own, days, minutes)
    fill_table(cap, order, links, t, me, ahead, slot, table)


def signal_kernel(days, totals, counts, residual, signal):
    blocks, _, width = totals.shape
    minutes = counts.shape[1]
    for b in range(blocks):
        cols = slice(b * width, (b + 1) * width)
        total = totals[b]
        for d in range(days):
            rows = slice(d * minutes, (d + 1) * minutes)
            seen = counts[d, :, cols]
            weight = seen + 1.0
            res = (total[rows] - seen) / weight
            residual[d, :, cols] = res
            signal[b, rows, :] = (res / weight).astype(signal.dtype)


def backward_local_kernel(days, path, link, lag, signal, mats, out):
    minutes = signal.shape[1] // days
    out[...] = jnp.zeros_like(out)
    unroll = step_of(mats.shape[0])
    mat, base, block = local_views(path, link, lag, mats, unroll, days * (HALO + minutes))
    backward_blocks(
        mats.shape[0] // unroll,
        unroll,
        mat,
        base,
        lambda g, u: signal[block(g, u)],
        out,
        days,
        minutes,
    )


def backward_remote_kernel(days, cap, first, end, links, t, table, mats, start, *rest):
    count = (end - first) * links
    signals, sources, rest = [], 0, list(rest)
    while sources < count:
        signals.append(rest.pop(0))
        sources += signals[-1].shape[0]
    out, early, everyone = rest[0], rest[1:-1], rest[-1]
    minutes = signals[0].shape[1] // days
    place = first * links
    for part in signals:
        everyone[place : place + part.shape[0]] = part[...]
        place += part.shape[0]
    blank = everyone.shape[0] - 1
    everyone[blank] = jnp.zeros(everyone.shape[1:], everyone.dtype)
    out[...] = start[...]
    span = HALO + minutes
    slots = (end - first) * cap
    unroll = step_of(slots)
    mat, base, block = slot_views(table, t, mats, cap, first, unroll, blank)
    backward_blocks(
        slots // unroll,
        unroll,
        mat,
        base,
        lambda g, u: everyone[block(g, u)],
        out,
        days,
        minutes,
    )
    if early:
        for i in range(early[0].shape[0]):
            early[0][i] = out[i * span : i * span + HALO, :]


def finish_kernel(days, groups, group, total, spill, flows, gradient, new_flows):
    minutes = flows.shape[1]
    width = total.shape[1]
    span = HALO + minutes
    real = jnp.where(group[0] < groups - 1, 1.0, 0.0)
    for p in range(flows.shape[2] // width):
        cols = slice(p * width, (p + 1) * width)
        for d in range(days):
            row = (p * days + d) * span + HALO
            own = total[row : row + minutes, :]
            keep = minutes - HALO
            late = own[keep:] + spill[p * days + d] * real
            for rows, grad in ((slice(0, keep), own[:keep]), (slice(keep, minutes), late)):
                gradient[d, rows, cols] = grad
                new_flows[d, rows, cols] = jnp.maximum(
                    flows[d, rows, cols].astype(jnp.float32) - RATE * grad, 0.0
                )


SMEM = pl.BlockSpec(memory_space=pltpu.SMEM)
VMEM = pl.BlockSpec(memory_space=pltpu.VMEM)
HBM = pl.BlockSpec(memory_space=pltpu.HBM)


def kernel_call(body, scalars, arrays, out_shape, scratch=(), cost=None, outs=None):
    return pl.pallas_call(
        body,
        out_shape=out_shape,
        in_specs=[SMEM] * len(scalars) + [VMEM] * len(arrays),
        out_specs=outs or [VMEM] * len(out_shape),
        scratch_shapes=list(scratch),
        compiler_params=pltpu.CompilerParams(vmem_limit_bytes=40 * 1024 * 1024),
        cost_estimate=cost,
    )(*scalars, *arrays)


def per_device_dense(
    flows,
    counts,
    local_blocks,
    local_path,
    local_link,
    local_lag,
    remote_blocks,
    remote_path,
    remote_link,
    remote_lag,
    remote_slot,
):
    days, minutes, path_width = flows.shape
    width = local_blocks.shape[1]
    paths = path_width // width
    links = counts.shape[2] // width
    corridors = lax.axis_size("corr")
    remotes = remote_lag.shape[0]
    cap = (remotes + corridors - 2) // (corridors - 1)
    span = HALO + minutes
    through = sorted({2, corridors - 2})
    crossing = [s ^ 1 for s in through]
    direct = [s for s in range(corridors - 1, 1, -1) if s not in through + crossing]
    order = crossing + [1] + direct + through
    many = len(through)
    cuts = [0, *range(many, len(order) - many + 1), len(order)]
    t = Table(len(order), corridors * cap, remotes)
    me = lax.axis_index("corr").astype(jnp.int32).reshape(1)
    group = lax.axis_index("tm").astype(jnp.int32).reshape(1)
    groups = lax.axis_size("tm")
    shape = jax.ShapeDtypeStruct
    piece = (links, days * minutes, width)
    wide = pltpu.VMEM((paths * days * span, width), jnp.float32)
    slots_shape = (len(order) * links + 1, days * minutes, width)
    local_index = (local_path, local_link, local_lag)

    before = lax.ppermute(flows, "tm", [(i, (i + 1) % groups) for i in range(groups)])
    fixed = (remote_path, remote_link, remote_lag, remote_slot, remote_blocks)
    ahead, remote_mats = pl.pallas_call(
        functools.partial(prepare_kernel, cap, order, links, CHUNKS, days * span),
        out_shape=[
            shape((2 * remotes,), jnp.int32),
            shape(remote_blocks.shape, remote_blocks.dtype),
        ],
        in_specs=[SMEM] + [HBM] * len(fixed),
        out_specs=[SMEM, VMEM],
        scratch_shapes=[pltpu.SMEM(remote_slot.shape, jnp.int32) for _ in fixed[1:]]
        + [pltpu.SMEM((corridors,), jnp.int32), pltpu.SemaphoreType.DMA((len(fixed) - 1 + CHUNKS,))],
        compiler_params=pltpu.CompilerParams(vmem_limit_bytes=40 * 1024 * 1024),
    )(me, *(pltpu.with_memory_space_constraint(i, pltpu.HBM) for i in fixed))

    def exchanged(part, s):
        return lax.ppermute(part, "corr", [(i, i ^ s) for i in range(corridors)])

    f32 = jnp.float32
    crossed, *parts, kept = kernel_call(
        functools.partial(forward_remote_kernel, days, cuts, links),
        (group, ahead),
        (flows, before, remote_mats),
        [shape(((end - first) * links, *piece[1:]), f32) for first, end in zip(cuts, cuts[1:])],
        [wide, pltpu.VMEM((len(order) * links, *piece[1:]), f32)],
    )
    crossed = exchanged(crossed.astype(WIRE), 1)
    near, crossed = lax.optimization_barrier((parts[0].astype(WIRE), crossed))
    received = [exchanged(p.astype(WIRE), s) for p, s in zip(parts[1:], direct)]
    received.append(exchanged(near, 1))
    own, table = kernel_call(
        functools.partial(forward_local_kernel, days, cap, order, t, links),
        (group, me, ahead, remote_slot, *local_index),
        (flows, before, local_blocks),
        [shape(piece, f32), shape((t.size,), jnp.int32)],
        [wide],
        outs=[VMEM, SMEM],
    )
    kept = (kept + crossed.astype(f32)).astype(WIRE).reshape(many, *piece)
    received += [exchanged(kept[i], through[i]) for i in reversed(range(many))]
    totals = functools.reduce(jnp.add, [p.astype(f32) for p in received], own)
    link_residual, signal = kernel_call(
        functools.partial(signal_kernel, days),
        (),
        (totals, counts),
        [shape(counts.shape, f32), shape(piece, jnp.bfloat16)],
    )
    arrived = [exchanged(signal, s) for s in (*through, *direct)]
    both = jnp.concatenate([*arrived[:many], signal], axis=0)
    both, signal = lax.optimization_barrier((both, signal))
    rows = [shape((paths * days * span, width), f32)]
    (total,) = kernel_call(
        functools.partial(backward_local_kernel, days),
        local_index,
        (signal, local_blocks),
        rows,
    )
    passed = exchanged(both, 1)
    def weigh(first):
        if first == 0:
            return None
        return pl.CostEstimate(
            flops=2_700_000_000, transcendentals=0, bytes_accessed=8_100_000
        )

    edge = shape((paths * days, HALO, width), f32)
    for first, end, signals, made in (
        (many + 1, len(order), [*arrived[many:], *arrived[:many]], rows),
        (0, many + 1, [passed], [*rows, edge]),
    ):
        total, *early = kernel_call(
            functools.partial(backward_remote_kernel, days, cap, first, end, links, t),
            (table,),
            (remote_mats, total, *signals),
            made,
            [pltpu.VMEM(slots_shape, jnp.bfloat16)],
            weigh(first),
        )
    spill = lax.ppermute(early[0], "tm", [(i, (i - 1) % groups) for i in range(groups)])
    gradient, new_flows = kernel_call(
        functools.partial(finish_kernel, days, groups),
        (group,),
        (total, spill, flows),
        [shape(flows.shape, f32)] * 2,
    )
    return (link_residual, gradient, new_flows)


def per_device(*args):
    counts, blocks, lags = args[1], args[2], args[9]
    corridors = lax.axis_size("corr")
    links = counts.shape[2] // blocks.shape[1]
    cap = (lags.shape[0] + corridors - 2) // (corridors - 1)
    if cap >= links and corridors >= 4 and corridors & (corridors - 1) == 0:
        return per_device_dense(*args)
    return per_device_slots(*args)


def solution(mesh):
    placed = (
        P(None, "tm", "corr"),
        P(None, "tm", "corr"),
        P("corr", None, None),
        P("corr"),
        P("corr"),
        P("corr"),
        P("corr", None, None),
        P("corr"),
        P("corr"),
        P("corr"),
        P("corr"),
    )
    return jax.shard_map(
        per_device,
        mesh=mesh,
        in_specs=placed,
        out_specs=(P(None, "tm", "corr"), P(None, "tm", "corr"), P(None, "tm", "corr")),
        check_vma=False,
    )
```

```python
import functools
import jax
import jax.numpy as jnp
from jax import lax
from jax.experimental import pallas as pl
from jax.experimental.pallas import tpu as pltpu
from jax.sharding import PartitionSpec as P

LAGS = 16


HIGH = lax.Precision.HIGHEST
RATE = 0.5


def passed_along(block, axis, distance):
    devices = range(lax.axis_size(axis))
    route = [(i - distance, i) for i in devices if i - distance in devices]
    return lax.ppermute(block, axis, route)


def one_hot(labels, classes, dtype):
    return (labels[:, None] == jnp.arange(classes, dtype=jnp.int32)[None, :]).astype(dtype)


def shift_table(deltas, out_len, in_len, dtype):
    out_pos = jnp.arange(out_len, dtype=jnp.int32)[:, None]
    in_pos = jnp.arange(in_len, dtype=jnp.int32)[None, :]
    return ((in_pos - out_pos)[None, :, :] == deltas[:, None, None]).astype(dtype)


def pick_blocks(cube, hot):
    return jnp.einsum("dsqp,bq->dsbp", cube, hot, preferred_element_type=jnp.float32).astype(
        jnp.bfloat16
    )


def shift_narrow(picked, table):
    return jnp.einsum("dsbp,bts->dtbp", picked, table, preferred_element_type=jnp.float32).astype(
        jnp.bfloat16
    )


def route_partials(local_part, remote_part, local_route, remote_link, slot_hot, link_blocks):
    own = jnp.einsum("dtbl,bk->dtkl", local_part, local_route, precision=HIGH)
    outgoing = jnp.einsum("bdtl,bs->sdtl", remote_part, slot_hot, precision=HIGH)
    slot_int = slot_hot.astype(jnp.int32)
    labels = link_blocks + jnp.sum(slot_int * (remote_link[:, None] - link_blocks), axis=0)
    return (own, outgoing, labels)


def absorb(own, received, got_labels, link_blocks):
    landing = one_hot(got_labels, link_blocks, jnp.float32)
    return own + jnp.einsum("sdtl,sk->dtkl", received, landing, precision=HIGH)


def collect_paths(local_grad, remote_grad, local_paths, remote_paths):
    first_sum = jnp.einsum("dtbp,bq->dtqp", local_grad, local_paths, precision=HIGH)
    return first_sum + jnp.einsum("bdtp,bq->dtqp", remote_grad, remote_paths, precision=HIGH)


def per_device_slots(
    flows,
    counts,
    local_blocks,
    local_path,
    local_link,
    local_lag,
    remote_blocks,
    remote_path,
    remote_link,
    remote_lag,
    remote_slot,
):
    day_count, minutes, path_width = flows.shape
    block_width = local_blocks.shape[1]
    path_blocks = path_width // block_width
    link_blocks = counts.shape[2] // block_width
    lag_span = LAGS - 1
    corridors = lax.axis_size("corr")
    remote_count = remote_lag.shape[0]
    slot_count = corridors * ((remote_count + corridors - 2) // (corridors - 1))
    flow_cube = flows.reshape(day_count, minutes, path_blocks, block_width)
    local_route = one_hot(local_link, link_blocks, jnp.float32)
    slot_hot = one_hot(remote_slot, slot_count, jnp.float32)
    slot_pick = slot_hot.astype(jnp.bfloat16)
    local_path_hot = one_hot(local_path, path_blocks, jnp.bfloat16)
    remote_path_hot = one_hot(remote_path, path_blocks, jnp.bfloat16)
    local_link_hot = one_hot(local_link, link_blocks, jnp.bfloat16)
    local_in = pick_blocks(flow_cube, local_path_hot)
    remote_in = pick_blocks(flow_cube, remote_path_hot)
    local_plain = jnp.einsum(
        "dtbp,blp->dtbl", local_in, local_blocks, preferred_element_type=jnp.float32
    )
    remote_plain = jnp.einsum(
        "dtbp,blp->bdtl", remote_in, remote_blocks, preferred_element_type=jnp.float32
    )
    local_part = jnp.einsum(
        "dsbl,bts->dtbl",
        local_plain,
        shift_table(-local_lag, minutes + lag_span, minutes, jnp.float32),
        precision=HIGH,
    )
    remote_part = jnp.einsum(
        "bdsl,bts->bdtl",
        remote_plain,
        shift_table(-remote_lag, minutes + lag_span, minutes, jnp.float32),
        precision=HIGH,
    )
    own, outgoing, labels = route_partials(
        local_part, remote_part, local_route, remote_link, slot_hot, link_blocks
    )
    received, got_labels = (
        lax.all_to_all(outgoing, "corr", split_axis=0, concat_axis=0, tiled=True),
        lax.all_to_all(labels, "corr", split_axis=0, concat_axis=0, tiled=True),
    )
    extended = absorb(own, received, got_labels, link_blocks)
    spill = passed_along(extended[:, minutes:], "tm", 1)
    totals = extended[:, :minutes] + jnp.pad(
        spill, ((0, 0), (0, minutes - lag_span), (0, 0), (0, 0))
    )
    link_flow = totals.reshape(day_count, minutes, link_blocks * block_width)
    link_residual = (link_flow - counts) / (counts + 1.0)
    signal = (link_residual / (counts + 1.0)).astype(jnp.bfloat16)
    slot_route = one_hot(got_labels, link_blocks, jnp.bfloat16)
    local_paths = one_hot(local_path, path_blocks, jnp.float32)
    remote_paths = one_hot(remote_path, path_blocks, jnp.float32)
    ahead = passed_along(signal[:, :lag_span, :], "tm", -1)
    extended_signal = jnp.concatenate([signal, ahead], axis=1).reshape(
        day_count, minutes + lag_span, link_blocks, block_width
    )
    slot_signal = jnp.einsum(
        "dtkl,sk->sdtl", extended_signal, slot_route, preferred_element_type=jnp.float32
    ).astype(jnp.bfloat16)
    returned = lax.all_to_all(slot_signal, "corr", split_axis=0, concat_axis=0, tiled=True)
    remote_pick = jnp.einsum(
        "sdtl,bs->bdtl", returned, slot_pick, preferred_element_type=jnp.float32
    ).astype(jnp.bfloat16)
    remote_sig = jnp.einsum(
        "bdsl,bts->bdtl",
        remote_pick,
        shift_table(remote_lag, minutes, minutes + lag_span, jnp.bfloat16),
        preferred_element_type=jnp.float32,
    ).astype(jnp.bfloat16)
    local_sig = shift_narrow(
        pick_blocks(extended_signal, local_link_hot),
        shift_table(local_lag, minutes, minutes + lag_span, jnp.bfloat16),
    )
    local_grad = jnp.einsum(
        "dtbl,blp->dtbp", local_sig, local_blocks, preferred_element_type=jnp.float32
    )
    remote_grad = jnp.einsum(
        "bdtl,blp->bdtp", remote_sig, remote_blocks, preferred_element_type=jnp.float32
    )
    grad_cube = collect_paths(local_grad, remote_grad, local_paths, remote_paths)
    gradient = grad_cube.reshape(day_count, minutes, path_width)
    new_flows = jnp.maximum(flows.astype(jnp.float32) - RATE * gradient, 0.0)
    return (link_residual, gradient, new_flows)


HALO = 16
WIRE = jnp.float16
UNROLL = 32
CHUNKS = 8


def step_of(count):
    return next(u for u in range(min(count, UNROLL), 0, -1) if count % u == 0)


def stage_flows(group, flows_ref, before_ref, wide, days, width):
    real = jnp.where(group[0] > 0, 1.0, 0.0)
    minutes = flows_ref.shape[1]
    span = HALO + minutes
    for p in range(flows_ref.shape[2] // width):
        cols = slice(p * width, (p + 1) * width)
        for d in range(days):
            row = (p * days + d) * span
            before = before_ref[d, :, cols].astype(jnp.float32)
            wide[row : row + HALO, :] = before[minutes - HALO :] * real
            wide[row + HALO : row + span, :] = flows_ref[d, :, cols].astype(jnp.float32)


def forward_blocks(groups, unroll, mat, base, target, wide, acc, days, minutes):
    span = HALO + minutes

    def group(g, carry):
        parts = []
        for u in range(unroll):
            rows = [wide[pl.ds(base(g, u) + d * span, minutes), :] for d in range(days)]
            taken = jnp.concatenate(rows, axis=0).astype(jnp.bfloat16)
            parts.append(
                lax.dot_general(
                    taken,
                    mat(g, u),
                    (((1,), (1,)), ((), ())),
                    preferred_element_type=jnp.float32,
                )
            )
        for u in range(unroll):
            acc[target(g, u)] += parts[u]
        return carry

    lax.fori_loop(0, groups, group, 0)


def backward_blocks(groups, unroll, mat, base, signal, acc, days, minutes):
    span = HALO + minutes

    def group(g, carry):
        parts = [
            jnp.dot(signal(g, u), mat(g, u), preferred_element_type=jnp.float32)
            for u in range(unroll)
        ]
        for u in range(unroll):
            for d in range(days):
                rows = pl.ds(base(g, u) + d * span, minutes)
                acc[rows, :] += parts[u][d * minutes : (d + 1) * minutes]
        return carry

    lax.fori_loop(0, groups, group, 0)


class Table:
    def __init__(self, places, slots, blocks):
        self.start = 0
        self.block = self.start + places
        self.base = self.block + slots
        self.link = self.base + blocks
        self.size = self.link + blocks


def prepare_kernel(cap, order, links, chunks, row_step, me, *rest):
    sources, (ahead, mats_out, path, link, lag, slot, place, sems) = rest[:5], rest[5:]
    blocks = slot.shape[0]
    pairs = list(zip(sources[:4], (path, link, lag, slot)))
    step = blocks // chunks
    for c in range(chunks):
        rows = slice(c * step, blocks if c == chunks - 1 else (c + 1) * step)
        pairs.append((sources[4].at[rows], mats_out.at[rows]))
    copies = [pltpu.make_async_copy(a, b, sems.at[i]) for i, (a, b) in enumerate(pairs)]
    for copy in copies:
        copy.start()
    place[0] = 0
    for p, s in enumerate(order):
        place[s] = p * links
    for copy in copies[:4]:
        copy.wait()

    def entry(j, carry):
        ahead[j] = path[j] * row_step + HALO - lag[j]
        ahead[blocks + j] = place[lax.div(slot[j], cap) ^ me[0]] + link[j]
        return carry

    lax.fori_loop(0, blocks, entry, 0, unroll=16)
    for copy in copies[4:]:
        copy.wait()


def fill_table(cap, order, links, t, me, ahead, slot, table):
    blocks = slot.shape[0]
    for p, s in enumerate(order):
        table[t.start + p] = t.block + (me[0] ^ s) * cap
    for i in range((len(order) + 1) * cap):
        table[t.block + i] = -1

    def entry(j, carry):
        table[t.block + slot[j]] = j
        table[t.base + j] = ahead[j]
        table[t.link + j] = ahead[blocks + j]
        return carry

    lax.fori_loop(0, blocks, entry, 0, unroll=16)


def slot_views(table, t, mats, cap, first, unroll, blank):
    def index(g, u):
        at = first * cap + g * unroll + u
        place = lax.div(at, cap)
        return table[table[t.start + place] + at - place * cap]

    def mat(g, u):
        return mats[jnp.maximum(index(g, u), 0)]

    def base(g, u):
        return table[t.base + jnp.maximum(index(g, u), 0)]

    def block(g, u):
        j = index(g, u)
        return jnp.where(j < 0, blank, table[t.link + jnp.maximum(j, 0)])

    return mat, base, block


def forward_remote_kernel(days, cuts, links, group, ahead, flows, before, mats, *rest):
    outs, (wide, acc) = rest[:-2], rest[-2:]
    minutes, width = flows.shape[1], mats.shape[2]
    blocks = mats.shape[0]
    stage_flows(group, flows, before, wide, days, width)
    acc[...] = jnp.zeros_like(acc)
    unroll = step_of(blocks)
    forward_blocks(
        blocks // unroll,
        unroll,
        lambda g, u: mats[g * unroll + u],
        lambda g, u: ahead[g * unroll + u],
        lambda g, u: ahead[blocks + g * unroll + u],
        wide,
        acc,
        days,
        minutes,
    )
    for first, end, out in zip(cuts, cuts[1:], outs):
        out[...] = acc[first * links : end * links]


def local_views(path, link, lag, mats, unroll, row_step):
    return (
        lambda g, u: mats[g * unroll + u],
        lambda g, u: path[g * unroll + u] * row_step + HALO - lag[g * unroll + u],
        lambda g, u: link[g * unroll + u],
    )


def forward_local_kernel(
    days, cap, order, t, links, group, me, ahead, slot, path, link, lag, flows, before, mats, own, table, wide
):
    minutes, width = flows.shape[1], mats.shape[2]
    stage_flows(group, flows, before, wide, days, width)
    own[...] = jnp.zeros_like(own)
    unroll = step_of(mats.shape[0])
    views = local_views(path, link, lag, mats, unroll, days * (HALO + minutes))
    forward_blocks(mats.shape[0] // unroll, unroll, *views, wide, own, days, minutes)
    fill_table(cap, order, links, t, me, ahead, slot, table)


def signal_kernel(days, totals, counts, residual, signal):
    blocks, _, width = totals.shape
    minutes = counts.shape[1]
    for b in range(blocks):
        cols = slice(b * width, (b + 1) * width)
        total = totals[b]
        for d in range(days):
            rows = slice(d * minutes, (d + 1) * minutes)
            seen = counts[d, :, cols]
            weight = seen + 1.0
            res = (total[rows] - seen) / weight
            residual[d, :, cols] = res
            signal[b, rows, :] = (res / weight).astype(signal.dtype)


def backward_local_kernel(days, path, link, lag, signal, mats, out):
    minutes = signal.shape[1] // days
    out[...] = jnp.zeros_like(out)
    unroll = step_of(mats.shape[0])
    mat, base, block = local_views(path, link, lag, mats, unroll, days * (HALO + minutes))
    backward_blocks(
        mats.shape[0] // unroll,
        unroll,
        mat,
        base,
        lambda g, u: signal[block(g, u)],
        out,
        days,
        minutes,
    )


def backward_remote_kernel(days, cap, first, end, links, t, table, mats, start, *rest):
    count = (end - first) * links
    signals, sources, rest = [], 0, list(rest)
    while sources < count:
        signals.append(rest.pop(0))
        sources += signals[-1].shape[0]
    out, early, everyone = rest[0], rest[1:-1], rest[-1]
    minutes = signals[0].shape[1] // days
    place = first * links
    for part in signals:
        everyone[place : place + part.shape[0]] = part[...]
        place += part.shape[0]
    blank = everyone.shape[0] - 1
    everyone[blank] = jnp.zeros(everyone.shape[1:], everyone.dtype)
    out[...] = start[...]
    span = HALO + minutes
    slots = (end - first) * cap
    unroll = step_of(slots)
    mat, base, block = slot_views(table, t, mats, cap, first, unroll, blank)
    backward_blocks(
        slots // unroll,
        unroll,
        mat,
        base,
        lambda g, u: everyone[block(g, u)],
        out,
        days,
        minutes,
    )
    if early:
        for i in range(early[0].shape[0]):
            early[0][i] = out[i * span : i * span + HALO, :]


def finish_kernel(days, groups, group, total, spill, flows, gradient, new_flows):
    minutes = flows.shape[1]
    width = total.shape[1]
    span = HALO + minutes
    real = jnp.where(group[0] < groups - 1, 1.0, 0.0)
    for p in range(flows.shape[2] // width):
        cols = slice(p * width, (p + 1) * width)
        for d in range(days):
            row = (p * days + d) * span + HALO
            own = total[row : row + minutes, :]
            keep = minutes - HALO
            late = own[keep:] + spill[p * days + d] * real
            for rows, grad in ((slice(0, keep), own[:keep]), (slice(keep, minutes), late)):
                gradient[d, rows, cols] = grad
                new_flows[d, rows, cols] = jnp.maximum(
                    flows[d, rows, cols].astype(jnp.float32) - RATE * grad, 0.0
                )


SMEM = pl.BlockSpec(memory_space=pltpu.SMEM)
VMEM = pl.BlockSpec(memory_space=pltpu.VMEM)
HBM = pl.BlockSpec(memory_space=pltpu.HBM)


def kernel_call(body, scalars, arrays, out_shape, scratch=(), cost=None, outs=None):
    return pl.pallas_call(
        body,
        out_shape=out_shape,
        in_specs=[SMEM] * len(scalars) + [VMEM] * len(arrays),
        out_specs=outs or [VMEM] * len(out_shape),
        scratch_shapes=list(scratch),
        compiler_params=pltpu.CompilerParams(vmem_limit_bytes=40 * 1024 * 1024),
        cost_estimate=cost,
    )(*scalars, *arrays)


def per_device_dense(
    flows,
    counts,
    local_blocks,
    local_path,
    local_link,
    local_lag,
    remote_blocks,
    remote_path,
    remote_link,
    remote_lag,
    remote_slot,
):
    days, minutes, path_width = flows.shape
    width = local_blocks.shape[1]
    paths = path_width // width
    links = counts.shape[2] // width
    corridors = lax.axis_size("corr")
    remotes = remote_lag.shape[0]
    cap = (remotes + corridors - 2) // (corridors - 1)
    span = HALO + minutes
    through = sorted({2, corridors - 2})
    crossing = [s ^ 1 for s in through]
    direct = [s for s in range(corridors - 1, 1, -1) if s not in through + crossing]
    order = crossing + direct + [1] + through
    many = len(through)
    cuts = [0, *range(many, len(order) - many + 1), len(order)]
    t = Table(len(order), corridors * cap, remotes)
    me = lax.axis_index("corr").astype(jnp.int32).reshape(1)
    group = lax.axis_index("tm").astype(jnp.int32).reshape(1)
    groups = lax.axis_size("tm")
    shape = jax.ShapeDtypeStruct
    piece = (links, days * minutes, width)
    wide = pltpu.VMEM((paths * days * span, width), jnp.float32)
    slots_shape = (len(order) * links + 1, days * minutes, width)
    local_index = (local_path, local_link, local_lag)

    before = lax.ppermute(flows, "tm", [(i, (i + 1) % groups) for i in range(groups)])
    fixed = (remote_path, remote_link, remote_lag, remote_slot, remote_blocks)
    ahead, remote_mats = pl.pallas_call(
        functools.partial(prepare_kernel, cap, order, links, CHUNKS, days * span),
        out_shape=[
            shape((2 * remotes,), jnp.int32),
            shape(remote_blocks.shape, remote_blocks.dtype),
        ],
        in_specs=[SMEM] + [HBM] * len(fixed),
        out_specs=[SMEM, VMEM],
        scratch_shapes=[pltpu.SMEM(remote_slot.shape, jnp.int32) for _ in fixed[1:]]
        + [pltpu.SMEM((corridors,), jnp.int32), pltpu.SemaphoreType.DMA((len(fixed) - 1 + CHUNKS,))],
        compiler_params=pltpu.CompilerParams(vmem_limit_bytes=40 * 1024 * 1024),
    )(me, *(pltpu.with_memory_space_constraint(i, pltpu.HBM) for i in fixed))

    def exchanged(part, s):
        return lax.ppermute(part, "corr", [(i, i ^ s) for i in range(corridors)])

    f32 = jnp.float32
    crossed, *parts, kept = kernel_call(
        functools.partial(forward_remote_kernel, days, cuts, links),
        (group, ahead),
        (flows, before, remote_mats),
        [shape(((end - first) * links, *piece[1:]), f32) for first, end in zip(cuts, cuts[1:])],
        [wide, pltpu.VMEM((len(order) * links, *piece[1:]), f32)],
    )
    crossed = exchanged(crossed.astype(WIRE), 1)
    near, crossed = lax.optimization_barrier((parts[-1].astype(WIRE), crossed))
    received = [exchanged(p.astype(WIRE), s) for p, s in zip(parts[:-1], direct)]
    received.append(exchanged(near, 1))
    own, table = kernel_call(
        functools.partial(forward_local_kernel, days, cap, order, t, links),
        (group, me, ahead, remote_slot, *local_index),
        (flows, before, local_blocks),
        [shape(piece, f32), shape((t.size,), jnp.int32)],
        [wide],
        outs=[VMEM, SMEM],
    )
    kept = (kept + crossed.astype(f32)).astype(WIRE).reshape(many, *piece)
    received += [exchanged(kept[i], through[i]) for i in reversed(range(many))]
    totals = functools.reduce(jnp.add, [p.astype(f32) for p in received], own)
    link_residual, signal = kernel_call(
        functools.partial(signal_kernel, days),
        (),
        (totals, counts),
        [shape(counts.shape, f32), shape(piece, jnp.bfloat16)],
    )
    arrived = [exchanged(signal, s) for s in (*through, *direct)]
    near = exchanged(signal, 1)
    passed = [exchanged(a, 1) for a in arrived[:many]]
    *held, signal = lax.optimization_barrier((*arrived[:many], signal))
    rows = [shape((paths * days * span, width), f32)]
    (total,) = kernel_call(
        functools.partial(backward_local_kernel, days),
        local_index,
        (signal, local_blocks),
        rows,
    )
    def weigh(first):
        if first == 0:
            return None
        return pl.CostEstimate(
            flops=500_000_000, transcendentals=0, bytes_accessed=1_500_000
        )

    edge = shape((paths * days, HALO, width), f32)
    for first, end, signals, made in (
        (many, len(order), [*arrived[many:], near, *held], rows),
        (0, many, passed, [*rows, edge]),
    ):
        total, *early = kernel_call(
            functools.partial(backward_remote_kernel, days, cap, first, end, links, t),
            (table,),
            (remote_mats, total, *signals),
            made,
            [pltpu.VMEM(slots_shape, jnp.bfloat16)],
            weigh(first),
        )
    spill = lax.ppermute(early[0], "tm", [(i, (i - 1) % groups) for i in range(groups)])
    gradient, new_flows = kernel_call(
        functools.partial(finish_kernel, days, groups),
        (group,),
        (total, spill, flows),
        [shape(flows.shape, f32)] * 2,
    )
    return (link_residual, gradient, new_flows)


def per_device(*args):
    counts, blocks, lags = args[1], args[2], args[9]
    corridors = lax.axis_size("corr")
    links = counts.shape[2] // blocks.shape[1]
    cap = (lags.shape[0] + corridors - 2) // (corridors - 1)
    if cap >= links and corridors >= 4 and corridors & (corridors - 1) == 0:
        return per_device_dense(*args)
    return per_device_slots(*args)


def solution(mesh):
    placed = (
        P(None, "tm", "corr"),
        P(None, "tm", "corr"),
        P("corr", None, None),
        P("corr"),
        P("corr"),
        P("corr"),
        P("corr", None, None),
        P("corr"),
        P("corr"),
        P("corr"),
        P("corr"),
    )
    return jax.shard_map(
        per_device,
        mesh=mesh,
        in_specs=placed,
        out_specs=(P(None, "tm", "corr"), P(None, "tm", "corr"), P(None, "tm", "corr")),
        check_vma=False,
    )
```

```python
import functools
import jax
import jax.numpy as jnp
from jax import lax
from jax.experimental import pallas as pl
from jax.experimental.pallas import tpu as pltpu
from jax.sharding import PartitionSpec as P

LAGS = 16


HIGH = lax.Precision.HIGHEST
RATE = 0.5


def passed_along(block, axis, distance):
    devices = range(lax.axis_size(axis))
    route = [(i - distance, i) for i in devices if i - distance in devices]
    return lax.ppermute(block, axis, route)


def one_hot(labels, classes, dtype):
    return (labels[:, None] == jnp.arange(classes, dtype=jnp.int32)[None, :]).astype(dtype)


def shift_table(deltas, out_len, in_len, dtype):
    out_pos = jnp.arange(out_len, dtype=jnp.int32)[:, None]
    in_pos = jnp.arange(in_len, dtype=jnp.int32)[None, :]
    return ((in_pos - out_pos)[None, :, :] == deltas[:, None, None]).astype(dtype)


def pick_blocks(cube, hot):
    return jnp.einsum("dsqp,bq->dsbp", cube, hot, preferred_element_type=jnp.float32).astype(
        jnp.bfloat16
    )


def shift_narrow(picked, table):
    return jnp.einsum("dsbp,bts->dtbp", picked, table, preferred_element_type=jnp.float32).astype(
        jnp.bfloat16
    )


def route_partials(local_part, remote_part, local_route, remote_link, slot_hot, link_blocks):
    own = jnp.einsum("dtbl,bk->dtkl", local_part, local_route, precision=HIGH)
    outgoing = jnp.einsum("bdtl,bs->sdtl", remote_part, slot_hot, precision=HIGH)
    slot_int = slot_hot.astype(jnp.int32)
    labels = link_blocks + jnp.sum(slot_int * (remote_link[:, None] - link_blocks), axis=0)
    return (own, outgoing, labels)


def absorb(own, received, got_labels, link_blocks):
    landing = one_hot(got_labels, link_blocks, jnp.float32)
    return own + jnp.einsum("sdtl,sk->dtkl", received, landing, precision=HIGH)


def collect_paths(local_grad, remote_grad, local_paths, remote_paths):
    first_sum = jnp.einsum("dtbp,bq->dtqp", local_grad, local_paths, precision=HIGH)
    return first_sum + jnp.einsum("bdtp,bq->dtqp", remote_grad, remote_paths, precision=HIGH)


def per_device_slots(
    flows,
    counts,
    local_blocks,
    local_path,
    local_link,
    local_lag,
    remote_blocks,
    remote_path,
    remote_link,
    remote_lag,
    remote_slot,
):
    day_count, minutes, path_width = flows.shape
    block_width = local_blocks.shape[1]
    path_blocks = path_width // block_width
    link_blocks = counts.shape[2] // block_width
    lag_span = LAGS - 1
    corridors = lax.axis_size("corr")
    remote_count = remote_lag.shape[0]
    slot_count = corridors * ((remote_count + corridors - 2) // (corridors - 1))
    flow_cube = flows.reshape(day_count, minutes, path_blocks, block_width)
    local_route = one_hot(local_link, link_blocks, jnp.float32)
    slot_hot = one_hot(remote_slot, slot_count, jnp.float32)
    slot_pick = slot_hot.astype(jnp.bfloat16)
    local_path_hot = one_hot(local_path, path_blocks, jnp.bfloat16)
    remote_path_hot = one_hot(remote_path, path_blocks, jnp.bfloat16)
    local_link_hot = one_hot(local_link, link_blocks, jnp.bfloat16)
    local_in = pick_blocks(flow_cube, local_path_hot)
    remote_in = pick_blocks(flow_cube, remote_path_hot)
    local_plain = jnp.einsum(
        "dtbp,blp->dtbl", local_in, local_blocks, preferred_element_type=jnp.float32
    )
    remote_plain = jnp.einsum(
        "dtbp,blp->bdtl", remote_in, remote_blocks, preferred_element_type=jnp.float32
    )
    local_part = jnp.einsum(
        "dsbl,bts->dtbl",
        local_plain,
        shift_table(-local_lag, minutes + lag_span, minutes, jnp.float32),
        precision=HIGH,
    )
    remote_part = jnp.einsum(
        "bdsl,bts->bdtl",
        remote_plain,
        shift_table(-remote_lag, minutes + lag_span, minutes, jnp.float32),
        precision=HIGH,
    )
    own, outgoing, labels = route_partials(
        local_part, remote_part, local_route, remote_link, slot_hot, link_blocks
    )
    received, got_labels = (
        lax.all_to_all(outgoing, "corr", split_axis=0, concat_axis=0, tiled=True),
        lax.all_to_all(labels, "corr", split_axis=0, concat_axis=0, tiled=True),
    )
    extended = absorb(own, received, got_labels, link_blocks)
    spill = passed_along(extended[:, minutes:], "tm", 1)
    totals = extended[:, :minutes] + jnp.pad(
        spill, ((0, 0), (0, minutes - lag_span), (0, 0), (0, 0))
    )
    link_flow = totals.reshape(day_count, minutes, link_blocks * block_width)
    link_residual = (link_flow - counts) / (counts + 1.0)
    signal = (link_residual / (counts + 1.0)).astype(jnp.bfloat16)
    slot_route = one_hot(got_labels, link_blocks, jnp.bfloat16)
    local_paths = one_hot(local_path, path_blocks, jnp.float32)
    remote_paths = one_hot(remote_path, path_blocks, jnp.float32)
    ahead = passed_along(signal[:, :lag_span, :], "tm", -1)
    extended_signal = jnp.concatenate([signal, ahead], axis=1).reshape(
        day_count, minutes + lag_span, link_blocks, block_width
    )
    slot_signal = jnp.einsum(
        "dtkl,sk->sdtl", extended_signal, slot_route, preferred_element_type=jnp.float32
    ).astype(jnp.bfloat16)
    returned = lax.all_to_all(slot_signal, "corr", split_axis=0, concat_axis=0, tiled=True)
    remote_pick = jnp.einsum(
        "sdtl,bs->bdtl", returned, slot_pick, preferred_element_type=jnp.float32
    ).astype(jnp.bfloat16)
    remote_sig = jnp.einsum(
        "bdsl,bts->bdtl",
        remote_pick,
        shift_table(remote_lag, minutes, minutes + lag_span, jnp.bfloat16),
        preferred_element_type=jnp.float32,
    ).astype(jnp.bfloat16)
    local_sig = shift_narrow(
        pick_blocks(extended_signal, local_link_hot),
        shift_table(local_lag, minutes, minutes + lag_span, jnp.bfloat16),
    )
    local_grad = jnp.einsum(
        "dtbl,blp->dtbp", local_sig, local_blocks, preferred_element_type=jnp.float32
    )
    remote_grad = jnp.einsum(
        "bdtl,blp->bdtp", remote_sig, remote_blocks, preferred_element_type=jnp.float32
    )
    grad_cube = collect_paths(local_grad, remote_grad, local_paths, remote_paths)
    gradient = grad_cube.reshape(day_count, minutes, path_width)
    new_flows = jnp.maximum(flows.astype(jnp.float32) - RATE * gradient, 0.0)
    return (link_residual, gradient, new_flows)


HALO = 16
WIRE = jnp.float16
UNROLL = 32
CHUNKS = 8


def step_of(count):
    return next(u for u in range(min(count, UNROLL), 0, -1) if count % u == 0)


def stage_flows(group, flows_ref, before_ref, wide, days, width):
    real = jnp.where(group[0] > 0, 1.0, 0.0)
    minutes = flows_ref.shape[1]
    span = HALO + minutes
    for p in range(flows_ref.shape[2] // width):
        cols = slice(p * width, (p + 1) * width)
        for d in range(days):
            row = (p * days + d) * span
            before = before_ref[d, :, cols].astype(jnp.float32)
            wide[row : row + HALO, :] = before[minutes - HALO :] * real
            wide[row + HALO : row + span, :] = flows_ref[d, :, cols].astype(jnp.float32)


def forward_blocks(groups, unroll, mat, base, target, wide, acc, days, minutes):
    span = HALO + minutes

    def group(g, carry):
        parts = []
        for u in range(unroll):
            rows = [wide[pl.ds(base(g, u) + d * span, minutes), :] for d in range(days)]
            taken = jnp.concatenate(rows, axis=0).astype(jnp.bfloat16)
            parts.append(
                lax.dot_general(
                    taken,
                    mat(g, u),
                    (((1,), (1,)), ((), ())),
                    preferred_element_type=jnp.float32,
                )
            )
        for u in range(unroll):
            acc[target(g, u)] += parts[u]
        return carry

    lax.fori_loop(0, groups, group, 0)


def backward_blocks(groups, unroll, mat, base, signal, acc, days, minutes):
    span = HALO + minutes

    def group(g, carry):
        parts = [
            jnp.dot(signal(g, u), mat(g, u), preferred_element_type=jnp.float32)
            for u in range(unroll)
        ]
        for u in range(unroll):
            for d in range(days):
                rows = pl.ds(base(g, u) + d * span, minutes)
                acc[rows, :] += parts[u][d * minutes : (d + 1) * minutes]
        return carry

    lax.fori_loop(0, groups, group, 0)


class Table:
    def __init__(self, places, slots, blocks):
        self.start = 0
        self.block = self.start + places
        self.base = self.block + slots
        self.link = self.base + blocks
        self.size = self.link + blocks


def prepare_kernel(cap, order, links, chunks, row_step, me, *rest):
    sources, (ahead, mats_out, path, link, lag, slot, place, sems) = rest[:5], rest[5:]
    blocks = slot.shape[0]
    pairs = list(zip(sources[:4], (path, link, lag, slot)))
    step = blocks // chunks
    for c in range(chunks):
        rows = slice(c * step, blocks if c == chunks - 1 else (c + 1) * step)
        pairs.append((sources[4].at[rows], mats_out.at[rows]))
    copies = [pltpu.make_async_copy(a, b, sems.at[i]) for i, (a, b) in enumerate(pairs)]
    for copy in copies:
        copy.start()
    place[0] = 0
    for p, s in enumerate(order):
        place[s] = p * links
    for copy in copies[:4]:
        copy.wait()

    def entry(j, carry):
        ahead[j] = path[j] * row_step + HALO - lag[j]
        ahead[blocks + j] = place[lax.div(slot[j], cap) ^ me[0]] + link[j]
        return carry

    lax.fori_loop(0, blocks, entry, 0, unroll=16)
    for copy in copies[4:]:
        copy.wait()


def fill_table(cap, order, links, t, me, ahead, slot, table):
    blocks = slot.shape[0]
    for p, s in enumerate(order):
        table[t.start + p] = t.block + (me[0] ^ s) * cap
    for i in range((len(order) + 1) * cap):
        table[t.block + i] = -1

    def entry(j, carry):
        table[t.block + slot[j]] = j
        table[t.base + j] = ahead[j]
        table[t.link + j] = ahead[blocks + j]
        return carry

    lax.fori_loop(0, blocks, entry, 0, unroll=16)


def slot_views(table, t, mats, cap, first, unroll, blank):
    def index(g, u):
        at = first * cap + g * unroll + u
        place = lax.div(at, cap)
        return table[table[t.start + place] + at - place * cap]

    def mat(g, u):
        return mats[jnp.maximum(index(g, u), 0)]

    def base(g, u):
        return table[t.base + jnp.maximum(index(g, u), 0)]

    def block(g, u):
        j = index(g, u)
        return jnp.where(j < 0, blank, table[t.link + jnp.maximum(j, 0)])

    return mat, base, block


def forward_remote_kernel(days, cuts, links, group, ahead, flows, before, mats, *rest):
    outs, (wide, acc) = rest[:-2], rest[-2:]
    minutes, width = flows.shape[1], mats.shape[2]
    blocks = mats.shape[0]
    stage_flows(group, flows, before, wide, days, width)
    acc[...] = jnp.zeros_like(acc)
    unroll = step_of(blocks)
    forward_blocks(
        blocks // unroll,
        unroll,
        lambda g, u: mats[g * unroll + u],
        lambda g, u: ahead[g * unroll + u],
        lambda g, u: ahead[blocks + g * unroll + u],
        wide,
        acc,
        days,
        minutes,
    )
    for first, end, out in zip(cuts, cuts[1:], outs):
        out[...] = acc[first * links : end * links]


def local_views(path, link, lag, mats, unroll, row_step):
    return (
        lambda g, u: mats[g * unroll + u],
        lambda g, u: path[g * unroll + u] * row_step + HALO - lag[g * unroll + u],
        lambda g, u: link[g * unroll + u],
    )


def forward_local_kernel(
    days, cap, order, t, links, group, me, ahead, slot, path, link, lag, flows, before, mats, own, table, wide
):
    minutes, width = flows.shape[1], mats.shape[2]
    stage_flows(group, flows, before, wide, days, width)
    own[...] = jnp.zeros_like(own)
    unroll = step_of(mats.shape[0])
    views = local_views(path, link, lag, mats, unroll, days * (HALO + minutes))
    forward_blocks(mats.shape[0] // unroll, unroll, *views, wide, own, days, minutes)
    fill_table(cap, order, links, t, me, ahead, slot, table)


def signal_kernel(days, totals, counts, residual, signal):
    blocks, _, width = totals.shape
    minutes = counts.shape[1]
    for b in range(blocks):
        cols = slice(b * width, (b + 1) * width)
        total = totals[b]
        for d in range(days):
            rows = slice(d * minutes, (d + 1) * minutes)
            seen = counts[d, :, cols]
            weight = seen + 1.0
            res = (total[rows] - seen) / weight
            residual[d, :, cols] = res
            signal[b, rows, :] = (res / weight).astype(signal.dtype)


def backward_local_kernel(days, path, link, lag, signal, mats, out):
    minutes = signal.shape[1] // days
    out[...] = jnp.zeros_like(out)
    unroll = step_of(mats.shape[0])
    mat, base, block = local_views(path, link, lag, mats, unroll, days * (HALO + minutes))
    backward_blocks(
        mats.shape[0] // unroll,
        unroll,
        mat,
        base,
        lambda g, u: signal[block(g, u)],
        out,
        days,
        minutes,
    )


def backward_remote_kernel(days, cap, first, end, links, t, table, mats, start, *rest):
    count = (end - first) * links
    signals, sources, rest = [], 0, list(rest)
    while sources < count:
        signals.append(rest.pop(0))
        sources += signals[-1].shape[0]
    out, early, everyone = rest[0], rest[1:-1], rest[-1]
    minutes = signals[0].shape[1] // days
    place = first * links
    for part in signals:
        everyone[place : place + part.shape[0]] = part[...]
        place += part.shape[0]
    blank = everyone.shape[0] - 1
    everyone[blank] = jnp.zeros(everyone.shape[1:], everyone.dtype)
    out[...] = start[...]
    span = HALO + minutes
    slots = (end - first) * cap
    unroll = step_of(slots)
    mat, base, block = slot_views(table, t, mats, cap, first, unroll, blank)
    backward_blocks(
        slots // unroll,
        unroll,
        mat,
        base,
        lambda g, u: everyone[block(g, u)],
        out,
        days,
        minutes,
    )
    if early:
        for i in range(early[0].shape[0]):
            early[0][i] = out[i * span : i * span + HALO, :]


def finish_kernel(days, groups, group, total, spill, flows, gradient, new_flows):
    minutes = flows.shape[1]
    width = total.shape[1]
    span = HALO + minutes
    real = jnp.where(group[0] < groups - 1, 1.0, 0.0)
    for p in range(flows.shape[2] // width):
        cols = slice(p * width, (p + 1) * width)
        for d in range(days):
            row = (p * days + d) * span + HALO
            own = total[row : row + minutes, :]
            keep = minutes - HALO
            late = own[keep:] + spill[p * days + d] * real
            for rows, grad in ((slice(0, keep), own[:keep]), (slice(keep, minutes), late)):
                gradient[d, rows, cols] = grad
                new_flows[d, rows, cols] = jnp.maximum(
                    flows[d, rows, cols].astype(jnp.float32) - RATE * grad, 0.0
                )


BACKWARD_COST = 500


def weight(nanoseconds):
    return pl.CostEstimate(
        flops=1_000_000 * nanoseconds, transcendentals=0, bytes_accessed=3_000 * nanoseconds
    )


SMEM = pl.BlockSpec(memory_space=pltpu.SMEM)
VMEM = pl.BlockSpec(memory_space=pltpu.VMEM)
HBM = pl.BlockSpec(memory_space=pltpu.HBM)


def kernel_call(body, scalars, arrays, out_shape, scratch=(), cost=None, outs=None):
    return pl.pallas_call(
        body,
        out_shape=out_shape,
        in_specs=[SMEM] * len(scalars) + [VMEM] * len(arrays),
        out_specs=outs or [VMEM] * len(out_shape),
        scratch_shapes=list(scratch),
        compiler_params=pltpu.CompilerParams(vmem_limit_bytes=40 * 1024 * 1024),
        cost_estimate=cost,
    )(*scalars, *arrays)


def per_device_dense(
    flows,
    counts,
    local_blocks,
    local_path,
    local_link,
    local_lag,
    remote_blocks,
    remote_path,
    remote_link,
    remote_lag,
    remote_slot,
):
    days, minutes, path_width = flows.shape
    width = local_blocks.shape[1]
    paths = path_width // width
    links = counts.shape[2] // width
    corridors = lax.axis_size("corr")
    remotes = remote_lag.shape[0]
    cap = (remotes + corridors - 2) // (corridors - 1)
    span = HALO + minutes
    through = list(range(corridors - 2, 0, -2))
    final = through[len(through) // 2]
    rest = [s for s in through if s != final]
    order = [final ^ 1] + [s ^ 1 for s in rest] + [1] + through
    through = through[::-1]
    order[-len(through):] = through
    t = Table(len(order), corridors * cap, remotes)
    me = lax.axis_index("corr").astype(jnp.int32).reshape(1)
    group = lax.axis_index("tm").astype(jnp.int32).reshape(1)
    groups = lax.axis_size("tm")
    shape = jax.ShapeDtypeStruct
    piece = (links, days * minutes, width)
    wide = pltpu.VMEM((paths * days * span, width), jnp.float32)
    slots_shape = (len(order) * links + 1, days * minutes, width)
    local_index = (local_path, local_link, local_lag)

    before = lax.ppermute(flows, "tm", [(i, (i + 1) % groups) for i in range(groups)])
    fixed = (remote_path, remote_link, remote_lag, remote_slot, remote_blocks)
    ahead, remote_mats = pl.pallas_call(
        functools.partial(prepare_kernel, cap, order, links, CHUNKS, days * span),
        out_shape=[
            shape((2 * remotes,), jnp.int32),
            shape(remote_blocks.shape, remote_blocks.dtype),
        ],
        in_specs=[SMEM] + [HBM] * len(fixed),
        out_specs=[SMEM, VMEM],
        scratch_shapes=[pltpu.SMEM(remote_slot.shape, jnp.int32) for _ in fixed[1:]]
        + [pltpu.SMEM((corridors,), jnp.int32), pltpu.SemaphoreType.DMA((len(fixed) - 1 + CHUNKS,))],
        compiler_params=pltpu.CompilerParams(vmem_limit_bytes=40 * 1024 * 1024),
    )(me, *(pltpu.with_memory_space_constraint(i, pltpu.HBM) for i in fixed))

    def exchanged(part, s):
        return lax.ppermute(part, "corr", [(i, i ^ s) for i in range(corridors)])

    f32 = jnp.float32
    cuts = [*range(len(rest) + 1), *range(len(rest) + 2, len(order) + 1)]
    outgoing = kernel_call(
        functools.partial(forward_remote_kernel, days, cuts, links),
        (group, ahead),
        (flows, before, remote_mats),
        [shape(((end - first) * links, *piece[1:]), f32) for first, end in zip(cuts, cuts[1:])],
        [wide, pltpu.VMEM((len(order) * links, *piece[1:]), f32)],
    )
    count = len(through)
    crossed = [exchanged(part.astype(WIRE), 1) for part in outgoing[:count]]
    received = []
    for s, kept in zip(through, outgoing[count:]):
        met = crossed[order.index(s ^ 1)][:links].astype(f32)
        received.append(exchanged((kept + met).astype(WIRE), s))
    received.append(crossed[-1][links:])
    own, table = kernel_call(
        functools.partial(forward_local_kernel, days, cap, order, t, links),
        (group, me, ahead, remote_slot, *local_index),
        (flows, before, local_blocks),
        [shape(piece, f32), shape((t.size,), jnp.int32)],
        [wide],
        outs=[VMEM, SMEM],
    )
    totals = functools.reduce(jnp.add, [p.astype(f32) for p in received], own)
    link_residual, signal = kernel_call(
        functools.partial(signal_kernel, days),
        (),
        (totals, counts),
        [shape(counts.shape, f32), shape(piece, jnp.bfloat16)],
    )
    arrived = {s: exchanged(signal, s) for s in (*through, 1)}
    for s in through:
        arrived[s ^ 1] = exchanged(arrived[s], 1)
    rows = [shape((paths * days * span, width), f32)]
    (total,) = kernel_call(
        functools.partial(backward_local_kernel, days),
        local_index,
        (signal, local_blocks),
        rows,
    )
    edge = shape((paths * days, HALO, width), f32)
    for first, end, made in ((1, len(order), rows), (0, 1, [*rows, edge])):
        total, *early = kernel_call(
            functools.partial(backward_remote_kernel, days, cap, first, end, links, t),
            (table,),
            (remote_mats, total, *(arrived[s] for s in order[first:end])),
            made,
            [pltpu.VMEM(slots_shape, jnp.bfloat16)],
            cost=weight(BACKWARD_COST) if first else None,
        )
    spill = lax.ppermute(early[0], "tm", [(i, (i - 1) % groups) for i in range(groups)])
    gradient, new_flows = kernel_call(
        functools.partial(finish_kernel, days, groups),
        (group,),
        (total, spill, flows),
        [shape(flows.shape, f32)] * 2,
    )
    return (link_residual, gradient, new_flows)


def per_device(*args):
    counts, blocks, lags = args[1], args[2], args[9]
    corridors = lax.axis_size("corr")
    links = counts.shape[2] // blocks.shape[1]
    cap = (lags.shape[0] + corridors - 2) // (corridors - 1)
    if cap >= links and corridors >= 4 and corridors & (corridors - 1) == 0:
        return per_device_dense(*args)
    return per_device_slots(*args)


def solution(mesh):
    placed = (
        P(None, "tm", "corr"),
        P(None, "tm", "corr"),
        P("corr", None, None),
        P("corr"),
        P("corr"),
        P("corr"),
        P("corr", None, None),
        P("corr"),
        P("corr"),
        P("corr"),
        P("corr"),
    )
    return jax.shard_map(
        per_device,
        mesh=mesh,
        in_specs=placed,
        out_specs=(P(None, "tm", "corr"), P(None, "tm", "corr"), P(None, "tm", "corr")),
        check_vma=False,
    )
```

```python
import functools
import jax
import jax.numpy as jnp
from jax import lax
from jax.experimental import pallas as pl
from jax.experimental.pallas import tpu as pltpu
from jax.sharding import PartitionSpec as P

LAGS = 16


HIGH = lax.Precision.HIGHEST
RATE = 0.5


def passed_along(block, axis, distance):
    devices = range(lax.axis_size(axis))
    route = [(i - distance, i) for i in devices if i - distance in devices]
    return lax.ppermute(block, axis, route)


def one_hot(labels, classes, dtype):
    return (labels[:, None] == jnp.arange(classes, dtype=jnp.int32)[None, :]).astype(dtype)


def shift_table(deltas, out_len, in_len, dtype):
    out_pos = jnp.arange(out_len, dtype=jnp.int32)[:, None]
    in_pos = jnp.arange(in_len, dtype=jnp.int32)[None, :]
    return ((in_pos - out_pos)[None, :, :] == deltas[:, None, None]).astype(dtype)


def pick_blocks(cube, hot):
    return jnp.einsum("dsqp,bq->dsbp", cube, hot, preferred_element_type=jnp.float32).astype(
        jnp.bfloat16
    )


def shift_narrow(picked, table):
    return jnp.einsum("dsbp,bts->dtbp", picked, table, preferred_element_type=jnp.float32).astype(
        jnp.bfloat16
    )


def route_partials(local_part, remote_part, local_route, remote_link, slot_hot, link_blocks):
    own = jnp.einsum("dtbl,bk->dtkl", local_part, local_route, precision=HIGH)
    outgoing = jnp.einsum("bdtl,bs->sdtl", remote_part, slot_hot, precision=HIGH)
    slot_int = slot_hot.astype(jnp.int32)
    labels = link_blocks + jnp.sum(slot_int * (remote_link[:, None] - link_blocks), axis=0)
    return (own, outgoing, labels)


def absorb(own, received, got_labels, link_blocks):
    landing = one_hot(got_labels, link_blocks, jnp.float32)
    return own + jnp.einsum("sdtl,sk->dtkl", received, landing, precision=HIGH)


def collect_paths(local_grad, remote_grad, local_paths, remote_paths):
    first_sum = jnp.einsum("dtbp,bq->dtqp", local_grad, local_paths, precision=HIGH)
    return first_sum + jnp.einsum("bdtp,bq->dtqp", remote_grad, remote_paths, precision=HIGH)


def per_device_slots(
    flows,
    counts,
    local_blocks,
    local_path,
    local_link,
    local_lag,
    remote_blocks,
    remote_path,
    remote_link,
    remote_lag,
    remote_slot,
):
    day_count, minutes, path_width = flows.shape
    block_width = local_blocks.shape[1]
    path_blocks = path_width // block_width
    link_blocks = counts.shape[2] // block_width
    lag_span = LAGS - 1
    corridors = lax.axis_size("corr")
    remote_count = remote_lag.shape[0]
    slot_count = corridors * ((remote_count + corridors - 2) // (corridors - 1))
    flow_cube = flows.reshape(day_count, minutes, path_blocks, block_width)
    local_route = one_hot(local_link, link_blocks, jnp.float32)
    slot_hot = one_hot(remote_slot, slot_count, jnp.float32)
    slot_pick = slot_hot.astype(jnp.bfloat16)
    local_path_hot = one_hot(local_path, path_blocks, jnp.bfloat16)
    remote_path_hot = one_hot(remote_path, path_blocks, jnp.bfloat16)
    local_link_hot = one_hot(local_link, link_blocks, jnp.bfloat16)
    local_in = pick_blocks(flow_cube, local_path_hot)
    remote_in = pick_blocks(flow_cube, remote_path_hot)
    local_plain = jnp.einsum(
        "dtbp,blp->dtbl", local_in, local_blocks, preferred_element_type=jnp.float32
    )
    remote_plain = jnp.einsum(
        "dtbp,blp->bdtl", remote_in, remote_blocks, preferred_element_type=jnp.float32
    )
    local_part = jnp.einsum(
        "dsbl,bts->dtbl",
        local_plain,
        shift_table(-local_lag, minutes + lag_span, minutes, jnp.float32),
        precision=HIGH,
    )
    remote_part = jnp.einsum(
        "bdsl,bts->bdtl",
        remote_plain,
        shift_table(-remote_lag, minutes + lag_span, minutes, jnp.float32),
        precision=HIGH,
    )
    own, outgoing, labels = route_partials(
        local_part, remote_part, local_route, remote_link, slot_hot, link_blocks
    )
    received, got_labels = (
        lax.all_to_all(outgoing, "corr", split_axis=0, concat_axis=0, tiled=True),
        lax.all_to_all(labels, "corr", split_axis=0, concat_axis=0, tiled=True),
    )
    extended = absorb(own, received, got_labels, link_blocks)
    spill = passed_along(extended[:, minutes:], "tm", 1)
    totals = extended[:, :minutes] + jnp.pad(
        spill, ((0, 0), (0, minutes - lag_span), (0, 0), (0, 0))
    )
    link_flow = totals.reshape(day_count, minutes, link_blocks * block_width)
    link_residual = (link_flow - counts) / (counts + 1.0)
    signal = (link_residual / (counts + 1.0)).astype(jnp.bfloat16)
    slot_route = one_hot(got_labels, link_blocks, jnp.bfloat16)
    local_paths = one_hot(local_path, path_blocks, jnp.float32)
    remote_paths = one_hot(remote_path, path_blocks, jnp.float32)
    ahead = passed_along(signal[:, :lag_span, :], "tm", -1)
    extended_signal = jnp.concatenate([signal, ahead], axis=1).reshape(
        day_count, minutes + lag_span, link_blocks, block_width
    )
    slot_signal = jnp.einsum(
        "dtkl,sk->sdtl", extended_signal, slot_route, preferred_element_type=jnp.float32
    ).astype(jnp.bfloat16)
    returned = lax.all_to_all(slot_signal, "corr", split_axis=0, concat_axis=0, tiled=True)
    remote_pick = jnp.einsum(
        "sdtl,bs->bdtl", returned, slot_pick, preferred_element_type=jnp.float32
    ).astype(jnp.bfloat16)
    remote_sig = jnp.einsum(
        "bdsl,bts->bdtl",
        remote_pick,
        shift_table(remote_lag, minutes, minutes + lag_span, jnp.bfloat16),
        preferred_element_type=jnp.float32,
    ).astype(jnp.bfloat16)
    local_sig = shift_narrow(
        pick_blocks(extended_signal, local_link_hot),
        shift_table(local_lag, minutes, minutes + lag_span, jnp.bfloat16),
    )
    local_grad = jnp.einsum(
        "dtbl,blp->dtbp", local_sig, local_blocks, preferred_element_type=jnp.float32
    )
    remote_grad = jnp.einsum(
        "bdtl,blp->bdtp", remote_sig, remote_blocks, preferred_element_type=jnp.float32
    )
    grad_cube = collect_paths(local_grad, remote_grad, local_paths, remote_paths)
    gradient = grad_cube.reshape(day_count, minutes, path_width)
    new_flows = jnp.maximum(flows.astype(jnp.float32) - RATE * gradient, 0.0)
    return (link_residual, gradient, new_flows)


HALO = 16
WIRE = jnp.float16
UNROLL = 32
CHUNKS = 8


def step_of(count):
    return next(u for u in range(min(count, UNROLL), 0, -1) if count % u == 0)


def stage_flows(group, flows_ref, before_ref, wide, days, width):
    real = jnp.where(group[0] > 0, 1.0, 0.0)
    minutes = flows_ref.shape[1]
    span = HALO + minutes
    for p in range(flows_ref.shape[2] // width):
        cols = slice(p * width, (p + 1) * width)
        for d in range(days):
            row = (p * days + d) * span
            before = before_ref[d, :, cols].astype(jnp.float32)
            wide[row : row + HALO, :] = before[minutes - HALO :] * real
            wide[row + HALO : row + span, :] = flows_ref[d, :, cols].astype(jnp.float32)


def forward_blocks(groups, unroll, mat, base, target, wide, acc, days, minutes):
    span = HALO + minutes

    def group(g, carry):
        parts = []
        for u in range(unroll):
            rows = [wide[pl.ds(base(g, u) + d * span, minutes), :] for d in range(days)]
            taken = jnp.concatenate(rows, axis=0).astype(jnp.bfloat16)
            parts.append(
                lax.dot_general(
                    taken,
                    mat(g, u),
                    (((1,), (1,)), ((), ())),
                    preferred_element_type=jnp.float32,
                )
            )
        for u in range(unroll):
            acc[target(g, u)] += parts[u]
        return carry

    lax.fori_loop(0, groups, group, 0)


def backward_blocks(groups, unroll, mat, base, signal, acc, days, minutes):
    span = HALO + minutes

    def group(g, carry):
        parts = [
            jnp.dot(signal(g, u), mat(g, u), preferred_element_type=jnp.float32)
            for u in range(unroll)
        ]
        for u in range(unroll):
            for d in range(days):
                rows = pl.ds(base(g, u) + d * span, minutes)
                acc[rows, :] += parts[u][d * minutes : (d + 1) * minutes]
        return carry

    lax.fori_loop(0, groups, group, 0)


class Table:
    def __init__(self, places, slots, blocks):
        self.start = 0
        self.block = self.start + places
        self.base = self.block + slots
        self.link = self.base + blocks
        self.size = self.link + blocks


def prepare_kernel(cap, order, links, chunks, row_step, me, *rest):
    sources, (ahead, mats_out, path, link, lag, slot, place, sems) = rest[:5], rest[5:]
    blocks = slot.shape[0]
    pairs = list(zip(sources[:4], (path, link, lag, slot)))
    step = blocks // chunks
    for c in range(chunks):
        rows = slice(c * step, blocks if c == chunks - 1 else (c + 1) * step)
        pairs.append((sources[4].at[rows], mats_out.at[rows]))
    copies = [pltpu.make_async_copy(a, b, sems.at[i]) for i, (a, b) in enumerate(pairs)]
    for copy in copies:
        copy.start()
    place[0] = 0
    for p, s in enumerate(order):
        place[s] = p * links
    for copy in copies[:4]:
        copy.wait()

    def entry(j, carry):
        ahead[j] = path[j] * row_step + HALO - lag[j]
        ahead[blocks + j] = place[lax.div(slot[j], cap) ^ me[0]] + link[j]
        return carry

    lax.fori_loop(0, blocks, entry, 0, unroll=16)
    for copy in copies[4:]:
        copy.wait()


def fill_table(cap, order, links, t, me, ahead, slot, table):
    blocks = slot.shape[0]
    for p, s in enumerate(order):
        table[t.start + p] = t.block + (me[0] ^ s) * cap
    for i in range((len(order) + 1) * cap):
        table[t.block + i] = -1

    def entry(j, carry):
        table[t.block + slot[j]] = j
        table[t.base + j] = ahead[j]
        table[t.link + j] = ahead[blocks + j]
        return carry

    lax.fori_loop(0, blocks, entry, 0, unroll=16)


def slot_views(table, t, mats, cap, first, unroll, blank):
    def index(g, u):
        at = first * cap + g * unroll + u
        place = lax.div(at, cap)
        return table[table[t.start + place] + at - place * cap]

    def mat(g, u):
        return mats[jnp.maximum(index(g, u), 0)]

    def base(g, u):
        return table[t.base + jnp.maximum(index(g, u), 0)]

    def block(g, u):
        j = index(g, u)
        return jnp.where(j < 0, blank, table[t.link + jnp.maximum(j, 0)])

    return mat, base, block


def forward_remote_kernel(days, cuts, links, group, ahead, flows, before, mats, *rest):
    outs, (wide, acc) = rest[:-2], rest[-2:]
    minutes, width = flows.shape[1], mats.shape[2]
    blocks = mats.shape[0]
    stage_flows(group, flows, before, wide, days, width)
    acc[...] = jnp.zeros_like(acc)
    unroll = step_of(blocks)
    forward_blocks(
        blocks // unroll,
        unroll,
        lambda g, u: mats[g * unroll + u],
        lambda g, u: ahead[g * unroll + u],
        lambda g, u: ahead[blocks + g * unroll + u],
        wide,
        acc,
        days,
        minutes,
    )
    for first, end, out in zip(cuts, cuts[1:], outs):
        out[...] = acc[first * links : end * links]


def local_views(path, link, lag, mats, unroll, row_step):
    return (
        lambda g, u: mats[g * unroll + u],
        lambda g, u: path[g * unroll + u] * row_step + HALO - lag[g * unroll + u],
        lambda g, u: link[g * unroll + u],
    )


def forward_local_kernel(
    days, cap, order, t, links, group, me, ahead, slot, path, link, lag, flows, before, mats, own, table, wide
):
    minutes, width = flows.shape[1], mats.shape[2]
    stage_flows(group, flows, before, wide, days, width)
    own[...] = jnp.zeros_like(own)
    unroll = step_of(mats.shape[0])
    views = local_views(path, link, lag, mats, unroll, days * (HALO + minutes))
    forward_blocks(mats.shape[0] // unroll, unroll, *views, wide, own, days, minutes)
    fill_table(cap, order, links, t, me, ahead, slot, table)


def signal_kernel(days, totals, counts, residual, signal):
    blocks, _, width = totals.shape
    minutes = counts.shape[1]
    for b in range(blocks):
        cols = slice(b * width, (b + 1) * width)
        total = totals[b]
        for d in range(days):
            rows = slice(d * minutes, (d + 1) * minutes)
            seen = counts[d, :, cols]
            weight = seen + 1.0
            res = (total[rows] - seen) / weight
            residual[d, :, cols] = res
            signal[b, rows, :] = (res / weight).astype(signal.dtype)


def backward_local_kernel(days, path, link, lag, signal, mats, out):
    minutes = signal.shape[1] // days
    out[...] = jnp.zeros_like(out)
    unroll = step_of(mats.shape[0])
    mat, base, block = local_views(path, link, lag, mats, unroll, days * (HALO + minutes))
    backward_blocks(
        mats.shape[0] // unroll,
        unroll,
        mat,
        base,
        lambda g, u: signal[block(g, u)],
        out,
        days,
        minutes,
    )


def backward_remote_kernel(days, cap, first, end, links, t, table, mats, start, *rest):
    count = (end - first) * links
    signals, sources, rest = [], 0, list(rest)
    while sources < count:
        signals.append(rest.pop(0))
        sources += signals[-1].shape[0]
    out, early, everyone = rest[0], rest[1:-1], rest[-1]
    minutes = signals[0].shape[1] // days
    place = first * links
    for part in signals:
        everyone[place : place + part.shape[0]] = part[...]
        place += part.shape[0]
    blank = everyone.shape[0] - 1
    everyone[blank] = jnp.zeros(everyone.shape[1:], everyone.dtype)
    out[...] = start[...]
    span = HALO + minutes
    slots = (end - first) * cap
    unroll = step_of(slots)
    mat, base, block = slot_views(table, t, mats, cap, first, unroll, blank)
    backward_blocks(
        slots // unroll,
        unroll,
        mat,
        base,
        lambda g, u: everyone[block(g, u)],
        out,
        days,
        minutes,
    )
    if early:
        for i in range(early[0].shape[0]):
            early[0][i] = out[i * span : i * span + HALO, :]


def finish_kernel(days, groups, group, total, spill, flows, gradient, new_flows):
    minutes = flows.shape[1]
    width = total.shape[1]
    span = HALO + minutes
    real = jnp.where(group[0] < groups - 1, 1.0, 0.0)
    for p in range(flows.shape[2] // width):
        cols = slice(p * width, (p + 1) * width)
        for d in range(days):
            row = (p * days + d) * span + HALO
            own = total[row : row + minutes, :]
            keep = minutes - HALO
            late = own[keep:] + spill[p * days + d] * real
            for rows, grad in ((slice(0, keep), own[:keep]), (slice(keep, minutes), late)):
                gradient[d, rows, cols] = grad
                new_flows[d, rows, cols] = jnp.maximum(
                    flows[d, rows, cols].astype(jnp.float32) - RATE * grad, 0.0
                )


BACKWARD_COST = 500


def weight(nanoseconds):
    return pl.CostEstimate(
        flops=1_000_000 * nanoseconds, transcendentals=0, bytes_accessed=3_000 * nanoseconds
    )


SMEM = pl.BlockSpec(memory_space=pltpu.SMEM)
VMEM = pl.BlockSpec(memory_space=pltpu.VMEM)
HBM = pl.BlockSpec(memory_space=pltpu.HBM)


def kernel_call(body, scalars, arrays, out_shape, scratch=(), cost=None, outs=None):
    return pl.pallas_call(
        body,
        out_shape=out_shape,
        in_specs=[SMEM] * len(scalars) + [VMEM] * len(arrays),
        out_specs=outs or [VMEM] * len(out_shape),
        scratch_shapes=list(scratch),
        compiler_params=pltpu.CompilerParams(vmem_limit_bytes=40 * 1024 * 1024),
        cost_estimate=cost,
    )(*scalars, *arrays)


def per_device_dense(
    flows,
    counts,
    local_blocks,
    local_path,
    local_link,
    local_lag,
    remote_blocks,
    remote_path,
    remote_link,
    remote_lag,
    remote_slot,
):
    days, minutes, path_width = flows.shape
    width = local_blocks.shape[1]
    paths = path_width // width
    links = counts.shape[2] // width
    corridors = lax.axis_size("corr")
    remotes = remote_lag.shape[0]
    cap = (remotes + corridors - 2) // (corridors - 1)
    span = HALO + minutes
    through = list(range(corridors - 2, 0, -2))
    final = through[len(through) // 2]
    rest = [s for s in through if s != final]
    order = [final ^ 1] + [s ^ 1 for s in rest] + [1] + through
    through = through[::-1]
    order[-len(through):] = through
    t = Table(len(order), corridors * cap, remotes)
    me = lax.axis_index("corr").astype(jnp.int32).reshape(1)
    group = lax.axis_index("tm").astype(jnp.int32).reshape(1)
    groups = lax.axis_size("tm")
    shape = jax.ShapeDtypeStruct
    piece = (links, days * minutes, width)
    wide = pltpu.VMEM((paths * days * span, width), jnp.float32)
    slots_shape = (len(order) * links + 1, days * minutes, width)
    local_index = (local_path, local_link, local_lag)

    before = lax.ppermute(flows, "tm", [(i, (i + 1) % groups) for i in range(groups)])
    fixed = (remote_path, remote_link, remote_lag, remote_slot, remote_blocks)
    ahead, remote_mats = pl.pallas_call(
        functools.partial(prepare_kernel, cap, order, links, CHUNKS, days * span),
        out_shape=[
            shape((2 * remotes,), jnp.int32),
            shape(remote_blocks.shape, remote_blocks.dtype),
        ],
        in_specs=[SMEM] + [HBM] * len(fixed),
        out_specs=[SMEM, VMEM],
        scratch_shapes=[pltpu.SMEM(remote_slot.shape, jnp.int32) for _ in fixed[1:]]
        + [pltpu.SMEM((corridors,), jnp.int32), pltpu.SemaphoreType.DMA((len(fixed) - 1 + CHUNKS,))],
        compiler_params=pltpu.CompilerParams(vmem_limit_bytes=40 * 1024 * 1024),
    )(me, *(pltpu.with_memory_space_constraint(i, pltpu.HBM) for i in fixed))

    def exchanged(part, s):
        return lax.ppermute(part, "corr", [(i, i ^ s) for i in range(corridors)])

    f32 = jnp.float32
    cuts = [*range(len(rest) + 1), *range(len(rest) + 2, len(order) + 1)]
    outgoing = kernel_call(
        functools.partial(forward_remote_kernel, days, cuts, links),
        (group, ahead),
        (flows, before, remote_mats),
        [shape(((end - first) * links, *piece[1:]), f32) for first, end in zip(cuts, cuts[1:])],
        [wide, pltpu.VMEM((len(order) * links, *piece[1:]), f32)],
    )
    count = len(through)
    crossed = [exchanged(part.astype(WIRE), 1) for part in outgoing[:count]]
    crossed[0], before = lax.optimization_barrier((crossed[0], before))
    own, table = kernel_call(
        functools.partial(forward_local_kernel, days, cap, order, t, links),
        (group, me, ahead, remote_slot, *local_index),
        (flows, before, local_blocks),
        [shape(piece, f32), shape((t.size,), jnp.int32)],
        [wide],
        outs=[VMEM, SMEM],
    )
    crossed[-1], own = lax.optimization_barrier((crossed[-1], own))
    received = []
    for s, kept in zip(through, outgoing[count:]):
        met = crossed[order.index(s ^ 1)][:links].astype(f32)
        received.append(exchanged((kept + met).astype(WIRE), s))
    received.append(crossed[-1][links:])
    totals = functools.reduce(jnp.add, [p.astype(f32) for p in received], own)
    link_residual, signal = kernel_call(
        functools.partial(signal_kernel, days),
        (),
        (totals, counts),
        [shape(counts.shape, f32), shape(piece, jnp.bfloat16)],
    )
    arrived = {s: exchanged(signal, s) for s in (*through, 1)}
    rows = [shape((paths * days * span, width), f32)]
    (total,) = kernel_call(
        functools.partial(backward_local_kernel, days),
        local_index,
        (signal, local_blocks),
        rows,
    )
    arrived[final], total = lax.optimization_barrier((arrived[final], total))
    for s in through:
        arrived[s ^ 1] = exchanged(arrived[s], 1)
    edge = shape((paths * days, HALO, width), f32)
    for first, end, made in ((1, len(order), rows), (0, 1, [*rows, edge])):
        total, *early = kernel_call(
            functools.partial(backward_remote_kernel, days, cap, first, end, links, t),
            (table,),
            (remote_mats, total, *(arrived[s] for s in order[first:end])),
            made,
            [pltpu.VMEM(slots_shape, jnp.bfloat16)],
            cost=weight(BACKWARD_COST) if first else None,
        )
    spill = lax.ppermute(early[0], "tm", [(i, (i - 1) % groups) for i in range(groups)])
    gradient, new_flows = kernel_call(
        functools.partial(finish_kernel, days, groups),
        (group,),
        (total, spill, flows),
        [shape(flows.shape, f32)] * 2,
    )
    return (link_residual, gradient, new_flows)


def per_device(*args):
    counts, blocks, lags = args[1], args[2], args[9]
    corridors = lax.axis_size("corr")
    links = counts.shape[2] // blocks.shape[1]
    cap = (lags.shape[0] + corridors - 2) // (corridors - 1)
    if cap >= links and corridors >= 4 and corridors & (corridors - 1) == 0:
        return per_device_dense(*args)
    return per_device_slots(*args)


def solution(mesh):
    placed = (
        P(None, "tm", "corr"),
        P(None, "tm", "corr"),
        P("corr", None, None),
        P("corr"),
        P("corr"),
        P("corr"),
        P("corr", None, None),
        P("corr"),
        P("corr"),
        P("corr"),
        P("corr"),
    )
    return jax.shard_map(
        per_device,
        mesh=mesh,
        in_specs=placed,
        out_specs=(P(None, "tm", "corr"), P(None, "tm", "corr"), P(None, "tm", "corr")),
        check_vma=False,
    )
```

```python
import functools
import jax
import jax.numpy as jnp
from jax import lax
from jax.experimental import pallas as pl
from jax.experimental.pallas import tpu as pltpu
from jax.sharding import PartitionSpec as P

LAGS = 16


HIGH = lax.Precision.HIGHEST
RATE = 0.5


def passed_along(block, axis, distance):
    devices = range(lax.axis_size(axis))
    route = [(i - distance, i) for i in devices if i - distance in devices]
    return lax.ppermute(block, axis, route)


def one_hot(labels, classes, dtype):
    return (labels[:, None] == jnp.arange(classes, dtype=jnp.int32)[None, :]).astype(dtype)


def shift_table(deltas, out_len, in_len, dtype):
    out_pos = jnp.arange(out_len, dtype=jnp.int32)[:, None]
    in_pos = jnp.arange(in_len, dtype=jnp.int32)[None, :]
    return ((in_pos - out_pos)[None, :, :] == deltas[:, None, None]).astype(dtype)


def pick_blocks(cube, hot):
    return jnp.einsum("dsqp,bq->dsbp", cube, hot, preferred_element_type=jnp.float32).astype(
        jnp.bfloat16
    )


def shift_narrow(picked, table):
    return jnp.einsum("dsbp,bts->dtbp", picked, table, preferred_element_type=jnp.float32).astype(
        jnp.bfloat16
    )


def route_partials(local_part, remote_part, local_route, remote_link, slot_hot, link_blocks):
    own = jnp.einsum("dtbl,bk->dtkl", local_part, local_route, precision=HIGH)
    outgoing = jnp.einsum("bdtl,bs->sdtl", remote_part, slot_hot, precision=HIGH)
    slot_int = slot_hot.astype(jnp.int32)
    labels = link_blocks + jnp.sum(slot_int * (remote_link[:, None] - link_blocks), axis=0)
    return (own, outgoing, labels)


def absorb(own, received, got_labels, link_blocks):
    landing = one_hot(got_labels, link_blocks, jnp.float32)
    return own + jnp.einsum("sdtl,sk->dtkl", received, landing, precision=HIGH)


def collect_paths(local_grad, remote_grad, local_paths, remote_paths):
    first_sum = jnp.einsum("dtbp,bq->dtqp", local_grad, local_paths, precision=HIGH)
    return first_sum + jnp.einsum("bdtp,bq->dtqp", remote_grad, remote_paths, precision=HIGH)


def per_device_slots(
    flows,
    counts,
    local_blocks,
    local_path,
    local_link,
    local_lag,
    remote_blocks,
    remote_path,
    remote_link,
    remote_lag,
    remote_slot,
):
    day_count, minutes, path_width = flows.shape
    block_width = local_blocks.shape[1]
    path_blocks = path_width // block_width
    link_blocks = counts.shape[2] // block_width
    lag_span = LAGS - 1
    corridors = lax.axis_size("corr")
    remote_count = remote_lag.shape[0]
    slot_count = corridors * ((remote_count + corridors - 2) // (corridors - 1))
    flow_cube = flows.reshape(day_count, minutes, path_blocks, block_width)
    local_route = one_hot(local_link, link_blocks, jnp.float32)
    slot_hot = one_hot(remote_slot, slot_count, jnp.float32)
    slot_pick = slot_hot.astype(jnp.bfloat16)
    local_path_hot = one_hot(local_path, path_blocks, jnp.bfloat16)
    remote_path_hot = one_hot(remote_path, path_blocks, jnp.bfloat16)
    local_link_hot = one_hot(local_link, link_blocks, jnp.bfloat16)
    local_in = pick_blocks(flow_cube, local_path_hot)
    remote_in = pick_blocks(flow_cube, remote_path_hot)
    local_plain = jnp.einsum(
        "dtbp,blp->dtbl", local_in, local_blocks, preferred_element_type=jnp.float32
    )
    remote_plain = jnp.einsum(
        "dtbp,blp->bdtl", remote_in, remote_blocks, preferred_element_type=jnp.float32
    )
    local_part = jnp.einsum(
        "dsbl,bts->dtbl",
        local_plain,
        shift_table(-local_lag, minutes + lag_span, minutes, jnp.float32),
        precision=HIGH,
    )
    remote_part = jnp.einsum(
        "bdsl,bts->bdtl",
        remote_plain,
        shift_table(-remote_lag, minutes + lag_span, minutes, jnp.float32),
        precision=HIGH,
    )
    own, outgoing, labels = route_partials(
        local_part, remote_part, local_route, remote_link, slot_hot, link_blocks
    )
    received, got_labels = (
        lax.all_to_all(outgoing, "corr", split_axis=0, concat_axis=0, tiled=True),
        lax.all_to_all(labels, "corr", split_axis=0, concat_axis=0, tiled=True),
    )
    extended = absorb(own, received, got_labels, link_blocks)
    spill = passed_along(extended[:, minutes:], "tm", 1)
    totals = extended[:, :minutes] + jnp.pad(
        spill, ((0, 0), (0, minutes - lag_span), (0, 0), (0, 0))
    )
    link_flow = totals.reshape(day_count, minutes, link_blocks * block_width)
    link_residual = (link_flow - counts) / (counts + 1.0)
    signal = (link_residual / (counts + 1.0)).astype(jnp.bfloat16)
    slot_route = one_hot(got_labels, link_blocks, jnp.bfloat16)
    local_paths = one_hot(local_path, path_blocks, jnp.float32)
    remote_paths = one_hot(remote_path, path_blocks, jnp.float32)
    ahead = passed_along(signal[:, :lag_span, :], "tm", -1)
    extended_signal = jnp.concatenate([signal, ahead], axis=1).reshape(
        day_count, minutes + lag_span, link_blocks, block_width
    )
    slot_signal = jnp.einsum(
        "dtkl,sk->sdtl", extended_signal, slot_route, preferred_element_type=jnp.float32
    ).astype(jnp.bfloat16)
    returned = lax.all_to_all(slot_signal, "corr", split_axis=0, concat_axis=0, tiled=True)
    remote_pick = jnp.einsum(
        "sdtl,bs->bdtl", returned, slot_pick, preferred_element_type=jnp.float32
    ).astype(jnp.bfloat16)
    remote_sig = jnp.einsum(
        "bdsl,bts->bdtl",
        remote_pick,
        shift_table(remote_lag, minutes, minutes + lag_span, jnp.bfloat16),
        preferred_element_type=jnp.float32,
    ).astype(jnp.bfloat16)
    local_sig = shift_narrow(
        pick_blocks(extended_signal, local_link_hot),
        shift_table(local_lag, minutes, minutes + lag_span, jnp.bfloat16),
    )
    local_grad = jnp.einsum(
        "dtbl,blp->dtbp", local_sig, local_blocks, preferred_element_type=jnp.float32
    )
    remote_grad = jnp.einsum(
        "bdtl,blp->bdtp", remote_sig, remote_blocks, preferred_element_type=jnp.float32
    )
    grad_cube = collect_paths(local_grad, remote_grad, local_paths, remote_paths)
    gradient = grad_cube.reshape(day_count, minutes, path_width)
    new_flows = jnp.maximum(flows.astype(jnp.float32) - RATE * gradient, 0.0)
    return (link_residual, gradient, new_flows)


HALO = 16
WIRE = jnp.float16
UNROLL = 32
CHUNKS = 8


def step_of(count):
    return next(u for u in range(min(count, UNROLL), 0, -1) if count % u == 0)


def stage_flows(group, flows_ref, before_ref, wide, days, width):
    real = jnp.where(group[0] > 0, 1.0, 0.0)
    minutes = flows_ref.shape[1]
    span = HALO + minutes
    for p in range(flows_ref.shape[2] // width):
        cols = slice(p * width, (p + 1) * width)
        for d in range(days):
            row = (p * days + d) * span
            before = before_ref[d, :, cols].astype(jnp.float32)
            wide[row : row + HALO, :] = before[minutes - HALO :] * real
            wide[row + HALO : row + span, :] = flows_ref[d, :, cols].astype(jnp.float32)


def forward_blocks(groups, unroll, mat, base, target, wide, acc, days, minutes):
    span = HALO + minutes

    def group(g, carry):
        parts = []
        for u in range(unroll):
            rows = [wide[pl.ds(base(g, u) + d * span, minutes), :] for d in range(days)]
            taken = jnp.concatenate(rows, axis=0).astype(jnp.bfloat16)
            parts.append(
                lax.dot_general(
                    taken,
                    mat(g, u),
                    (((1,), (1,)), ((), ())),
                    preferred_element_type=jnp.float32,
                )
            )
        for u in range(unroll):
            acc[target(g, u)] += parts[u]
        return carry

    lax.fori_loop(0, groups, group, 0)


def backward_blocks(groups, unroll, mat, base, signal, acc, days, minutes):
    span = HALO + minutes

    def group(g, carry):
        parts = [
            jnp.dot(signal(g, u), mat(g, u), preferred_element_type=jnp.float32)
            for u in range(unroll)
        ]
        for u in range(unroll):
            for d in range(days):
                rows = pl.ds(base(g, u) + d * span, minutes)
                acc[rows, :] += parts[u][d * minutes : (d + 1) * minutes]
        return carry

    lax.fori_loop(0, groups, group, 0)


def prepare_kernel(cap, order, links, chunks, row_step, me, *rest):
    sources, (ahead, mats_out, path, link, lag, slot, place, sems) = rest[:5], rest[5:]
    blocks = slot.shape[0]
    pairs = list(zip(sources[:4], (path, link, lag, slot)))
    step = blocks // chunks
    for c in range(chunks):
        rows = slice(c * step, blocks if c == chunks - 1 else (c + 1) * step)
        pairs.append((sources[4].at[rows], mats_out.at[rows]))
    copies = [pltpu.make_async_copy(a, b, sems.at[i]) for i, (a, b) in enumerate(pairs)]
    for copy in copies:
        copy.start()
    place[0] = 0
    for p, s in enumerate(order):
        place[s] = p * links
    for copy in copies[:4]:
        copy.wait()

    def entry(j, carry):
        ahead[j] = path[j] * row_step + HALO - lag[j]
        ahead[blocks + j] = place[lax.div(slot[j], cap) ^ me[0]] + link[j]
        return carry

    lax.fori_loop(0, blocks, entry, 0, unroll=16)
    for copy in copies[4:]:
        copy.wait()


def fill_table(cap, order, me, slot, table):
    first = len(order)
    for p, s in enumerate(order):
        table[p] = first + (me[0] ^ s) * cap
    for i in range((first + 1) * cap):
        table[first + i] = -1

    def entry(j, carry):
        table[first + slot[j]] = j
        return carry

    lax.fori_loop(0, slot.shape[0], entry, 0, unroll=16)


def slot_views(table, ahead, mats, cap, first, unroll, blank):
    def index(g, u):
        at = first * cap + g * unroll + u
        place = lax.div(at, cap)
        return table[table[place] + at - place * cap]

    def mat(g, u):
        return mats[jnp.maximum(index(g, u), 0)]

    def base(g, u):
        return ahead[jnp.maximum(index(g, u), 0)]

    def block(g, u):
        j = index(g, u)
        return jnp.where(j < 0, blank, ahead[mats.shape[0] + jnp.maximum(j, 0)])

    return mat, base, block


def forward_remote_kernel(days, cuts, links, group, ahead, flows, before, mats, *rest):
    outs, (wide, acc) = rest[:-2], rest[-2:]
    minutes, width = flows.shape[1], mats.shape[2]
    blocks = mats.shape[0]
    stage_flows(group, flows, before, wide, days, width)
    acc[...] = jnp.zeros_like(acc)
    unroll = step_of(blocks)
    forward_blocks(
        blocks // unroll,
        unroll,
        lambda g, u: mats[g * unroll + u],
        lambda g, u: ahead[g * unroll + u],
        lambda g, u: ahead[blocks + g * unroll + u],
        wide,
        acc,
        days,
        minutes,
    )
    for first, end, out in zip(cuts, cuts[1:], outs):
        out[...] = acc[first * links : end * links]


def local_views(path, link, lag, mats, unroll, row_step):
    return (
        lambda g, u: mats[g * unroll + u],
        lambda g, u: path[g * unroll + u] * row_step + HALO - lag[g * unroll + u],
        lambda g, u: link[g * unroll + u],
    )


def forward_local_kernel(
    days, cap, order, group, me, slot, path, link, lag, flows, before, mats, own, table, wide
):
    minutes, width = flows.shape[1], mats.shape[2]
    stage_flows(group, flows, before, wide, days, width)
    own[...] = jnp.zeros_like(own)
    unroll = step_of(mats.shape[0])
    views = local_views(path, link, lag, mats, unroll, days * (HALO + minutes))
    forward_blocks(mats.shape[0] // unroll, unroll, *views, wide, own, days, minutes)
    fill_table(cap, order, me, slot, table)


def signal_kernel(days, totals, counts, residual, signal):
    blocks, _, width = totals.shape
    minutes = counts.shape[1]
    for b in range(blocks):
        cols = slice(b * width, (b + 1) * width)
        total = totals[b]
        for d in range(days):
            rows = slice(d * minutes, (d + 1) * minutes)
            seen = counts[d, :, cols]
            weight = seen + 1.0
            res = (total[rows] - seen) / weight
            residual[d, :, cols] = res
            signal[b, rows, :] = (res / weight).astype(signal.dtype)


def backward_local_kernel(days, path, link, lag, signal, mats, out):
    minutes = signal.shape[1] // days
    out[...] = jnp.zeros_like(out)
    unroll = step_of(mats.shape[0])
    mat, base, block = local_views(path, link, lag, mats, unroll, days * (HALO + minutes))
    backward_blocks(
        mats.shape[0] // unroll,
        unroll,
        mat,
        base,
        lambda g, u: signal[block(g, u)],
        out,
        days,
        minutes,
    )


def backward_remote_kernel(days, cap, first, end, links, table, ahead, mats, start, *rest):
    count = (end - first) * links
    signals, sources, rest = [], 0, list(rest)
    while sources < count:
        signals.append(rest.pop(0))
        sources += signals[-1].shape[0]
    out, early, everyone = rest[0], rest[1:-1], rest[-1]
    minutes = signals[0].shape[1] // days
    place = first * links
    for part in signals:
        everyone[place : place + part.shape[0]] = part[...]
        place += part.shape[0]
    blank = everyone.shape[0] - 1
    everyone[blank] = jnp.zeros(everyone.shape[1:], everyone.dtype)
    out[...] = start[...]
    span = HALO + minutes
    slots = (end - first) * cap
    unroll = step_of(slots)
    mat, base, block = slot_views(table, ahead, mats, cap, first, unroll, blank)
    backward_blocks(
        slots // unroll,
        unroll,
        mat,
        base,
        lambda g, u: everyone[block(g, u)],
        out,
        days,
        minutes,
    )
    if early:
        for i in range(early[0].shape[0]):
            early[0][i] = out[i * span : i * span + HALO, :]


def finish_kernel(days, groups, group, total, spill, flows, gradient, new_flows):
    minutes = flows.shape[1]
    width = total.shape[1]
    span = HALO + minutes
    real = jnp.where(group[0] < groups - 1, 1.0, 0.0)
    for p in range(flows.shape[2] // width):
        cols = slice(p * width, (p + 1) * width)
        for d in range(days):
            row = (p * days + d) * span + HALO
            own = total[row : row + minutes, :]
            keep = minutes - HALO
            late = own[keep:] + spill[p * days + d] * real
            for rows, grad in ((slice(0, keep), own[:keep]), (slice(keep, minutes), late)):
                gradient[d, rows, cols] = grad
                new_flows[d, rows, cols] = jnp.maximum(
                    flows[d, rows, cols].astype(jnp.float32) - RATE * grad, 0.0
                )


BACKWARD_COST = 500


def weight(nanoseconds):
    return pl.CostEstimate(
        flops=1_000_000 * nanoseconds, transcendentals=0, bytes_accessed=3_000 * nanoseconds
    )


SMEM = pl.BlockSpec(memory_space=pltpu.SMEM)
VMEM = pl.BlockSpec(memory_space=pltpu.VMEM)
HBM = pl.BlockSpec(memory_space=pltpu.HBM)


def kernel_call(body, scalars, arrays, out_shape, scratch=(), cost=None, outs=None):
    return pl.pallas_call(
        body,
        out_shape=out_shape,
        in_specs=[SMEM] * len(scalars) + [VMEM] * len(arrays),
        out_specs=outs or [VMEM] * len(out_shape),
        scratch_shapes=list(scratch),
        compiler_params=pltpu.CompilerParams(vmem_limit_bytes=40 * 1024 * 1024),
        cost_estimate=cost,
    )(*scalars, *arrays)


def per_device_dense(
    flows,
    counts,
    local_blocks,
    local_path,
    local_link,
    local_lag,
    remote_blocks,
    remote_path,
    remote_link,
    remote_lag,
    remote_slot,
):
    days, minutes, path_width = flows.shape
    width = local_blocks.shape[1]
    paths = path_width // width
    links = counts.shape[2] // width
    corridors = lax.axis_size("corr")
    remotes = remote_lag.shape[0]
    cap = (remotes + corridors - 2) // (corridors - 1)
    span = HALO + minutes
    through = list(range(corridors - 2, 0, -2))
    final = through[len(through) // 2]
    rest = [s for s in through if s != final]
    order = [s ^ 1 for s in (*rest, final)] + [1] + through
    through = through[::-1]
    order[-len(through):] = through
    me = lax.axis_index("corr").astype(jnp.int32).reshape(1)
    group = lax.axis_index("tm").astype(jnp.int32).reshape(1)
    groups = lax.axis_size("tm")
    shape = jax.ShapeDtypeStruct
    piece = (links, days * minutes, width)
    wide = pltpu.VMEM((paths * days * span, width), jnp.float32)
    slots_shape = (len(order) * links + 1, days * minutes, width)
    local_index = (local_path, local_link, local_lag)

    before = lax.ppermute(flows, "tm", [(i, (i + 1) % groups) for i in range(groups)])
    fixed = (remote_path, remote_link, remote_lag, remote_slot, remote_blocks)
    ahead, remote_mats = pl.pallas_call(
        functools.partial(prepare_kernel, cap, order, links, CHUNKS, days * span),
        out_shape=[
            shape((2 * remotes,), jnp.int32),
            shape(remote_blocks.shape, remote_blocks.dtype),
        ],
        in_specs=[SMEM] + [HBM] * len(fixed),
        out_specs=[SMEM, VMEM],
        scratch_shapes=[pltpu.SMEM(remote_slot.shape, jnp.int32) for _ in fixed[1:]]
        + [pltpu.SMEM((corridors,), jnp.int32), pltpu.SemaphoreType.DMA((len(fixed) - 1 + CHUNKS,))],
        compiler_params=pltpu.CompilerParams(vmem_limit_bytes=40 * 1024 * 1024),
    )(me, *(pltpu.with_memory_space_constraint(i, pltpu.HBM) for i in fixed))

    def exchanged(part, s):
        return lax.ppermute(part, "corr", [(i, i ^ s) for i in range(corridors)])

    f32 = jnp.float32
    cuts = range(len(order) + 1)
    outgoing = kernel_call(
        functools.partial(forward_remote_kernel, days, cuts, links),
        (group, ahead),
        (flows, before, remote_mats),
        [shape(((end - first) * links, *piece[1:]), f32) for first, end in zip(cuts, cuts[1:])],
        [wide, pltpu.VMEM((len(order) * links, *piece[1:]), f32)],
    )
    count = len(through)
    crossed = [exchanged(part.astype(WIRE), 1) for part in outgoing[:count]]
    near = exchanged(outgoing[count].astype(WIRE), 1)
    received = []
    for s, kept in reversed(list(zip(through, outgoing[count + 1 :]))):
        met = crossed[order.index(s ^ 1)].astype(f32)
        received.append(exchanged((kept + met).astype(WIRE), s))
    received.append(near)
    own, table = kernel_call(
        functools.partial(forward_local_kernel, days, cap, order),
        (group, me, remote_slot, *local_index),
        (flows, before, local_blocks),
        [shape(piece, f32), shape((len(order) + corridors * cap,), jnp.int32)],
        [wide],
        outs=[VMEM, SMEM],
    )
    totals = functools.reduce(jnp.add, [p.astype(f32) for p in received], own)
    link_residual, signal = kernel_call(
        functools.partial(signal_kernel, days),
        (),
        (totals, counts),
        [shape(counts.shape, f32), shape(piece, jnp.bfloat16)],
    )
    arrived = {s: exchanged(signal, s) for s in (*through, 1)}
    rows = [shape((paths * days * span, width), f32)]
    (total,) = kernel_call(
        functools.partial(backward_local_kernel, days),
        local_index,
        (signal, local_blocks),
        rows,
    )
    arrived[2], total = lax.optimization_barrier((arrived[2], total))
    for s in through:
        arrived[s ^ 1] = exchanged(arrived[s], 1)
    edge = shape((paths * days, HALO, width), f32)
    for first, end, made in ((count, len(order), rows), (0, count, [*rows, edge])):
        total, *early = kernel_call(
            functools.partial(backward_remote_kernel, days, cap, first, end, links),
            (table, ahead),
            (remote_mats, total, *(arrived[s] for s in order[first:end])),
            made,
            [pltpu.VMEM(slots_shape, jnp.bfloat16)],
            cost=weight(BACKWARD_COST) if first else None,
        )
    spill = lax.ppermute(early[0], "tm", [(i, (i - 1) % groups) for i in range(groups)])
    gradient, new_flows = kernel_call(
        functools.partial(finish_kernel, days, groups),
        (group,),
        (total, spill, flows),
        [shape(flows.shape, f32)] * 2,
    )
    return (link_residual, gradient, new_flows)


def per_device(*args):
    counts, blocks, lags = args[1], args[2], args[9]
    corridors = lax.axis_size("corr")
    links = counts.shape[2] // blocks.shape[1]
    cap = (lags.shape[0] + corridors - 2) // (corridors - 1)
    if cap >= links and corridors >= 4 and corridors & (corridors - 1) == 0:
        return per_device_dense(*args)
    return per_device_slots(*args)


def solution(mesh):
    placed = (
        P(None, "tm", "corr"),
        P(None, "tm", "corr"),
        P("corr", None, None),
        P("corr"),
        P("corr"),
        P("corr"),
        P("corr", None, None),
        P("corr"),
        P("corr"),
        P("corr"),
        P("corr"),
    )
    return jax.shard_map(
        per_device,
        mesh=mesh,
        in_specs=placed,
        out_specs=(P(None, "tm", "corr"), P(None, "tm", "corr"), P(None, "tm", "corr")),
        check_vma=False,
    )
```

```python
import functools
import jax
import jax.numpy as jnp
from jax import lax
from jax.experimental import pallas as pl
from jax.experimental.pallas import tpu as pltpu
from jax.sharding import PartitionSpec as P

LAGS = 16


HIGH = lax.Precision.HIGHEST
RATE = 0.5


def passed_along(block, axis, distance):
    devices = range(lax.axis_size(axis))
    route = [(i - distance, i) for i in devices if i - distance in devices]
    return lax.ppermute(block, axis, route)


def one_hot(labels, classes, dtype):
    return (labels[:, None] == jnp.arange(classes, dtype=jnp.int32)[None, :]).astype(dtype)


def shift_table(deltas, out_len, in_len, dtype):
    out_pos = jnp.arange(out_len, dtype=jnp.int32)[:, None]
    in_pos = jnp.arange(in_len, dtype=jnp.int32)[None, :]
    return ((in_pos - out_pos)[None, :, :] == deltas[:, None, None]).astype(dtype)


def pick_blocks(cube, hot):
    return jnp.einsum("dsqp,bq->dsbp", cube, hot, preferred_element_type=jnp.float32).astype(
        jnp.bfloat16
    )


def shift_narrow(picked, table):
    return jnp.einsum("dsbp,bts->dtbp", picked, table, preferred_element_type=jnp.float32).astype(
        jnp.bfloat16
    )


def route_partials(local_part, remote_part, local_route, remote_link, slot_hot, link_blocks):
    own = jnp.einsum("dtbl,bk->dtkl", local_part, local_route, precision=HIGH)
    outgoing = jnp.einsum("bdtl,bs->sdtl", remote_part, slot_hot, precision=HIGH)
    slot_int = slot_hot.astype(jnp.int32)
    labels = link_blocks + jnp.sum(slot_int * (remote_link[:, None] - link_blocks), axis=0)
    return (own, outgoing, labels)


def absorb(own, received, got_labels, link_blocks):
    landing = one_hot(got_labels, link_blocks, jnp.float32)
    return own + jnp.einsum("sdtl,sk->dtkl", received, landing, precision=HIGH)


def collect_paths(local_grad, remote_grad, local_paths, remote_paths):
    first_sum = jnp.einsum("dtbp,bq->dtqp", local_grad, local_paths, precision=HIGH)
    return first_sum + jnp.einsum("bdtp,bq->dtqp", remote_grad, remote_paths, precision=HIGH)


def per_device_slots(
    flows,
    counts,
    local_blocks,
    local_path,
    local_link,
    local_lag,
    remote_blocks,
    remote_path,
    remote_link,
    remote_lag,
    remote_slot,
):
    day_count, minutes, path_width = flows.shape
    block_width = local_blocks.shape[1]
    path_blocks = path_width // block_width
    link_blocks = counts.shape[2] // block_width
    lag_span = LAGS - 1
    corridors = lax.axis_size("corr")
    remote_count = remote_lag.shape[0]
    slot_count = corridors * ((remote_count + corridors - 2) // (corridors - 1))
    flow_cube = flows.reshape(day_count, minutes, path_blocks, block_width)
    local_route = one_hot(local_link, link_blocks, jnp.float32)
    slot_hot = one_hot(remote_slot, slot_count, jnp.float32)
    slot_pick = slot_hot.astype(jnp.bfloat16)
    local_path_hot = one_hot(local_path, path_blocks, jnp.bfloat16)
    remote_path_hot = one_hot(remote_path, path_blocks, jnp.bfloat16)
    local_link_hot = one_hot(local_link, link_blocks, jnp.bfloat16)
    local_in = pick_blocks(flow_cube, local_path_hot)
    remote_in = pick_blocks(flow_cube, remote_path_hot)
    local_plain = jnp.einsum(
        "dtbp,blp->dtbl", local_in, local_blocks, preferred_element_type=jnp.float32
    )
    remote_plain = jnp.einsum(
        "dtbp,blp->bdtl", remote_in, remote_blocks, preferred_element_type=jnp.float32
    )
    local_part = jnp.einsum(
        "dsbl,bts->dtbl",
        local_plain,
        shift_table(-local_lag, minutes + lag_span, minutes, jnp.float32),
        precision=HIGH,
    )
    remote_part = jnp.einsum(
        "bdsl,bts->bdtl",
        remote_plain,
        shift_table(-remote_lag, minutes + lag_span, minutes, jnp.float32),
        precision=HIGH,
    )
    own, outgoing, labels = route_partials(
        local_part, remote_part, local_route, remote_link, slot_hot, link_blocks
    )
    received, got_labels = (
        lax.all_to_all(outgoing, "corr", split_axis=0, concat_axis=0, tiled=True),
        lax.all_to_all(labels, "corr", split_axis=0, concat_axis=0, tiled=True),
    )
    extended = absorb(own, received, got_labels, link_blocks)
    spill = passed_along(extended[:, minutes:], "tm", 1)
    totals = extended[:, :minutes] + jnp.pad(
        spill, ((0, 0), (0, minutes - lag_span), (0, 0), (0, 0))
    )
    link_flow = totals.reshape(day_count, minutes, link_blocks * block_width)
    link_residual = (link_flow - counts) / (counts + 1.0)
    signal = (link_residual / (counts + 1.0)).astype(jnp.bfloat16)
    slot_route = one_hot(got_labels, link_blocks, jnp.bfloat16)
    local_paths = one_hot(local_path, path_blocks, jnp.float32)
    remote_paths = one_hot(remote_path, path_blocks, jnp.float32)
    ahead = passed_along(signal[:, :lag_span, :], "tm", -1)
    extended_signal = jnp.concatenate([signal, ahead], axis=1).reshape(
        day_count, minutes + lag_span, link_blocks, block_width
    )
    slot_signal = jnp.einsum(
        "dtkl,sk->sdtl", extended_signal, slot_route, preferred_element_type=jnp.float32
    ).astype(jnp.bfloat16)
    returned = lax.all_to_all(slot_signal, "corr", split_axis=0, concat_axis=0, tiled=True)
    remote_pick = jnp.einsum(
        "sdtl,bs->bdtl", returned, slot_pick, preferred_element_type=jnp.float32
    ).astype(jnp.bfloat16)
    remote_sig = jnp.einsum(
        "bdsl,bts->bdtl",
        remote_pick,
        shift_table(remote_lag, minutes, minutes + lag_span, jnp.bfloat16),
        preferred_element_type=jnp.float32,
    ).astype(jnp.bfloat16)
    local_sig = shift_narrow(
        pick_blocks(extended_signal, local_link_hot),
        shift_table(local_lag, minutes, minutes + lag_span, jnp.bfloat16),
    )
    local_grad = jnp.einsum(
        "dtbl,blp->dtbp", local_sig, local_blocks, preferred_element_type=jnp.float32
    )
    remote_grad = jnp.einsum(
        "bdtl,blp->bdtp", remote_sig, remote_blocks, preferred_element_type=jnp.float32
    )
    grad_cube = collect_paths(local_grad, remote_grad, local_paths, remote_paths)
    gradient = grad_cube.reshape(day_count, minutes, path_width)
    new_flows = jnp.maximum(flows.astype(jnp.float32) - RATE * gradient, 0.0)
    return (link_residual, gradient, new_flows)


HALO = 16
WIRE = jnp.float16
UNROLL = 32
CHUNKS = 8


def step_of(count):
    return next(u for u in range(min(count, UNROLL), 0, -1) if count % u == 0)


def stage_flows(group, flows_ref, before_ref, wide, days, width):
    real = jnp.where(group[0] > 0, 1.0, 0.0)
    minutes = flows_ref.shape[1]
    span = HALO + minutes
    for p in range(flows_ref.shape[2] // width):
        cols = slice(p * width, (p + 1) * width)
        for d in range(days):
            row = (p * days + d) * span
            before = before_ref[d, :, cols].astype(jnp.float32)
            wide[row : row + HALO, :] = before[minutes - HALO :] * real
            wide[row + HALO : row + span, :] = flows_ref[d, :, cols].astype(jnp.float32)


def forward_blocks(groups, unroll, mat, base, target, wide, acc, days, minutes):
    span = HALO + minutes

    def group(g, carry):
        parts = []
        for u in range(unroll):
            rows = [wide[pl.ds(base(g, u) + d * span, minutes), :] for d in range(days)]
            taken = jnp.concatenate(rows, axis=0).astype(jnp.bfloat16)
            parts.append(
                lax.dot_general(
                    taken,
                    mat(g, u),
                    (((1,), (1,)), ((), ())),
                    preferred_element_type=jnp.float32,
                )
            )
        for u in range(unroll):
            acc[target(g, u)] += parts[u]
        return carry

    lax.fori_loop(0, groups, group, 0)


def backward_blocks(groups, unroll, mat, base, signal, acc, days, minutes):
    span = HALO + minutes

    def group(g, carry):
        parts = [
            jnp.dot(signal(g, u), mat(g, u), preferred_element_type=jnp.float32)
            for u in range(unroll)
        ]
        for u in range(unroll):
            for d in range(days):
                rows = pl.ds(base(g, u) + d * span, minutes)
                acc[rows, :] += parts[u][d * minutes : (d + 1) * minutes]
        return carry

    lax.fori_loop(0, groups, group, 0)


def prepare_kernel(cap, order, links, chunks, row_step, me, *rest):
    sources, (ahead, mats_out, path, link, lag, slot, place, sems) = rest[:5], rest[5:]
    blocks = slot.shape[0]
    pairs = list(zip(sources[:4], (path, link, lag, slot)))
    step = blocks // chunks
    for c in range(chunks):
        rows = slice(c * step, blocks if c == chunks - 1 else (c + 1) * step)
        pairs.append((sources[4].at[rows], mats_out.at[rows]))
    copies = [pltpu.make_async_copy(a, b, sems.at[i]) for i, (a, b) in enumerate(pairs)]
    for copy in copies:
        copy.start()
    place[0] = 0
    for p, s in enumerate(order):
        place[s] = p * links
    for copy in copies[:4]:
        copy.wait()

    def entry(j, carry):
        ahead[j] = path[j] * row_step + HALO - lag[j]
        ahead[blocks + j] = place[lax.div(slot[j], cap) ^ me[0]] + link[j]
        return carry

    lax.fori_loop(0, blocks, entry, 0, unroll=16)
    for copy in copies[4:]:
        copy.wait()


def fill_table(cap, order, me, slot, table):
    first = len(order)
    for p, s in enumerate(order):
        table[p] = first + (me[0] ^ s) * cap
    for i in range((first + 1) * cap):
        table[first + i] = -1

    def entry(j, carry):
        table[first + slot[j]] = j
        return carry

    lax.fori_loop(0, slot.shape[0], entry, 0, unroll=16)


def slot_views(table, ahead, mats, cap, first, unroll, blank):
    def index(g, u):
        at = first * cap + g * unroll + u
        place = lax.div(at, cap)
        return table[table[place] + at - place * cap]

    def mat(g, u):
        return mats[jnp.maximum(index(g, u), 0)]

    def base(g, u):
        return ahead[jnp.maximum(index(g, u), 0)]

    def block(g, u):
        j = index(g, u)
        return jnp.where(j < 0, blank, ahead[mats.shape[0] + jnp.maximum(j, 0)])

    return mat, base, block


def forward_remote_kernel(days, links, group, ahead, flows, before, mats, *rest):
    outs, (wide, acc) = rest[:-2], rest[-2:]
    minutes, width = flows.shape[1], mats.shape[2]
    blocks = mats.shape[0]
    stage_flows(group, flows, before, wide, days, width)
    acc[...] = jnp.zeros_like(acc)
    unroll = step_of(blocks)
    forward_blocks(
        blocks // unroll,
        unroll,
        lambda g, u: mats[g * unroll + u],
        lambda g, u: ahead[g * unroll + u],
        lambda g, u: ahead[blocks + g * unroll + u],
        wide,
        acc,
        days,
        minutes,
    )
    for p, out in enumerate(outs):
        out[...] = acc[p * links : (p + 1) * links]


def local_views(path, link, lag, mats, unroll, row_step):
    return (
        lambda g, u: mats[g * unroll + u],
        lambda g, u: path[g * unroll + u] * row_step + HALO - lag[g * unroll + u],
        lambda g, u: link[g * unroll + u],
    )


def forward_local_kernel(
    days, cap, order, group, me, slot, path, link, lag, flows, before, mats, own, table, wide
):
    minutes, width = flows.shape[1], mats.shape[2]
    stage_flows(group, flows, before, wide, days, width)
    own[...] = jnp.zeros_like(own)
    unroll = step_of(mats.shape[0])
    views = local_views(path, link, lag, mats, unroll, days * (HALO + minutes))
    forward_blocks(mats.shape[0] // unroll, unroll, *views, wide, own, days, minutes)
    fill_table(cap, order, me, slot, table)


def residual_of(days, totals, counts, b, d):
    width, minutes = totals.shape[2], counts.shape[1]
    seen = counts[d, :, b * width : (b + 1) * width]
    weight = seen + 1.0
    return (totals[b, d * minutes : (d + 1) * minutes, :] - seen) / weight, weight


def signal_kernel(days, totals, counts, signal):
    minutes = counts.shape[1]
    for b in range(totals.shape[0]):
        for d in range(days):
            res, weight = residual_of(days, totals, counts, b, d)
            signal[b, d * minutes : (d + 1) * minutes, :] = (res / weight).astype(signal.dtype)


def backward_local_kernel(days, path, link, lag, signal, mats, totals, counts, out, residual):
    minutes, width = signal.shape[1] // days, totals.shape[2]
    for b in range(totals.shape[0]):
        for d in range(days):
            res, _ = residual_of(days, totals, counts, b, d)
            residual[d, :, b * width : (b + 1) * width] = res
    out[...] = jnp.zeros_like(out)
    unroll = step_of(mats.shape[0])
    mat, base, block = local_views(path, link, lag, mats, unroll, days * (HALO + minutes))
    backward_blocks(
        mats.shape[0] // unroll,
        unroll,
        mat,
        base,
        lambda g, u: signal[block(g, u)],
        out,
        days,
        minutes,
    )


def backward_remote_kernel(days, cap, first, end, links, table, ahead, mats, start, *rest):
    count = (end - first) * links
    signals, sources, rest = [], 0, list(rest)
    while sources < count:
        signals.append(rest.pop(0))
        sources += signals[-1].shape[0]
    out, early, everyone = rest[0], rest[1:-1], rest[-1]
    minutes = signals[0].shape[1] // days
    place = first * links
    for part in signals:
        everyone[place : place + part.shape[0]] = part[...]
        place += part.shape[0]
    blank = everyone.shape[0] - 1
    everyone[blank] = jnp.zeros(everyone.shape[1:], everyone.dtype)
    out[...] = start[...]
    span = HALO + minutes
    slots = (end - first) * cap
    unroll = step_of(slots)
    mat, base, block = slot_views(table, ahead, mats, cap, first, unroll, blank)
    backward_blocks(
        slots // unroll,
        unroll,
        mat,
        base,
        lambda g, u: everyone[block(g, u)],
        out,
        days,
        minutes,
    )
    if early:
        for i in range(early[0].shape[0]):
            early[0][i] = out[i * span : i * span + HALO, :]


def finish_kernel(days, groups, group, total, spill, flows, gradient, new_flows):
    minutes = flows.shape[1]
    width = total.shape[1]
    span = HALO + minutes
    real = jnp.where(group[0] < groups - 1, 1.0, 0.0)
    for p in range(flows.shape[2] // width):
        cols = slice(p * width, (p + 1) * width)
        for d in range(days):
            row = (p * days + d) * span + HALO
            own = total[row : row + minutes, :]
            keep = minutes - HALO
            late = own[keep:] + spill[p * days + d] * real
            for rows, grad in ((slice(0, keep), own[:keep]), (slice(keep, minutes), late)):
                gradient[d, rows, cols] = grad
                new_flows[d, rows, cols] = jnp.maximum(
                    flows[d, rows, cols].astype(jnp.float32) - RATE * grad, 0.0
                )


BACKWARD_COST = 500


def weight(nanoseconds):
    return pl.CostEstimate(
        flops=1_000_000 * nanoseconds, transcendentals=0, bytes_accessed=3_000 * nanoseconds
    )


SMEM = pl.BlockSpec(memory_space=pltpu.SMEM)
VMEM = pl.BlockSpec(memory_space=pltpu.VMEM)
HBM = pl.BlockSpec(memory_space=pltpu.HBM)


def kernel_call(body, scalars, arrays, out_shape, scratch=(), cost=None, outs=None):
    return pl.pallas_call(
        body,
        out_shape=out_shape,
        in_specs=[SMEM] * len(scalars) + [VMEM] * len(arrays),
        out_specs=outs or [VMEM] * len(out_shape),
        scratch_shapes=list(scratch),
        compiler_params=pltpu.CompilerParams(vmem_limit_bytes=40 * 1024 * 1024),
        cost_estimate=cost,
    )(*scalars, *arrays)


def per_device_dense(
    flows,
    counts,
    local_blocks,
    local_path,
    local_link,
    local_lag,
    remote_blocks,
    remote_path,
    remote_link,
    remote_lag,
    remote_slot,
):
    days, minutes, path_width = flows.shape
    width = local_blocks.shape[1]
    paths = path_width // width
    links = counts.shape[2] // width
    corridors = lax.axis_size("corr")
    remotes = remote_lag.shape[0]
    cap = (remotes + corridors - 2) // (corridors - 1)
    span = HALO + minutes
    through = list(range(corridors - 2, 0, -2))
    final = through[len(through) // 2]
    rest = [s for s in through if s != final]
    order = [s ^ 1 for s in (*rest, final)] + [1] + through
    through = through[::-1]
    order[-len(through):] = through
    me = lax.axis_index("corr").astype(jnp.int32).reshape(1)
    group = lax.axis_index("tm").astype(jnp.int32).reshape(1)
    groups = lax.axis_size("tm")
    shape = jax.ShapeDtypeStruct
    piece = (links, days * minutes, width)
    wide = pltpu.VMEM((paths * days * span, width), jnp.float32)
    slots_shape = (len(order) * links + 1, days * minutes, width)
    local_index = (local_path, local_link, local_lag)

    before = lax.ppermute(flows, "tm", [(i, (i + 1) % groups) for i in range(groups)])
    fixed = (remote_path, remote_link, remote_lag, remote_slot, remote_blocks)
    ahead, remote_mats = pl.pallas_call(
        functools.partial(prepare_kernel, cap, order, links, CHUNKS, days * span),
        out_shape=[
            shape((2 * remotes,), jnp.int32),
            shape(remote_blocks.shape, remote_blocks.dtype),
        ],
        in_specs=[SMEM] + [HBM] * len(fixed),
        out_specs=[SMEM, VMEM],
        scratch_shapes=[pltpu.SMEM(remote_slot.shape, jnp.int32) for _ in fixed[1:]]
        + [pltpu.SMEM((corridors,), jnp.int32), pltpu.SemaphoreType.DMA((len(fixed) - 1 + CHUNKS,))],
        compiler_params=pltpu.CompilerParams(vmem_limit_bytes=40 * 1024 * 1024),
    )(me, *(pltpu.with_memory_space_constraint(i, pltpu.HBM) for i in fixed))

    def exchanged(part, s):
        return lax.ppermute(part, "corr", [(i, i ^ s) for i in range(corridors)])

    f32 = jnp.float32
    outgoing = kernel_call(
        functools.partial(forward_remote_kernel, days, links),
        (group, ahead),
        (flows, before, remote_mats),
        [shape(piece, f32) for _ in order],
        [wide, pltpu.VMEM((len(order) * links, *piece[1:]), f32)],
    )
    count = len(through)
    crossed = [exchanged(part.astype(WIRE), 1) for part in outgoing[:count]]
    near = exchanged(outgoing[count].astype(WIRE), 1)
    received = []
    for s, kept in reversed(list(zip(through, outgoing[count + 1 :]))):
        met = crossed[order.index(s ^ 1)].astype(f32)
        received.append(exchanged((kept + met).astype(WIRE), s))
    received.append(near)
    own, table = kernel_call(
        functools.partial(forward_local_kernel, days, cap, order),
        (group, me, remote_slot, *local_index),
        (flows, before, local_blocks),
        [shape(piece, f32), shape((len(order) + corridors * cap,), jnp.int32)],
        [wide],
        outs=[VMEM, SMEM],
    )
    totals = functools.reduce(jnp.add, [p.astype(f32) for p in received], own)
    (signal,) = kernel_call(
        functools.partial(signal_kernel, days),
        (),
        (totals, counts),
        [shape(piece, jnp.bfloat16)],
    )
    arrived = {s: exchanged(signal, s) for s in (*through, 1)}
    rows = [shape((paths * days * span, width), f32)]
    total, link_residual = kernel_call(
        functools.partial(backward_local_kernel, days),
        local_index,
        (signal, local_blocks, totals, counts),
        [*rows, shape(counts.shape, f32)],
    )
    arrived[through[-1]], total = lax.optimization_barrier((arrived[through[-1]], total))
    for s in through:
        arrived[s ^ 1] = exchanged(arrived[s], 1)
    edge = shape((paths * days, HALO, width), f32)
    for first, end, made in ((count, len(order), rows), (0, count, [*rows, edge])):
        total, *early = kernel_call(
            functools.partial(backward_remote_kernel, days, cap, first, end, links),
            (table, ahead),
            (remote_mats, total, *(arrived[s] for s in order[first:end])),
            made,
            [pltpu.VMEM(slots_shape, jnp.bfloat16)],
            cost=weight(BACKWARD_COST) if first else None,
        )
    spill = lax.ppermute(early[0], "tm", [(i, (i - 1) % groups) for i in range(groups)])
    gradient, new_flows = kernel_call(
        functools.partial(finish_kernel, days, groups),
        (group,),
        (total, spill, flows),
        [shape(flows.shape, f32)] * 2,
    )
    return (link_residual, gradient, new_flows)


def per_device(*args):
    counts, blocks, lags = args[1], args[2], args[9]
    corridors = lax.axis_size("corr")
    links = counts.shape[2] // blocks.shape[1]
    cap = (lags.shape[0] + corridors - 2) // (corridors - 1)
    if cap >= links and corridors >= 4 and corridors & (corridors - 1) == 0:
        return per_device_dense(*args)
    return per_device_slots(*args)


def solution(mesh):
    placed = (
        P(None, "tm", "corr"),
        P(None, "tm", "corr"),
        P("corr", None, None),
        P("corr"),
        P("corr"),
        P("corr"),
        P("corr", None, None),
        P("corr"),
        P("corr"),
        P("corr"),
        P("corr"),
    )
    return jax.shard_map(
        per_device,
        mesh=mesh,
        in_specs=placed,
        out_specs=(P(None, "tm", "corr"), P(None, "tm", "corr"), P(None, "tm", "corr")),
        check_vma=False,
    )
```

```python
import functools
import jax
import jax.numpy as jnp
from jax import lax
from jax.experimental import pallas as pl
from jax.experimental.pallas import tpu as pltpu
from jax.sharding import PartitionSpec as P

LAGS = 16


HIGH = lax.Precision.HIGHEST
RATE = 0.5


def passed_along(block, axis, distance):
    devices = range(lax.axis_size(axis))
    route = [(i - distance, i) for i in devices if i - distance in devices]
    return lax.ppermute(block, axis, route)


def one_hot(labels, classes, dtype):
    return (labels[:, None] == jnp.arange(classes, dtype=jnp.int32)[None, :]).astype(dtype)


def shift_table(deltas, out_len, in_len, dtype):
    out_pos = jnp.arange(out_len, dtype=jnp.int32)[:, None]
    in_pos = jnp.arange(in_len, dtype=jnp.int32)[None, :]
    return ((in_pos - out_pos)[None, :, :] == deltas[:, None, None]).astype(dtype)


def pick_blocks(cube, hot):
    return jnp.einsum("dsqp,bq->dsbp", cube, hot, preferred_element_type=jnp.float32).astype(
        jnp.bfloat16
    )


def shift_narrow(picked, table):
    return jnp.einsum("dsbp,bts->dtbp", picked, table, preferred_element_type=jnp.float32).astype(
        jnp.bfloat16
    )


def route_partials(local_part, remote_part, local_route, remote_link, slot_hot, link_blocks):
    own = jnp.einsum("dtbl,bk->dtkl", local_part, local_route, precision=HIGH)
    outgoing = jnp.einsum("bdtl,bs->sdtl", remote_part, slot_hot, precision=HIGH)
    slot_int = slot_hot.astype(jnp.int32)
    labels = link_blocks + jnp.sum(slot_int * (remote_link[:, None] - link_blocks), axis=0)
    return (own, outgoing, labels)


def absorb(own, received, got_labels, link_blocks):
    landing = one_hot(got_labels, link_blocks, jnp.float32)
    return own + jnp.einsum("sdtl,sk->dtkl", received, landing, precision=HIGH)


def collect_paths(local_grad, remote_grad, local_paths, remote_paths):
    first_sum = jnp.einsum("dtbp,bq->dtqp", local_grad, local_paths, precision=HIGH)
    return first_sum + jnp.einsum("bdtp,bq->dtqp", remote_grad, remote_paths, precision=HIGH)


def per_device_slots(
    flows,
    counts,
    local_blocks,
    local_path,
    local_link,
    local_lag,
    remote_blocks,
    remote_path,
    remote_link,
    remote_lag,
    remote_slot,
):
    day_count, minutes, path_width = flows.shape
    block_width = local_blocks.shape[1]
    path_blocks = path_width // block_width
    link_blocks = counts.shape[2] // block_width
    lag_span = LAGS - 1
    corridors = lax.axis_size("corr")
    remote_count = remote_lag.shape[0]
    slot_count = corridors * ((remote_count + corridors - 2) // (corridors - 1))
    flow_cube = flows.reshape(day_count, minutes, path_blocks, block_width)
    local_route = one_hot(local_link, link_blocks, jnp.float32)
    slot_hot = one_hot(remote_slot, slot_count, jnp.float32)
    slot_pick = slot_hot.astype(jnp.bfloat16)
    local_path_hot = one_hot(local_path, path_blocks, jnp.bfloat16)
    remote_path_hot = one_hot(remote_path, path_blocks, jnp.bfloat16)
    local_link_hot = one_hot(local_link, link_blocks, jnp.bfloat16)
    local_in = pick_blocks(flow_cube, local_path_hot)
    remote_in = pick_blocks(flow_cube, remote_path_hot)
    local_plain = jnp.einsum(
        "dtbp,blp->dtbl", local_in, local_blocks, preferred_element_type=jnp.float32
    )
    remote_plain = jnp.einsum(
        "dtbp,blp->bdtl", remote_in, remote_blocks, preferred_element_type=jnp.float32
    )
    local_part = jnp.einsum(
        "dsbl,bts->dtbl",
        local_plain,
        shift_table(-local_lag, minutes + lag_span, minutes, jnp.float32),
        precision=HIGH,
    )
    remote_part = jnp.einsum(
        "bdsl,bts->bdtl",
        remote_plain,
        shift_table(-remote_lag, minutes + lag_span, minutes, jnp.float32),
        precision=HIGH,
    )
    own, outgoing, labels = route_partials(
        local_part, remote_part, local_route, remote_link, slot_hot, link_blocks
    )
    received, got_labels = (
        lax.all_to_all(outgoing, "corr", split_axis=0, concat_axis=0, tiled=True),
        lax.all_to_all(labels, "corr", split_axis=0, concat_axis=0, tiled=True),
    )
    extended = absorb(own, received, got_labels, link_blocks)
    spill = passed_along(extended[:, minutes:], "tm", 1)
    totals = extended[:, :minutes] + jnp.pad(
        spill, ((0, 0), (0, minutes - lag_span), (0, 0), (0, 0))
    )
    link_flow = totals.reshape(day_count, minutes, link_blocks * block_width)
    link_residual = (link_flow - counts) / (counts + 1.0)
    signal = (link_residual / (counts + 1.0)).astype(jnp.bfloat16)
    slot_route = one_hot(got_labels, link_blocks, jnp.bfloat16)
    local_paths = one_hot(local_path, path_blocks, jnp.float32)
    remote_paths = one_hot(remote_path, path_blocks, jnp.float32)
    ahead = passed_along(signal[:, :lag_span, :], "tm", -1)
    extended_signal = jnp.concatenate([signal, ahead], axis=1).reshape(
        day_count, minutes + lag_span, link_blocks, block_width
    )
    slot_signal = jnp.einsum(
        "dtkl,sk->sdtl", extended_signal, slot_route, preferred_element_type=jnp.float32
    ).astype(jnp.bfloat16)
    returned = lax.all_to_all(slot_signal, "corr", split_axis=0, concat_axis=0, tiled=True)
    remote_pick = jnp.einsum(
        "sdtl,bs->bdtl", returned, slot_pick, preferred_element_type=jnp.float32
    ).astype(jnp.bfloat16)
    remote_sig = jnp.einsum(
        "bdsl,bts->bdtl",
        remote_pick,
        shift_table(remote_lag, minutes, minutes + lag_span, jnp.bfloat16),
        preferred_element_type=jnp.float32,
    ).astype(jnp.bfloat16)
    local_sig = shift_narrow(
        pick_blocks(extended_signal, local_link_hot),
        shift_table(local_lag, minutes, minutes + lag_span, jnp.bfloat16),
    )
    local_grad = jnp.einsum(
        "dtbl,blp->dtbp", local_sig, local_blocks, preferred_element_type=jnp.float32
    )
    remote_grad = jnp.einsum(
        "bdtl,blp->bdtp", remote_sig, remote_blocks, preferred_element_type=jnp.float32
    )
    grad_cube = collect_paths(local_grad, remote_grad, local_paths, remote_paths)
    gradient = grad_cube.reshape(day_count, minutes, path_width)
    new_flows = jnp.maximum(flows.astype(jnp.float32) - RATE * gradient, 0.0)
    return (link_residual, gradient, new_flows)


HALO = 16
WIRE = jnp.float16
UNROLL = 32
CHUNKS = 8


def step_of(count):
    return next(u for u in range(min(count, UNROLL), 0, -1) if count % u == 0)


def stage_flows(group, flows_ref, before_ref, wide, days, width):
    real = jnp.where(group[0] > 0, 1.0, 0.0)
    minutes = flows_ref.shape[1]
    span = HALO + minutes
    for p in range(flows_ref.shape[2] // width):
        cols = slice(p * width, (p + 1) * width)
        for d in range(days):
            row = (p * days + d) * span
            before = before_ref[d, :, cols].astype(jnp.float32)
            wide[row : row + HALO, :] = before[minutes - HALO :] * real
            wide[row + HALO : row + span, :] = flows_ref[d, :, cols].astype(jnp.float32)


def forward_blocks(groups, unroll, mat, base, target, wide, acc, days, minutes):
    span = HALO + minutes

    def group(g, carry):
        parts = []
        for u in range(unroll):
            rows = [wide[pl.ds(base(g, u) + d * span, minutes), :] for d in range(days)]
            taken = jnp.concatenate(rows, axis=0).astype(jnp.bfloat16)
            parts.append(
                lax.dot_general(
                    taken,
                    mat(g, u),
                    (((1,), (1,)), ((), ())),
                    preferred_element_type=jnp.float32,
                )
            )
        for u in range(unroll):
            acc[target(g, u)] += parts[u]
        return carry

    lax.fori_loop(0, groups, group, 0)


def backward_blocks(groups, unroll, mat, base, signal, acc, days, minutes):
    span = HALO + minutes

    def group(g, carry):
        parts = [
            jnp.dot(signal(g, u), mat(g, u), preferred_element_type=jnp.float32)
            for u in range(unroll)
        ]
        for u in range(unroll):
            for d in range(days):
                rows = pl.ds(base(g, u) + d * span, minutes)
                acc[rows, :] += parts[u][d * minutes : (d + 1) * minutes]
        return carry

    lax.fori_loop(0, groups, group, 0)


def prepare_kernel(cap, order, links, chunks, row_step, me, *rest):
    sources, (ahead, mats_out, path, link, lag, slot, place, sems) = rest[:5], rest[5:]
    blocks = slot.shape[0]
    pairs = list(zip(sources[:4], (path, link, lag, slot)))
    step = blocks // chunks
    for c in range(chunks):
        rows = slice(c * step, blocks if c == chunks - 1 else (c + 1) * step)
        pairs.append((sources[4].at[rows], mats_out.at[rows]))
    copies = [pltpu.make_async_copy(a, b, sems.at[i]) for i, (a, b) in enumerate(pairs)]
    for copy in copies:
        copy.start()
    place[0] = 0
    for p, s in enumerate(order):
        place[s] = p * links
    for copy in copies[:4]:
        copy.wait()

    def entry(j, carry):
        ahead[j] = path[j] * row_step + HALO - lag[j]
        ahead[blocks + j] = place[lax.div(slot[j], cap) ^ me[0]] + link[j]
        return carry

    lax.fori_loop(0, blocks, entry, 0, unroll=16)
    for copy in copies[4:]:
        copy.wait()


def fill_table(cap, order, me, slot, table):
    first = len(order)
    for p, s in enumerate(order):
        table[p] = first + (me[0] ^ s) * cap
    for i in range((first + 1) * cap):
        table[first + i] = -1

    def entry(j, carry):
        table[first + slot[j]] = j
        return carry

    lax.fori_loop(0, slot.shape[0], entry, 0, unroll=16)


def slot_views(table, ahead, mats, cap, first, unroll, blank):
    def index(g, u):
        at = first * cap + g * unroll + u
        place = lax.div(at, cap)
        return table[table[place] + at - place * cap]

    def mat(g, u):
        return mats[jnp.maximum(index(g, u), 0)]

    def base(g, u):
        return ahead[jnp.maximum(index(g, u), 0)]

    def block(g, u):
        j = index(g, u)
        return jnp.where(j < 0, blank, ahead[mats.shape[0] + jnp.maximum(j, 0)])

    return mat, base, block


def forward_remote_kernel(days, links, group, ahead, flows, before, mats, *rest):
    outs, (wide, acc) = rest[:-2], rest[-2:]
    minutes, width = flows.shape[1], mats.shape[2]
    blocks = mats.shape[0]
    stage_flows(group, flows, before, wide, days, width)
    acc[...] = jnp.zeros_like(acc)
    unroll = step_of(blocks)
    forward_blocks(
        blocks // unroll,
        unroll,
        lambda g, u: mats[g * unroll + u],
        lambda g, u: ahead[g * unroll + u],
        lambda g, u: ahead[blocks + g * unroll + u],
        wide,
        acc,
        days,
        minutes,
    )
    for p, out in enumerate(outs):
        out[...] = acc[p * links : (p + 1) * links]


def local_views(path, link, lag, mats, unroll, row_step):
    return (
        lambda g, u: mats[g * unroll + u],
        lambda g, u: path[g * unroll + u] * row_step + HALO - lag[g * unroll + u],
        lambda g, u: link[g * unroll + u],
    )


def forward_local_kernel(
    days, cap, order, group, me, slot, path, link, lag, flows, before, mats, own, table, wide
):
    minutes, width = flows.shape[1], mats.shape[2]
    stage_flows(group, flows, before, wide, days, width)
    own[...] = jnp.zeros_like(own)
    unroll = step_of(mats.shape[0])
    views = local_views(path, link, lag, mats, unroll, days * (HALO + minutes))
    forward_blocks(mats.shape[0] // unroll, unroll, *views, wide, own, days, minutes)
    fill_table(cap, order, me, slot, table)


def residual_of(days, totals, counts, b, d):
    width, minutes = totals.shape[2], counts.shape[1]
    seen = counts[d, :, b * width : (b + 1) * width]
    weight = seen + 1.0
    return (totals[b, d * minutes : (d + 1) * minutes, :] - seen) / weight, weight


def signal_kernel(days, totals, counts, signal):
    minutes = counts.shape[1]
    for b in range(totals.shape[0]):
        for d in range(days):
            res, weight = residual_of(days, totals, counts, b, d)
            signal[b, d * minutes : (d + 1) * minutes, :] = (res / weight).astype(signal.dtype)


def residual_kernel(days, totals, counts, residual):
    width = totals.shape[2]
    for b in range(totals.shape[0]):
        for d in range(days):
            res, _ = residual_of(days, totals, counts, b, d)
            residual[d, :, b * width : (b + 1) * width] = res


def backward_local_kernel(days, path, link, lag, signal, mats, out):
    minutes = signal.shape[1] // days
    out[...] = jnp.zeros_like(out)
    unroll = step_of(mats.shape[0])
    mat, base, block = local_views(path, link, lag, mats, unroll, days * (HALO + minutes))
    backward_blocks(
        mats.shape[0] // unroll,
        unroll,
        mat,
        base,
        lambda g, u: signal[block(g, u)],
        out,
        days,
        minutes,
    )


def backward_remote_kernel(days, cap, first, end, links, table, ahead, mats, start, *rest):
    count = (end - first) * links
    signals, sources, rest = [], 0, list(rest)
    while sources < count:
        signals.append(rest.pop(0))
        sources += signals[-1].shape[0]
    out, early, everyone = rest[0], rest[1:-1], rest[-1]
    minutes = signals[0].shape[1] // days
    place = first * links
    for part in signals:
        everyone[place : place + part.shape[0]] = part[...]
        place += part.shape[0]
    blank = everyone.shape[0] - 1
    everyone[blank] = jnp.zeros(everyone.shape[1:], everyone.dtype)
    out[...] = start[...]
    span = HALO + minutes
    slots = (end - first) * cap
    unroll = step_of(slots)
    mat, base, block = slot_views(table, ahead, mats, cap, first, unroll, blank)
    backward_blocks(
        slots // unroll,
        unroll,
        mat,
        base,
        lambda g, u: everyone[block(g, u)],
        out,
        days,
        minutes,
    )
    if early:
        for i in range(early[0].shape[0]):
            early[0][i] = out[i * span : i * span + HALO, :]


def finish_kernel(days, groups, group, total, spill, flows, gradient, new_flows):
    minutes = flows.shape[1]
    width = total.shape[1]
    span = HALO + minutes
    real = jnp.where(group[0] < groups - 1, 1.0, 0.0)
    for p in range(flows.shape[2] // width):
        cols = slice(p * width, (p + 1) * width)
        for d in range(days):
            row = (p * days + d) * span + HALO
            own = total[row : row + minutes, :]
            keep = minutes - HALO
            late = own[keep:] + spill[p * days + d] * real
            for rows, grad in ((slice(0, keep), own[:keep]), (slice(keep, minutes), late)):
                gradient[d, rows, cols] = grad
                new_flows[d, rows, cols] = jnp.maximum(
                    flows[d, rows, cols].astype(jnp.float32) - RATE * grad, 0.0
                )


BACKWARD_COST = 500


def weight(nanoseconds):
    return pl.CostEstimate(
        flops=1_000_000 * nanoseconds, transcendentals=0, bytes_accessed=3_000 * nanoseconds
    )


SMEM = pl.BlockSpec(memory_space=pltpu.SMEM)
VMEM = pl.BlockSpec(memory_space=pltpu.VMEM)
HBM = pl.BlockSpec(memory_space=pltpu.HBM)


def kernel_call(body, scalars, arrays, out_shape, scratch=(), cost=None, outs=None):
    return pl.pallas_call(
        body,
        out_shape=out_shape,
        in_specs=[SMEM] * len(scalars) + [VMEM] * len(arrays),
        out_specs=outs or [VMEM] * len(out_shape),
        scratch_shapes=list(scratch),
        compiler_params=pltpu.CompilerParams(vmem_limit_bytes=40 * 1024 * 1024),
        cost_estimate=cost,
    )(*scalars, *arrays)


def per_device_dense(
    flows,
    counts,
    local_blocks,
    local_path,
    local_link,
    local_lag,
    remote_blocks,
    remote_path,
    remote_link,
    remote_lag,
    remote_slot,
):
    days, minutes, path_width = flows.shape
    width = local_blocks.shape[1]
    paths = path_width // width
    links = counts.shape[2] // width
    corridors = lax.axis_size("corr")
    remotes = remote_lag.shape[0]
    cap = (remotes + corridors - 2) // (corridors - 1)
    span = HALO + minutes
    through = list(range(2, corridors, 2))
    order = [s ^ 1 for s in reversed(through)] + [1] + through
    me = lax.axis_index("corr").astype(jnp.int32).reshape(1)
    group = lax.axis_index("tm").astype(jnp.int32).reshape(1)
    groups = lax.axis_size("tm")
    shape = jax.ShapeDtypeStruct
    piece = (links, days * minutes, width)
    wide = pltpu.VMEM((paths * days * span, width), jnp.float32)
    slots_shape = (len(order) * links + 1, days * minutes, width)
    local_index = (local_path, local_link, local_lag)

    before = lax.ppermute(flows, "tm", [(i, (i + 1) % groups) for i in range(groups)])
    fixed = (remote_path, remote_link, remote_lag, remote_slot, remote_blocks)
    ahead, remote_mats = pl.pallas_call(
        functools.partial(prepare_kernel, cap, order, links, CHUNKS, days * span),
        out_shape=[
            shape((2 * remotes,), jnp.int32),
            shape(remote_blocks.shape, remote_blocks.dtype),
        ],
        in_specs=[SMEM] + [HBM] * len(fixed),
        out_specs=[SMEM, VMEM],
        scratch_shapes=[pltpu.SMEM(remote_slot.shape, jnp.int32) for _ in fixed[1:]]
        + [pltpu.SMEM((corridors,), jnp.int32), pltpu.SemaphoreType.DMA((len(fixed) - 1 + CHUNKS,))],
        compiler_params=pltpu.CompilerParams(vmem_limit_bytes=40 * 1024 * 1024),
    )(me, *(pltpu.with_memory_space_constraint(i, pltpu.HBM) for i in fixed))

    def exchanged(part, s):
        return lax.ppermute(part, "corr", [(i, i ^ s) for i in range(corridors)])

    f32 = jnp.float32
    outgoing = kernel_call(
        functools.partial(forward_remote_kernel, days, links),
        (group, ahead),
        (flows, before, remote_mats),
        [shape(piece, f32) for _ in order],
        [wide, pltpu.VMEM((len(order) * links, *piece[1:]), f32)],
    )
    count = len(through)
    crossed = [exchanged(part.astype(WIRE), 1) for part in outgoing[:count]]
    near = exchanged(outgoing[count].astype(WIRE), 1)
    received = []
    for s, kept in reversed(list(zip(through, outgoing[count + 1 :]))):
        met = crossed[order.index(s ^ 1)].astype(f32)
        received.append(exchanged((kept + met).astype(WIRE), s))
    received.append(near)
    own, table = kernel_call(
        functools.partial(forward_local_kernel, days, cap, order),
        (group, me, remote_slot, *local_index),
        (flows, before, local_blocks),
        [shape(piece, f32), shape((len(order) + corridors * cap,), jnp.int32)],
        [wide],
        outs=[VMEM, SMEM],
    )
    totals = functools.reduce(jnp.add, [p.astype(f32) for p in received], own)
    (signal,) = kernel_call(
        functools.partial(signal_kernel, days),
        (),
        (totals, counts),
        [shape(piece, jnp.bfloat16)],
    )
    arrived = {s: exchanged(signal, s) for s in through}
    rows = [shape((paths * days * span, width), f32)]
    (total,) = kernel_call(
        functools.partial(backward_local_kernel, days),
        local_index,
        (signal, local_blocks),
        rows,
    )
    arrived[through[-1]], total = lax.optimization_barrier((arrived[through[-1]], total))
    for s in through[1:]:
        arrived[s ^ 1] = exchanged(arrived[s], 1)
    passed = exchanged(jnp.concatenate([arrived[through[0]], signal], axis=0), 1)
    edge = shape((paths * days, HALO, width), f32)
    for first, end, parts, made in (
        (count + 1, len(order), [arrived[s] for s in through], rows),
        (0, count + 1, [*(arrived[s] for s in order[: count - 1]), passed], [*rows, edge]),
    ):
        total, *early = kernel_call(
            functools.partial(backward_remote_kernel, days, cap, first, end, links),
            (table, ahead),
            (remote_mats, total, *parts),
            made,
            [pltpu.VMEM(slots_shape, jnp.bfloat16)],
            cost=weight(BACKWARD_COST) if first else None,
        )
    spill = lax.ppermute(early[0], "tm", [(i, (i - 1) % groups) for i in range(groups)])
    totals, total = lax.optimization_barrier((totals, total))
    (link_residual,) = kernel_call(
        functools.partial(residual_kernel, days),
        (),
        (totals, counts),
        [shape(counts.shape, f32)],
    )
    gradient, new_flows = kernel_call(
        functools.partial(finish_kernel, days, groups),
        (group,),
        (total, spill, flows),
        [shape(flows.shape, f32)] * 2,
    )
    return (link_residual, gradient, new_flows)


def per_device(*args):
    counts, blocks, lags = args[1], args[2], args[9]
    corridors = lax.axis_size("corr")
    links = counts.shape[2] // blocks.shape[1]
    cap = (lags.shape[0] + corridors - 2) // (corridors - 1)
    if cap >= links and corridors >= 4 and corridors & (corridors - 1) == 0:
        return per_device_dense(*args)
    return per_device_slots(*args)


def solution(mesh):
    placed = (
        P(None, "tm", "corr"),
        P(None, "tm", "corr"),
        P("corr", None, None),
        P("corr"),
        P("corr"),
        P("corr"),
        P("corr", None, None),
        P("corr"),
        P("corr"),
        P("corr"),
        P("corr"),
    )
    return jax.shard_map(
        per_device,
        mesh=mesh,
        in_specs=placed,
        out_specs=(P(None, "tm", "corr"), P(None, "tm", "corr"), P(None, "tm", "corr")),
        check_vma=False,
    )
```

```python
import functools
import jax
import jax.numpy as jnp
from jax import lax
from jax.experimental import pallas as pl
from jax.experimental.pallas import tpu as pltpu
from jax.sharding import PartitionSpec as P

LAGS = 16


HIGH = lax.Precision.HIGHEST
RATE = 0.5


def passed_along(block, axis, distance):
    devices = range(lax.axis_size(axis))
    route = [(i - distance, i) for i in devices if i - distance in devices]
    return lax.ppermute(block, axis, route)


def one_hot(labels, classes, dtype):
    return (labels[:, None] == jnp.arange(classes, dtype=jnp.int32)[None, :]).astype(dtype)


def shift_table(deltas, out_len, in_len, dtype):
    out_pos = jnp.arange(out_len, dtype=jnp.int32)[:, None]
    in_pos = jnp.arange(in_len, dtype=jnp.int32)[None, :]
    return ((in_pos - out_pos)[None, :, :] == deltas[:, None, None]).astype(dtype)


def pick_blocks(cube, hot):
    return jnp.einsum("dsqp,bq->dsbp", cube, hot, preferred_element_type=jnp.float32).astype(
        jnp.bfloat16
    )


def shift_narrow(picked, table):
    return jnp.einsum("dsbp,bts->dtbp", picked, table, preferred_element_type=jnp.float32).astype(
        jnp.bfloat16
    )


def route_partials(local_part, remote_part, local_route, remote_link, slot_hot, link_blocks):
    own = jnp.einsum("dtbl,bk->dtkl", local_part, local_route, precision=HIGH)
    outgoing = jnp.einsum("bdtl,bs->sdtl", remote_part, slot_hot, precision=HIGH)
    slot_int = slot_hot.astype(jnp.int32)
    labels = link_blocks + jnp.sum(slot_int * (remote_link[:, None] - link_blocks), axis=0)
    return (own, outgoing, labels)


def absorb(own, received, got_labels, link_blocks):
    landing = one_hot(got_labels, link_blocks, jnp.float32)
    return own + jnp.einsum("sdtl,sk->dtkl", received, landing, precision=HIGH)


def collect_paths(local_grad, remote_grad, local_paths, remote_paths):
    first_sum = jnp.einsum("dtbp,bq->dtqp", local_grad, local_paths, precision=HIGH)
    return first_sum + jnp.einsum("bdtp,bq->dtqp", remote_grad, remote_paths, precision=HIGH)


def per_device_slots(
    flows,
    counts,
    local_blocks,
    local_path,
    local_link,
    local_lag,
    remote_blocks,
    remote_path,
    remote_link,
    remote_lag,
    remote_slot,
):
    day_count, minutes, path_width = flows.shape
    block_width = local_blocks.shape[1]
    path_blocks = path_width // block_width
    link_blocks = counts.shape[2] // block_width
    lag_span = LAGS - 1
    corridors = lax.axis_size("corr")
    remote_count = remote_lag.shape[0]
    slot_count = corridors * ((remote_count + corridors - 2) // (corridors - 1))
    flow_cube = flows.reshape(day_count, minutes, path_blocks, block_width)
    local_route = one_hot(local_link, link_blocks, jnp.float32)
    slot_hot = one_hot(remote_slot, slot_count, jnp.float32)
    slot_pick = slot_hot.astype(jnp.bfloat16)
    local_path_hot = one_hot(local_path, path_blocks, jnp.bfloat16)
    remote_path_hot = one_hot(remote_path, path_blocks, jnp.bfloat16)
    local_link_hot = one_hot(local_link, link_blocks, jnp.bfloat16)
    local_in = pick_blocks(flow_cube, local_path_hot)
    remote_in = pick_blocks(flow_cube, remote_path_hot)
    local_plain = jnp.einsum(
        "dtbp,blp->dtbl", local_in, local_blocks, preferred_element_type=jnp.float32
    )
    remote_plain = jnp.einsum(
        "dtbp,blp->bdtl", remote_in, remote_blocks, preferred_element_type=jnp.float32
    )
    local_part = jnp.einsum(
        "dsbl,bts->dtbl",
        local_plain,
        shift_table(-local_lag, minutes + lag_span, minutes, jnp.float32),
        precision=HIGH,
    )
    remote_part = jnp.einsum(
        "bdsl,bts->bdtl",
        remote_plain,
        shift_table(-remote_lag, minutes + lag_span, minutes, jnp.float32),
        precision=HIGH,
    )
    own, outgoing, labels = route_partials(
        local_part, remote_part, local_route, remote_link, slot_hot, link_blocks
    )
    received, got_labels = (
        lax.all_to_all(outgoing, "corr", split_axis=0, concat_axis=0, tiled=True),
        lax.all_to_all(labels, "corr", split_axis=0, concat_axis=0, tiled=True),
    )
    extended = absorb(own, received, got_labels, link_blocks)
    spill = passed_along(extended[:, minutes:], "tm", 1)
    totals = extended[:, :minutes] + jnp.pad(
        spill, ((0, 0), (0, minutes - lag_span), (0, 0), (0, 0))
    )
    link_flow = totals.reshape(day_count, minutes, link_blocks * block_width)
    link_residual = (link_flow - counts) / (counts + 1.0)
    signal = (link_residual / (counts + 1.0)).astype(jnp.bfloat16)
    slot_route = one_hot(got_labels, link_blocks, jnp.bfloat16)
    local_paths = one_hot(local_path, path_blocks, jnp.float32)
    remote_paths = one_hot(remote_path, path_blocks, jnp.float32)
    ahead = passed_along(signal[:, :lag_span, :], "tm", -1)
    extended_signal = jnp.concatenate([signal, ahead], axis=1).reshape(
        day_count, minutes + lag_span, link_blocks, block_width
    )
    slot_signal = jnp.einsum(
        "dtkl,sk->sdtl", extended_signal, slot_route, preferred_element_type=jnp.float32
    ).astype(jnp.bfloat16)
    returned = lax.all_to_all(slot_signal, "corr", split_axis=0, concat_axis=0, tiled=True)
    remote_pick = jnp.einsum(
        "sdtl,bs->bdtl", returned, slot_pick, preferred_element_type=jnp.float32
    ).astype(jnp.bfloat16)
    remote_sig = jnp.einsum(
        "bdsl,bts->bdtl",
        remote_pick,
        shift_table(remote_lag, minutes, minutes + lag_span, jnp.bfloat16),
        preferred_element_type=jnp.float32,
    ).astype(jnp.bfloat16)
    local_sig = shift_narrow(
        pick_blocks(extended_signal, local_link_hot),
        shift_table(local_lag, minutes, minutes + lag_span, jnp.bfloat16),
    )
    local_grad = jnp.einsum(
        "dtbl,blp->dtbp", local_sig, local_blocks, preferred_element_type=jnp.float32
    )
    remote_grad = jnp.einsum(
        "bdtl,blp->bdtp", remote_sig, remote_blocks, preferred_element_type=jnp.float32
    )
    grad_cube = collect_paths(local_grad, remote_grad, local_paths, remote_paths)
    gradient = grad_cube.reshape(day_count, minutes, path_width)
    new_flows = jnp.maximum(flows.astype(jnp.float32) - RATE * gradient, 0.0)
    return (link_residual, gradient, new_flows)


HALO = 16
WIRE = jnp.float16
UNROLL = 32
CHUNKS = 8


def step_of(count):
    return next(u for u in range(min(count, UNROLL), 0, -1) if count % u == 0)


def stage_flows(group, flows_ref, before_ref, wide, days, width):
    real = jnp.where(group[0] > 0, 1.0, 0.0)
    minutes = flows_ref.shape[1]
    span = HALO + minutes
    for p in range(flows_ref.shape[2] // width):
        cols = slice(p * width, (p + 1) * width)
        for d in range(days):
            row = (p * days + d) * span
            before = before_ref[d, :, cols].astype(jnp.float32)
            wide[row : row + HALO, :] = before[minutes - HALO :] * real
            wide[row + HALO : row + span, :] = flows_ref[d, :, cols].astype(jnp.float32)


def forward_blocks(groups, unroll, mat, base, target, wide, acc, days, minutes):
    span = HALO + minutes

    def group(g, carry):
        parts = []
        for u in range(unroll):
            rows = [wide[pl.ds(base(g, u) + d * span, minutes), :] for d in range(days)]
            taken = jnp.concatenate(rows, axis=0).astype(jnp.bfloat16)
            parts.append(
                lax.dot_general(
                    taken,
                    mat(g, u),
                    (((1,), (1,)), ((), ())),
                    preferred_element_type=jnp.float32,
                )
            )
        for u in range(unroll):
            acc[target(g, u)] += parts[u]
        return carry

    lax.fori_loop(0, groups, group, 0)


def backward_blocks(groups, unroll, mat, base, signal, acc, days, minutes):
    span = HALO + minutes

    def group(g, carry):
        parts = [
            jnp.dot(signal(g, u), mat(g, u), preferred_element_type=jnp.float32)
            for u in range(unroll)
        ]
        for u in range(unroll):
            for d in range(days):
                rows = pl.ds(base(g, u) + d * span, minutes)
                acc[rows, :] += parts[u][d * minutes : (d + 1) * minutes]
        return carry

    lax.fori_loop(0, groups, group, 0)


def prepare_kernel(cap, order, links, chunks, row_step, me, *rest):
    sources, (ahead, mats_out, path, link, lag, slot, place, sems) = rest[:5], rest[5:]
    blocks = slot.shape[0]
    pairs = list(zip(sources[:4], (path, link, lag, slot)))
    step = blocks // chunks
    for c in range(chunks):
        rows = slice(c * step, blocks if c == chunks - 1 else (c + 1) * step)
        pairs.append((sources[4].at[rows], mats_out.at[rows]))
    copies = [pltpu.make_async_copy(a, b, sems.at[i]) for i, (a, b) in enumerate(pairs)]
    for copy in copies:
        copy.start()
    place[0] = 0
    for p, s in enumerate(order):
        place[s] = p * links
    for copy in copies[:4]:
        copy.wait()

    def entry(j, carry):
        ahead[j] = path[j] * row_step + HALO - lag[j]
        ahead[blocks + j] = place[lax.div(slot[j], cap) ^ me[0]] + link[j]
        return carry

    lax.fori_loop(0, blocks, entry, 0, unroll=16)
    for copy in copies[4:]:
        copy.wait()


def fill_table(cap, order, me, slot, table):
    first = len(order)
    for p, s in enumerate(order):
        table[p] = first + (me[0] ^ s) * cap
    for i in range((first + 1) * cap):
        table[first + i] = -1

    def entry(j, carry):
        table[first + slot[j]] = j
        return carry

    lax.fori_loop(0, slot.shape[0], entry, 0, unroll=16)


def slot_views(table, ahead, mats, cap, first, unroll, blank):
    def index(g, u):
        at = first * cap + g * unroll + u
        place = lax.div(at, cap)
        return table[table[place] + at - place * cap]

    def mat(g, u):
        return mats[jnp.maximum(index(g, u), 0)]

    def base(g, u):
        return ahead[jnp.maximum(index(g, u), 0)]

    def block(g, u):
        j = index(g, u)
        return jnp.where(j < 0, blank, ahead[mats.shape[0] + jnp.maximum(j, 0)])

    return mat, base, block


def forward_remote_kernel(days, links, group, ahead, flows, before, mats, *rest):
    outs, (wide, acc) = rest[:-2], rest[-2:]
    minutes, width = flows.shape[1], mats.shape[2]
    blocks = mats.shape[0]
    stage_flows(group, flows, before, wide, days, width)
    acc[...] = jnp.zeros_like(acc)
    unroll = step_of(blocks)
    forward_blocks(
        blocks // unroll,
        unroll,
        lambda g, u: mats[g * unroll + u],
        lambda g, u: ahead[g * unroll + u],
        lambda g, u: ahead[blocks + g * unroll + u],
        wide,
        acc,
        days,
        minutes,
    )
    for p, out in enumerate(outs):
        out[...] = acc[p * links : (p + 1) * links]


def local_views(path, link, lag, mats, unroll, row_step):
    return (
        lambda g, u: mats[g * unroll + u],
        lambda g, u: path[g * unroll + u] * row_step + HALO - lag[g * unroll + u],
        lambda g, u: link[g * unroll + u],
    )


def forward_local_kernel(
    days, cap, order, group, me, slot, path, link, lag, flows, before, mats, own, table, wide
):
    minutes, width = flows.shape[1], mats.shape[2]
    stage_flows(group, flows, before, wide, days, width)
    own[...] = jnp.zeros_like(own)
    unroll = step_of(mats.shape[0])
    views = local_views(path, link, lag, mats, unroll, days * (HALO + minutes))
    forward_blocks(mats.shape[0] // unroll, unroll, *views, wide, own, days, minutes)
    fill_table(cap, order, me, slot, table)


def residual_of(days, totals, counts, b, d):
    width, minutes = totals.shape[2], counts.shape[1]
    seen = counts[d, :, b * width : (b + 1) * width]
    weight = seen + 1.0
    return (totals[b, d * minutes : (d + 1) * minutes, :] - seen) / weight, weight


def signal_kernel(days, totals, counts, signal):
    minutes = counts.shape[1]
    for b in range(totals.shape[0]):
        for d in range(days):
            res, weight = residual_of(days, totals, counts, b, d)
            signal[b, d * minutes : (d + 1) * minutes, :] = (res / weight).astype(signal.dtype)


def residual_kernel(days, totals, counts, residual):
    width = totals.shape[2]
    for b in range(totals.shape[0]):
        for d in range(days):
            res, _ = residual_of(days, totals, counts, b, d)
            residual[d, :, b * width : (b + 1) * width] = res


def backward_local_kernel(days, path, link, lag, signal, mats, out):
    minutes = signal.shape[1] // days
    out[...] = jnp.zeros_like(out)
    unroll = step_of(mats.shape[0])
    mat, base, block = local_views(path, link, lag, mats, unroll, days * (HALO + minutes))
    backward_blocks(
        mats.shape[0] // unroll,
        unroll,
        mat,
        base,
        lambda g, u: signal[block(g, u)],
        out,
        days,
        minutes,
    )


def backward_remote_kernel(days, cap, first, end, links, table, ahead, mats, start, *rest):
    count = (end - first) * links
    signals, sources, rest = [], 0, list(rest)
    while sources < count:
        signals.append(rest.pop(0))
        sources += signals[-1].shape[0]
    out, early, everyone = rest[0], rest[1:-1], rest[-1]
    minutes = signals[0].shape[1] // days
    place = first * links
    for part in signals:
        everyone[place : place + links] = part[...]
        place += links
    if first == 0:
        half = links // 2
        everyone[place - links : place - half] = signals[-1][links - half :]
        everyone[place - half : place] = signals[-1][: links - half]
    blank = everyone.shape[0] - 1
    everyone[blank] = jnp.zeros(everyone.shape[1:], everyone.dtype)
    out[...] = start[...]
    span = HALO + minutes
    slots = (end - first) * cap
    unroll = step_of(slots)
    mat, base, block = slot_views(table, ahead, mats, cap, first, unroll, blank)
    backward_blocks(
        slots // unroll,
        unroll,
        mat,
        base,
        lambda g, u: everyone[block(g, u)],
        out,
        days,
        minutes,
    )
    if early:
        for i in range(early[0].shape[0]):
            early[0][i] = out[i * span : i * span + HALO, :]


def finish_kernel(days, groups, group, total, spill, flows, gradient, new_flows):
    minutes = flows.shape[1]
    width = total.shape[1]
    span = HALO + minutes
    real = jnp.where(group[0] < groups - 1, 1.0, 0.0)
    for p in range(flows.shape[2] // width):
        cols = slice(p * width, (p + 1) * width)
        for d in range(days):
            row = (p * days + d) * span + HALO
            own = total[row : row + minutes, :]
            keep = minutes - HALO
            late = own[keep:] + spill[p * days + d] * real
            for rows, grad in ((slice(0, keep), own[:keep]), (slice(keep, minutes), late)):
                gradient[d, rows, cols] = grad
                new_flows[d, rows, cols] = jnp.maximum(
                    flows[d, rows, cols].astype(jnp.float32) - RATE * grad, 0.0
                )


BACKWARD_COST = 500


def weight(nanoseconds):
    return pl.CostEstimate(
        flops=1_000_000 * nanoseconds, transcendentals=0, bytes_accessed=3_000 * nanoseconds
    )


SMEM = pl.BlockSpec(memory_space=pltpu.SMEM)
VMEM = pl.BlockSpec(memory_space=pltpu.VMEM)
HBM = pl.BlockSpec(memory_space=pltpu.HBM)


def kernel_call(body, scalars, arrays, out_shape, scratch=(), cost=None, outs=None):
    return pl.pallas_call(
        body,
        out_shape=out_shape,
        in_specs=[SMEM] * len(scalars) + [VMEM] * len(arrays),
        out_specs=outs or [VMEM] * len(out_shape),
        scratch_shapes=list(scratch),
        compiler_params=pltpu.CompilerParams(vmem_limit_bytes=40 * 1024 * 1024),
        cost_estimate=cost,
    )(*scalars, *arrays)


def per_device_dense(
    flows,
    counts,
    local_blocks,
    local_path,
    local_link,
    local_lag,
    remote_blocks,
    remote_path,
    remote_link,
    remote_lag,
    remote_slot,
):
    days, minutes, path_width = flows.shape
    width = local_blocks.shape[1]
    paths = path_width // width
    links = counts.shape[2] // width
    corridors = lax.axis_size("corr")
    remotes = remote_lag.shape[0]
    cap = (remotes + corridors - 2) // (corridors - 1)
    span = HALO + minutes
    through = list(range(2, corridors, 2))
    order = [s ^ 1 for s in reversed(through)] + [1] + through
    me = lax.axis_index("corr").astype(jnp.int32).reshape(1)
    group = lax.axis_index("tm").astype(jnp.int32).reshape(1)
    groups = lax.axis_size("tm")
    shape = jax.ShapeDtypeStruct
    piece = (links, days * minutes, width)
    wide = pltpu.VMEM((paths * days * span, width), jnp.float32)
    slots_shape = (len(order) * links + 1, days * minutes, width)
    local_index = (local_path, local_link, local_lag)

    before = lax.ppermute(flows, "tm", [(i, (i + 1) % groups) for i in range(groups)])
    fixed = (remote_path, remote_link, remote_lag, remote_slot, remote_blocks)
    ahead, remote_mats = pl.pallas_call(
        functools.partial(prepare_kernel, cap, order, links, CHUNKS, days * span),
        out_shape=[
            shape((2 * remotes,), jnp.int32),
            shape(remote_blocks.shape, remote_blocks.dtype),
        ],
        in_specs=[SMEM] + [HBM] * len(fixed),
        out_specs=[SMEM, VMEM],
        scratch_shapes=[pltpu.SMEM(remote_slot.shape, jnp.int32) for _ in fixed[1:]]
        + [pltpu.SMEM((corridors,), jnp.int32), pltpu.SemaphoreType.DMA((len(fixed) - 1 + CHUNKS,))],
        compiler_params=pltpu.CompilerParams(vmem_limit_bytes=40 * 1024 * 1024),
    )(me, *(pltpu.with_memory_space_constraint(i, pltpu.HBM) for i in fixed))

    def exchanged(part, s):
        return lax.ppermute(part, "corr", [(i, i ^ s) for i in range(corridors)])

    f32 = jnp.float32
    outgoing = kernel_call(
        functools.partial(forward_remote_kernel, days, links),
        (group, ahead),
        (flows, before, remote_mats),
        [shape(piece, f32) for _ in order],
        [wide, pltpu.VMEM((len(order) * links, *piece[1:]), f32)],
    )
    count = len(through)
    crossed = [exchanged(part.astype(WIRE), 1) for part in outgoing[:count]]
    near = exchanged(outgoing[count].astype(WIRE), 1)
    received = []
    for s, kept in reversed(list(zip(through, outgoing[count + 1 :]))):
        met = crossed[order.index(s ^ 1)].astype(f32)
        received.append(exchanged((kept + met).astype(WIRE), s))
    received.append(near)
    own, table = kernel_call(
        functools.partial(forward_local_kernel, days, cap, order),
        (group, me, remote_slot, *local_index),
        (flows, before, local_blocks),
        [shape(piece, f32), shape((len(order) + corridors * cap,), jnp.int32)],
        [wide],
        outs=[VMEM, SMEM],
    )
    totals = functools.reduce(jnp.add, [p.astype(f32) for p in received], own)
    (signal,) = kernel_call(
        functools.partial(signal_kernel, days),
        (),
        (totals, counts),
        [shape(piece, jnp.bfloat16)],
    )
    arrived = {s: exchanged(signal, s) for s in (*through, 1)}
    half = links // 2
    first = arrived[through[0]]
    turned = jnp.concatenate([first[half:], first[:half]], axis=0)
    passed = exchanged(turned, 1)
    rows = [shape((paths * days * span, width), f32)]
    (total,) = kernel_call(
        functools.partial(backward_local_kernel, days),
        local_index,
        (signal, local_blocks),
        rows,
    )
    for s in through[1:]:
        arrived[s ^ 1] = exchanged(arrived[s], 1)
    edge = shape((paths * days, HALO, width), f32)
    for first, end, parts, made in (
        (count, len(order), [arrived[s] for s in (1, *through)], rows),
        (0, count, [*(arrived[s] for s in order[: count - 1]), passed], [*rows, edge]),
    ):
        total, *early = kernel_call(
            functools.partial(backward_remote_kernel, days, cap, first, end, links),
            (table, ahead),
            (remote_mats, total, *parts),
            made,
            [pltpu.VMEM(slots_shape, jnp.bfloat16)],
            cost=weight(BACKWARD_COST) if first else None,
        )
    spill = lax.ppermute(early[0], "tm", [(i, (i - 1) % groups) for i in range(groups)])
    totals, total = lax.optimization_barrier((totals, total))
    (link_residual,) = kernel_call(
        functools.partial(residual_kernel, days),
        (),
        (totals, counts),
        [shape(counts.shape, f32)],
    )
    gradient, new_flows = kernel_call(
        functools.partial(finish_kernel, days, groups),
        (group,),
        (total, spill, flows),
        [shape(flows.shape, f32)] * 2,
    )
    return (link_residual, gradient, new_flows)


def per_device(*args):
    counts, blocks, lags = args[1], args[2], args[9]
    corridors = lax.axis_size("corr")
    links = counts.shape[2] // blocks.shape[1]
    cap = (lags.shape[0] + corridors - 2) // (corridors - 1)
    if cap >= links and corridors >= 4 and corridors & (corridors - 1) == 0:
        return per_device_dense(*args)
    return per_device_slots(*args)


def solution(mesh):
    placed = (
        P(None, "tm", "corr"),
        P(None, "tm", "corr"),
        P("corr", None, None),
        P("corr"),
        P("corr"),
        P("corr"),
        P("corr", None, None),
        P("corr"),
        P("corr"),
        P("corr"),
        P("corr"),
    )
    return jax.shard_map(
        per_device,
        mesh=mesh,
        in_specs=placed,
        out_specs=(P(None, "tm", "corr"), P(None, "tm", "corr"), P(None, "tm", "corr")),
        check_vma=False,
    )
```

```python
import functools
import jax
import jax.numpy as jnp
from jax import lax
from jax.experimental import pallas as pl
from jax.experimental.pallas import tpu as pltpu
from jax.sharding import PartitionSpec as P

LAGS = 16


HIGH = lax.Precision.HIGHEST
RATE = 0.5


def passed_along(block, axis, distance):
    devices = range(lax.axis_size(axis))
    route = [(i - distance, i) for i in devices if i - distance in devices]
    return lax.ppermute(block, axis, route)


def one_hot(labels, classes, dtype):
    return (labels[:, None] == jnp.arange(classes, dtype=jnp.int32)[None, :]).astype(dtype)


def shift_table(deltas, out_len, in_len, dtype):
    out_pos = jnp.arange(out_len, dtype=jnp.int32)[:, None]
    in_pos = jnp.arange(in_len, dtype=jnp.int32)[None, :]
    return ((in_pos - out_pos)[None, :, :] == deltas[:, None, None]).astype(dtype)


def pick_blocks(cube, hot):
    return jnp.einsum("dsqp,bq->dsbp", cube, hot, preferred_element_type=jnp.float32).astype(
        jnp.bfloat16
    )


def shift_narrow(picked, table):
    return jnp.einsum("dsbp,bts->dtbp", picked, table, preferred_element_type=jnp.float32).astype(
        jnp.bfloat16
    )


def route_partials(local_part, remote_part, local_route, remote_link, slot_hot, link_blocks):
    own = jnp.einsum("dtbl,bk->dtkl", local_part, local_route, precision=HIGH)
    outgoing = jnp.einsum("bdtl,bs->sdtl", remote_part, slot_hot, precision=HIGH)
    slot_int = slot_hot.astype(jnp.int32)
    labels = link_blocks + jnp.sum(slot_int * (remote_link[:, None] - link_blocks), axis=0)
    return (own, outgoing, labels)


def absorb(own, received, got_labels, link_blocks):
    landing = one_hot(got_labels, link_blocks, jnp.float32)
    return own + jnp.einsum("sdtl,sk->dtkl", received, landing, precision=HIGH)


def collect_paths(local_grad, remote_grad, local_paths, remote_paths):
    first_sum = jnp.einsum("dtbp,bq->dtqp", local_grad, local_paths, precision=HIGH)
    return first_sum + jnp.einsum("bdtp,bq->dtqp", remote_grad, remote_paths, precision=HIGH)


def per_device_slots(
    flows,
    counts,
    local_blocks,
    local_path,
    local_link,
    local_lag,
    remote_blocks,
    remote_path,
    remote_link,
    remote_lag,
    remote_slot,
):
    day_count, minutes, path_width = flows.shape
    block_width = local_blocks.shape[1]
    path_blocks = path_width // block_width
    link_blocks = counts.shape[2] // block_width
    lag_span = LAGS - 1
    corridors = lax.axis_size("corr")
    remote_count = remote_lag.shape[0]
    slot_count = corridors * ((remote_count + corridors - 2) // (corridors - 1))
    flow_cube = flows.reshape(day_count, minutes, path_blocks, block_width)
    local_route = one_hot(local_link, link_blocks, jnp.float32)
    slot_hot = one_hot(remote_slot, slot_count, jnp.float32)
    slot_pick = slot_hot.astype(jnp.bfloat16)
    local_path_hot = one_hot(local_path, path_blocks, jnp.bfloat16)
    remote_path_hot = one_hot(remote_path, path_blocks, jnp.bfloat16)
    local_link_hot = one_hot(local_link, link_blocks, jnp.bfloat16)
    local_in = pick_blocks(flow_cube, local_path_hot)
    remote_in = pick_blocks(flow_cube, remote_path_hot)
    local_plain = jnp.einsum(
        "dtbp,blp->dtbl", local_in, local_blocks, preferred_element_type=jnp.float32
    )
    remote_plain = jnp.einsum(
        "dtbp,blp->bdtl", remote_in, remote_blocks, preferred_element_type=jnp.float32
    )
    local_part = jnp.einsum(
        "dsbl,bts->dtbl",
        local_plain,
        shift_table(-local_lag, minutes + lag_span, minutes, jnp.float32),
        precision=HIGH,
    )
    remote_part = jnp.einsum(
        "bdsl,bts->bdtl",
        remote_plain,
        shift_table(-remote_lag, minutes + lag_span, minutes, jnp.float32),
        precision=HIGH,
    )
    own, outgoing, labels = route_partials(
        local_part, remote_part, local_route, remote_link, slot_hot, link_blocks
    )
    received, got_labels = (
        lax.all_to_all(outgoing, "corr", split_axis=0, concat_axis=0, tiled=True),
        lax.all_to_all(labels, "corr", split_axis=0, concat_axis=0, tiled=True),
    )
    extended = absorb(own, received, got_labels, link_blocks)
    spill = passed_along(extended[:, minutes:], "tm", 1)
    totals = extended[:, :minutes] + jnp.pad(
        spill, ((0, 0), (0, minutes - lag_span), (0, 0), (0, 0))
    )
    link_flow = totals.reshape(day_count, minutes, link_blocks * block_width)
    link_residual = (link_flow - counts) / (counts + 1.0)
    signal = (link_residual / (counts + 1.0)).astype(jnp.bfloat16)
    slot_route = one_hot(got_labels, link_blocks, jnp.bfloat16)
    local_paths = one_hot(local_path, path_blocks, jnp.float32)
    remote_paths = one_hot(remote_path, path_blocks, jnp.float32)
    ahead = passed_along(signal[:, :lag_span, :], "tm", -1)
    extended_signal = jnp.concatenate([signal, ahead], axis=1).reshape(
        day_count, minutes + lag_span, link_blocks, block_width
    )
    slot_signal = jnp.einsum(
        "dtkl,sk->sdtl", extended_signal, slot_route, preferred_element_type=jnp.float32
    ).astype(jnp.bfloat16)
    returned = lax.all_to_all(slot_signal, "corr", split_axis=0, concat_axis=0, tiled=True)
    remote_pick = jnp.einsum(
        "sdtl,bs->bdtl", returned, slot_pick, preferred_element_type=jnp.float32
    ).astype(jnp.bfloat16)
    remote_sig = jnp.einsum(
        "bdsl,bts->bdtl",
        remote_pick,
        shift_table(remote_lag, minutes, minutes + lag_span, jnp.bfloat16),
        preferred_element_type=jnp.float32,
    ).astype(jnp.bfloat16)
    local_sig = shift_narrow(
        pick_blocks(extended_signal, local_link_hot),
        shift_table(local_lag, minutes, minutes + lag_span, jnp.bfloat16),
    )
    local_grad = jnp.einsum(
        "dtbl,blp->dtbp", local_sig, local_blocks, preferred_element_type=jnp.float32
    )
    remote_grad = jnp.einsum(
        "bdtl,blp->bdtp", remote_sig, remote_blocks, preferred_element_type=jnp.float32
    )
    grad_cube = collect_paths(local_grad, remote_grad, local_paths, remote_paths)
    gradient = grad_cube.reshape(day_count, minutes, path_width)
    new_flows = jnp.maximum(flows.astype(jnp.float32) - RATE * gradient, 0.0)
    return (link_residual, gradient, new_flows)


HALO = 16
WIRE = jnp.float16
UNROLL = 32
CHUNKS = 8


def step_of(count):
    return next(u for u in range(min(count, UNROLL), 0, -1) if count % u == 0)


def stage_flows(group, flows_ref, before_ref, wide, days, width):
    real = jnp.where(group[0] > 0, 1.0, 0.0)
    minutes = flows_ref.shape[1]
    span = HALO + minutes
    for p in range(flows_ref.shape[2] // width):
        cols = slice(p * width, (p + 1) * width)
        for d in range(days):
            row = (p * days + d) * span
            before = before_ref[d, :, cols].astype(jnp.float32)
            wide[row : row + HALO, :] = before[minutes - HALO :] * real
            wide[row + HALO : row + span, :] = flows_ref[d, :, cols].astype(jnp.float32)


def forward_blocks(groups, unroll, mat, base, target, wide, acc, days, minutes):
    span = HALO + minutes

    def group(g, carry):
        parts = []
        for u in range(unroll):
            rows = [wide[pl.ds(base(g, u) + d * span, minutes), :] for d in range(days)]
            taken = jnp.concatenate(rows, axis=0).astype(jnp.bfloat16)
            parts.append(
                lax.dot_general(
                    taken,
                    mat(g, u),
                    (((1,), (1,)), ((), ())),
                    preferred_element_type=jnp.float32,
                )
            )
        for u in range(unroll):
            acc[target(g, u)] += parts[u]
        return carry

    lax.fori_loop(0, groups, group, 0)


def backward_blocks(groups, unroll, mat, base, signal, acc, days, minutes):
    span = HALO + minutes

    def group(g, carry):
        parts = [
            jnp.dot(signal(g, u), mat(g, u), preferred_element_type=jnp.float32)
            for u in range(unroll)
        ]
        for u in range(unroll):
            for d in range(days):
                rows = pl.ds(base(g, u) + d * span, minutes)
                acc[rows, :] += parts[u][d * minutes : (d + 1) * minutes]
        return carry

    lax.fori_loop(0, groups, group, 0)


def prepare_kernel(cap, order, links, chunks, row_step, me, *rest):
    sources, (ahead, mats_out, path, link, lag, slot, place, sems) = rest[:5], rest[5:]
    blocks = slot.shape[0]
    pairs = list(zip(sources[:4], (path, link, lag, slot)))
    step = blocks // chunks
    for c in range(chunks):
        rows = slice(c * step, blocks if c == chunks - 1 else (c + 1) * step)
        pairs.append((sources[4].at[rows], mats_out.at[rows]))
    copies = [pltpu.make_async_copy(a, b, sems.at[i]) for i, (a, b) in enumerate(pairs)]
    for copy in copies:
        copy.start()
    place[0] = 0
    for p, s in enumerate(order):
        place[s] = p * links
    for copy in copies[:4]:
        copy.wait()

    def entry(j, carry):
        ahead[j] = path[j] * row_step + HALO - lag[j]
        ahead[blocks + j] = place[lax.div(slot[j], cap) ^ me[0]] + link[j]
        return carry

    lax.fori_loop(0, blocks, entry, 0, unroll=16)
    for copy in copies[4:]:
        copy.wait()


def fill_table(cap, order, me, slot, table):
    first = len(order)
    for p, s in enumerate(order):
        table[p] = first + (me[0] ^ s) * cap
    for i in range((first + 1) * cap):
        table[first + i] = -1

    def entry(j, carry):
        table[first + slot[j]] = j
        return carry

    lax.fori_loop(0, slot.shape[0], entry, 0, unroll=16)


def slot_views(table, ahead, mats, cap, first, unroll, blank):
    def index(g, u):
        at = first * cap + g * unroll + u
        place = lax.div(at, cap)
        return table[table[place] + at - place * cap]

    def mat(g, u):
        return mats[jnp.maximum(index(g, u), 0)]

    def base(g, u):
        return ahead[jnp.maximum(index(g, u), 0)]

    def block(g, u):
        j = index(g, u)
        return jnp.where(j < 0, blank, ahead[mats.shape[0] + jnp.maximum(j, 0)])

    return mat, base, block


def forward_remote_kernel(days, links, group, ahead, flows, before, mats, *rest):
    outs, (wide, acc) = rest[:-2], rest[-2:]
    minutes, width = flows.shape[1], mats.shape[2]
    blocks = mats.shape[0]
    stage_flows(group, flows, before, wide, days, width)
    acc[...] = jnp.zeros_like(acc)
    unroll = step_of(blocks)
    forward_blocks(
        blocks // unroll,
        unroll,
        lambda g, u: mats[g * unroll + u],
        lambda g, u: ahead[g * unroll + u],
        lambda g, u: ahead[blocks + g * unroll + u],
        wide,
        acc,
        days,
        minutes,
    )
    for p, out in enumerate(outs):
        out[...] = acc[p * links : (p + 1) * links]


def local_views(path, link, lag, mats, unroll, row_step):
    return (
        lambda g, u: mats[g * unroll + u],
        lambda g, u: path[g * unroll + u] * row_step + HALO - lag[g * unroll + u],
        lambda g, u: link[g * unroll + u],
    )


def forward_local_kernel(
    days, cap, order, group, me, slot, path, link, lag, flows, before, mats, own, table, wide
):
    minutes, width = flows.shape[1], mats.shape[2]
    stage_flows(group, flows, before, wide, days, width)
    own[...] = jnp.zeros_like(own)
    unroll = step_of(mats.shape[0])
    views = local_views(path, link, lag, mats, unroll, days * (HALO + minutes))
    forward_blocks(mats.shape[0] // unroll, unroll, *views, wide, own, days, minutes)
    fill_table(cap, order, me, slot, table)


def residual_of(days, totals, counts, b, d):
    width, minutes = totals.shape[2], counts.shape[1]
    seen = counts[d, :, b * width : (b + 1) * width]
    weight = seen + 1.0
    return (totals[b, d * minutes : (d + 1) * minutes, :] - seen) / weight, weight


def signal_kernel(days, totals, counts, signal):
    minutes = counts.shape[1]
    for b in range(totals.shape[0]):
        for d in range(days):
            res, weight = residual_of(days, totals, counts, b, d)
            signal[b, d * minutes : (d + 1) * minutes, :] = (res / weight).astype(signal.dtype)


def residual_kernel(days, totals, counts, residual):
    width = totals.shape[2]
    for b in range(totals.shape[0]):
        for d in range(days):
            res, _ = residual_of(days, totals, counts, b, d)
            residual[d, :, b * width : (b + 1) * width] = res


def backward_local_kernel(days, path, link, lag, signal, mats, out):
    minutes = signal.shape[1] // days
    out[...] = jnp.zeros_like(out)
    unroll = step_of(mats.shape[0])
    mat, base, block = local_views(path, link, lag, mats, unroll, days * (HALO + minutes))
    backward_blocks(
        mats.shape[0] // unroll,
        unroll,
        mat,
        base,
        lambda g, u: signal[block(g, u)],
        out,
        days,
        minutes,
    )


def backward_remote_kernel(days, cap, first, end, links, table, ahead, mats, start, *rest):
    count = (end - first) * links
    signals, sources, rest = [], 0, list(rest)
    while sources < count:
        signals.append(rest.pop(0))
        sources += signals[-1].shape[0]
    out, early, everyone = rest[0], rest[1:-1], rest[-1]
    minutes = signals[0].shape[1] // days
    place = first * links
    for part in signals:
        everyone[place : place + part.shape[0]] = part[...]
        place += part.shape[0]
    blank = everyone.shape[0] - 1
    everyone[blank] = jnp.zeros(everyone.shape[1:], everyone.dtype)
    out[...] = start[...]
    span = HALO + minutes
    slots = (end - first) * cap
    unroll = step_of(slots)
    mat, base, block = slot_views(table, ahead, mats, cap, first, unroll, blank)
    backward_blocks(
        slots // unroll,
        unroll,
        mat,
        base,
        lambda g, u: everyone[block(g, u)],
        out,
        days,
        minutes,
    )
    if early:
        for i in range(early[0].shape[0]):
            early[0][i] = out[i * span : i * span + HALO, :]


def finish_kernel(days, groups, group, total, spill, flows, gradient, new_flows):
    minutes = flows.shape[1]
    width = total.shape[1]
    span = HALO + minutes
    real = jnp.where(group[0] < groups - 1, 1.0, 0.0)
    for p in range(flows.shape[2] // width):
        cols = slice(p * width, (p + 1) * width)
        for d in range(days):
            row = (p * days + d) * span + HALO
            own = total[row : row + minutes, :]
            keep = minutes - HALO
            late = own[keep:] + spill[p * days + d] * real
            for rows, grad in ((slice(0, keep), own[:keep]), (slice(keep, minutes), late)):
                gradient[d, rows, cols] = grad
                new_flows[d, rows, cols] = jnp.maximum(
                    flows[d, rows, cols].astype(jnp.float32) - RATE * grad, 0.0
                )


BACKWARD_COST = 500


def weight(nanoseconds):
    return pl.CostEstimate(
        flops=1_000_000 * nanoseconds, transcendentals=0, bytes_accessed=3_000 * nanoseconds
    )


SMEM = pl.BlockSpec(memory_space=pltpu.SMEM)
VMEM = pl.BlockSpec(memory_space=pltpu.VMEM)
HBM = pl.BlockSpec(memory_space=pltpu.HBM)


def kernel_call(body, scalars, arrays, out_shape, scratch=(), cost=None, outs=None):
    return pl.pallas_call(
        body,
        out_shape=out_shape,
        in_specs=[SMEM] * len(scalars) + [VMEM] * len(arrays),
        out_specs=outs or [VMEM] * len(out_shape),
        scratch_shapes=list(scratch),
        compiler_params=pltpu.CompilerParams(vmem_limit_bytes=40 * 1024 * 1024),
        cost_estimate=cost,
    )(*scalars, *arrays)


def per_device_dense(
    flows,
    counts,
    local_blocks,
    local_path,
    local_link,
    local_lag,
    remote_blocks,
    remote_path,
    remote_link,
    remote_lag,
    remote_slot,
):
    days, minutes, path_width = flows.shape
    width = local_blocks.shape[1]
    paths = path_width // width
    links = counts.shape[2] // width
    corridors = lax.axis_size("corr")
    remotes = remote_lag.shape[0]
    cap = (remotes + corridors - 2) // (corridors - 1)
    span = HALO + minutes
    through = list(range(corridors - 2, 0, -2))
    final = through[len(through) // 2]
    rest = [s for s in through if s != final]
    order = [s ^ 1 for s in (*rest, final)] + [1] + through
    through = through[::-1]
    order[-len(through):] = through
    me = lax.axis_index("corr").astype(jnp.int32).reshape(1)
    group = lax.axis_index("tm").astype(jnp.int32).reshape(1)
    groups = lax.axis_size("tm")
    shape = jax.ShapeDtypeStruct
    piece = (links, days * minutes, width)
    wide = pltpu.VMEM((paths * days * span, width), jnp.float32)
    slots_shape = (len(order) * links + 1, days * minutes, width)
    local_index = (local_path, local_link, local_lag)

    before = lax.ppermute(flows, "tm", [(i, (i + 1) % groups) for i in range(groups)])
    fixed = (remote_path, remote_link, remote_lag, remote_slot, remote_blocks)
    ahead, remote_mats = pl.pallas_call(
        functools.partial(prepare_kernel, cap, order, links, CHUNKS, days * span),
        out_shape=[
            shape((2 * remotes,), jnp.int32),
            shape(remote_blocks.shape, remote_blocks.dtype),
        ],
        in_specs=[SMEM] + [HBM] * len(fixed),
        out_specs=[SMEM, VMEM],
        scratch_shapes=[pltpu.SMEM(remote_slot.shape, jnp.int32) for _ in fixed[1:]]
        + [pltpu.SMEM((corridors,), jnp.int32), pltpu.SemaphoreType.DMA((len(fixed) - 1 + CHUNKS,))],
        compiler_params=pltpu.CompilerParams(vmem_limit_bytes=40 * 1024 * 1024),
    )(me, *(pltpu.with_memory_space_constraint(i, pltpu.HBM) for i in fixed))

    def exchanged(part, s):
        return lax.ppermute(part, "corr", [(i, i ^ s) for i in range(corridors)])

    f32 = jnp.float32
    outgoing = kernel_call(
        functools.partial(forward_remote_kernel, days, links),
        (group, ahead),
        (flows, before, remote_mats),
        [shape(piece, f32) for _ in order],
        [wide, pltpu.VMEM((len(order) * links, *piece[1:]), f32)],
    )
    count = len(through)
    crossed = [exchanged(part.astype(WIRE), 1) for part in outgoing[:count]]
    near = exchanged(outgoing[count].astype(WIRE), 1)
    received = []
    for s, kept in reversed(list(zip(through, outgoing[count + 1 :]))):
        met = crossed[order.index(s ^ 1)].astype(f32)
        received.append(exchanged((kept + met).astype(WIRE), s))
    received.append(near)
    own, table = kernel_call(
        functools.partial(forward_local_kernel, days, cap, order),
        (group, me, remote_slot, *local_index),
        (flows, before, local_blocks),
        [shape(piece, f32), shape((len(order) + corridors * cap,), jnp.int32)],
        [wide],
        outs=[VMEM, SMEM],
    )
    totals = functools.reduce(jnp.add, [p.astype(f32) for p in received], own)
    (signal,) = kernel_call(
        functools.partial(signal_kernel, days),
        (),
        (totals, counts),
        [shape(piece, jnp.bfloat16)],
    )
    arrived = {s: exchanged(signal, s) for s in (*through, 1)}
    rows = [shape((paths * days * span, width), f32)]
    (total,) = kernel_call(
        functools.partial(backward_local_kernel, days),
        local_index,
        (signal, local_blocks),
        rows,
    )
    arrived[through[-1]], total = lax.optimization_barrier((arrived[through[-1]], total))
    for s in through:
        arrived[s ^ 1] = exchanged(arrived[s], 1)
    edge = shape((paths * days, HALO, width), f32)
    for first, end, made in ((count, len(order), rows), (0, count, [*rows, edge])):
        total, *early = kernel_call(
            functools.partial(backward_remote_kernel, days, cap, first, end, links),
            (table, ahead),
            (remote_mats, total, *(arrived[s] for s in order[first:end])),
            made,
            [pltpu.VMEM(slots_shape, jnp.bfloat16)],
            cost=weight(BACKWARD_COST) if first else None,
        )
    spill = lax.ppermute(early[0], "tm", [(i, (i - 1) % groups) for i in range(groups)])
    totals, total = lax.optimization_barrier((totals, total))
    (link_residual,) = kernel_call(
        functools.partial(residual_kernel, days),
        (),
        (totals, counts),
        [shape(counts.shape, f32)],
    )
    gradient, new_flows = kernel_call(
        functools.partial(finish_kernel, days, groups),
        (group,),
        (total, spill, flows),
        [shape(flows.shape, f32)] * 2,
    )
    return (link_residual, gradient, new_flows)


def per_device(*args):
    counts, blocks, lags = args[1], args[2], args[9]
    corridors = lax.axis_size("corr")
    links = counts.shape[2] // blocks.shape[1]
    cap = (lags.shape[0] + corridors - 2) // (corridors - 1)
    if cap >= links and corridors >= 4 and corridors & (corridors - 1) == 0:
        return per_device_dense(*args)
    return per_device_slots(*args)


def solution(mesh):
    placed = (
        P(None, "tm", "corr"),
        P(None, "tm", "corr"),
        P("corr", None, None),
        P("corr"),
        P("corr"),
        P("corr"),
        P("corr", None, None),
        P("corr"),
        P("corr"),
        P("corr"),
        P("corr"),
    )
    return jax.shard_map(
        per_device,
        mesh=mesh,
        in_specs=placed,
        out_specs=(P(None, "tm", "corr"), P(None, "tm", "corr"), P(None, "tm", "corr")),
        check_vma=False,
    )
```

```python
import functools
import jax
import jax.numpy as jnp
from jax import lax
from jax.experimental import pallas as pl
from jax.experimental.pallas import tpu as pltpu
from jax.sharding import PartitionSpec as P

LAGS = 16


HIGH = lax.Precision.HIGHEST
RATE = 0.5


def passed_along(block, axis, distance):
    devices = range(lax.axis_size(axis))
    route = [(i - distance, i) for i in devices if i - distance in devices]
    return lax.ppermute(block, axis, route)


def one_hot(labels, classes, dtype):
    return (labels[:, None] == jnp.arange(classes, dtype=jnp.int32)[None, :]).astype(dtype)


def shift_table(deltas, out_len, in_len, dtype):
    out_pos = jnp.arange(out_len, dtype=jnp.int32)[:, None]
    in_pos = jnp.arange(in_len, dtype=jnp.int32)[None, :]
    return ((in_pos - out_pos)[None, :, :] == deltas[:, None, None]).astype(dtype)


def pick_blocks(cube, hot):
    return jnp.einsum("dsqp,bq->dsbp", cube, hot, preferred_element_type=jnp.float32).astype(
        jnp.bfloat16
    )


def shift_narrow(picked, table):
    return jnp.einsum("dsbp,bts->dtbp", picked, table, preferred_element_type=jnp.float32).astype(
        jnp.bfloat16
    )


def route_partials(local_part, remote_part, local_route, remote_link, slot_hot, link_blocks):
    own = jnp.einsum("dtbl,bk->dtkl", local_part, local_route, precision=HIGH)
    outgoing = jnp.einsum("bdtl,bs->sdtl", remote_part, slot_hot, precision=HIGH)
    slot_int = slot_hot.astype(jnp.int32)
    labels = link_blocks + jnp.sum(slot_int * (remote_link[:, None] - link_blocks), axis=0)
    return (own, outgoing, labels)


def absorb(own, received, got_labels, link_blocks):
    landing = one_hot(got_labels, link_blocks, jnp.float32)
    return own + jnp.einsum("sdtl,sk->dtkl", received, landing, precision=HIGH)


def collect_paths(local_grad, remote_grad, local_paths, remote_paths):
    first_sum = jnp.einsum("dtbp,bq->dtqp", local_grad, local_paths, precision=HIGH)
    return first_sum + jnp.einsum("bdtp,bq->dtqp", remote_grad, remote_paths, precision=HIGH)


def per_device_slots(
    flows,
    counts,
    local_blocks,
    local_path,
    local_link,
    local_lag,
    remote_blocks,
    remote_path,
    remote_link,
    remote_lag,
    remote_slot,
):
    day_count, minutes, path_width = flows.shape
    block_width = local_blocks.shape[1]
    path_blocks = path_width // block_width
    link_blocks = counts.shape[2] // block_width
    lag_span = LAGS - 1
    corridors = lax.axis_size("corr")
    remote_count = remote_lag.shape[0]
    slot_count = corridors * ((remote_count + corridors - 2) // (corridors - 1))
    flow_cube = flows.reshape(day_count, minutes, path_blocks, block_width)
    local_route = one_hot(local_link, link_blocks, jnp.float32)
    slot_hot = one_hot(remote_slot, slot_count, jnp.float32)
    slot_pick = slot_hot.astype(jnp.bfloat16)
    local_path_hot = one_hot(local_path, path_blocks, jnp.bfloat16)
    remote_path_hot = one_hot(remote_path, path_blocks, jnp.bfloat16)
    local_link_hot = one_hot(local_link, link_blocks, jnp.bfloat16)
    local_in = pick_blocks(flow_cube, local_path_hot)
    remote_in = pick_blocks(flow_cube, remote_path_hot)
    local_plain = jnp.einsum(
        "dtbp,blp->dtbl", local_in, local_blocks, preferred_element_type=jnp.float32
    )
    remote_plain = jnp.einsum(
        "dtbp,blp->bdtl", remote_in, remote_blocks, preferred_element_type=jnp.float32
    )
    local_part = jnp.einsum(
        "dsbl,bts->dtbl",
        local_plain,
        shift_table(-local_lag, minutes + lag_span, minutes, jnp.float32),
        precision=HIGH,
    )
    remote_part = jnp.einsum(
        "bdsl,bts->bdtl",
        remote_plain,
        shift_table(-remote_lag, minutes + lag_span, minutes, jnp.float32),
        precision=HIGH,
    )
    own, outgoing, labels = route_partials(
        local_part, remote_part, local_route, remote_link, slot_hot, link_blocks
    )
    received, got_labels = (
        lax.all_to_all(outgoing, "corr", split_axis=0, concat_axis=0, tiled=True),
        lax.all_to_all(labels, "corr", split_axis=0, concat_axis=0, tiled=True),
    )
    extended = absorb(own, received, got_labels, link_blocks)
    spill = passed_along(extended[:, minutes:], "tm", 1)
    totals = extended[:, :minutes] + jnp.pad(
        spill, ((0, 0), (0, minutes - lag_span), (0, 0), (0, 0))
    )
    link_flow = totals.reshape(day_count, minutes, link_blocks * block_width)
    link_residual = (link_flow - counts) / (counts + 1.0)
    signal = (link_residual / (counts + 1.0)).astype(jnp.bfloat16)
    slot_route = one_hot(got_labels, link_blocks, jnp.bfloat16)
    local_paths = one_hot(local_path, path_blocks, jnp.float32)
    remote_paths = one_hot(remote_path, path_blocks, jnp.float32)
    ahead = passed_along(signal[:, :lag_span, :], "tm", -1)
    extended_signal = jnp.concatenate([signal, ahead], axis=1).reshape(
        day_count, minutes + lag_span, link_blocks, block_width
    )
    slot_signal = jnp.einsum(
        "dtkl,sk->sdtl", extended_signal, slot_route, preferred_element_type=jnp.float32
    ).astype(jnp.bfloat16)
    returned = lax.all_to_all(slot_signal, "corr", split_axis=0, concat_axis=0, tiled=True)
    remote_pick = jnp.einsum(
        "sdtl,bs->bdtl", returned, slot_pick, preferred_element_type=jnp.float32
    ).astype(jnp.bfloat16)
    remote_sig = jnp.einsum(
        "bdsl,bts->bdtl",
        remote_pick,
        shift_table(remote_lag, minutes, minutes + lag_span, jnp.bfloat16),
        preferred_element_type=jnp.float32,
    ).astype(jnp.bfloat16)
    local_sig = shift_narrow(
        pick_blocks(extended_signal, local_link_hot),
        shift_table(local_lag, minutes, minutes + lag_span, jnp.bfloat16),
    )
    local_grad = jnp.einsum(
        "dtbl,blp->dtbp", local_sig, local_blocks, preferred_element_type=jnp.float32
    )
    remote_grad = jnp.einsum(
        "bdtl,blp->bdtp", remote_sig, remote_blocks, preferred_element_type=jnp.float32
    )
    grad_cube = collect_paths(local_grad, remote_grad, local_paths, remote_paths)
    gradient = grad_cube.reshape(day_count, minutes, path_width)
    new_flows = jnp.maximum(flows.astype(jnp.float32) - RATE * gradient, 0.0)
    return (link_residual, gradient, new_flows)


HALO = 16
WIRE = jnp.float16
UNROLL = 32
CHUNKS = 8


def step_of(count):
    return next(u for u in range(min(count, UNROLL), 0, -1) if count % u == 0)


def stage_flows(group, flows_ref, before_ref, wide, days, width):
    real = jnp.where(group[0] > 0, 1.0, 0.0)
    minutes = flows_ref.shape[1]
    span = HALO + minutes
    for p in range(flows_ref.shape[2] // width):
        cols = slice(p * width, (p + 1) * width)
        for d in range(days):
            row = (p * days + d) * span
            before = before_ref[d, :, cols].astype(jnp.float32)
            wide[row : row + HALO, :] = before[minutes - HALO :] * real
            wide[row + HALO : row + span, :] = flows_ref[d, :, cols].astype(jnp.float32)


def forward_blocks(groups, unroll, mat, base, target, wide, acc, days, minutes):
    span = HALO + minutes

    def group(g, carry):
        parts = []
        for u in range(unroll):
            rows = [wide[pl.ds(base(g, u) + d * span, minutes), :] for d in range(days)]
            taken = jnp.concatenate(rows, axis=0).astype(jnp.bfloat16)
            parts.append(
                lax.dot_general(
                    taken,
                    mat(g, u),
                    (((1,), (1,)), ((), ())),
                    preferred_element_type=jnp.float32,
                )
            )
        for u in range(unroll):
            acc[target(g, u)] += parts[u]
        return carry

    lax.fori_loop(0, groups, group, 0)


def backward_blocks(groups, unroll, mat, base, signal, acc, days, minutes):
    span = HALO + minutes

    def group(g, carry):
        parts = [
            jnp.dot(signal(g, u), mat(g, u), preferred_element_type=jnp.float32)
            for u in range(unroll)
        ]
        for u in range(unroll):
            for d in range(days):
                rows = pl.ds(base(g, u) + d * span, minutes)
                acc[rows, :] += parts[u][d * minutes : (d + 1) * minutes]
        return carry

    lax.fori_loop(0, groups, group, 0)


def prepare_kernel(cap, order, links, chunks, row_step, me, *rest):
    sources, (ahead, mats_out, path, link, lag, slot, place, sems) = rest[:5], rest[5:]
    blocks = slot.shape[0]
    pairs = list(zip(sources[:4], (path, link, lag, slot)))
    step = blocks // chunks
    for c in range(chunks):
        rows = slice(c * step, blocks if c == chunks - 1 else (c + 1) * step)
        pairs.append((sources[4].at[rows], mats_out.at[rows]))
    copies = [pltpu.make_async_copy(a, b, sems.at[i]) for i, (a, b) in enumerate(pairs)]
    for copy in copies:
        copy.start()
    place[0] = 0
    for p, s in enumerate(order):
        place[s] = p * links
    for copy in copies[:4]:
        copy.wait()

    def entry(j, carry):
        ahead[j] = path[j] * row_step + HALO - lag[j]
        ahead[blocks + j] = place[lax.div(slot[j], cap) ^ me[0]] + link[j]
        return carry

    lax.fori_loop(0, blocks, entry, 0, unroll=16)
    for copy in copies[4:]:
        copy.wait()


def fill_table(cap, order, me, slot, table):
    first = len(order)
    for p, s in enumerate(order):
        table[p] = first + (me[0] ^ s) * cap
    for i in range((first + 1) * cap):
        table[first + i] = -1

    def entry(j, carry):
        table[first + slot[j]] = j
        return carry

    lax.fori_loop(0, slot.shape[0], entry, 0, unroll=16)


def slot_views(table, ahead, mats, cap, first, unroll, blank):
    def index(g, u):
        at = first * cap + g * unroll + u
        place = lax.div(at, cap)
        return table[table[place] + at - place * cap]

    def mat(g, u):
        return mats[jnp.maximum(index(g, u), 0)]

    def base(g, u):
        return ahead[jnp.maximum(index(g, u), 0)]

    def block(g, u):
        j = index(g, u)
        return jnp.where(j < 0, blank, ahead[mats.shape[0] + jnp.maximum(j, 0)])

    return mat, base, block


def forward_remote_kernel(days, links, group, ahead, flows, before, mats, *rest):
    outs, (wide, acc) = rest[:-2], rest[-2:]
    minutes, width = flows.shape[1], mats.shape[2]
    blocks = mats.shape[0]
    stage_flows(group, flows, before, wide, days, width)
    acc[...] = jnp.zeros_like(acc)
    unroll = step_of(blocks)
    forward_blocks(
        blocks // unroll,
        unroll,
        lambda g, u: mats[g * unroll + u],
        lambda g, u: ahead[g * unroll + u],
        lambda g, u: ahead[blocks + g * unroll + u],
        wide,
        acc,
        days,
        minutes,
    )
    for p, out in enumerate(outs):
        out[...] = acc[p * links : (p + 1) * links]


def local_views(path, link, lag, mats, unroll, row_step):
    return (
        lambda g, u: mats[g * unroll + u],
        lambda g, u: path[g * unroll + u] * row_step + HALO - lag[g * unroll + u],
        lambda g, u: link[g * unroll + u],
    )


def forward_local_kernel(
    days, cap, order, group, me, slot, path, link, lag, flows, before, mats, own, table, wide
):
    minutes, width = flows.shape[1], mats.shape[2]
    stage_flows(group, flows, before, wide, days, width)
    own[...] = jnp.zeros_like(own)
    unroll = step_of(mats.shape[0])
    views = local_views(path, link, lag, mats, unroll, days * (HALO + minutes))
    forward_blocks(mats.shape[0] // unroll, unroll, *views, wide, own, days, minutes)
    fill_table(cap, order, me, slot, table)


def residual_of(days, totals, counts, b, d):
    width, minutes = totals.shape[2], counts.shape[1]
    seen = counts[d, :, b * width : (b + 1) * width]
    weight = seen + 1.0
    return (totals[b, d * minutes : (d + 1) * minutes, :] - seen) / weight, weight


def signal_kernel(days, totals, counts, signal):
    minutes = counts.shape[1]
    for b in range(totals.shape[0]):
        for d in range(days):
            res, weight = residual_of(days, totals, counts, b, d)
            signal[b, d * minutes : (d + 1) * minutes, :] = (res / weight).astype(signal.dtype)


def residual_kernel(days, totals, counts, residual):
    width = totals.shape[2]
    for b in range(totals.shape[0]):
        for d in range(days):
            res, _ = residual_of(days, totals, counts, b, d)
            residual[d, :, b * width : (b + 1) * width] = res


def backward_local_kernel(days, path, link, lag, signal, mats, out):
    minutes = signal.shape[1] // days
    out[...] = jnp.zeros_like(out)
    unroll = step_of(mats.shape[0])
    mat, base, block = local_views(path, link, lag, mats, unroll, days * (HALO + minutes))
    backward_blocks(
        mats.shape[0] // unroll,
        unroll,
        mat,
        base,
        lambda g, u: signal[block(g, u)],
        out,
        days,
        minutes,
    )


def backward_remote_kernel(days, cap, first, end, links, table, ahead, mats, start, *rest):
    count = (end - first) * links
    signals, sources, rest = [], 0, list(rest)
    while sources < count:
        signals.append(rest.pop(0))
        sources += signals[-1].shape[0]
    out, early, everyone = rest[0], rest[1:-1], rest[-1]
    minutes = signals[0].shape[1] // days
    place = first * links
    for part in signals:
        everyone[place : place + part.shape[0]] = part[...]
        place += part.shape[0]
    blank = everyone.shape[0] - 1
    everyone[blank] = jnp.zeros(everyone.shape[1:], everyone.dtype)
    out[...] = start[...]
    span = HALO + minutes
    slots = (end - first) * cap
    unroll = step_of(slots)
    mat, base, block = slot_views(table, ahead, mats, cap, first, unroll, blank)
    backward_blocks(
        slots // unroll,
        unroll,
        mat,
        base,
        lambda g, u: everyone[block(g, u)],
        out,
        days,
        minutes,
    )
    if early:
        for i in range(early[0].shape[0]):
            early[0][i] = out[i * span : i * span + HALO, :]


def finish_kernel(days, groups, group, total, spill, flows, gradient, new_flows):
    minutes = flows.shape[1]
    width = total.shape[1]
    span = HALO + minutes
    real = jnp.where(group[0] < groups - 1, 1.0, 0.0)
    for p in range(flows.shape[2] // width):
        cols = slice(p * width, (p + 1) * width)
        for d in range(days):
            row = (p * days + d) * span + HALO
            own = total[row : row + minutes, :]
            keep = minutes - HALO
            late = own[keep:] + spill[p * days + d] * real
            for rows, grad in ((slice(0, keep), own[:keep]), (slice(keep, minutes), late)):
                gradient[d, rows, cols] = grad
                new_flows[d, rows, cols] = jnp.maximum(
                    flows[d, rows, cols].astype(jnp.float32) - RATE * grad, 0.0
                )


BACKWARD_COST = 500


def weight(nanoseconds):
    return pl.CostEstimate(
        flops=1_000_000 * nanoseconds, transcendentals=0, bytes_accessed=3_000 * nanoseconds
    )


SMEM = pl.BlockSpec(memory_space=pltpu.SMEM)
VMEM = pl.BlockSpec(memory_space=pltpu.VMEM)
HBM = pl.BlockSpec(memory_space=pltpu.HBM)


def kernel_call(body, scalars, arrays, out_shape, scratch=(), cost=None, outs=None):
    return pl.pallas_call(
        body,
        out_shape=out_shape,
        in_specs=[SMEM] * len(scalars) + [VMEM] * len(arrays),
        out_specs=outs or [VMEM] * len(out_shape),
        scratch_shapes=list(scratch),
        compiler_params=pltpu.CompilerParams(vmem_limit_bytes=40 * 1024 * 1024),
        cost_estimate=cost,
    )(*scalars, *arrays)


def per_device_dense(
    flows,
    counts,
    local_blocks,
    local_path,
    local_link,
    local_lag,
    remote_blocks,
    remote_path,
    remote_link,
    remote_lag,
    remote_slot,
):
    days, minutes, path_width = flows.shape
    width = local_blocks.shape[1]
    paths = path_width // width
    links = counts.shape[2] // width
    corridors = lax.axis_size("corr")
    remotes = remote_lag.shape[0]
    cap = (remotes + corridors - 2) // (corridors - 1)
    span = HALO + minutes
    through = list(range(corridors - 2, 0, -2))
    final = through[len(through) // 2]
    rest = [s for s in through if s != final]
    order = [s ^ 1 for s in (*rest, final)] + [1] + through
    through = through[::-1]
    order[-len(through):] = through
    me = lax.axis_index("corr").astype(jnp.int32).reshape(1)
    group = lax.axis_index("tm").astype(jnp.int32).reshape(1)
    groups = lax.axis_size("tm")
    shape = jax.ShapeDtypeStruct
    piece = (links, days * minutes, width)
    wide = pltpu.VMEM((paths * days * span, width), jnp.float32)
    slots_shape = (len(order) * links + 1, days * minutes, width)
    local_index = (local_path, local_link, local_lag)

    before = lax.ppermute(flows, "tm", [(i, (i + 1) % groups) for i in range(groups)])
    fixed = (remote_path, remote_link, remote_lag, remote_slot, remote_blocks)
    ahead, remote_mats = pl.pallas_call(
        functools.partial(prepare_kernel, cap, order, links, CHUNKS, days * span),
        out_shape=[
            shape((2 * remotes,), jnp.int32),
            shape(remote_blocks.shape, remote_blocks.dtype),
        ],
        in_specs=[SMEM] + [HBM] * len(fixed),
        out_specs=[SMEM, VMEM],
        scratch_shapes=[pltpu.SMEM(remote_slot.shape, jnp.int32) for _ in fixed[1:]]
        + [pltpu.SMEM((corridors,), jnp.int32), pltpu.SemaphoreType.DMA((len(fixed) - 1 + CHUNKS,))],
        compiler_params=pltpu.CompilerParams(vmem_limit_bytes=40 * 1024 * 1024),
    )(me, *(pltpu.with_memory_space_constraint(i, pltpu.HBM) for i in fixed))

    def exchanged(part, s):
        return lax.ppermute(part, "corr", [(i, i ^ s) for i in range(corridors)])

    f32 = jnp.float32
    outgoing = kernel_call(
        functools.partial(forward_remote_kernel, days, links),
        (group, ahead),
        (flows, before, remote_mats),
        [shape(piece, f32) for _ in order],
        [wide, pltpu.VMEM((len(order) * links, *piece[1:]), f32)],
    )
    count = len(through)
    waves = [part.astype(WIRE) for part in outgoing[: count + 1]]
    lead = exchanged(waves[0], 1)
    held = [i for i in range(1, count + 1) if order[i] != final ^ 1]
    lead, *late = lax.optimization_barrier((lead, *(waves[i] for i in held)))
    for i, wave in zip(held, late):
        waves[i] = wave
    crossed = [lead, *(exchanged(wave, 1) for wave in waves[1:count])]
    near = exchanged(waves[count], 1)
    received = []
    for s, kept in reversed(list(zip(through, outgoing[count + 1 :]))):
        met = crossed[order.index(s ^ 1)].astype(f32)
        received.append(exchanged((kept + met).astype(WIRE), s))
    received.append(near)
    own, table = kernel_call(
        functools.partial(forward_local_kernel, days, cap, order),
        (group, me, remote_slot, *local_index),
        (flows, before, local_blocks),
        [shape(piece, f32), shape((len(order) + corridors * cap,), jnp.int32)],
        [wide],
        outs=[VMEM, SMEM],
    )
    totals = functools.reduce(jnp.add, [p.astype(f32) for p in received], own)
    (signal,) = kernel_call(
        functools.partial(signal_kernel, days),
        (),
        (totals, counts),
        [shape(piece, jnp.bfloat16)],
    )
    arrived = {s: exchanged(signal, s) for s in (*through, 1)}
    rows = [shape((paths * days * span, width), f32)]
    (total,) = kernel_call(
        functools.partial(backward_local_kernel, days),
        local_index,
        (signal, local_blocks),
        rows,
    )
    arrived[through[-1]], total = lax.optimization_barrier((arrived[through[-1]], total))
    for s in through:
        arrived[s ^ 1] = exchanged(arrived[s], 1)
    edge = shape((paths * days, HALO, width), f32)
    for first, end, made in ((count, len(order), rows), (0, count, [*rows, edge])):
        total, *early = kernel_call(
            functools.partial(backward_remote_kernel, days, cap, first, end, links),
            (table, ahead),
            (remote_mats, total, *(arrived[s] for s in order[first:end])),
            made,
            [pltpu.VMEM(slots_shape, jnp.bfloat16)],
            cost=weight(BACKWARD_COST) if first else None,
        )
    spill = lax.ppermute(early[0], "tm", [(i, (i - 1) % groups) for i in range(groups)])
    totals, total = lax.optimization_barrier((totals, total))
    (link_residual,) = kernel_call(
        functools.partial(residual_kernel, days),
        (),
        (totals, counts),
        [shape(counts.shape, f32)],
    )
    gradient, new_flows = kernel_call(
        functools.partial(finish_kernel, days, groups),
        (group,),
        (total, spill, flows),
        [shape(flows.shape, f32)] * 2,
    )
    return (link_residual, gradient, new_flows)


def per_device(*args):
    counts, blocks, lags = args[1], args[2], args[9]
    corridors = lax.axis_size("corr")
    links = counts.shape[2] // blocks.shape[1]
    cap = (lags.shape[0] + corridors - 2) // (corridors - 1)
    if cap >= links and corridors >= 4 and corridors & (corridors - 1) == 0:
        return per_device_dense(*args)
    return per_device_slots(*args)


def solution(mesh):
    placed = (
        P(None, "tm", "corr"),
        P(None, "tm", "corr"),
        P("corr", None, None),
        P("corr"),
        P("corr"),
        P("corr"),
        P("corr", None, None),
        P("corr"),
        P("corr"),
        P("corr"),
        P("corr"),
    )
    return jax.shard_map(
        per_device,
        mesh=mesh,
        in_specs=placed,
        out_specs=(P(None, "tm", "corr"), P(None, "tm", "corr"), P(None, "tm", "corr")),
        check_vma=False,
    )
```

```python
import functools
import jax
import jax.numpy as jnp
from jax import lax
from jax.experimental import pallas as pl
from jax.experimental.pallas import tpu as pltpu
from jax.sharding import PartitionSpec as P

LAGS = 16


HIGH = lax.Precision.HIGHEST
RATE = 0.5


def passed_along(block, axis, distance):
    devices = range(lax.axis_size(axis))
    route = [(i - distance, i) for i in devices if i - distance in devices]
    return lax.ppermute(block, axis, route)


def one_hot(labels, classes, dtype):
    return (labels[:, None] == jnp.arange(classes, dtype=jnp.int32)[None, :]).astype(dtype)


def shift_table(deltas, out_len, in_len, dtype):
    out_pos = jnp.arange(out_len, dtype=jnp.int32)[:, None]
    in_pos = jnp.arange(in_len, dtype=jnp.int32)[None, :]
    return ((in_pos - out_pos)[None, :, :] == deltas[:, None, None]).astype(dtype)


def pick_blocks(cube, hot):
    return jnp.einsum("dsqp,bq->dsbp", cube, hot, preferred_element_type=jnp.float32).astype(
        jnp.bfloat16
    )


def shift_narrow(picked, table):
    return jnp.einsum("dsbp,bts->dtbp", picked, table, preferred_element_type=jnp.float32).astype(
        jnp.bfloat16
    )


def route_partials(local_part, remote_part, local_route, remote_link, slot_hot, link_blocks):
    own = jnp.einsum("dtbl,bk->dtkl", local_part, local_route, precision=HIGH)
    outgoing = jnp.einsum("bdtl,bs->sdtl", remote_part, slot_hot, precision=HIGH)
    slot_int = slot_hot.astype(jnp.int32)
    labels = link_blocks + jnp.sum(slot_int * (remote_link[:, None] - link_blocks), axis=0)
    return (own, outgoing, labels)


def absorb(own, received, got_labels, link_blocks):
    landing = one_hot(got_labels, link_blocks, jnp.float32)
    return own + jnp.einsum("sdtl,sk->dtkl", received, landing, precision=HIGH)


def collect_paths(local_grad, remote_grad, local_paths, remote_paths):
    first_sum = jnp.einsum("dtbp,bq->dtqp", local_grad, local_paths, precision=HIGH)
    return first_sum + jnp.einsum("bdtp,bq->dtqp", remote_grad, remote_paths, precision=HIGH)


def per_device_slots(
    flows,
    counts,
    local_blocks,
    local_path,
    local_link,
    local_lag,
    remote_blocks,
    remote_path,
    remote_link,
    remote_lag,
    remote_slot,
):
    day_count, minutes, path_width = flows.shape
    block_width = local_blocks.shape[1]
    path_blocks = path_width // block_width
    link_blocks = counts.shape[2] // block_width
    lag_span = LAGS - 1
    corridors = lax.axis_size("corr")
    remote_count = remote_lag.shape[0]
    slot_count = corridors * ((remote_count + corridors - 2) // (corridors - 1))
    flow_cube = flows.reshape(day_count, minutes, path_blocks, block_width)
    local_route = one_hot(local_link, link_blocks, jnp.float32)
    slot_hot = one_hot(remote_slot, slot_count, jnp.float32)
    slot_pick = slot_hot.astype(jnp.bfloat16)
    local_path_hot = one_hot(local_path, path_blocks, jnp.bfloat16)
    remote_path_hot = one_hot(remote_path, path_blocks, jnp.bfloat16)
    local_link_hot = one_hot(local_link, link_blocks, jnp.bfloat16)
    local_in = pick_blocks(flow_cube, local_path_hot)
    remote_in = pick_blocks(flow_cube, remote_path_hot)
    local_plain = jnp.einsum(
        "dtbp,blp->dtbl", local_in, local_blocks, preferred_element_type=jnp.float32
    )
    remote_plain = jnp.einsum(
        "dtbp,blp->bdtl", remote_in, remote_blocks, preferred_element_type=jnp.float32
    )
    local_part = jnp.einsum(
        "dsbl,bts->dtbl",
        local_plain,
        shift_table(-local_lag, minutes + lag_span, minutes, jnp.float32),
        precision=HIGH,
    )
    remote_part = jnp.einsum(
        "bdsl,bts->bdtl",
        remote_plain,
        shift_table(-remote_lag, minutes + lag_span, minutes, jnp.float32),
        precision=HIGH,
    )
    own, outgoing, labels = route_partials(
        local_part, remote_part, local_route, remote_link, slot_hot, link_blocks
    )
    received, got_labels = (
        lax.all_to_all(outgoing, "corr", split_axis=0, concat_axis=0, tiled=True),
        lax.all_to_all(labels, "corr", split_axis=0, concat_axis=0, tiled=True),
    )
    extended = absorb(own, received, got_labels, link_blocks)
    spill = passed_along(extended[:, minutes:], "tm", 1)
    totals = extended[:, :minutes] + jnp.pad(
        spill, ((0, 0), (0, minutes - lag_span), (0, 0), (0, 0))
    )
    link_flow = totals.reshape(day_count, minutes, link_blocks * block_width)
    link_residual = (link_flow - counts) / (counts + 1.0)
    signal = (link_residual / (counts + 1.0)).astype(jnp.bfloat16)
    slot_route = one_hot(got_labels, link_blocks, jnp.bfloat16)
    local_paths = one_hot(local_path, path_blocks, jnp.float32)
    remote_paths = one_hot(remote_path, path_blocks, jnp.float32)
    ahead = passed_along(signal[:, :lag_span, :], "tm", -1)
    extended_signal = jnp.concatenate([signal, ahead], axis=1).reshape(
        day_count, minutes + lag_span, link_blocks, block_width
    )
    slot_signal = jnp.einsum(
        "dtkl,sk->sdtl", extended_signal, slot_route, preferred_element_type=jnp.float32
    ).astype(jnp.bfloat16)
    returned = lax.all_to_all(slot_signal, "corr", split_axis=0, concat_axis=0, tiled=True)
    remote_pick = jnp.einsum(
        "sdtl,bs->bdtl", returned, slot_pick, preferred_element_type=jnp.float32
    ).astype(jnp.bfloat16)
    remote_sig = jnp.einsum(
        "bdsl,bts->bdtl",
        remote_pick,
        shift_table(remote_lag, minutes, minutes + lag_span, jnp.bfloat16),
        preferred_element_type=jnp.float32,
    ).astype(jnp.bfloat16)
    local_sig = shift_narrow(
        pick_blocks(extended_signal, local_link_hot),
        shift_table(local_lag, minutes, minutes + lag_span, jnp.bfloat16),
    )
    local_grad = jnp.einsum(
        "dtbl,blp->dtbp", local_sig, local_blocks, preferred_element_type=jnp.float32
    )
    remote_grad = jnp.einsum(
        "bdtl,blp->bdtp", remote_sig, remote_blocks, preferred_element_type=jnp.float32
    )
    grad_cube = collect_paths(local_grad, remote_grad, local_paths, remote_paths)
    gradient = grad_cube.reshape(day_count, minutes, path_width)
    new_flows = jnp.maximum(flows.astype(jnp.float32) - RATE * gradient, 0.0)
    return (link_residual, gradient, new_flows)


HALO = 16
WIRE = jnp.float16
UNROLL = 32
CHUNKS = 8


def step_of(count):
    return next(u for u in range(min(count, UNROLL), 0, -1) if count % u == 0)


def stage_flows(group, flows_ref, before_ref, wide, days, width):
    real = jnp.where(group[0] > 0, 1.0, 0.0)
    minutes = flows_ref.shape[1]
    span = HALO + minutes
    for p in range(flows_ref.shape[2] // width):
        cols = slice(p * width, (p + 1) * width)
        for d in range(days):
            row = (p * days + d) * span
            before = before_ref[d, :, cols].astype(jnp.float32)
            wide[row : row + HALO, :] = before[minutes - HALO :] * real
            wide[row + HALO : row + span, :] = flows_ref[d, :, cols].astype(jnp.float32)


def forward_blocks(groups, unroll, mat, base, target, wide, acc, days, minutes):
    span = HALO + minutes

    def group(g, carry):
        parts = []
        for u in range(unroll):
            rows = [wide[pl.ds(base(g, u) + d * span, minutes), :] for d in range(days)]
            taken = jnp.concatenate(rows, axis=0).astype(jnp.bfloat16)
            parts.append(
                lax.dot_general(
                    taken,
                    mat(g, u),
                    (((1,), (1,)), ((), ())),
                    preferred_element_type=jnp.float32,
                )
            )
        for u in range(unroll):
            acc[target(g, u)] += parts[u]
        return carry

    lax.fori_loop(0, groups, group, 0)


def backward_blocks(groups, unroll, mat, base, signal, acc, days, minutes):
    span = HALO + minutes

    def group(g, carry):
        parts = [
            jnp.dot(signal(g, u), mat(g, u), preferred_element_type=jnp.float32)
            for u in range(unroll)
        ]
        for u in range(unroll):
            for d in range(days):
                rows = pl.ds(base(g, u) + d * span, minutes)
                acc[rows, :] += parts[u][d * minutes : (d + 1) * minutes]
        return carry

    lax.fori_loop(0, groups, group, 0)


def prepare_kernel(cap, order, links, chunks, row_step, me, *rest):
    sources, (ahead, mats_out, path, link, lag, slot, place, sems) = rest[:5], rest[5:]
    blocks = slot.shape[0]
    pairs = list(zip(sources[:4], (path, link, lag, slot)))
    step = blocks // chunks
    for c in range(chunks):
        rows = slice(c * step, blocks if c == chunks - 1 else (c + 1) * step)
        pairs.append((sources[4].at[rows], mats_out.at[rows]))
    copies = [pltpu.make_async_copy(a, b, sems.at[i]) for i, (a, b) in enumerate(pairs)]
    for copy in copies:
        copy.start()
    place[0] = 0
    for p, s in enumerate(order):
        place[s] = p * links
    for copy in copies[:4]:
        copy.wait()

    def entry(j, carry):
        ahead[j] = path[j] * row_step + HALO - lag[j]
        ahead[blocks + j] = place[lax.div(slot[j], cap) ^ me[0]] + link[j]
        return carry

    lax.fori_loop(0, blocks, entry, 0, unroll=16)
    for copy in copies[4:]:
        copy.wait()


def fill_table(cap, order, me, slot, table):
    first = len(order)
    for p, s in enumerate(order):
        table[p] = first + (me[0] ^ s) * cap
    for i in range((first + 1) * cap):
        table[first + i] = -1

    def entry(j, carry):
        table[first + slot[j]] = j
        return carry

    lax.fori_loop(0, slot.shape[0], entry, 0, unroll=16)


def slot_views(table, ahead, mats, cap, first, unroll, blank):
    def index(g, u):
        at = first * cap + g * unroll + u
        place = lax.div(at, cap)
        return table[table[place] + at - place * cap]

    def mat(g, u):
        return mats[jnp.maximum(index(g, u), 0)]

    def base(g, u):
        return ahead[jnp.maximum(index(g, u), 0)]

    def block(g, u):
        j = index(g, u)
        return jnp.where(j < 0, blank, ahead[mats.shape[0] + jnp.maximum(j, 0)])

    return mat, base, block


def forward_remote_kernel(days, links, group, ahead, flows, before, mats, *rest):
    outs, (wide, acc) = rest[:-2], rest[-2:]
    minutes, width = flows.shape[1], mats.shape[2]
    blocks = mats.shape[0]
    stage_flows(group, flows, before, wide, days, width)
    acc[...] = jnp.zeros_like(acc)
    unroll = step_of(blocks)
    forward_blocks(
        blocks // unroll,
        unroll,
        lambda g, u: mats[g * unroll + u],
        lambda g, u: ahead[g * unroll + u],
        lambda g, u: ahead[blocks + g * unroll + u],
        wide,
        acc,
        days,
        minutes,
    )
    for p, out in enumerate(outs):
        out[...] = acc[p * links : (p + 1) * links]


def local_views(path, link, lag, mats, unroll, row_step):
    return (
        lambda g, u: mats[g * unroll + u],
        lambda g, u: path[g * unroll + u] * row_step + HALO - lag[g * unroll + u],
        lambda g, u: link[g * unroll + u],
    )


def forward_local_kernel(
    days, cap, order, group, me, slot, path, link, lag, flows, before, mats, own, table, wide
):
    minutes, width = flows.shape[1], mats.shape[2]
    stage_flows(group, flows, before, wide, days, width)
    own[...] = jnp.zeros_like(own)
    unroll = step_of(mats.shape[0])
    views = local_views(path, link, lag, mats, unroll, days * (HALO + minutes))
    forward_blocks(mats.shape[0] // unroll, unroll, *views, wide, own, days, minutes)
    fill_table(cap, order, me, slot, table)


def residual_of(days, totals, counts, b, d):
    width, minutes = totals.shape[2], counts.shape[1]
    seen = counts[d, :, b * width : (b + 1) * width]
    weight = seen + 1.0
    return (totals[b, d * minutes : (d + 1) * minutes, :] - seen) / weight, weight


def signal_kernel(days, totals, counts, signal):
    minutes = counts.shape[1]
    for b in range(totals.shape[0]):
        for d in range(days):
            res, weight = residual_of(days, totals, counts, b, d)
            signal[b, d * minutes : (d + 1) * minutes, :] = (res / weight).astype(signal.dtype)


def residual_kernel(days, totals, counts, residual):
    width = totals.shape[2]
    for b in range(totals.shape[0]):
        for d in range(days):
            res, _ = residual_of(days, totals, counts, b, d)
            residual[d, :, b * width : (b + 1) * width] = res


def backward_local_kernel(days, path, link, lag, signal, mats, out):
    minutes = signal.shape[1] // days
    out[...] = jnp.zeros_like(out)
    unroll = step_of(mats.shape[0])
    mat, base, block = local_views(path, link, lag, mats, unroll, days * (HALO + minutes))
    backward_blocks(
        mats.shape[0] // unroll,
        unroll,
        mat,
        base,
        lambda g, u: signal[block(g, u)],
        out,
        days,
        minutes,
    )


def backward_remote_kernel(days, cap, first, end, links, table, ahead, mats, start, *rest):
    count = (end - first) * links
    signals, sources, rest = [], 0, list(rest)
    while sources < count:
        signals.append(rest.pop(0))
        sources += signals[-1].shape[0]
    out, early, everyone = rest[0], rest[1:-1], rest[-1]
    minutes = signals[0].shape[1] // days
    place = first * links
    for part in signals:
        everyone[place : place + part.shape[0]] = part[...]
        place += part.shape[0]
    blank = everyone.shape[0] - 1
    everyone[blank] = jnp.zeros(everyone.shape[1:], everyone.dtype)
    out[...] = start[...]
    span = HALO + minutes
    slots = (end - first) * cap
    unroll = step_of(slots)
    mat, base, block = slot_views(table, ahead, mats, cap, first, unroll, blank)
    backward_blocks(
        slots // unroll,
        unroll,
        mat,
        base,
        lambda g, u: everyone[block(g, u)],
        out,
        days,
        minutes,
    )
    if early:
        for i in range(early[0].shape[0]):
            early[0][i] = out[i * span : i * span + HALO, :]


def finish_kernel(days, groups, group, total, spill, flows, gradient, new_flows):
    minutes = flows.shape[1]
    width = total.shape[1]
    span = HALO + minutes
    real = jnp.where(group[0] < groups - 1, 1.0, 0.0)
    for p in range(flows.shape[2] // width):
        cols = slice(p * width, (p + 1) * width)
        for d in range(days):
            row = (p * days + d) * span + HALO
            own = total[row : row + minutes, :]
            keep = minutes - HALO
            late = own[keep:] + spill[p * days + d] * real
            for rows, grad in ((slice(0, keep), own[:keep]), (slice(keep, minutes), late)):
                gradient[d, rows, cols] = grad
                new_flows[d, rows, cols] = jnp.maximum(
                    flows[d, rows, cols].astype(jnp.float32) - RATE * grad, 0.0
                )


BACKWARD_COST = 500


def weight(nanoseconds):
    return pl.CostEstimate(
        flops=1_000_000 * nanoseconds, transcendentals=0, bytes_accessed=3_000 * nanoseconds
    )


SMEM = pl.BlockSpec(memory_space=pltpu.SMEM)
VMEM = pl.BlockSpec(memory_space=pltpu.VMEM)
HBM = pl.BlockSpec(memory_space=pltpu.HBM)


def kernel_call(body, scalars, arrays, out_shape, scratch=(), cost=None, outs=None):
    return pl.pallas_call(
        body,
        out_shape=out_shape,
        in_specs=[SMEM] * len(scalars) + [VMEM] * len(arrays),
        out_specs=outs or [VMEM] * len(out_shape),
        scratch_shapes=list(scratch),
        compiler_params=pltpu.CompilerParams(vmem_limit_bytes=40 * 1024 * 1024),
        cost_estimate=cost,
    )(*scalars, *arrays)


def per_device_dense(
    flows,
    counts,
    local_blocks,
    local_path,
    local_link,
    local_lag,
    remote_blocks,
    remote_path,
    remote_link,
    remote_lag,
    remote_slot,
):
    days, minutes, path_width = flows.shape
    width = local_blocks.shape[1]
    paths = path_width // width
    links = counts.shape[2] // width
    corridors = lax.axis_size("corr")
    remotes = remote_lag.shape[0]
    cap = (remotes + corridors - 2) // (corridors - 1)
    span = HALO + minutes
    through = list(range(2, corridors, 2))
    order = [s ^ 1 for s in reversed(through)] + [1] + through
    me = lax.axis_index("corr").astype(jnp.int32).reshape(1)
    group = lax.axis_index("tm").astype(jnp.int32).reshape(1)
    groups = lax.axis_size("tm")
    shape = jax.ShapeDtypeStruct
    piece = (links, days * minutes, width)
    wide = pltpu.VMEM((paths * days * span, width), jnp.float32)
    slots_shape = (len(order) * links + 1, days * minutes, width)
    local_index = (local_path, local_link, local_lag)

    before = lax.ppermute(flows, "tm", [(i, (i + 1) % groups) for i in range(groups)])
    fixed = (remote_path, remote_link, remote_lag, remote_slot, remote_blocks)
    ahead, remote_mats = pl.pallas_call(
        functools.partial(prepare_kernel, cap, order, links, CHUNKS, days * span),
        out_shape=[
            shape((2 * remotes,), jnp.int32),
            shape(remote_blocks.shape, remote_blocks.dtype),
        ],
        in_specs=[SMEM] + [HBM] * len(fixed),
        out_specs=[SMEM, VMEM],
        scratch_shapes=[pltpu.SMEM(remote_slot.shape, jnp.int32) for _ in fixed[1:]]
        + [pltpu.SMEM((corridors,), jnp.int32), pltpu.SemaphoreType.DMA((len(fixed) - 1 + CHUNKS,))],
        compiler_params=pltpu.CompilerParams(vmem_limit_bytes=40 * 1024 * 1024),
    )(me, *(pltpu.with_memory_space_constraint(i, pltpu.HBM) for i in fixed))

    def exchanged(part, s):
        return lax.ppermute(part, "corr", [(i, i ^ s) for i in range(corridors)])

    f32 = jnp.float32
    outgoing = kernel_call(
        functools.partial(forward_remote_kernel, days, links),
        (group, ahead),
        (flows, before, remote_mats),
        [shape(piece, f32) for _ in order],
        [wide, pltpu.VMEM((len(order) * links, *piece[1:]), f32)],
    )
    count = len(through)
    crossed = [exchanged(part.astype(WIRE), 1) for part in outgoing[:count]]
    near = exchanged(outgoing[count].astype(WIRE), 1)
    received = []
    for s, kept in reversed(list(zip(through, outgoing[count + 1 :]))):
        met = crossed[order.index(s ^ 1)].astype(f32)
        received.append(exchanged((kept + met).astype(WIRE), s))
    received.append(near)
    own, table = kernel_call(
        functools.partial(forward_local_kernel, days, cap, order),
        (group, me, remote_slot, *local_index),
        (flows, before, local_blocks),
        [shape(piece, f32), shape((len(order) + corridors * cap,), jnp.int32)],
        [wide],
        outs=[VMEM, SMEM],
    )
    totals = functools.reduce(jnp.add, [p.astype(f32) for p in received], own)
    (signal,) = kernel_call(
        functools.partial(signal_kernel, days),
        (),
        (totals, counts),
        [shape(piece, jnp.bfloat16)],
    )
    arrived = {s: exchanged(signal, s) for s in through}
    rows = [shape((paths * days * span, width), f32)]
    (total,) = kernel_call(
        functools.partial(backward_local_kernel, days),
        local_index,
        (signal, local_blocks),
        rows,
    )
    arrived[through[-1]], total = lax.optimization_barrier((arrived[through[-1]], total))
    for s in through[1:]:
        arrived[s ^ 1] = exchanged(arrived[s], 1)
    passed = exchanged(jnp.concatenate([arrived[through[0]], signal], axis=0), 1)
    edge = shape((paths * days, HALO, width), f32)
    for first, end, parts, made in (
        (count + 1, len(order), [arrived[s] for s in through], rows),
        (0, count + 1, [*(arrived[s] for s in order[: count - 1]), passed], [*rows, edge]),
    ):
        total, *early = kernel_call(
            functools.partial(backward_remote_kernel, days, cap, first, end, links),
            (table, ahead),
            (remote_mats, total, *parts),
            made,
            [pltpu.VMEM(slots_shape, jnp.bfloat16)],
            cost=weight(BACKWARD_COST) if first else None,
        )
    route = [(i, (i - 1) % groups) for i in range(groups)]
    spill = lax.ppermute(early[0].astype(WIRE), "tm", route).astype(f32)
    totals, total = lax.optimization_barrier((totals, total))
    (link_residual,) = kernel_call(
        functools.partial(residual_kernel, days),
        (),
        (totals, counts),
        [shape(counts.shape, f32)],
    )
    gradient, new_flows = kernel_call(
        functools.partial(finish_kernel, days, groups),
        (group,),
        (total, spill, flows),
        [shape(flows.shape, f32)] * 2,
    )
    return (link_residual, gradient, new_flows)


def per_device(*args):
    counts, blocks, lags = args[1], args[2], args[9]
    corridors = lax.axis_size("corr")
    links = counts.shape[2] // blocks.shape[1]
    cap = (lags.shape[0] + corridors - 2) // (corridors - 1)
    if cap >= links and corridors >= 4 and corridors & (corridors - 1) == 0:
        return per_device_dense(*args)
    return per_device_slots(*args)


def solution(mesh):
    placed = (
        P(None, "tm", "corr"),
        P(None, "tm", "corr"),
        P("corr", None, None),
        P("corr"),
        P("corr"),
        P("corr"),
        P("corr", None, None),
        P("corr"),
        P("corr"),
        P("corr"),
        P("corr"),
    )
    return jax.shard_map(
        per_device,
        mesh=mesh,
        in_specs=placed,
        out_specs=(P(None, "tm", "corr"), P(None, "tm", "corr"), P(None, "tm", "corr")),
        check_vma=False,
    )
```

```python
import functools
import jax
import jax.numpy as jnp
from jax import lax
from jax.experimental import pallas as pl
from jax.experimental.pallas import tpu as pltpu
from jax.sharding import PartitionSpec as P

LAGS = 16


HIGH = lax.Precision.HIGHEST
RATE = 0.5


def passed_along(block, axis, distance):
    devices = range(lax.axis_size(axis))
    route = [(i - distance, i) for i in devices if i - distance in devices]
    return lax.ppermute(block, axis, route)


def one_hot(labels, classes, dtype):
    return (labels[:, None] == jnp.arange(classes, dtype=jnp.int32)[None, :]).astype(dtype)


def shift_table(deltas, out_len, in_len, dtype):
    out_pos = jnp.arange(out_len, dtype=jnp.int32)[:, None]
    in_pos = jnp.arange(in_len, dtype=jnp.int32)[None, :]
    return ((in_pos - out_pos)[None, :, :] == deltas[:, None, None]).astype(dtype)


def pick_blocks(cube, hot):
    return jnp.einsum("dsqp,bq->dsbp", cube, hot, preferred_element_type=jnp.float32).astype(
        jnp.bfloat16
    )


def shift_narrow(picked, table):
    return jnp.einsum("dsbp,bts->dtbp", picked, table, preferred_element_type=jnp.float32).astype(
        jnp.bfloat16
    )


def route_partials(local_part, remote_part, local_route, remote_link, slot_hot, link_blocks):
    own = jnp.einsum("dtbl,bk->dtkl", local_part, local_route, precision=HIGH)
    outgoing = jnp.einsum("bdtl,bs->sdtl", remote_part, slot_hot, precision=HIGH)
    slot_int = slot_hot.astype(jnp.int32)
    labels = link_blocks + jnp.sum(slot_int * (remote_link[:, None] - link_blocks), axis=0)
    return (own, outgoing, labels)


def absorb(own, received, got_labels, link_blocks):
    landing = one_hot(got_labels, link_blocks, jnp.float32)
    return own + jnp.einsum("sdtl,sk->dtkl", received, landing, precision=HIGH)


def collect_paths(local_grad, remote_grad, local_paths, remote_paths):
    first_sum = jnp.einsum("dtbp,bq->dtqp", local_grad, local_paths, precision=HIGH)
    return first_sum + jnp.einsum("bdtp,bq->dtqp", remote_grad, remote_paths, precision=HIGH)


def per_device_slots(
    flows,
    counts,
    local_blocks,
    local_path,
    local_link,
    local_lag,
    remote_blocks,
    remote_path,
    remote_link,
    remote_lag,
    remote_slot,
):
    day_count, minutes, path_width = flows.shape
    block_width = local_blocks.shape[1]
    path_blocks = path_width // block_width
    link_blocks = counts.shape[2] // block_width
    lag_span = LAGS - 1
    corridors = lax.axis_size("corr")
    remote_count = remote_lag.shape[0]
    slot_count = corridors * ((remote_count + corridors - 2) // (corridors - 1))
    flow_cube = flows.reshape(day_count, minutes, path_blocks, block_width)
    local_route = one_hot(local_link, link_blocks, jnp.float32)
    slot_hot = one_hot(remote_slot, slot_count, jnp.float32)
    slot_pick = slot_hot.astype(jnp.bfloat16)
    local_path_hot = one_hot(local_path, path_blocks, jnp.bfloat16)
    remote_path_hot = one_hot(remote_path, path_blocks, jnp.bfloat16)
    local_link_hot = one_hot(local_link, link_blocks, jnp.bfloat16)
    local_in = pick_blocks(flow_cube, local_path_hot)
    remote_in = pick_blocks(flow_cube, remote_path_hot)
    local_plain = jnp.einsum(
        "dtbp,blp->dtbl", local_in, local_blocks, preferred_element_type=jnp.float32
    )
    remote_plain = jnp.einsum(
        "dtbp,blp->bdtl", remote_in, remote_blocks, preferred_element_type=jnp.float32
    )
    local_part = jnp.einsum(
        "dsbl,bts->dtbl",
        local_plain,
        shift_table(-local_lag, minutes + lag_span, minutes, jnp.float32),
        precision=HIGH,
    )
    remote_part = jnp.einsum(
        "bdsl,bts->bdtl",
        remote_plain,
        shift_table(-remote_lag, minutes + lag_span, minutes, jnp.float32),
        precision=HIGH,
    )
    own, outgoing, labels = route_partials(
        local_part, remote_part, local_route, remote_link, slot_hot, link_blocks
    )
    received, got_labels = (
        lax.all_to_all(outgoing, "corr", split_axis=0, concat_axis=0, tiled=True),
        lax.all_to_all(labels, "corr", split_axis=0, concat_axis=0, tiled=True),
    )
    extended = absorb(own, received, got_labels, link_blocks)
    spill = passed_along(extended[:, minutes:], "tm", 1)
    totals = extended[:, :minutes] + jnp.pad(
        spill, ((0, 0), (0, minutes - lag_span), (0, 0), (0, 0))
    )
    link_flow = totals.reshape(day_count, minutes, link_blocks * block_width)
    link_residual = (link_flow - counts) / (counts + 1.0)
    signal = (link_residual / (counts + 1.0)).astype(jnp.bfloat16)
    slot_route = one_hot(got_labels, link_blocks, jnp.bfloat16)
    local_paths = one_hot(local_path, path_blocks, jnp.float32)
    remote_paths = one_hot(remote_path, path_blocks, jnp.float32)
    ahead = passed_along(signal[:, :lag_span, :], "tm", -1)
    extended_signal = jnp.concatenate([signal, ahead], axis=1).reshape(
        day_count, minutes + lag_span, link_blocks, block_width
    )
    slot_signal = jnp.einsum(
        "dtkl,sk->sdtl", extended_signal, slot_route, preferred_element_type=jnp.float32
    ).astype(jnp.bfloat16)
    returned = lax.all_to_all(slot_signal, "corr", split_axis=0, concat_axis=0, tiled=True)
    remote_pick = jnp.einsum(
        "sdtl,bs->bdtl", returned, slot_pick, preferred_element_type=jnp.float32
    ).astype(jnp.bfloat16)
    remote_sig = jnp.einsum(
        "bdsl,bts->bdtl",
        remote_pick,
        shift_table(remote_lag, minutes, minutes + lag_span, jnp.bfloat16),
        preferred_element_type=jnp.float32,
    ).astype(jnp.bfloat16)
    local_sig = shift_narrow(
        pick_blocks(extended_signal, local_link_hot),
        shift_table(local_lag, minutes, minutes + lag_span, jnp.bfloat16),
    )
    local_grad = jnp.einsum(
        "dtbl,blp->dtbp", local_sig, local_blocks, preferred_element_type=jnp.float32
    )
    remote_grad = jnp.einsum(
        "bdtl,blp->bdtp", remote_sig, remote_blocks, preferred_element_type=jnp.float32
    )
    grad_cube = collect_paths(local_grad, remote_grad, local_paths, remote_paths)
    gradient = grad_cube.reshape(day_count, minutes, path_width)
    new_flows = jnp.maximum(flows.astype(jnp.float32) - RATE * gradient, 0.0)
    return (link_residual, gradient, new_flows)


HALO = 16
WIRE = jnp.float16
UNROLL = 64
CHUNKS = 8


def step_of(count):
    return next(u for u in range(min(count, UNROLL), 0, -1) if count % u == 0)


def stage_flows(group, flows_ref, before_ref, wide, days, width):
    real = jnp.where(group[0] > 0, 1.0, 0.0)
    minutes = flows_ref.shape[1]
    span = HALO + minutes
    for p in range(flows_ref.shape[2] // width):
        cols = slice(p * width, (p + 1) * width)
        for d in range(days):
            row = (p * days + d) * span
            before = before_ref[d, :, cols].astype(jnp.float32)
            wide[row : row + HALO, :] = before[minutes - HALO :] * real
            wide[row + HALO : row + span, :] = flows_ref[d, :, cols].astype(jnp.float32)


def forward_blocks(groups, unroll, mat, base, target, wide, acc, days, minutes):
    span = HALO + minutes

    def group(g, carry):
        parts = []
        for u in range(unroll):
            rows = [wide[pl.ds(base(g, u) + d * span, minutes), :] for d in range(days)]
            taken = jnp.concatenate(rows, axis=0).astype(jnp.bfloat16)
            parts.append(
                lax.dot_general(
                    taken,
                    mat(g, u),
                    (((1,), (1,)), ((), ())),
                    preferred_element_type=jnp.float32,
                )
            )
        for u in range(unroll):
            acc[target(g, u)] += parts[u]
        return carry

    lax.fori_loop(0, groups, group, 0)


def backward_blocks(groups, unroll, mat, base, signal, acc, days, minutes):
    span = HALO + minutes

    def group(g, carry):
        parts = [
            jnp.dot(signal(g, u), mat(g, u), preferred_element_type=jnp.float32)
            for u in range(unroll)
        ]
        for u in range(unroll):
            for d in range(days):
                rows = pl.ds(base(g, u) + d * span, minutes)
                acc[rows, :] += parts[u][d * minutes : (d + 1) * minutes]
        return carry

    lax.fori_loop(0, groups, group, 0)


def prepare_kernel(cap, order, links, chunks, row_step, me, *rest):
    sources, (ahead, mats_out, path, link, lag, slot, place, sems) = rest[:5], rest[5:]
    blocks = slot.shape[0]
    pairs = list(zip(sources[:4], (path, link, lag, slot)))
    step = blocks // chunks
    for c in range(chunks):
        rows = slice(c * step, blocks if c == chunks - 1 else (c + 1) * step)
        pairs.append((sources[4].at[rows], mats_out.at[rows]))
    copies = [pltpu.make_async_copy(a, b, sems.at[i]) for i, (a, b) in enumerate(pairs)]
    for copy in copies:
        copy.start()
    place[0] = 0
    for p, s in enumerate(order):
        place[s] = p * links
    for copy in copies[:4]:
        copy.wait()

    def entry(j, carry):
        ahead[j] = path[j] * row_step + HALO - lag[j]
        ahead[blocks + j] = place[lax.div(slot[j], cap) ^ me[0]] + link[j]
        return carry

    lax.fori_loop(0, blocks, entry, 0, unroll=16)
    for copy in copies[4:]:
        copy.wait()


def fill_table(cap, order, me, slot, table):
    first = len(order)
    for p, s in enumerate(order):
        table[p] = first + (me[0] ^ s) * cap
    for i in range((first + 1) * cap):
        table[first + i] = -1

    def entry(j, carry):
        table[first + slot[j]] = j
        return carry

    lax.fori_loop(0, slot.shape[0], entry, 0, unroll=16)


def slot_views(table, ahead, mats, cap, first, unroll, blank):
    def index(g, u):
        at = first * cap + g * unroll + u
        place = lax.div(at, cap)
        return table[table[place] + at - place * cap]

    def mat(g, u):
        return mats[jnp.maximum(index(g, u), 0)]

    def base(g, u):
        return ahead[jnp.maximum(index(g, u), 0)]

    def block(g, u):
        j = index(g, u)
        return jnp.where(j < 0, blank, ahead[mats.shape[0] + jnp.maximum(j, 0)])

    return mat, base, block


def forward_remote_kernel(days, links, group, ahead, flows, before, mats, *rest):
    outs, (wide, acc) = rest[:-2], rest[-2:]
    minutes, width = flows.shape[1], mats.shape[2]
    blocks = mats.shape[0]
    stage_flows(group, flows, before, wide, days, width)
    acc[...] = jnp.zeros_like(acc)
    unroll = step_of(blocks)
    forward_blocks(
        blocks // unroll,
        unroll,
        lambda g, u: mats[g * unroll + u],
        lambda g, u: ahead[g * unroll + u],
        lambda g, u: ahead[blocks + g * unroll + u],
        wide,
        acc,
        days,
        minutes,
    )
    for p, out in enumerate(outs):
        out[...] = acc[p * links : (p + 1) * links]


def local_views(path, link, lag, mats, unroll, row_step):
    return (
        lambda g, u: mats[g * unroll + u],
        lambda g, u: path[g * unroll + u] * row_step + HALO - lag[g * unroll + u],
        lambda g, u: link[g * unroll + u],
    )


def forward_local_kernel(
    days, cap, order, group, me, slot, path, link, lag, flows, before, mats, own, table, wide
):
    minutes, width = flows.shape[1], mats.shape[2]
    stage_flows(group, flows, before, wide, days, width)
    own[...] = jnp.zeros_like(own)
    unroll = step_of(mats.shape[0])
    views = local_views(path, link, lag, mats, unroll, days * (HALO + minutes))
    forward_blocks(mats.shape[0] // unroll, unroll, *views, wide, own, days, minutes)
    fill_table(cap, order, me, slot, table)


def residual_of(days, totals, counts, b, d):
    width, minutes = totals.shape[2], counts.shape[1]
    seen = counts[d, :, b * width : (b + 1) * width]
    weight = seen + 1.0
    return (totals[b, d * minutes : (d + 1) * minutes, :] - seen) / weight, weight


def signal_kernel(days, totals, counts, signal):
    minutes = counts.shape[1]
    for b in range(totals.shape[0]):
        for d in range(days):
            res, weight = residual_of(days, totals, counts, b, d)
            signal[b, d * minutes : (d + 1) * minutes, :] = (res / weight).astype(signal.dtype)


def residual_kernel(days, totals, counts, residual):
    width = totals.shape[2]
    for b in range(totals.shape[0]):
        for d in range(days):
            res, _ = residual_of(days, totals, counts, b, d)
            residual[d, :, b * width : (b + 1) * width] = res


def backward_local_kernel(days, path, link, lag, signal, mats, out):
    minutes = signal.shape[1] // days
    out[...] = jnp.zeros_like(out)
    unroll = step_of(mats.shape[0])
    mat, base, block = local_views(path, link, lag, mats, unroll, days * (HALO + minutes))
    backward_blocks(
        mats.shape[0] // unroll,
        unroll,
        mat,
        base,
        lambda g, u: signal[block(g, u)],
        out,
        days,
        minutes,
    )


def backward_remote_kernel(days, cap, first, end, links, table, ahead, mats, start, *rest):
    count = (end - first) * links
    signals, sources, rest = [], 0, list(rest)
    while sources < count:
        signals.append(rest.pop(0))
        sources += signals[-1].shape[0]
    out, early, everyone = rest[0], rest[1:-1], rest[-1]
    minutes = signals[0].shape[1] // days
    place = first * links
    for part in signals:
        everyone[place : place + part.shape[0]] = part[...]
        place += part.shape[0]
    blank = everyone.shape[0] - 1
    everyone[blank] = jnp.zeros(everyone.shape[1:], everyone.dtype)
    out[...] = start[...]
    span = HALO + minutes
    slots = (end - first) * cap
    unroll = step_of(slots)
    mat, base, block = slot_views(table, ahead, mats, cap, first, unroll, blank)
    backward_blocks(
        slots // unroll,
        unroll,
        mat,
        base,
        lambda g, u: everyone[block(g, u)],
        out,
        days,
        minutes,
    )
    if early:
        for i in range(early[0].shape[0]):
            early[0][i] = out[i * span : i * span + HALO, :]


def finish_kernel(days, groups, group, total, spill, flows, gradient, new_flows):
    minutes = flows.shape[1]
    width = total.shape[1]
    span = HALO + minutes
    real = jnp.where(group[0] < groups - 1, 1.0, 0.0)
    for p in range(flows.shape[2] // width):
        cols = slice(p * width, (p + 1) * width)
        for d in range(days):
            row = (p * days + d) * span + HALO
            own = total[row : row + minutes, :]
            keep = minutes - HALO
            late = own[keep:] + spill[p * days + d] * real
            for rows, grad in ((slice(0, keep), own[:keep]), (slice(keep, minutes), late)):
                gradient[d, rows, cols] = grad
                new_flows[d, rows, cols] = jnp.maximum(
                    flows[d, rows, cols].astype(jnp.float32) - RATE * grad, 0.0
                )


BACKWARD_COST = 500


def weight(nanoseconds):
    return pl.CostEstimate(
        flops=1_000_000 * nanoseconds, transcendentals=0, bytes_accessed=3_000 * nanoseconds
    )


SMEM = pl.BlockSpec(memory_space=pltpu.SMEM)
VMEM = pl.BlockSpec(memory_space=pltpu.VMEM)
HBM = pl.BlockSpec(memory_space=pltpu.HBM)


def kernel_call(body, scalars, arrays, out_shape, scratch=(), cost=None, outs=None):
    return pl.pallas_call(
        body,
        out_shape=out_shape,
        in_specs=[SMEM] * len(scalars) + [VMEM] * len(arrays),
        out_specs=outs or [VMEM] * len(out_shape),
        scratch_shapes=list(scratch),
        compiler_params=pltpu.CompilerParams(vmem_limit_bytes=40 * 1024 * 1024),
        cost_estimate=cost,
    )(*scalars, *arrays)


def per_device_dense(
    flows,
    counts,
    local_blocks,
    local_path,
    local_link,
    local_lag,
    remote_blocks,
    remote_path,
    remote_link,
    remote_lag,
    remote_slot,
):
    days, minutes, path_width = flows.shape
    width = local_blocks.shape[1]
    paths = path_width // width
    links = counts.shape[2] // width
    corridors = lax.axis_size("corr")
    remotes = remote_lag.shape[0]
    cap = (remotes + corridors - 2) // (corridors - 1)
    span = HALO + minutes
    through = list(range(2, corridors, 2))
    order = [s ^ 1 for s in reversed(through)] + [1] + through
    me = lax.axis_index("corr").astype(jnp.int32).reshape(1)
    group = lax.axis_index("tm").astype(jnp.int32).reshape(1)
    groups = lax.axis_size("tm")
    shape = jax.ShapeDtypeStruct
    piece = (links, days * minutes, width)
    wide = pltpu.VMEM((paths * days * span, width), jnp.float32)
    slots_shape = (len(order) * links + 1, days * minutes, width)
    local_index = (local_path, local_link, local_lag)

    before = lax.ppermute(flows, "tm", [(i, (i + 1) % groups) for i in range(groups)])
    fixed = (remote_path, remote_link, remote_lag, remote_slot, remote_blocks)
    ahead, remote_mats = pl.pallas_call(
        functools.partial(prepare_kernel, cap, order, links, CHUNKS, days * span),
        out_shape=[
            shape((2 * remotes,), jnp.int32),
            shape(remote_blocks.shape, remote_blocks.dtype),
        ],
        in_specs=[SMEM] + [HBM] * len(fixed),
        out_specs=[SMEM, VMEM],
        scratch_shapes=[pltpu.SMEM(remote_slot.shape, jnp.int32) for _ in fixed[1:]]
        + [pltpu.SMEM((corridors,), jnp.int32), pltpu.SemaphoreType.DMA((len(fixed) - 1 + CHUNKS,))],
        compiler_params=pltpu.CompilerParams(vmem_limit_bytes=40 * 1024 * 1024),
    )(me, *(pltpu.with_memory_space_constraint(i, pltpu.HBM) for i in fixed))

    def exchanged(part, s):
        return lax.ppermute(part, "corr", [(i, i ^ s) for i in range(corridors)])

    f32 = jnp.float32
    outgoing = kernel_call(
        functools.partial(forward_remote_kernel, days, links),
        (group, ahead),
        (flows, before, remote_mats),
        [shape(piece, f32) for _ in order],
        [wide, pltpu.VMEM((len(order) * links, *piece[1:]), f32)],
    )
    count = len(through)
    crossed = [exchanged(part.astype(WIRE), 1) for part in outgoing[:count]]
    near = exchanged(outgoing[count].astype(WIRE), 1)
    received = []
    for s, kept in reversed(list(zip(through, outgoing[count + 1 :]))):
        met = crossed[order.index(s ^ 1)].astype(f32)
        received.append(exchanged((kept + met).astype(WIRE), s))
    received.append(near)
    own, table = kernel_call(
        functools.partial(forward_local_kernel, days, cap, order),
        (group, me, remote_slot, *local_index),
        (flows, before, local_blocks),
        [shape(piece, f32), shape((len(order) + corridors * cap,), jnp.int32)],
        [wide],
        outs=[VMEM, SMEM],
    )
    totals = functools.reduce(jnp.add, [p.astype(f32) for p in received], own)
    (signal,) = kernel_call(
        functools.partial(signal_kernel, days),
        (),
        (totals, counts),
        [shape(piece, jnp.bfloat16)],
    )
    arrived = {s: exchanged(signal, s) for s in through}
    rows = [shape((paths * days * span, width), f32)]
    (total,) = kernel_call(
        functools.partial(backward_local_kernel, days),
        local_index,
        (signal, local_blocks),
        rows,
    )
    arrived[through[-1]], total = lax.optimization_barrier((arrived[through[-1]], total))
    for s in through[1:]:
        arrived[s ^ 1] = exchanged(arrived[s], 1)
    passed = exchanged(jnp.concatenate([arrived[through[0]], signal], axis=0), 1)
    edge = shape((paths * days, HALO, width), f32)
    for first, end, parts, made in (
        (count + 1, len(order), [arrived[s] for s in through], rows),
        (0, count + 1, [*(arrived[s] for s in order[: count - 1]), passed], [*rows, edge]),
    ):
        total, *early = kernel_call(
            functools.partial(backward_remote_kernel, days, cap, first, end, links),
            (table, ahead),
            (remote_mats, total, *parts),
            made,
            [pltpu.VMEM(slots_shape, jnp.bfloat16)],
            cost=weight(BACKWARD_COST) if first else None,
        )
    route = [(i, (i - 1) % groups) for i in range(groups)]
    spill = lax.ppermute(early[0].astype(WIRE), "tm", route).astype(f32)
    totals, total = lax.optimization_barrier((totals, total))
    (link_residual,) = kernel_call(
        functools.partial(residual_kernel, days),
        (),
        (totals, counts),
        [shape(counts.shape, f32)],
    )
    gradient, new_flows = kernel_call(
        functools.partial(finish_kernel, days, groups),
        (group,),
        (total, spill, flows),
        [shape(flows.shape, f32)] * 2,
    )
    return (link_residual, gradient, new_flows)


def per_device(*args):
    counts, blocks, lags = args[1], args[2], args[9]
    corridors = lax.axis_size("corr")
    links = counts.shape[2] // blocks.shape[1]
    cap = (lags.shape[0] + corridors - 2) // (corridors - 1)
    if cap >= links and corridors >= 4 and corridors & (corridors - 1) == 0:
        return per_device_dense(*args)
    return per_device_slots(*args)


def solution(mesh):
    placed = (
        P(None, "tm", "corr"),
        P(None, "tm", "corr"),
        P("corr", None, None),
        P("corr"),
        P("corr"),
        P("corr"),
        P("corr", None, None),
        P("corr"),
        P("corr"),
        P("corr"),
        P("corr"),
    )
    return jax.shard_map(
        per_device,
        mesh=mesh,
        in_specs=placed,
        out_specs=(P(None, "tm", "corr"), P(None, "tm", "corr"), P(None, "tm", "corr")),
        check_vma=False,
    )
```

```python
import functools
import jax
import jax.numpy as jnp
from jax import lax
from jax.experimental import pallas as pl
from jax.experimental.pallas import tpu as pltpu
from jax.sharding import PartitionSpec as P

LAGS = 16


HIGH = lax.Precision.HIGHEST
RATE = 0.5


def passed_along(block, axis, distance):
    devices = range(lax.axis_size(axis))
    route = [(i - distance, i) for i in devices if i - distance in devices]
    return lax.ppermute(block, axis, route)


def one_hot(labels, classes, dtype):
    return (labels[:, None] == jnp.arange(classes, dtype=jnp.int32)[None, :]).astype(dtype)


def shift_table(deltas, out_len, in_len, dtype):
    out_pos = jnp.arange(out_len, dtype=jnp.int32)[:, None]
    in_pos = jnp.arange(in_len, dtype=jnp.int32)[None, :]
    return ((in_pos - out_pos)[None, :, :] == deltas[:, None, None]).astype(dtype)


def pick_blocks(cube, hot):
    return jnp.einsum("dsqp,bq->dsbp", cube, hot, preferred_element_type=jnp.float32).astype(
        jnp.bfloat16
    )


def shift_narrow(picked, table):
    return jnp.einsum("dsbp,bts->dtbp", picked, table, preferred_element_type=jnp.float32).astype(
        jnp.bfloat16
    )


def route_partials(local_part, remote_part, local_route, remote_link, slot_hot, link_blocks):
    own = jnp.einsum("dtbl,bk->dtkl", local_part, local_route, precision=HIGH)
    outgoing = jnp.einsum("bdtl,bs->sdtl", remote_part, slot_hot, precision=HIGH)
    slot_int = slot_hot.astype(jnp.int32)
    labels = link_blocks + jnp.sum(slot_int * (remote_link[:, None] - link_blocks), axis=0)
    return (own, outgoing, labels)


def absorb(own, received, got_labels, link_blocks):
    landing = one_hot(got_labels, link_blocks, jnp.float32)
    return own + jnp.einsum("sdtl,sk->dtkl", received, landing, precision=HIGH)


def collect_paths(local_grad, remote_grad, local_paths, remote_paths):
    first_sum = jnp.einsum("dtbp,bq->dtqp", local_grad, local_paths, precision=HIGH)
    return first_sum + jnp.einsum("bdtp,bq->dtqp", remote_grad, remote_paths, precision=HIGH)


def per_device_slots(
    flows,
    counts,
    local_blocks,
    local_path,
    local_link,
    local_lag,
    remote_blocks,
    remote_path,
    remote_link,
    remote_lag,
    remote_slot,
):
    day_count, minutes, path_width = flows.shape
    block_width = local_blocks.shape[1]
    path_blocks = path_width // block_width
    link_blocks = counts.shape[2] // block_width
    lag_span = LAGS - 1
    corridors = lax.axis_size("corr")
    remote_count = remote_lag.shape[0]
    slot_count = corridors * ((remote_count + corridors - 2) // (corridors - 1))
    flow_cube = flows.reshape(day_count, minutes, path_blocks, block_width)
    local_route = one_hot(local_link, link_blocks, jnp.float32)
    slot_hot = one_hot(remote_slot, slot_count, jnp.float32)
    slot_pick = slot_hot.astype(jnp.bfloat16)
    local_path_hot = one_hot(local_path, path_blocks, jnp.bfloat16)
    remote_path_hot = one_hot(remote_path, path_blocks, jnp.bfloat16)
    local_link_hot = one_hot(local_link, link_blocks, jnp.bfloat16)
    local_in = pick_blocks(flow_cube, local_path_hot)
    remote_in = pick_blocks(flow_cube, remote_path_hot)
    local_plain = jnp.einsum(
        "dtbp,blp->dtbl", local_in, local_blocks, preferred_element_type=jnp.float32
    )
    remote_plain = jnp.einsum(
        "dtbp,blp->bdtl", remote_in, remote_blocks, preferred_element_type=jnp.float32
    )
    local_part = jnp.einsum(
        "dsbl,bts->dtbl",
        local_plain,
        shift_table(-local_lag, minutes + lag_span, minutes, jnp.float32),
        precision=HIGH,
    )
    remote_part = jnp.einsum(
        "bdsl,bts->bdtl",
        remote_plain,
        shift_table(-remote_lag, minutes + lag_span, minutes, jnp.float32),
        precision=HIGH,
    )
    own, outgoing, labels = route_partials(
        local_part, remote_part, local_route, remote_link, slot_hot, link_blocks
    )
    received, got_labels = (
        lax.all_to_all(outgoing, "corr", split_axis=0, concat_axis=0, tiled=True),
        lax.all_to_all(labels, "corr", split_axis=0, concat_axis=0, tiled=True),
    )
    extended = absorb(own, received, got_labels, link_blocks)
    spill = passed_along(extended[:, minutes:], "tm", 1)
    totals = extended[:, :minutes] + jnp.pad(
        spill, ((0, 0), (0, minutes - lag_span), (0, 0), (0, 0))
    )
    link_flow = totals.reshape(day_count, minutes, link_blocks * block_width)
    link_residual = (link_flow - counts) / (counts + 1.0)
    signal = (link_residual / (counts + 1.0)).astype(jnp.bfloat16)
    slot_route = one_hot(got_labels, link_blocks, jnp.bfloat16)
    local_paths = one_hot(local_path, path_blocks, jnp.float32)
    remote_paths = one_hot(remote_path, path_blocks, jnp.float32)
    ahead = passed_along(signal[:, :lag_span, :], "tm", -1)
    extended_signal = jnp.concatenate([signal, ahead], axis=1).reshape(
        day_count, minutes + lag_span, link_blocks, block_width
    )
    slot_signal = jnp.einsum(
        "dtkl,sk->sdtl", extended_signal, slot_route, preferred_element_type=jnp.float32
    ).astype(jnp.bfloat16)
    returned = lax.all_to_all(slot_signal, "corr", split_axis=0, concat_axis=0, tiled=True)
    remote_pick = jnp.einsum(
        "sdtl,bs->bdtl", returned, slot_pick, preferred_element_type=jnp.float32
    ).astype(jnp.bfloat16)
    remote_sig = jnp.einsum(
        "bdsl,bts->bdtl",
        remote_pick,
        shift_table(remote_lag, minutes, minutes + lag_span, jnp.bfloat16),
        preferred_element_type=jnp.float32,
    ).astype(jnp.bfloat16)
    local_sig = shift_narrow(
        pick_blocks(extended_signal, local_link_hot),
        shift_table(local_lag, minutes, minutes + lag_span, jnp.bfloat16),
    )
    local_grad = jnp.einsum(
        "dtbl,blp->dtbp", local_sig, local_blocks, preferred_element_type=jnp.float32
    )
    remote_grad = jnp.einsum(
        "bdtl,blp->bdtp", remote_sig, remote_blocks, preferred_element_type=jnp.float32
    )
    grad_cube = collect_paths(local_grad, remote_grad, local_paths, remote_paths)
    gradient = grad_cube.reshape(day_count, minutes, path_width)
    new_flows = jnp.maximum(flows.astype(jnp.float32) - RATE * gradient, 0.0)
    return (link_residual, gradient, new_flows)


HALO = 16
WIRE = jnp.float16
UNROLL = 64
CHUNKS = 8


def step_of(count):
    return next(u for u in range(min(count, UNROLL), 0, -1) if count % u == 0)


def stage_flows(group, flows_ref, before_ref, wide, days, width):
    real = jnp.where(group[0] > 0, 1.0, 0.0)
    minutes = flows_ref.shape[1]
    span = HALO + minutes
    for p in range(flows_ref.shape[2] // width):
        cols = slice(p * width, (p + 1) * width)
        for d in range(days):
            row = (p * days + d) * span
            before = before_ref[d, :, cols].astype(jnp.float32)
            wide[row : row + HALO, :] = before[minutes - HALO :] * real
            wide[row + HALO : row + span, :] = flows_ref[d, :, cols].astype(jnp.float32)


def forward_blocks(groups, unroll, mat, base, target, wide, acc, days, minutes):
    span = HALO + minutes

    def group(g, carry):
        parts = []
        for u in range(unroll):
            rows = [wide[pl.ds(base(g, u) + d * span, minutes), :] for d in range(days)]
            taken = jnp.concatenate(rows, axis=0).astype(jnp.bfloat16)
            parts.append(
                lax.dot_general(
                    taken,
                    mat(g, u),
                    (((1,), (1,)), ((), ())),
                    preferred_element_type=jnp.float32,
                )
            )
        for u in range(unroll):
            acc[target(g, u)] += parts[u]
        return carry

    lax.fori_loop(0, groups, group, 0)


def backward_blocks(groups, unroll, mat, base, signal, acc, days, minutes):
    span = HALO + minutes

    def group(g, carry):
        parts = [
            jnp.dot(signal(g, u), mat(g, u), preferred_element_type=jnp.float32)
            for u in range(unroll)
        ]
        for u in range(unroll):
            for d in range(days):
                rows = pl.ds(base(g, u) + d * span, minutes)
                acc[rows, :] += parts[u][d * minutes : (d + 1) * minutes]
        return carry

    lax.fori_loop(0, groups, group, 0)


def prepare_kernel(cap, order, links, chunks, row_step, me, *rest):
    sources, (ahead, mats_out, path, link, lag, slot, place, sems) = rest[:5], rest[5:]
    blocks = slot.shape[0]
    pairs = list(zip(sources[:4], (path, link, lag, slot)))
    step = blocks // chunks
    for c in range(chunks):
        rows = slice(c * step, blocks if c == chunks - 1 else (c + 1) * step)
        pairs.append((sources[4].at[rows], mats_out.at[rows]))
    copies = [pltpu.make_async_copy(a, b, sems.at[i]) for i, (a, b) in enumerate(pairs)]
    for copy in copies:
        copy.start()
    place[0] = 0
    for p, s in enumerate(order):
        place[s] = p * links
    for copy in copies[:4]:
        copy.wait()

    def entry(j, carry):
        ahead[j] = path[j] * row_step + HALO - lag[j]
        ahead[blocks + j] = place[lax.div(slot[j], cap) ^ me[0]] + link[j]
        return carry

    lax.fori_loop(0, blocks, entry, 0, unroll=16)
    for copy in copies[4:]:
        copy.wait()


def fill_table(cap, order, me, slot, table):
    first = len(order)
    for p, s in enumerate(order):
        table[p] = first + (me[0] ^ s) * cap
    for i in range((first + 1) * cap):
        table[first + i] = -1

    def entry(j, carry):
        table[first + slot[j]] = j
        return carry

    lax.fori_loop(0, slot.shape[0], entry, 0, unroll=16)


def slot_views(table, ahead, mats, cap, first, unroll, blank):
    def index(g, u):
        at = first * cap + g * unroll + u
        place = lax.div(at, cap)
        return table[table[place] + at - place * cap]

    def mat(g, u):
        return mats[jnp.maximum(index(g, u), 0)]

    def base(g, u):
        return ahead[jnp.maximum(index(g, u), 0)]

    def block(g, u):
        j = index(g, u)
        return jnp.where(j < 0, blank, ahead[mats.shape[0] + jnp.maximum(j, 0)])

    return mat, base, block


def forward_remote_kernel(days, links, group, ahead, flows, before, mats, *rest):
    outs, (wide, acc) = rest[:-2], rest[-2:]
    minutes, width = flows.shape[1], mats.shape[2]
    blocks = mats.shape[0]
    stage_flows(group, flows, before, wide, days, width)
    acc[...] = jnp.zeros_like(acc)
    unroll = step_of(blocks)
    forward_blocks(
        blocks // unroll,
        unroll,
        lambda g, u: mats[g * unroll + u],
        lambda g, u: ahead[g * unroll + u],
        lambda g, u: ahead[blocks + g * unroll + u],
        wide,
        acc,
        days,
        minutes,
    )
    for p, out in enumerate(outs):
        out[...] = acc[p * links : (p + 1) * links]


def local_views(path, link, lag, mats, unroll, row_step):
    return (
        lambda g, u: mats[g * unroll + u],
        lambda g, u: path[g * unroll + u] * row_step + HALO - lag[g * unroll + u],
        lambda g, u: link[g * unroll + u],
    )


def forward_local_kernel(
    days, cap, order, group, me, slot, path, link, lag, flows, before, mats, own, table, wide
):
    minutes, width = flows.shape[1], mats.shape[2]
    stage_flows(group, flows, before, wide, days, width)
    own[...] = jnp.zeros_like(own)
    unroll = step_of(mats.shape[0])
    views = local_views(path, link, lag, mats, unroll, days * (HALO + minutes))
    forward_blocks(mats.shape[0] // unroll, unroll, *views, wide, own, days, minutes)
    fill_table(cap, order, me, slot, table)


def residual_of(days, totals, counts, b, d):
    width, minutes = totals.shape[2], counts.shape[1]
    seen = counts[d, :, b * width : (b + 1) * width]
    weight = seen + 1.0
    return (totals[b, d * minutes : (d + 1) * minutes, :] - seen) / weight, weight


def signal_kernel(days, totals, counts, signal):
    minutes = counts.shape[1]
    for b in range(totals.shape[0]):
        for d in range(days):
            res, weight = residual_of(days, totals, counts, b, d)
            signal[b, d * minutes : (d + 1) * minutes, :] = (res / weight).astype(signal.dtype)


def residual_kernel(days, totals, counts, residual):
    width = totals.shape[2]
    for b in range(totals.shape[0]):
        for d in range(days):
            res, _ = residual_of(days, totals, counts, b, d)
            residual[d, :, b * width : (b + 1) * width] = res


def backward_local_kernel(days, path, link, lag, signal, mats, out):
    minutes = signal.shape[1] // days
    out[...] = jnp.zeros_like(out)
    unroll = step_of(mats.shape[0])
    mat, base, block = local_views(path, link, lag, mats, unroll, days * (HALO + minutes))
    backward_blocks(
        mats.shape[0] // unroll,
        unroll,
        mat,
        base,
        lambda g, u: signal[block(g, u)],
        out,
        days,
        minutes,
    )


def backward_remote_kernel(days, cap, first, end, links, table, ahead, mats, start, *rest):
    count = (end - first) * links
    signals, sources, rest = [], 0, list(rest)
    while sources < count:
        signals.append(rest.pop(0))
        sources += signals[-1].shape[0]
    out, early, everyone = rest[0], rest[1:-1], rest[-1]
    minutes = signals[0].shape[1] // days
    place = first * links
    for part in signals:
        everyone[place : place + part.shape[0]] = part[...]
        place += part.shape[0]
    blank = everyone.shape[0] - 1
    everyone[blank] = jnp.zeros(everyone.shape[1:], everyone.dtype)
    out[...] = start[...]
    span = HALO + minutes
    slots = (end - first) * cap
    unroll = step_of(slots)
    mat, base, block = slot_views(table, ahead, mats, cap, first, unroll, blank)
    backward_blocks(
        slots // unroll,
        unroll,
        mat,
        base,
        lambda g, u: everyone[block(g, u)],
        out,
        days,
        minutes,
    )
    if early:
        for i in range(early[0].shape[0]):
            early[0][i] = out[i * span : i * span + HALO, :]


def finish_kernel(days, groups, group, total, spill, flows, gradient, new_flows):
    minutes = flows.shape[1]
    width = total.shape[1]
    span = HALO + minutes
    real = jnp.where(group[0] < groups - 1, 1.0, 0.0)
    for p in range(flows.shape[2] // width):
        cols = slice(p * width, (p + 1) * width)
        for d in range(days):
            row = (p * days + d) * span + HALO
            own = total[row : row + minutes, :]
            keep = minutes - HALO
            late = own[keep:] + spill[p * days + d] * real
            for rows, grad in ((slice(0, keep), own[:keep]), (slice(keep, minutes), late)):
                gradient[d, rows, cols] = grad
                new_flows[d, rows, cols] = jnp.maximum(
                    flows[d, rows, cols].astype(jnp.float32) - RATE * grad, 0.0
                )


BACKWARD_COST = 500


def weight(nanoseconds):
    return pl.CostEstimate(
        flops=1_000_000 * nanoseconds, transcendentals=0, bytes_accessed=3_000 * nanoseconds
    )


SMEM = pl.BlockSpec(memory_space=pltpu.SMEM)
VMEM = pl.BlockSpec(memory_space=pltpu.VMEM)
HBM = pl.BlockSpec(memory_space=pltpu.HBM)


def kernel_call(body, scalars, arrays, out_shape, scratch=(), cost=None, outs=None):
    return pl.pallas_call(
        body,
        out_shape=out_shape,
        in_specs=[SMEM] * len(scalars) + [VMEM] * len(arrays),
        out_specs=outs or [VMEM] * len(out_shape),
        scratch_shapes=list(scratch),
        compiler_params=pltpu.CompilerParams(vmem_limit_bytes=40 * 1024 * 1024),
        cost_estimate=cost,
    )(*scalars, *arrays)


def per_device_dense(
    flows,
    counts,
    local_blocks,
    local_path,
    local_link,
    local_lag,
    remote_blocks,
    remote_path,
    remote_link,
    remote_lag,
    remote_slot,
):
    days, minutes, path_width = flows.shape
    width = local_blocks.shape[1]
    paths = path_width // width
    links = counts.shape[2] // width
    corridors = lax.axis_size("corr")
    remotes = remote_lag.shape[0]
    cap = (remotes + corridors - 2) // (corridors - 1)
    span = HALO + minutes
    through = list(range(2, corridors, 2))
    order = [s ^ 1 for s in reversed(through)] + [1] + through
    me = lax.axis_index("corr").astype(jnp.int32).reshape(1)
    group = lax.axis_index("tm").astype(jnp.int32).reshape(1)
    groups = lax.axis_size("tm")
    shape = jax.ShapeDtypeStruct
    piece = (links, days * minutes, width)
    wide = pltpu.VMEM((paths * days * span, width), jnp.float32)
    slots_shape = (len(order) * links + 1, days * minutes, width)
    local_index = (local_path, local_link, local_lag)

    before = lax.ppermute(flows, "tm", [(i, (i + 1) % groups) for i in range(groups)])
    fixed = (remote_path, remote_link, remote_lag, remote_slot, remote_blocks)
    ahead, remote_mats = pl.pallas_call(
        functools.partial(prepare_kernel, cap, order, links, CHUNKS, days * span),
        out_shape=[
            shape((2 * remotes,), jnp.int32),
            shape(remote_blocks.shape, remote_blocks.dtype),
        ],
        in_specs=[SMEM] + [HBM] * len(fixed),
        out_specs=[SMEM, VMEM],
        scratch_shapes=[pltpu.SMEM(remote_slot.shape, jnp.int32) for _ in fixed[1:]]
        + [pltpu.SMEM((corridors,), jnp.int32), pltpu.SemaphoreType.DMA((len(fixed) - 1 + CHUNKS,))],
        compiler_params=pltpu.CompilerParams(vmem_limit_bytes=40 * 1024 * 1024),
    )(me, *(pltpu.with_memory_space_constraint(i, pltpu.HBM) for i in fixed))

    def exchanged(part, s):
        return lax.ppermute(part, "corr", [(i, i ^ s) for i in range(corridors)])

    f32 = jnp.float32
    outgoing = kernel_call(
        functools.partial(forward_remote_kernel, days, links),
        (group, ahead),
        (flows, before, remote_mats),
        [shape(piece, f32) for _ in order],
        [wide, pltpu.VMEM((len(order) * links, *piece[1:]), f32)],
    )
    count = len(through)
    crossed = [exchanged(part.astype(WIRE), 1) for part in outgoing[:count]]
    near = exchanged(outgoing[count].astype(WIRE), 1)
    received = []
    for s, kept in reversed(list(zip(through, outgoing[count + 1 :]))):
        met = crossed[order.index(s ^ 1)].astype(f32)
        received.append(exchanged((kept + met).astype(WIRE), s))
    received.append(near)
    own, table = kernel_call(
        functools.partial(forward_local_kernel, days, cap, order),
        (group, me, remote_slot, *local_index),
        (flows, before, local_blocks),
        [shape(piece, f32), shape((len(order) + corridors * cap,), jnp.int32)],
        [wide],
        outs=[VMEM, SMEM],
    )
    totals = functools.reduce(jnp.add, [p.astype(f32) for p in received], own)
    (signal,) = kernel_call(
        functools.partial(signal_kernel, days),
        (),
        (totals, counts),
        [shape(piece, jnp.bfloat16)],
    )
    arrived = {s: exchanged(signal, s) for s in through}
    rows = [shape((paths * days * span, width), f32)]
    (total,) = kernel_call(
        functools.partial(backward_local_kernel, days),
        local_index,
        (signal, local_blocks),
        rows,
    )
    middle = through[len(through) // 2]
    arrived[middle], total = lax.optimization_barrier((arrived[middle], total))
    for s in through[1:]:
        arrived[s ^ 1] = exchanged(arrived[s], 1)
    passed = exchanged(jnp.concatenate([arrived[through[0]], signal], axis=0), 1)
    edge = shape((paths * days, HALO, width), f32)
    for first, end, parts, made in (
        (count + 1, len(order), [arrived[s] for s in through], rows),
        (0, count + 1, [*(arrived[s] for s in order[: count - 1]), passed], [*rows, edge]),
    ):
        total, *early = kernel_call(
            functools.partial(backward_remote_kernel, days, cap, first, end, links),
            (table, ahead),
            (remote_mats, total, *parts),
            made,
            [pltpu.VMEM(slots_shape, jnp.bfloat16)],
            cost=weight(BACKWARD_COST) if first else None,
        )
    route = [(i, (i - 1) % groups) for i in range(groups)]
    spill = lax.ppermute(early[0].astype(WIRE), "tm", route).astype(f32)
    totals, total = lax.optimization_barrier((totals, total))
    (link_residual,) = kernel_call(
        functools.partial(residual_kernel, days),
        (),
        (totals, counts),
        [shape(counts.shape, f32)],
    )
    gradient, new_flows = kernel_call(
        functools.partial(finish_kernel, days, groups),
        (group,),
        (total, spill, flows),
        [shape(flows.shape, f32)] * 2,
    )
    return (link_residual, gradient, new_flows)


def per_device(*args):
    counts, blocks, lags = args[1], args[2], args[9]
    corridors = lax.axis_size("corr")
    links = counts.shape[2] // blocks.shape[1]
    cap = (lags.shape[0] + corridors - 2) // (corridors - 1)
    if cap >= links and corridors >= 4 and corridors & (corridors - 1) == 0:
        return per_device_dense(*args)
    return per_device_slots(*args)


def solution(mesh):
    placed = (
        P(None, "tm", "corr"),
        P(None, "tm", "corr"),
        P("corr", None, None),
        P("corr"),
        P("corr"),
        P("corr"),
        P("corr", None, None),
        P("corr"),
        P("corr"),
        P("corr"),
        P("corr"),
    )
    return jax.shard_map(
        per_device,
        mesh=mesh,
        in_specs=placed,
        out_specs=(P(None, "tm", "corr"), P(None, "tm", "corr"), P(None, "tm", "corr")),
        check_vma=False,
    )
```

```python
import functools
import jax
import jax.numpy as jnp
from jax import lax
from jax.experimental import pallas as pl
from jax.experimental.pallas import tpu as pltpu
from jax.sharding import PartitionSpec as P

LAGS = 16


HIGH = lax.Precision.HIGHEST
RATE = 0.5


def passed_along(block, axis, distance):
    devices = range(lax.axis_size(axis))
    route = [(i - distance, i) for i in devices if i - distance in devices]
    return lax.ppermute(block, axis, route)


def one_hot(labels, classes, dtype):
    return (labels[:, None] == jnp.arange(classes, dtype=jnp.int32)[None, :]).astype(dtype)


def shift_table(deltas, out_len, in_len, dtype):
    out_pos = jnp.arange(out_len, dtype=jnp.int32)[:, None]
    in_pos = jnp.arange(in_len, dtype=jnp.int32)[None, :]
    return ((in_pos - out_pos)[None, :, :] == deltas[:, None, None]).astype(dtype)


def pick_blocks(cube, hot):
    return jnp.einsum("dsqp,bq->dsbp", cube, hot, preferred_element_type=jnp.float32).astype(
        jnp.bfloat16
    )


def shift_narrow(picked, table):
    return jnp.einsum("dsbp,bts->dtbp", picked, table, preferred_element_type=jnp.float32).astype(
        jnp.bfloat16
    )


def route_partials(local_part, remote_part, local_route, remote_link, slot_hot, link_blocks):
    own = jnp.einsum("dtbl,bk->dtkl", local_part, local_route, precision=HIGH)
    outgoing = jnp.einsum("bdtl,bs->sdtl", remote_part, slot_hot, precision=HIGH)
    slot_int = slot_hot.astype(jnp.int32)
    labels = link_blocks + jnp.sum(slot_int * (remote_link[:, None] - link_blocks), axis=0)
    return (own, outgoing, labels)


def absorb(own, received, got_labels, link_blocks):
    landing = one_hot(got_labels, link_blocks, jnp.float32)
    return own + jnp.einsum("sdtl,sk->dtkl", received, landing, precision=HIGH)


def collect_paths(local_grad, remote_grad, local_paths, remote_paths):
    first_sum = jnp.einsum("dtbp,bq->dtqp", local_grad, local_paths, precision=HIGH)
    return first_sum + jnp.einsum("bdtp,bq->dtqp", remote_grad, remote_paths, precision=HIGH)


def per_device_slots(
    flows,
    counts,
    local_blocks,
    local_path,
    local_link,
    local_lag,
    remote_blocks,
    remote_path,
    remote_link,
    remote_lag,
    remote_slot,
):
    day_count, minutes, path_width = flows.shape
    block_width = local_blocks.shape[1]
    path_blocks = path_width // block_width
    link_blocks = counts.shape[2] // block_width
    lag_span = LAGS - 1
    corridors = lax.axis_size("corr")
    remote_count = remote_lag.shape[0]
    slot_count = corridors * ((remote_count + corridors - 2) // (corridors - 1))
    flow_cube = flows.reshape(day_count, minutes, path_blocks, block_width)
    local_route = one_hot(local_link, link_blocks, jnp.float32)
    slot_hot = one_hot(remote_slot, slot_count, jnp.float32)
    slot_pick = slot_hot.astype(jnp.bfloat16)
    local_path_hot = one_hot(local_path, path_blocks, jnp.bfloat16)
    remote_path_hot = one_hot(remote_path, path_blocks, jnp.bfloat16)
    local_link_hot = one_hot(local_link, link_blocks, jnp.bfloat16)
    local_in = pick_blocks(flow_cube, local_path_hot)
    remote_in = pick_blocks(flow_cube, remote_path_hot)
    local_plain = jnp.einsum(
        "dtbp,blp->dtbl", local_in, local_blocks, preferred_element_type=jnp.float32
    )
    remote_plain = jnp.einsum(
        "dtbp,blp->bdtl", remote_in, remote_blocks, preferred_element_type=jnp.float32
    )
    local_part = jnp.einsum(
        "dsbl,bts->dtbl",
        local_plain,
        shift_table(-local_lag, minutes + lag_span, minutes, jnp.float32),
        precision=HIGH,
    )
    remote_part = jnp.einsum(
        "bdsl,bts->bdtl",
        remote_plain,
        shift_table(-remote_lag, minutes + lag_span, minutes, jnp.float32),
        precision=HIGH,
    )
    own, outgoing, labels = route_partials(
        local_part, remote_part, local_route, remote_link, slot_hot, link_blocks
    )
    received, got_labels = (
        lax.all_to_all(outgoing, "corr", split_axis=0, concat_axis=0, tiled=True),
        lax.all_to_all(labels, "corr", split_axis=0, concat_axis=0, tiled=True),
    )
    extended = absorb(own, received, got_labels, link_blocks)
    spill = passed_along(extended[:, minutes:], "tm", 1)
    totals = extended[:, :minutes] + jnp.pad(
        spill, ((0, 0), (0, minutes - lag_span), (0, 0), (0, 0))
    )
    link_flow = totals.reshape(day_count, minutes, link_blocks * block_width)
    link_residual = (link_flow - counts) / (counts + 1.0)
    signal = (link_residual / (counts + 1.0)).astype(jnp.bfloat16)
    slot_route = one_hot(got_labels, link_blocks, jnp.bfloat16)
    local_paths = one_hot(local_path, path_blocks, jnp.float32)
    remote_paths = one_hot(remote_path, path_blocks, jnp.float32)
    ahead = passed_along(signal[:, :lag_span, :], "tm", -1)
    extended_signal = jnp.concatenate([signal, ahead], axis=1).reshape(
        day_count, minutes + lag_span, link_blocks, block_width
    )
    slot_signal = jnp.einsum(
        "dtkl,sk->sdtl", extended_signal, slot_route, preferred_element_type=jnp.float32
    ).astype(jnp.bfloat16)
    returned = lax.all_to_all(slot_signal, "corr", split_axis=0, concat_axis=0, tiled=True)
    remote_pick = jnp.einsum(
        "sdtl,bs->bdtl", returned, slot_pick, preferred_element_type=jnp.float32
    ).astype(jnp.bfloat16)
    remote_sig = jnp.einsum(
        "bdsl,bts->bdtl",
        remote_pick,
        shift_table(remote_lag, minutes, minutes + lag_span, jnp.bfloat16),
        preferred_element_type=jnp.float32,
    ).astype(jnp.bfloat16)
    local_sig = shift_narrow(
        pick_blocks(extended_signal, local_link_hot),
        shift_table(local_lag, minutes, minutes + lag_span, jnp.bfloat16),
    )
    local_grad = jnp.einsum(
        "dtbl,blp->dtbp", local_sig, local_blocks, preferred_element_type=jnp.float32
    )
    remote_grad = jnp.einsum(
        "bdtl,blp->bdtp", remote_sig, remote_blocks, preferred_element_type=jnp.float32
    )
    grad_cube = collect_paths(local_grad, remote_grad, local_paths, remote_paths)
    gradient = grad_cube.reshape(day_count, minutes, path_width)
    new_flows = jnp.maximum(flows.astype(jnp.float32) - RATE * gradient, 0.0)
    return (link_residual, gradient, new_flows)


HALO = 16
WIRE = jnp.float16
UNROLL = 64
CHUNKS = 8


def step_of(count):
    return next(u for u in range(min(count, UNROLL), 0, -1) if count % u == 0)


def stage_flows(group, flows_ref, before_ref, wide, days, width):
    real = jnp.where(group[0] > 0, 1.0, 0.0)
    minutes = flows_ref.shape[1]
    span = HALO + minutes
    for p in range(flows_ref.shape[2] // width):
        cols = slice(p * width, (p + 1) * width)
        for d in range(days):
            row = (p * days + d) * span
            before = before_ref[d, :, cols].astype(jnp.float32)
            wide[row : row + HALO, :] = before[minutes - HALO :] * real
            wide[row + HALO : row + span, :] = flows_ref[d, :, cols].astype(jnp.float32)


def forward_blocks(groups, unroll, mat, base, target, wide, acc, days, minutes):
    span = HALO + minutes

    def group(g, carry):
        parts = []
        for u in range(unroll):
            rows = [wide[pl.ds(base(g, u) + d * span, minutes), :] for d in range(days)]
            taken = jnp.concatenate(rows, axis=0).astype(jnp.bfloat16)
            parts.append(
                lax.dot_general(
                    taken,
                    mat(g, u),
                    (((1,), (1,)), ((), ())),
                    preferred_element_type=jnp.float32,
                )
            )
        for u in range(unroll):
            acc[target(g, u)] += parts[u]
        return carry

    lax.fori_loop(0, groups, group, 0)


def backward_blocks(groups, unroll, mat, base, signal, acc, days, minutes):
    span = HALO + minutes

    def group(g, carry):
        parts = [
            jnp.dot(signal(g, u), mat(g, u), preferred_element_type=jnp.float32)
            for u in range(unroll)
        ]
        for u in range(unroll):
            for d in range(days):
                rows = pl.ds(base(g, u) + d * span, minutes)
                acc[rows, :] += parts[u][d * minutes : (d + 1) * minutes]
        return carry

    lax.fori_loop(0, groups, group, 0)


def prepare_kernel(cap, order, links, chunks, row_step, me, *rest):
    sources, (ahead, mats_out, path, link, lag, slot, place, sems) = rest[:5], rest[5:]
    blocks = slot.shape[0]
    pairs = list(zip(sources[:4], (path, link, lag, slot)))
    step = blocks // chunks
    for c in range(chunks):
        rows = slice(c * step, blocks if c == chunks - 1 else (c + 1) * step)
        pairs.append((sources[4].at[rows], mats_out.at[rows]))
    copies = [pltpu.make_async_copy(a, b, sems.at[i]) for i, (a, b) in enumerate(pairs)]
    for copy in copies:
        copy.start()
    place[0] = 0
    for p, s in enumerate(order):
        place[s] = p * links
    for copy in copies[:4]:
        copy.wait()

    def entry(j, carry):
        ahead[j] = path[j] * row_step + HALO - lag[j]
        ahead[blocks + j] = place[lax.div(slot[j], cap) ^ me[0]] + link[j]
        return carry

    lax.fori_loop(0, blocks, entry, 0, unroll=16)
    for copy in copies[4:]:
        copy.wait()


def fill_table(cap, order, me, slot, table):
    first = len(order)
    for p, s in enumerate(order):
        table[p] = first + (me[0] ^ s) * cap
    for i in range((first + 1) * cap):
        table[first + i] = -1

    def entry(j, carry):
        table[first + slot[j]] = j
        return carry

    lax.fori_loop(0, slot.shape[0], entry, 0, unroll=16)


def slot_views(table, ahead, mats, cap, first, unroll, blank):
    def index(g, u):
        at = first * cap + g * unroll + u
        place = lax.div(at, cap)
        return table[table[place] + at - place * cap]

    def mat(g, u):
        return mats[jnp.maximum(index(g, u), 0)]

    def base(g, u):
        return ahead[jnp.maximum(index(g, u), 0)]

    def block(g, u):
        j = index(g, u)
        return jnp.where(j < 0, blank, ahead[mats.shape[0] + jnp.maximum(j, 0)])

    return mat, base, block


def forward_remote_kernel(days, links, group, ahead, flows, before, mats, *rest):
    outs, (wide, acc) = rest[:-2], rest[-2:]
    minutes, width = flows.shape[1], mats.shape[2]
    blocks = mats.shape[0]
    stage_flows(group, flows, before, wide, days, width)
    acc[...] = jnp.zeros_like(acc)
    unroll = step_of(blocks)
    forward_blocks(
        blocks // unroll,
        unroll,
        lambda g, u: mats[g * unroll + u],
        lambda g, u: ahead[g * unroll + u],
        lambda g, u: ahead[blocks + g * unroll + u],
        wide,
        acc,
        days,
        minutes,
    )
    for p, out in enumerate(outs):
        out[...] = acc[p * links : (p + 1) * links]


def local_views(path, link, lag, mats, unroll, row_step):
    return (
        lambda g, u: mats[g * unroll + u],
        lambda g, u: path[g * unroll + u] * row_step + HALO - lag[g * unroll + u],
        lambda g, u: link[g * unroll + u],
    )


def forward_local_kernel(
    days, cap, order, group, me, slot, path, link, lag, flows, before, mats, own, table, wide
):
    minutes, width = flows.shape[1], mats.shape[2]
    stage_flows(group, flows, before, wide, days, width)
    own[...] = jnp.zeros_like(own)
    unroll = step_of(mats.shape[0])
    views = local_views(path, link, lag, mats, unroll, days * (HALO + minutes))
    forward_blocks(mats.shape[0] // unroll, unroll, *views, wide, own, days, minutes)
    fill_table(cap, order, me, slot, table)


def residual_of(days, totals, counts, b, d):
    width, minutes = totals.shape[2], counts.shape[1]
    seen = counts[d, :, b * width : (b + 1) * width]
    weight = seen + 1.0
    return (totals[b, d * minutes : (d + 1) * minutes, :] - seen) / weight, weight


def signal_kernel(days, totals, counts, signal):
    minutes = counts.shape[1]
    for b in range(totals.shape[0]):
        for d in range(days):
            res, weight = residual_of(days, totals, counts, b, d)
            signal[b, d * minutes : (d + 1) * minutes, :] = (res / weight).astype(signal.dtype)


def residual_kernel(days, totals, counts, residual):
    width = totals.shape[2]
    for b in range(totals.shape[0]):
        for d in range(days):
            res, _ = residual_of(days, totals, counts, b, d)
            residual[d, :, b * width : (b + 1) * width] = res


def backward_local_kernel(days, path, link, lag, signal, mats, out):
    minutes = signal.shape[1] // days
    out[...] = jnp.zeros_like(out)
    unroll = step_of(mats.shape[0])
    mat, base, block = local_views(path, link, lag, mats, unroll, days * (HALO + minutes))
    backward_blocks(
        mats.shape[0] // unroll,
        unroll,
        mat,
        base,
        lambda g, u: signal[block(g, u)],
        out,
        days,
        minutes,
    )


def backward_remote_kernel(days, cap, first, end, links, table, ahead, mats, start, *rest):
    count = (end - first) * links
    signals, sources, rest = [], 0, list(rest)
    while sources < count:
        signals.append(rest.pop(0))
        sources += signals[-1].shape[0]
    out, early, everyone = rest[0], rest[1:-1], rest[-1]
    minutes = signals[0].shape[1] // days
    place = first * links
    for part in signals:
        everyone[place : place + part.shape[0]] = part[...]
        place += part.shape[0]
    blank = everyone.shape[0] - 1
    everyone[blank] = jnp.zeros(everyone.shape[1:], everyone.dtype)
    out[...] = start[...]
    span = HALO + minutes
    slots = (end - first) * cap
    unroll = step_of(slots)
    mat, base, block = slot_views(table, ahead, mats, cap, first, unroll, blank)
    backward_blocks(
        slots // unroll,
        unroll,
        mat,
        base,
        lambda g, u: everyone[block(g, u)],
        out,
        days,
        minutes,
    )
    if early:
        for i in range(early[0].shape[0]):
            early[0][i] = out[i * span : i * span + HALO, :]


def finish_kernel(days, groups, group, total, spill, flows, gradient, new_flows):
    minutes = flows.shape[1]
    width = total.shape[1]
    span = HALO + minutes
    real = jnp.where(group[0] < groups - 1, 1.0, 0.0)
    for p in range(flows.shape[2] // width):
        cols = slice(p * width, (p + 1) * width)
        for d in range(days):
            row = (p * days + d) * span + HALO
            own = total[row : row + minutes, :]
            keep = minutes - HALO
            late = own[keep:] + spill[p * days + d] * real
            for rows, grad in ((slice(0, keep), own[:keep]), (slice(keep, minutes), late)):
                gradient[d, rows, cols] = grad
                new_flows[d, rows, cols] = jnp.maximum(
                    flows[d, rows, cols].astype(jnp.float32) - RATE * grad, 0.0
                )


BACKWARD_COST = 500


def weight(nanoseconds):
    return pl.CostEstimate(
        flops=1_000_000 * nanoseconds, transcendentals=0, bytes_accessed=3_000 * nanoseconds
    )


SMEM = pl.BlockSpec(memory_space=pltpu.SMEM)
VMEM = pl.BlockSpec(memory_space=pltpu.VMEM)
HBM = pl.BlockSpec(memory_space=pltpu.HBM)


def kernel_call(body, scalars, arrays, out_shape, scratch=(), cost=None, outs=None):
    return pl.pallas_call(
        body,
        out_shape=out_shape,
        in_specs=[SMEM] * len(scalars) + [VMEM] * len(arrays),
        out_specs=outs or [VMEM] * len(out_shape),
        scratch_shapes=list(scratch),
        compiler_params=pltpu.CompilerParams(vmem_limit_bytes=40 * 1024 * 1024),
        cost_estimate=cost,
    )(*scalars, *arrays)


def per_device_dense(
    flows,
    counts,
    local_blocks,
    local_path,
    local_link,
    local_lag,
    remote_blocks,
    remote_path,
    remote_link,
    remote_lag,
    remote_slot,
):
    days, minutes, path_width = flows.shape
    width = local_blocks.shape[1]
    paths = path_width // width
    links = counts.shape[2] // width
    corridors = lax.axis_size("corr")
    remotes = remote_lag.shape[0]
    cap = (remotes + corridors - 2) // (corridors - 1)
    span = HALO + minutes
    through = list(range(2, corridors, 2))
    order = [s ^ 1 for s in reversed(through)] + [1] + through
    me = lax.axis_index("corr").astype(jnp.int32).reshape(1)
    group = lax.axis_index("tm").astype(jnp.int32).reshape(1)
    groups = lax.axis_size("tm")
    shape = jax.ShapeDtypeStruct
    piece = (links, days * minutes, width)
    wide = pltpu.VMEM((paths * days * span, width), jnp.float32)
    slots_shape = (len(order) * links + 1, days * minutes, width)
    local_index = (local_path, local_link, local_lag)

    before = lax.ppermute(flows, "tm", [(i, (i + 1) % groups) for i in range(groups)])
    fixed = (remote_path, remote_link, remote_lag, remote_slot, remote_blocks)
    ahead, remote_mats = pl.pallas_call(
        functools.partial(prepare_kernel, cap, order, links, CHUNKS, days * span),
        out_shape=[
            shape((2 * remotes,), jnp.int32),
            shape(remote_blocks.shape, remote_blocks.dtype),
        ],
        in_specs=[SMEM] + [HBM] * len(fixed),
        out_specs=[SMEM, VMEM],
        scratch_shapes=[pltpu.SMEM(remote_slot.shape, jnp.int32) for _ in fixed[1:]]
        + [pltpu.SMEM((corridors,), jnp.int32), pltpu.SemaphoreType.DMA((len(fixed) - 1 + CHUNKS,))],
        compiler_params=pltpu.CompilerParams(vmem_limit_bytes=40 * 1024 * 1024),
    )(me, *(pltpu.with_memory_space_constraint(i, pltpu.HBM) for i in fixed))

    def exchanged(part, s):
        return lax.ppermute(part, "corr", [(i, i ^ s) for i in range(corridors)])

    f32 = jnp.float32
    outgoing = kernel_call(
        functools.partial(forward_remote_kernel, days, links),
        (group, ahead),
        (flows, before, remote_mats),
        [shape(piece, f32) for _ in order],
        [wide, pltpu.VMEM((len(order) * links, *piece[1:]), f32)],
    )
    count = len(through)
    crossed = [exchanged(part.astype(WIRE), 1) for part in outgoing[:count]]
    crossed[0], near = lax.optimization_barrier((crossed[0], outgoing[count].astype(WIRE)))
    near = exchanged(near, 1)
    received = []
    for s, kept in reversed(list(zip(through, outgoing[count + 1 :]))):
        met = crossed[order.index(s ^ 1)].astype(f32)
        received.append(exchanged((kept + met).astype(WIRE), s))
    received.append(near)
    own, table = kernel_call(
        functools.partial(forward_local_kernel, days, cap, order),
        (group, me, remote_slot, *local_index),
        (flows, before, local_blocks),
        [shape(piece, f32), shape((len(order) + corridors * cap,), jnp.int32)],
        [wide],
        outs=[VMEM, SMEM],
    )
    totals = functools.reduce(jnp.add, [p.astype(f32) for p in received], own)
    (signal,) = kernel_call(
        functools.partial(signal_kernel, days),
        (),
        (totals, counts),
        [shape(piece, jnp.bfloat16)],
    )
    arrived = {s: exchanged(signal, s) for s in through}
    rows = [shape((paths * days * span, width), f32)]
    (total,) = kernel_call(
        functools.partial(backward_local_kernel, days),
        local_index,
        (signal, local_blocks),
        rows,
    )
    arrived[through[-1]], total = lax.optimization_barrier((arrived[through[-1]], total))
    for s in through[1:]:
        arrived[s ^ 1] = exchanged(arrived[s], 1)
    passed = exchanged(jnp.concatenate([arrived[through[0]], signal], axis=0), 1)
    edge = shape((paths * days, HALO, width), f32)
    for first, end, parts, made in (
        (count + 1, len(order), [arrived[s] for s in through], rows),
        (0, count + 1, [*(arrived[s] for s in order[: count - 1]), passed], [*rows, edge]),
    ):
        total, *early = kernel_call(
            functools.partial(backward_remote_kernel, days, cap, first, end, links),
            (table, ahead),
            (remote_mats, total, *parts),
            made,
            [pltpu.VMEM(slots_shape, jnp.bfloat16)],
            cost=weight(BACKWARD_COST) if first else None,
        )
    route = [(i, (i - 1) % groups) for i in range(groups)]
    spill = lax.ppermute(early[0].astype(WIRE), "tm", route).astype(f32)
    totals, total = lax.optimization_barrier((totals, total))
    (link_residual,) = kernel_call(
        functools.partial(residual_kernel, days),
        (),
        (totals, counts),
        [shape(counts.shape, f32)],
    )
    gradient, new_flows = kernel_call(
        functools.partial(finish_kernel, days, groups),
        (group,),
        (total, spill, flows),
        [shape(flows.shape, f32)] * 2,
    )
    return (link_residual, gradient, new_flows)


def per_device(*args):
    counts, blocks, lags = args[1], args[2], args[9]
    corridors = lax.axis_size("corr")
    links = counts.shape[2] // blocks.shape[1]
    cap = (lags.shape[0] + corridors - 2) // (corridors - 1)
    if cap >= links and corridors >= 4 and corridors & (corridors - 1) == 0:
        return per_device_dense(*args)
    return per_device_slots(*args)


def solution(mesh):
    placed = (
        P(None, "tm", "corr"),
        P(None, "tm", "corr"),
        P("corr", None, None),
        P("corr"),
        P("corr"),
        P("corr"),
        P("corr", None, None),
        P("corr"),
        P("corr"),
        P("corr"),
        P("corr"),
    )
    return jax.shard_map(
        per_device,
        mesh=mesh,
        in_specs=placed,
        out_specs=(P(None, "tm", "corr"), P(None, "tm", "corr"), P(None, "tm", "corr")),
        check_vma=False,
    )
```
